32 devices in a mesh: dp: 8 (over z, x), pair: 4 (over y, core).
Axes of the slice: x: 2, y: 2, z: 4, core: 2. Of those that a mesh axis runs over, the one named last changes fastest.
Arguments:
- patches: bfloat16 [128, 196, 768], P(('dp', 'pair')), may hold values from -6 to 6
- patch_order: int32 [128, 196], P(('dp', 'pair')), may hold values from 0 to 195, each once within a row
- counts: int32 [128], P(('dp', 'pair')), may hold values from 40 to 60
- master: float32 [11608064], P(('dp', 'pair'))
- moment1: float32 [11608064], P(('dp', 'pair')), may hold values from -1.4901161e-07 to 1.4901161e-07
- moment2: float32 [11608064], P(('dp', 'pair')), may hold values from 4.1350566e-16 to 1.6367932e-15
- block_rates: float32 [2], replicated, may hold values from 0.01 to 0.04
- clip_limit: float32 [1], replicated, may hold values from 0.0002 to 0.0004
- step_count: int32 [1], replicated, may hold values from 1 to 20
Outputs:
- loss: float32 [1], replicated
- grad_norm: float32 [1], replicated
- moment1_new: float32 [11608064], P(('dp', 'pair'))
- moment2_new: float32 [11608064], P(('dp', 'pair'))
- master_new: float32 [11608064], P(('dp', 'pair'))
The draws below stay inside these ranges and needn't reach their ends.
Inputs may be any that keep to these rules, and one draw needn't show every extreme that they name: `patch_order`: each row is a permutation; the first count entries name the image's visible patches.
All inputs are finite; a program needn't handle non-finite values.
Results may differ from the reference program's by a relative error of at most 0.00035.
The reference program's roundings to bfloat16 on the way count: a program that leaves them out, or rounds other values in their place, can miss the bound.
Values may be sent and summed in bfloat16 or wider, within the bound.
A program may use at most 256 MiB of HBM per device.

```python
import math
import jax
import jax.numpy as jnp
from jax import lax

PIX = 768
HEADS = 12
F = 3072
DHEADS = 16
FD = 2048
GRID = 14
KEEP = 64
IMG_DEV = 4
D = 768
DD = 512
PATCHES = 196
IMAGES = 128
ENC_PARAMS = 7672320
PARAMS = 11608064
FLAT = 11608064
N_DP = 8
N_PAIR = 4


def draw_master(key, part):
    row_spread = jnp.array([0.2, 0.3, 0.2, 0.3, 0.2, 0.3], jnp.float32)[:, None]
    row_center = jnp.array([1.0, 0.0, 1.0, 0.0, 1.0, 0.0], jnp.float32)[:, None]
    layout = [((PIX, D), PIX ** (-0.5), 0.0), ((D, 3 * D), D ** (-0.5), 0.0), ((D, D), 6.0 * D ** (-0.5), 0.0), ((D, F), D ** (-0.5), 0.0), ((F, D), F ** (-0.5), 0.0), ((6, D), row_spread, row_center), ((D, DD), D ** (-0.5), 0.0), ((DD, 3 * DD), DD ** (-0.5), 0.0), ((DD, DD), 10.0 * DD ** (-0.5), 0.0), ((DD, FD), DD ** (-0.5), 0.0), ((FD, DD), FD ** (-0.5), 0.0), ((DD, PIX), DD ** (-0.5), 0.0), ((6, DD), row_spread, row_center), ((1, DD), 1.0, 0.0)]
    pieces = []
    for index, (shape, spread, center) in enumerate(layout):
        sub_key = jax.random.fold_in(key, index)
        base = jax.random.normal(sub_key, shape, jnp.float32)
        pieces.append((center + spread * base).reshape(-1))
    pieces.append(0.02 * jax.random.normal(jax.random.fold_in(key, 99), (FLAT - PARAMS,), jnp.float32))
    return jnp.concatenate(pieces)


def plant(values, key, smallest, largest):
    index_at = [jax.random.randint(jax.random.fold_in(key, axis), (), 0, length) for axis, length in enumerate(values.shape)]
    longest = values.shape.index(max(values.shape))
    beside = index_at[:longest] + [(index_at[longest] + 1) % values.shape[longest]] + index_at[longest + 1:]
    return values.at[tuple(index_at)].set(smallest).at[tuple(beside)].set(largest)


def steps_of(own_key, shape, cuts, low, largest):
    level = 1.0
    for axis_at, blocks in cuts:
        draws = jax.random.uniform(jax.random.fold_in(jax.random.fold_in(own_key, 6), axis_at), (blocks,), jnp.float32, low / len(cuts), largest / len(cuts))
        level = level * jnp.repeat(jnp.exp(draws), shape[axis_at] // blocks).reshape((-1,) + (1,) * (len(shape) - 1 - axis_at))
    return level


def centred(own_key, shape, scale, limit, cuts=(), kind=jnp.bfloat16):
    values = jax.random.normal(own_key, shape, jnp.float32) * scale
    if len(cuts) > 0:
        values = steps_of(own_key, shape, cuts, -0.22, 0.18) * values
    return jnp.clip(values, min=-limit, max=limit).astype(kind)


def setup_inputs(seed: int = 0) -> dict:
    key_of = jax.random.split(jax.random.key(seed), 10)
    return {
        "patches": centred(key_of[0], (IMAGES, PATCHES, PIX), 1.0, 6.0, ((0, 32),)),
        "patch_order": jax.vmap(lambda own: jax.random.permutation(own, PATCHES))(jax.random.split(key_of[1], IMAGES)).reshape((IMAGES, PATCHES)).astype(jnp.int32),
        "counts": plant(jax.random.randint(key_of[2], (IMAGES,), KEEP * 5 // 8, KEEP * 15 // 16 + 1), jax.random.fold_in(key_of[2], 1), KEEP * 5 // 8, (KEEP * 15 // 16 + 1) - 1).astype(jnp.int32),
        "master": draw_master(jax.random.fold_in(key_of[9], 71), 0),
        "moment1": centred(key_of[4], (FLAT,), (0.000033 / FLAT ** 0.5), 1.4901161193847656e-07, ((0, 32),), jnp.float32),
        "moment2": jnp.clip(jnp.exp(math.log(1.6367932323844091e-15) - 1.375823 * jax.random.uniform(key_of[5], (FLAT,), jnp.float32) ** steps_of(key_of[5], (FLAT,), ((0, 32),), -0.2, 0.2)), 4.135056559213476e-16, 1.6367932323844091e-15),
        "block_rates": jnp.clip(jnp.exp(jax.random.uniform(key_of[6], (2,), jnp.float32, math.log(0.01), math.log(0.04))), 0.01, 0.04),
        "clip_limit": jnp.clip(jnp.exp(jax.random.uniform(key_of[7], (1,), jnp.float32, math.log(0.0002), math.log(0.0004))), 0.0002, 0.0004),
        "step_count": jax.random.randint(key_of[8], (1,), 1, 21).astype(jnp.int32),
    }


HIGH = lax.Precision.HIGHEST
NORM_EPS = 1e-06
ADAM_EPS = 1e-08
BETA_ONE = 0.9
BETA_TWO = 0.95
DECAY = 0.05
NEG_FILL = -1000000000.0

@jax.custom_vjp
def low(v):
    return lax.optimization_barrier(v.astype(jnp.bfloat16)).astype(jnp.float32)

@jax.custom_vjp
def low_back(v):
    return v

def low_keep(v):
    return (low(v), None)

def low_pass(kept, grad):
    return (grad,)

def back_keep(v):
    return (v, None)

def back_low(kept, grad):
    return (low(grad),)
low.defvjp(low_keep, low_pass)
low_back.defvjp(back_keep, back_low)

def shapes():
    return [(PIX, D), (D, 3 * D), (D, D), (D, F), (F, D), (6, D), (D, DD), (DD, 3 * DD), (DD, DD), (DD, FD), (FD, DD), (DD, PIX), (6, DD), (1, DD)]

def unpack(flat):
    parts = []
    offset = 0
    for shape in shapes():
        amount = shape[0] * shape[1]
        parts.append(flat[offset:offset + amount].reshape(shape))
        offset += amount
    return parts

def dense(left, right):
    return jnp.einsum('bsi,ij->bsj', left, right, precision=HIGH)

def norm(x, gain, shift):
    centered = x - lax.optimization_barrier(jnp.mean(x, axis=-1, keepdims=True))
    return centered * lax.rsqrt(lax.optimization_barrier(jnp.mean(centered * centered, axis=-1, keepdims=True)) + NORM_EPS) * gain + shift

def positions(width):
    index = jnp.arange(PATCHES)
    quarter = width // 4
    freq = 10000.0 ** (-jnp.arange(quarter).astype(jnp.float32) / quarter)
    row = (index // GRID).astype(jnp.float32)[:, None] * freq[None, :]
    column = (index % GRID).astype(jnp.float32)[:, None] * freq[None, :]
    return jnp.concatenate([jnp.sin(row), jnp.cos(row), jnp.sin(column), jnp.cos(column)], axis=1)

def block(x, triple_w, proj_w, up_w, down_w, gains, heads, bias):
    batch, length, width = x.shape
    size = width // heads
    entry = low(norm(x, gains[0], gains[1]))
    triple = low(low_back(dense(entry, triple_w)))
    query, keys, values = [piece.reshape(batch, length, heads, size) for piece in jnp.split(triple, 3, axis=-1)]
    scores = low_back(jnp.einsum('bqhd,bkhd->bhqk', query, keys, precision=HIGH) * size ** (-0.5)) + bias[:, None, None, :]
    attend = jax.nn.softmax(scores, axis=-1)
    mixed = low(low_back(jnp.einsum('bhqk,bkhd->bqhd', low(attend), values, precision=HIGH))).reshape(batch, length, width)
    middle = x + low_back(dense(mixed, proj_w))
    inner = low(norm(middle, gains[2], gains[3]))
    hidden = low_back(dense(inner, up_w))
    return middle + low_back(dense(low(jax.nn.gelu(hidden, approximate=False)), down_w))

def group_loss(parts, patches, patch_order, counts):
    embed, enc_triple, enc_proj, enc_up, enc_down, enc_norms, dec_embed, dec_triple, dec_proj, dec_up, dec_down, head, dec_norms, token = parts
    slots = patch_order[:, :KEEP]
    live = jnp.arange(KEEP)[None, :] < counts[:, None]
    seen = jnp.take_along_axis(patches, slots[:, :, None], axis=1)
    x = low_back(dense(seen, embed)) + positions(D)[slots]
    enc_bias = jnp.where(live, 0.0, NEG_FILL).astype(x.dtype)
    x = block(x, enc_triple, enc_proj, enc_up, enc_down, enc_norms, HEADS, enc_bias)
    encoded = low(norm(x, enc_norms[4], enc_norms[5]))
    entering = low_back(dense(encoded, dec_embed))
    rank = jnp.argsort(patch_order, axis=1).astype(jnp.int32)
    shown = rank < counts[:, None]
    picked = jnp.take_along_axis(entering, jnp.minimum(rank, KEEP - 1)[:, :, None], axis=1)
    y = jnp.where(shown[:, :, None], picked, token[0]) + positions(DD)[None]
    y = block(y, dec_triple, dec_proj, dec_up, dec_down, dec_norms, DHEADS, jnp.zeros(shown.shape, y.dtype))
    final = low(norm(y, dec_norms[4], dec_norms[5]))
    pred = low_back(dense(final, head))
    centered = patches - lax.optimization_barrier(jnp.mean(patches, axis=-1, keepdims=True))
    target = centered * lax.rsqrt(lax.optimization_barrier(jnp.mean(centered * centered, axis=-1, keepdims=True)) + NORM_EPS)
    error = lax.optimization_barrier(jnp.mean((pred - target) ** 2, axis=-1))
    return jnp.sum(jnp.where(shown, 0.0, error))

def reference(patches, patch_order, counts, master, moment1, moment2, block_rates, clip_limit, step_count):
    groups = N_DP * N_PAIR
    data = (patches.astype(jnp.float32).reshape(groups, IMG_DEV, PATCHES, PIX), patch_order.reshape(groups, IMG_DEV, PATCHES), counts.reshape(groups, IMG_DEV))
    masked = jnp.sum(PATCHES - counts).astype(jnp.float32)
    parts = unpack(master.astype(jnp.bfloat16).astype(jnp.float32))
    checked = jax.checkpoint(group_loss)

    def total(params):

        def add(carry, group):
            return (carry + checked(params, group[0], group[1], group[2]), None)
        summed, _ = lax.scan(add, jnp.zeros((), jnp.float32), data)
        return summed / masked
    loss, pullback = jax.vjp(total, parts)
    grads = pullback(jnp.ones((), loss.dtype))[0]
    flat = jnp.concatenate([grad.reshape(-1) for grad in grads] + [jnp.zeros((FLAT - PARAMS,), jnp.float32)])
    grad_norm = jnp.sqrt(jnp.sum(flat * flat))
    clipped = flat * (clip_limit[0] / (grad_norm + NORM_EPS))
    first = BETA_ONE * moment1 + (1.0 - BETA_ONE) * clipped
    second = BETA_TWO * moment2 + (1.0 - BETA_TWO) * clipped * clipped
    steps_done = step_count[0].astype(jnp.float32)
    rate = jnp.where(jnp.arange(FLAT) < ENC_PARAMS, block_rates[0], block_rates[1])
    update = first / (1.0 - BETA_ONE ** steps_done) / (jnp.sqrt(second / (1.0 - BETA_TWO ** steps_done)) + ADAM_EPS)
    master_new = master - rate * (update + DECAY * master)
    return (loss.reshape(1), grad_norm.reshape(1), first, second, master_new)
```

```python
import functools

import jax
import jax.numpy as jnp
from jax import lax
from jax.experimental import pallas as pl
from jax.experimental.pallas import tpu as pltpu
from jax.sharding import PartitionSpec as P

MESH = pl.DeviceIdType.MESH
LANES = 128
TILE = 16 * LANES


def place():
    dp, pair = lax.axis_index("dp"), lax.axis_index("pair")
    return dp // 2, dp % 2, pair // 2, pair % 2


def slot_of(z, x, y, c):
    return (z * 2 + x) * 4 + y * 2 + c


def partners(z, x, y, c):
    return {
        "x": {"dp": z * 2 + (1 - x)},
        "y": {"pair": (1 - y) * 2 + c},
        "c": {"pair": y * 2 + (1 - c)},
        "up": {"dp": (z + 1) * 2 + x},
        "down": {"dp": (z - 1) * 2 + x},
    }


def greet(n_z, z, to):
    barrier = pltpu.get_barrier_semaphore()
    for name in ("x", "y", "c"):
        pl.semaphore_signal(barrier, inc=1, device_id=to[name], device_id_type=MESH)

    @pl.when(z < n_z - 1)
    def _():
        pl.semaphore_signal(barrier, inc=1, device_id=to["up"], device_id_type=MESH)

    @pl.when(z > 0)
    def _():
        pl.semaphore_signal(barrier, inc=1, device_id=to["down"], device_id_type=MESH)

    pl.semaphore_wait(barrier, 3 + jnp.where(z < n_z - 1, 1, 0) + jnp.where(z > 0, 1, 0))


def gather_kernel(n_z, slab_ref, out_ref, own_sem, send_sem, recv_sem):
    half = slab_ref.shape[0] // 2
    z, x, y, c = place()
    to = partners(z, x, y, c)
    me = slot_of(z, x, y, c)
    local = pltpu.make_async_copy(slab_ref, out_ref.at[me], own_sem)
    local.start()
    greet(n_z, z, to)
    local.wait()
    pending = []

    def copy(slot, part, name, index):
        rows = pl.ds(part * half, half)
        return pltpu.make_async_remote_copy(
            out_ref.at[slot, rows],
            out_ref.at[slot, rows],
            send_sem.at[index],
            recv_sem.at[slot, part],
            device_id=to[name],
            device_id_type=MESH,
        )

    def send(slot, part, name, where):
        index = len(pending)
        pending.append((slot, part, name, index, where))
        if where is None:
            copy(slot, part, name, index).start()
        else:
            pl.when(where)(lambda: copy(slot, part, name, index).start())

    def arrived(slot, part, where):
        if where is None:
            copy(slot, part, "c", 0).wait_recv()
        else:
            pl.when(where)(lambda: copy(slot, part, "c", 0).wait_recv())

    def both(one, two):
        return two if one is None else jnp.logical_and(one, two)

    levels = [[(z, None, None)]]
    for t in range(1, n_z):
        levels.append([(z - t, z >= t, "up"), (z + t, z + t < n_z, "down")])

    def first(level):
        for zz, where, onward in level:
            slot = slot_of(zz, x, y, c)
            for part in (0, 1):
                if onward is None:
                    send(slot, part, "up", z < n_z - 1)
                    send(slot, part, "down", z > 0)
                else:
                    arrived(slot, part, where)
                    more = z < n_z - 1 if onward == "up" else z > 0
                    send(slot, part, onward, both(where, more))
            for part in (0, 1):
                send(slot, part, ("x", "y")[part], where)
            for part in (0, 1):
                send(slot, part, ("y", "x")[part], where)
            for part in (0, 1):
                send(slot, part, "c", where)

    def second(level):
        for zz, where, _ in level:
            for part, slot in ((0, slot_of(zz, 1 - x, y, c)), (1, slot_of(zz, x, 1 - y, c))):
                arrived(slot, part, where)
                send(slot, part, ("y", "x")[part], where)
                send(slot, part, "c", where)

    def third(level):
        for zz, where, _ in level:
            for part, ox, oy in ((0, x, 1 - y), (1, 1 - x, y), (0, 1 - x, 1 - y), (1, 1 - x, 1 - y)):
                slot = slot_of(zz, ox, oy, c)
                arrived(slot, part, where)
                send(slot, part, "c", where)

    for t in range(n_z + 2):
        if t < n_z:
            first(levels[t])
        if 1 <= t < n_z + 1:
            second(levels[t - 1])
        if t >= 2:
            third(levels[t - 2])
    for level in levels:
        for zz, where, _ in level:
            for ox in (0, 1):
                for oy in (0, 1):
                    for part in (0, 1):
                        arrived(slot_of(zz, ox, oy, 1 - c), part, where)
    for slot, part, name, index, where in pending:
        if where is None:
            copy(slot, part, name, index).wait_send()
        else:
            pl.when(where)(lambda s=slot, p=part, n=name, i=index: copy(s, p, n, i).wait_send())


def gather(slab, n_dp, n_pair):
    n_z = n_dp // 2
    n = n_dp * n_pair
    sends = (2 * n_z - 1) * 16 + 8
    return pl.pallas_call(
        functools.partial(gather_kernel, n_z),
        name="gather",
        out_shape=jax.ShapeDtypeStruct((n,) + slab.shape, slab.dtype),
        in_specs=[pl.BlockSpec(memory_space=pl.ANY)],
        out_specs=pl.BlockSpec(memory_space=pl.ANY),
        scratch_shapes=[
            pltpu.SemaphoreType.DMA,
            pltpu.SemaphoreType.DMA((sends,)),
            pltpu.SemaphoreType.DMA((n, 2)),
        ],
        compiler_params=pltpu.CompilerParams(collective_id=0, has_side_effects=True),
    )(slab)


PIX, HEADS, F, DHEADS, FD, GRID, KEEP, D, DD, PATCHES = 768, 12, 3072, 16, 2048, 14, 64, 768, 512, 196
SHAPES = [(PIX, D), (D, 3 * D), (D, D), (D, F), (F, D), (6, D), (D, DD), (DD, 3 * DD), (DD, DD), (DD, FD), (FD, DD), (DD, PIX), (7, DD)]
SMALL = (5, 12)
ENC_PARAMS = 7672320
MB = 1 << 20
CELL = 8 * LANES
BLOCK = 96


def make_entries():
    entries, row, tile = [], 0, 0
    for number, (rows, width) in enumerate(SHAPES):
        lines = rows * width // LANES
        cols = 1 if number in SMALL else width // LANES
        groups = -(-lines // (8 * cols))
        entries.append((row, lines, cols, tile, groups))
        row += lines
        tile += groups * cols
    return entries, row, tile


ENTRIES, ROWS, TILES = make_entries()
MARGIN = 8 * max(cols for _, _, cols, _, _ in ENTRIES)


def first_tile(share, k):
    lo = share * k
    total = 0
    for row, lines, cols, tile, _ in ENTRIES:
        inside = jnp.logical_and(lo >= row * LANES, lo < (row + lines) * LANES)
        total = total + jnp.where(inside, tile + (lo - row * LANES) // (CELL * cols) * cols, 0)
    return total


def ranges(share, n):
    found = []
    for k in range(n):
        lo, hi = share * k, share * (k + 1)
        spans = []
        for row, lines, cols, tile, _ in ENTRIES:
            low, high = max(lo, row * LANES), min(hi, (row + lines) * LANES)
            if low < high:
                size = CELL * cols
                spans.append((tile + (low - row * LANES) // size * cols, tile + -(-(high - row * LANES) // size) * cols))
        found.append((spans[0][0], spans[-1][1]))
    return found


def slab_tiles(share, n):
    longest = max(b - a for a, b in ranges(share, n))
    return -(-longest // 24) * 24


def line_span(share, k):
    return share * k // LANES, (share * (k + 1) + LANES - 1) // LANES


def tiled(share, k, body):
    lo, hi = line_span(share, k)
    begin = first_tile(share, k)
    for number in SMALL + tuple(i for i in range(len(ENTRIES)) if i not in SMALL):
        row, lines, cols, tile, _ = ENTRIES[number]
        low = jnp.maximum(lo, row) - row
        high = jnp.minimum(hi, row + lines) - row
        size = 8 * cols

        def group(g, _, row=row, cols=cols, tile=tile, size=size):
            body(row + g * size - lo + MARGIN, tile + g * cols - begin, cols)
            return 0

        lax.fori_loop(jnp.where(low < high, low // size, 0), jnp.where(low < high, (high + size - 1) // size, 0), group, 0)


def tile_kernel(share, n_pair, lines_ref, extra_ref, out_ref, wide):
    k = lax.axis_index("dp") * n_pair + lax.axis_index("pair")
    rows = lines_ref.shape[0]
    wide[0:MARGIN, :] = jnp.zeros((MARGIN, LANES), jnp.float32)
    wide[MARGIN + rows :, :] = jnp.zeros((wide.shape[0] - MARGIN - rows, LANES), jnp.float32)
    wide[MARGIN : MARGIN + rows, :] = lines_ref[...]

    def body(line, tile, cols):
        for col in range(cols):
            out_ref[tile + col] = wide[pl.ds(line + col, 8, stride=cols), :].astype(out_ref.dtype)

    tiled(share, k, body)
    out_ref[out_ref.shape[0] - 2] = extra_ref[...].astype(out_ref.dtype)


def wide_rows(rows):
    return -(-(rows + 2 * MARGIN) // 8) * 8


def to_tiles(lines, extra, share, n, n_pair):
    rows = lines.shape[0]
    count = slab_tiles(share, n) + 2
    spec = pl.BlockSpec(memory_space=pltpu.VMEM)
    return pl.pallas_call(
        functools.partial(tile_kernel, share, n_pair),
        name="to_tiles",
        out_shape=jax.ShapeDtypeStruct((count, 8, LANES), jnp.bfloat16),
        in_specs=[spec, spec],
        out_specs=spec,
        scratch_shapes=[pltpu.VMEM((wide_rows(rows), LANES), jnp.float32)],
    )(lines, extra)


def line_kernel(share, n_pair, slab_ref, out_ref, wide):
    k = lax.axis_index("dp") * n_pair + lax.axis_index("pair")

    def body(line, tile, cols):
        for col in range(cols):
            wide[pl.ds(line + col, 8, stride=cols), :] = slab_ref[pl.ds(pl.multiple_of((tile + col) * 8, 8), 8), :]

    tiled(share, k, body)
    out_ref[...] = wide[MARGIN : MARGIN + out_ref.shape[0], :]


def to_lines(slab, rows, share, n_pair):
    spec = pl.BlockSpec(memory_space=pltpu.VMEM)
    return pl.pallas_call(
        functools.partial(line_kernel, share, n_pair),
        name="to_lines",
        out_shape=jax.ShapeDtypeStruct((rows, LANES), jnp.float32),
        in_specs=[spec],
        out_specs=spec,
        scratch_shapes=[pltpu.VMEM((wide_rows(rows), LANES), jnp.float32)],
    )(slab)


def pieces(share, n):
    spans = ranges(share, n)
    shared = [spans[k][1] > spans[k + 1][0] for k in range(n - 1)]
    plain, seams = [], []
    for number, (_, _, cols, tile, groups) in enumerate(ENTRIES):
        end = tile + groups * cols
        for k, (a, b) in enumerate(spans):
            low, high = max(a, tile), min(b, end)
            if low >= high:
                continue
            inner_low, inner_high = low, high
            if k > 0 and spans[k - 1][1] > low:
                inner_low = spans[k - 1][1]
            if k < n - 1 and spans[k + 1][0] < high:
                inner_high = spans[k + 1][0]
                seams.append((number, k, inner_high, high))
            if inner_low < inner_high:
                plain.append((number, k, inner_low, inner_high))
    return spans, plain, seams


def assemble_kernel(share, n, slots_ref, *refs):
    outs = refs[: len(ENTRIES)]
    whole, right, plain_sem, left_sem, right_sem, out_sem = refs[len(ENTRIES) :]
    spans, plain, seams = pieces(share, n)
    waits = [[] for _ in ENTRIES]
    for i, (number, k, low, high) in enumerate(plain):
        copy = pltpu.make_async_copy(slots_ref.at[k, pl.ds(low - spans[k][0], high - low)], whole.at[pl.ds(low, high - low)], plain_sem.at[i])
        copy.start()
        waits[number].append(copy)
    for i, (number, k, low, high) in enumerate(seams):
        one = pltpu.make_async_copy(slots_ref.at[k, pl.ds(low - spans[k][0], high - low)], whole.at[pl.ds(low, high - low)], left_sem.at[i])
        two = pltpu.make_async_copy(
            slots_ref.at[k + 1, pl.ds(low - spans[k + 1][0], high - low)], right.at[i, pl.ds(0, high - low)], right_sem.at[i]
        )
        one.start()
        two.start()
        waits[number] += [one, two]
    ended = []
    for number, (_, _, cols, tile, groups) in enumerate(ENTRIES):
        for copy in waits[number]:
            copy.wait()
        for i, (owner, k, low, high) in enumerate(seams):
            if owner == number:
                total = whole[low:high].astype(jnp.float32) + right[i, 0 : high - low].astype(jnp.float32)
                whole[low:high] = total.astype(jnp.bfloat16)
        copy = pltpu.make_async_copy(whole.at[pl.ds(tile, groups * cols)], outs[number], out_sem.at[number])
        copy.start()
        ended.append(copy)
    for copy in ended:
        copy.wait()


def assemble(slots, share):
    n = slots.shape[0]
    _, plain, seams = pieces(share, n)
    anyspec = pl.BlockSpec(memory_space=pl.ANY)
    dma = pltpu.SemaphoreType.DMA
    return pl.pallas_call(
        functools.partial(assemble_kernel, share, n),
        name="assemble",
        out_shape=[jax.ShapeDtypeStruct((groups * cols, 8, LANES), jnp.bfloat16) for _, _, cols, _, groups in ENTRIES],
        in_specs=[anyspec],
        out_specs=[anyspec] * len(ENTRIES),
        scratch_shapes=[
            pltpu.VMEM((TILES, 8, LANES), jnp.bfloat16),
            pltpu.VMEM((len(seams), MARGIN // 8, 8, LANES), jnp.bfloat16),
            dma((len(plain),)),
            dma((len(seams),)),
            dma((len(seams),)),
            dma((len(ENTRIES),)),
        ],
        compiler_params=pltpu.CompilerParams(vmem_limit_bytes=40 * MB),
    )(slots)


def matrix(tiles_, number):
    rows, width = SHAPES[number]
    cols = width // LANES
    return tiles_.reshape(rows // 8, cols, 8, LANES).transpose(0, 2, 1, 3).reshape(rows, width)


def matrix_tiles(value):
    rows, width = value.shape
    cols = width // LANES
    return value.reshape(rows // 8, 8, cols, LANES).transpose(0, 2, 1, 3).reshape(rows * cols, LANES)


def reduce_kernel(n_z, share, grad_ref, out_ref, sib_ref, gbuf, rbuf, keep, q1s, q1r, q2s, q2r, zs, zr, t1s, t1r, t2s, t2r, tzs, tzr, sib_sem, load_sem, s1_sem, s2_sem, z_sem):
    z, x, y, c = place()
    to = partners(z, x, y, c)
    rows = out_ref.shape[0]
    half = rows // 2
    count = half // BLOCK

    def start_of(k):
        return pl.multiple_of(first_tile(share, k) * 8, 8)

    def order(j):
        low = z < n_z // 2
        far = jnp.where(low, n_z - 1 - j, j)
        moved = jnp.where(low, jnp.where(far > z, far, far - 1), jnp.where(far < z, far, far + 1))
        return jnp.where(j == n_z - 1, z, moved)

    def sibling(j, xx, yy, core):
        k = slot_of(order(j), xx, yy, core)
        return pltpu.make_async_remote_copy(
            grad_ref.at[pl.ds(start_of(k), rows)],
            sib_ref.at[j, xx * 2 + yy],
            sib_sem.at[0, j, xx * 2 + yy],
            sib_sem.at[1, j, xx * 2 + yy],
            device_id=to["c"],
            device_id_type=MESH,
        )

    def loads(j, s, q):
        k = slot_of(order(j), q // 2, q % 2, c)
        return (
            pltpu.make_async_copy(grad_ref.at[pl.ds(start_of(k), rows)], gbuf.at[s, q], load_sem.at[0, s, q]),
            pltpu.make_async_copy(sib_ref.at[j, q], rbuf.at[s, q], load_sem.at[1, s, q]),
        )

    def load(j):
        s = lax.rem(j, 2)
        for q in range(4):
            sibling(j, q // 2, q % 2, 1 - c).wait_recv()
            for one in loads(j, s, q):
                one.start()

    def pack(value, q_ref, t_ref, b):
        top = jnp.max(jnp.abs(value), axis=0, keepdims=True)
        inverse = jnp.where(top > 1e-30, 32767.0 / jnp.maximum(top, 1e-30), 0.0)
        q_ref[pl.ds(pl.multiple_of(b * BLOCK, BLOCK), BLOCK), :] = jnp.round(value * inverse).astype(jnp.int32).astype(jnp.int16)
        t_ref[pl.ds(b, 1), :] = top * (1.0 / 32767.0)

    def unpack(q_ref, t_ref, b):
        return q_ref[pl.ds(pl.multiple_of(b * BLOCK, BLOCK), BLOCK), :].astype(jnp.int32).astype(jnp.float32) * t_ref[pl.ds(b, 1), :]

    def each(body):
        def one(b, _):
            body(b)
            return 0

        lax.fori_loop(0, count, one, 0)

    def own(s, q, part, b):
        at = pl.ds(pl.multiple_of(part * half + b * BLOCK, BLOCK), BLOCK)
        return gbuf[s, q, at, :] + rbuf[s, q, at, :]

    def message(qs, ts, qr, tr, sem, name):
        return (
            pltpu.make_async_remote_copy(qs, qr, sem.at[0, 0], sem.at[0, 1], device_id=to[name], device_id_type=MESH),
            pltpu.make_async_remote_copy(ts, tr, sem.at[1, 0], sem.at[1, 1], device_id=to[name], device_id_type=MESH),
        )

    def first_message(j, part, other):
        i = part * 2 + other
        return message(q1s.at[j, i], t1s.at[j, i], q1r.at[j, i], t1r.at[j, i], s1_sem.at[j, i], ("x", "y")[part])

    def second_message(j, part):
        return message(q2s.at[j, part], t2s.at[j, part], q2r.at[j, part], t2r.at[j, part], s2_sem.at[j, part], ("y", "x")[part])

    def z_message(zz, part, name):
        d = 0 if name == "up" else 1
        return message(zs.at[zz, part], tzs.at[zz, part], zr.at[d, zz, part], tzr.at[d, zz, part], z_sem.at[d, zz, part], name)

    def quarter(part, other, mine):
        if part == 0:
            return (x if mine else 1 - x) * 2 + other
        return other * 2 + (y if mine else 1 - y)

    def stage_one(j):
        s = lax.rem(j, 2)
        for q in range(4):
            for one in loads(j, s, q):
                one.wait()
        for part in (0, 1):
            for other in (0, 1):
                q = quarter(part, other, False)
                i = part * 2 + other
                each(lambda b: pack(own(s, q, part, b), q1s.at[j, i], t1s.at[j, i], b))
                for one in first_message(j, part, other):
                    one.start()

    def stage_two(j):
        s = lax.rem(j, 2)
        for part in (0, 1):
            for other in (0, 1):
                for one in first_message(j, part, other):
                    one.wait_recv()
            here = (y, x)[part]
            away = quarter(part, 1 - here, True)
            i = part * 2 + 1 - here
            each(lambda b: pack(own(s, away, part, b) + unpack(q1r.at[j, i], t1r.at[j, i], b), q2s.at[j, part], t2s.at[j, part], b))
            for one in second_message(j, part):
                one.start()
        for part in (0, 1):
            here = (y, x)[part]
            mine = x * 2 + y
            k = part * 2 + here

            def store(b, part=part, k=k):
                at = pl.ds(pl.multiple_of(part * half + b * BLOCK, BLOCK), BLOCK)
                keep[j, at, :] = own(s, mine, part, b) + unpack(q1r.at[j, k], t1r.at[j, k], b)

            each(store)

    def add_to_keep(j, part, q_ref, t_ref):
        def body(b):
            at = pl.ds(pl.multiple_of(part * half + b * BLOCK, BLOCK), BLOCK)
            keep[j, at, :] += unpack(q_ref, t_ref, b)

        each(body)

    def stage_three(j):
        for part in (0, 1):
            for one in second_message(j, part):
                one.wait_recv()
            add_to_keep(j, part, q2r.at[j, part], t2r.at[j, part])

    def pass_on(j, zz, part, name):
        def body(b):
            at = pl.ds(pl.multiple_of(part * half + b * BLOCK, BLOCK), BLOCK)
            pack(keep[j, at, :], zs.at[zz, part], tzs.at[zz, part], b)

        each(body)
        for one in z_message(zz, part, name):
            one.start()

    def stage_four(j):
        zz = order(j)
        for part in (0, 1):
            for d, name, has, onward in ((0, "up", z > 0, zz > z), (1, "down", z < n_z - 1, zz < z)):
                back = zz >= z if d == 0 else zz <= z

                @pl.when(jnp.logical_and(has, back))
                def _():
                    for one in z_message(zz, part, name):
                        one.wait_recv()
                    add_to_keep(j, part, zr.at[d, zz, part], tzr.at[d, zz, part])

                @pl.when(onward)
                def _():
                    pass_on(j, zz, part, name)

    greet(n_z, z, to)

    def begin(j, _):
        for q in range(4):
            sibling(j, q // 2, q % 2, 1 - c).start()
        return 0

    lax.fori_loop(0, n_z, begin, 0)
    load(0)

    def turn(t, _):
        pl.when(t < n_z)(lambda: stage_one(t))
        pl.when(jnp.logical_and(t >= 1, t <= n_z))(lambda: stage_two(t - 1))
        pl.when(t + 1 < n_z)(lambda: load(t + 1))
        pl.when(jnp.logical_and(t >= 2, t <= n_z + 1))(lambda: stage_three(t - 2))
        pl.when(t >= 3)(lambda: stage_four(t - 3))
        return 0

    lax.fori_loop(0, n_z + 3, turn, 0)
    out_ref[...] = keep[n_z - 1]

    def finish(j, _):
        zz = order(j)
        for q in range(4):
            sibling(j, q // 2, q % 2, 1 - c).wait_send()
        for part in (0, 1):
            for other in (0, 1):
                for one in first_message(j, part, other):
                    one.wait_send()
            for one in second_message(j, part):
                one.wait_send()

            @pl.when(zz > z)
            def _():
                for one in z_message(zz, part, "up"):
                    one.wait_send()

            @pl.when(zz < z)
            def _():
                for one in z_message(zz, part, "down"):
                    one.wait_send()

        return 0

    lax.fori_loop(0, n_z, finish, 0)


def reduce(flat, share, n_dp, n_pair):
    n_z, n = n_dp // 2, n_dp * n_pair
    rows = slab_tiles(share, n) * 8
    half = rows // 2
    marks = (half // BLOCK + 7) // 8 * 8
    anyspec = pl.BlockSpec(memory_space=pl.ANY)

    def q(*lead):
        return pltpu.VMEM(lead + (half, LANES), jnp.int16)

    def t(*lead):
        return pltpu.VMEM(lead + (marks, LANES), jnp.float32)

    dma = pltpu.SemaphoreType.DMA
    return pl.pallas_call(
        functools.partial(reduce_kernel, n_z, share),
        name="reduce_scatter",
        out_shape=[jax.ShapeDtypeStruct((rows, LANES), jnp.float32), jax.ShapeDtypeStruct((n_z, 4, rows, LANES), jnp.float32)],
        in_specs=[anyspec],
        out_specs=[pl.BlockSpec(memory_space=pltpu.VMEM), anyspec],
        scratch_shapes=[
            pltpu.VMEM((2, 4, rows, LANES), jnp.float32),
            pltpu.VMEM((2, 4, rows, LANES), jnp.float32),
            pltpu.VMEM((n_z, rows, LANES), jnp.float32),
            q(n_z, 4), q(n_z, 4), q(n_z, 2), q(n_z, 2), q(n_z, 2), q(2, n_z, 2),
            t(n_z, 4), t(n_z, 4), t(n_z, 2), t(n_z, 2), t(n_z, 2), t(2, n_z, 2),
            dma((2, n_z, 4)), dma((2, 2, 4)), dma((n_z, 4, 2, 2)), dma((n_z, 2, 2, 2)), dma((2, n_z, 2, 2, 2)),
        ],
        compiler_params=pltpu.CompilerParams(collective_id=1, has_side_effects=True, vmem_limit_bytes=60 * MB),
    )(flat)[0]


def share_kernel(n_dp, n_pair, in_ref, out_ref, send_sem, recv_sem):
    n = n_dp * n_pair
    me = lax.axis_index("dp") * n_pair + lax.axis_index("pair")
    barrier = pltpu.get_barrier_semaphore()

    def other(d):
        k = lax.rem(me + d, n)
        return {"dp": k // n_pair, "pair": lax.rem(k, n_pair)}

    def hello(d, _):
        pl.semaphore_signal(barrier, inc=1, device_id=other(d), device_id_type=MESH)
        return 0

    lax.fori_loop(1, n, hello, 0)
    pl.semaphore_wait(barrier, n - 1)
    out_ref[me] = in_ref[...]

    def copy(d):
        return pltpu.make_async_remote_copy(in_ref, out_ref.at[me], send_sem.at[d], recv_sem.at[d], device_id=other(d), device_id_type=MESH)

    def go(d, _):
        copy(d).start()
        return 0

    def stop(d, _):
        copy(d).wait()
        return 0

    lax.fori_loop(1, n, go, 0)
    lax.fori_loop(1, n, stop, 0)


def share_all(value, n_dp, n_pair, ident):
    n = n_dp * n_pair
    spec = pl.BlockSpec(memory_space=pltpu.VMEM)
    return pl.pallas_call(
        functools.partial(share_kernel, n_dp, n_pair),
        name="share_all",
        out_shape=jax.ShapeDtypeStruct((n,) + value.shape, value.dtype),
        in_specs=[spec],
        out_specs=spec,
        scratch_shapes=[pltpu.SemaphoreType.DMA((n,)), pltpu.SemaphoreType.DMA((n,))],
        compiler_params=pltpu.CompilerParams(collective_id=ident, has_side_effects=True),
    )(value)


NORM_EPS = 1e-06
ADAM_EPS = 1e-08
BETA_ONE = 0.9
BETA_TWO = 0.95
DECAY = 0.05
NEG_FILL = -1000000000.0


def mult(left, right):
    return jnp.einsum("bsi,ij->bsj", left, right, preferred_element_type=jnp.float32)


def mult_back(grad, right):
    return jnp.einsum("bsj,ij->bsi", grad, right, preferred_element_type=jnp.float32)


def outer(left, grad):
    return jnp.einsum("bsi,bsj->ij", left, grad, preferred_element_type=jnp.float32)


def layer_norm(x, gain, shift):
    centered = x - jnp.mean(x, axis=-1, keepdims=True)
    scale = lax.rsqrt(jnp.mean(centered * centered, axis=-1, keepdims=True) + NORM_EPS)
    normed = centered * scale
    return (normed * gain + shift, normed, scale)


def norm_back(grad, normed, scale, gain):
    inner = grad * gain
    back = scale * (
        inner
        - jnp.mean(inner, axis=-1, keepdims=True)
        - normed * jnp.mean(inner * normed, axis=-1, keepdims=True)
    )
    return (back, jnp.sum(grad * normed, axis=(0, 1)), jnp.sum(grad, axis=(0, 1)))


def positions(width):
    index = jnp.arange(PATCHES)
    quarter = width // 4
    freq = 10000.0 ** (-jnp.arange(quarter).astype(jnp.float32) / quarter)
    row = (index // GRID).astype(jnp.float32)[:, None] * freq[None, :]
    column = (index % GRID).astype(jnp.float32)[:, None] * freq[None, :]
    return jnp.concatenate([jnp.sin(row), jnp.cos(row), jnp.sin(column), jnp.cos(column)], axis=1)


def attention_scores(query, keys, bias, size):
    scores = jnp.einsum("bqhd,bkhd->bhqk", query, keys, preferred_element_type=jnp.float32)
    return scores * size ** (-0.5) + bias[:, None, None, :]


def block_forward(x, weights, gains, heads, bias):
    triple_w, proj_w, up_w, down_w = weights
    batch, length, width = x.shape
    size = width // heads
    normed_one, plain_one, scale_one = layer_norm(x, gains[0], gains[1])
    entry = normed_one.astype(jnp.bfloat16)
    triple = mult(entry, triple_w).astype(jnp.bfloat16).reshape(batch, length, 3, heads, size)
    query, keys, values = (triple[:, :, 0], triple[:, :, 1], triple[:, :, 2])
    scores = attention_scores(query, keys, bias, size)
    top = jnp.max(scores, axis=-1, keepdims=True)
    log_total = top + jnp.log(jnp.sum(jnp.exp(scores - top), axis=-1, keepdims=True))
    attend = jnp.exp(scores - log_total).astype(jnp.bfloat16)
    mixed = jnp.einsum("bhqk,bkhd->bqhd", attend, values, preferred_element_type=jnp.float32)
    mixed = mixed.astype(jnp.bfloat16).reshape(batch, length, width)
    middle = x + mult(mixed, proj_w)
    normed_two, plain_two, scale_two = layer_norm(middle, gains[2], gains[3])
    inner = normed_two.astype(jnp.bfloat16)
    hidden = mult(inner, up_w)
    activated = jax.nn.gelu(hidden, approximate=False).astype(jnp.bfloat16)
    result = middle + mult(activated, down_w)
    saved = (
        entry,
        plain_one,
        scale_one,
        query,
        keys,
        values,
        log_total,
        mixed,
        plain_two,
        scale_two,
        inner,
        hidden,
        activated,
    )
    return (result, saved)


def block_backward(grad, weights, gains, heads, bias, saved):
    triple_w, proj_w, up_w, down_w = weights
    (
        entry,
        plain_one,
        scale_one,
        query,
        keys,
        values,
        log_total,
        mixed,
        plain_two,
        scale_two,
        inner,
        hidden,
        activated,
    ) = saved
    batch, length, width = grad.shape
    size = width // heads
    low_grad = grad.astype(jnp.bfloat16)
    grad_down = outer(activated, low_grad)
    grad_act = mult_back(low_grad, down_w)
    density = jnp.exp(-0.5 * hidden * hidden) * 0.3989422804014327
    cumulative = 0.5 * (1.0 + lax.erf(hidden * 0.7071067811865476))
    grad_hidden = (grad_act * (cumulative + hidden * density)).astype(jnp.bfloat16)
    grad_up = outer(inner, grad_hidden)
    back_two, gain_two, shift_two = norm_back(
        mult_back(grad_hidden, up_w), plain_two, scale_two, gains[2]
    )
    grad_mid = grad + back_two
    mid_low = grad_mid.astype(jnp.bfloat16)
    grad_proj = outer(mixed, mid_low)
    grad_mixed = mult_back(mid_low, proj_w).astype(jnp.bfloat16).reshape(batch, length, heads, size)
    attend = jnp.exp(attention_scores(query, keys, bias, size) - log_total)
    grad_att = jnp.einsum("bqhd,bkhd->bhqk", grad_mixed, values, preferred_element_type=jnp.float32)
    grad_values = jnp.einsum(
        "bhqk,bqhd->bkhd",
        attend.astype(jnp.bfloat16),
        grad_mixed,
        preferred_element_type=jnp.float32,
    )
    grad_scores = attend * (grad_att - jnp.sum(attend * grad_att, axis=-1, keepdims=True))
    grad_scores = grad_scores.astype(jnp.bfloat16)
    grad_query = jnp.einsum(
        "bhqk,bkhd->bqhd", grad_scores, keys, preferred_element_type=jnp.float32
    ) * size ** (-0.5)
    grad_keys = jnp.einsum(
        "bhqk,bqhd->bkhd", grad_scores, query, preferred_element_type=jnp.float32
    ) * size ** (-0.5)
    grad_triple = jnp.stack([grad_query, grad_keys, grad_values], axis=2)
    grad_triple = grad_triple.astype(jnp.bfloat16).reshape(batch, length, 3 * width)
    grad_triple_w = outer(entry, grad_triple)
    back_one, gain_one, shift_one = norm_back(
        mult_back(grad_triple, triple_w), plain_one, scale_one, gains[0]
    )
    grad_in = grad_mid + back_one
    gain_grads = jnp.stack([gain_one, shift_one, gain_two, shift_two])
    return (grad_in, (grad_triple_w, grad_proj, grad_up, grad_down), gain_grads)


def own_lines(flat, share, index):
    if share % LANES == 0:
        return flat.reshape(-1, LANES)
    rows = (share + LANES - 1) // LANES + 1
    return lax.dynamic_update_slice(jnp.zeros((rows * LANES,), flat.dtype), flat, (share * index % LANES,)).reshape(rows, LANES)


def own_flat(lines, share, index):
    if share % LANES == 0:
        return lines.reshape(-1)
    return lax.dynamic_slice(lines.reshape(-1), (share * index % LANES,), (share,))


def body(
    n_dp, n_pair, patches, patch_order, counts, master, moment1, moment2, block_rates, clip_limit, step_count
):
    n = n_dp * n_pair
    share = master.shape[0]
    index = lax.axis_index("dp") * n_pair + lax.axis_index("pair")
    extra = jnp.zeros((8, LANES), jnp.float32).at[0, : counts.shape[0]].set((PATCHES - counts).astype(jnp.float32))
    slab = to_tiles(own_lines(master, share, index), extra, share, n, n_pair)
    slots = gather(slab, n_dp, n_pair)
    masked = jnp.sum(slots[:, slab.shape[0] - 2, 0, :].astype(jnp.float32))
    held = assemble(slots, share)
    parts = [held[i].reshape(-1)[: SHAPES[i][0] * SHAPES[i][1]].reshape(SHAPES[i]) if i in SMALL else matrix(held[i], i) for i in range(len(SHAPES))]
    enc_gains = parts[5].astype(jnp.float32)
    dec_gains = parts[12].astype(jnp.float32)
    slots = patch_order[:, :KEEP]
    live = jnp.arange(KEEP)[None, :] < counts[:, None]
    enc_bias = jnp.where(live, 0.0, NEG_FILL).astype(jnp.float32)
    seen = jnp.take_along_axis(patches, slots[:, :, None], axis=1)
    x_start = mult(seen, parts[0]) + jnp.take(positions(D), slots, axis=0)
    x_end, enc_saved = block_forward(x_start, tuple(parts[1:5]), enc_gains, HEADS, enc_bias)
    enc_normed, enc_plain, enc_scale = layer_norm(x_end, enc_gains[4], enc_gains[5])
    encoded = enc_normed.astype(jnp.bfloat16)
    entering = mult(encoded, parts[6])
    rank = jnp.argsort(patch_order, axis=1)
    shown = rank < counts[:, None]
    picked = jnp.take_along_axis(entering, jnp.minimum(rank, KEEP - 1)[:, :, None], axis=1)
    token = parts[12][6].astype(jnp.float32)
    y_start = jnp.where(shown[:, :, None], picked, token) + positions(DD)[None]
    dec_bias = jnp.zeros(shown.shape, jnp.float32)
    y_end, dec_saved = block_forward(y_start, tuple(parts[7:11]), dec_gains, DHEADS, dec_bias)
    final_normed, final_plain, final_scale = layer_norm(y_end, dec_gains[4], dec_gains[5])
    final = final_normed.astype(jnp.bfloat16)
    pred = mult(final, parts[11])
    pixels = patches.astype(jnp.float32)
    centered = pixels - jnp.mean(pixels, axis=-1, keepdims=True)
    target = centered * lax.rsqrt(jnp.mean(centered * centered, axis=-1, keepdims=True) + NORM_EPS)
    diff = pred - target
    hidden_mask = jnp.where(shown, 0.0, 1.0).astype(jnp.float32)
    loss_local = jnp.sum(jnp.mean(diff * diff, axis=-1) * hidden_mask)
    grad_pred = (diff * (hidden_mask[:, :, None] * (2.0 / PIX)) / masked).astype(jnp.bfloat16)
    again = parts
    enc_back_gains = again[5].astype(jnp.float32)
    dec_back_gains = again[12].astype(jnp.float32)
    grad_head = outer(final, grad_pred)
    back_final, gain_final, shift_final = norm_back(
        mult_back(grad_pred, again[11]), final_plain, final_scale, dec_back_gains[4]
    )
    grad_y, dec_grads, dec_gain_grads = block_backward(
        back_final, tuple(again[7:11]), dec_back_gains, DHEADS, dec_bias, dec_saved
    )
    grad_token = jnp.sum(grad_y * hidden_mask[:, :, None], axis=(0, 1))
    grad_entering = jnp.take_along_axis(grad_y, slots[:, :, None], axis=1)
    grad_entering = jnp.where(live[:, :, None], grad_entering, 0.0).astype(jnp.bfloat16)
    grad_dec_embed = outer(encoded, grad_entering)
    back_enc, gain_enc, shift_enc = norm_back(
        mult_back(grad_entering, again[6]), enc_plain, enc_scale, enc_back_gains[4]
    )
    grad_x, enc_grads, enc_gain_grads = block_backward(
        back_enc, tuple(again[1:5]), enc_back_gains, HEADS, enc_bias, enc_saved
    )
    grad_embed = outer(seen, grad_x.astype(jnp.bfloat16))
    enc_norm_grads = jnp.concatenate([enc_gain_grads, jnp.stack([gain_enc, shift_enc])])
    dec_norm_grads = jnp.concatenate([dec_gain_grads, jnp.stack([gain_final, shift_final])])
    grads = [
        grad_embed,
        enc_grads[0],
        enc_grads[1],
        enc_grads[2],
        enc_grads[3],
        enc_norm_grads,
        grad_dec_embed,
        dec_grads[0],
        dec_grads[1],
        dec_grads[2],
        dec_grads[3],
        grad_head,
        jnp.concatenate([dec_norm_grads, grad_token[None]]),
    ]
    total = max(a for a, _ in ranges(share, n)) + slab_tiles(share, n)
    pieces_ = []
    for i, grad in enumerate(grads):
        if i in SMALL:
            lines = grad.reshape(-1, LANES)
            pieces_.append(jnp.pad(lines, ((0, ENTRIES[i][4] * 8 - lines.shape[0]), (0, 0))))
        else:
            pieces_.append(matrix_tiles(grad))
    pieces_.append(jnp.zeros(((total - TILES) * 8, LANES), jnp.float32))
    slab_sum = reduce(jnp.concatenate(pieces_), share, n_dp, n_pair)
    rows = share // LANES if share % LANES == 0 else (share + LANES - 1) // LANES + 1
    grad_share = own_flat(to_lines(slab_sum, rows, share, n_pair), share, index)
    scalars = jnp.stack([jnp.sum(grad_share * grad_share), loss_local])
    shared = share_all(jnp.zeros((8, LANES), jnp.float32).at[0, :2].set(scalars), n_dp, n_pair, 2)
    squares, loss_sum = jnp.sum(shared[:, 0, 0]), jnp.sum(shared[:, 0, 1])
    grad_norm = jnp.sqrt(squares)
    loss = loss_sum / masked
    clipped = grad_share * (clip_limit[0] / (grad_norm + NORM_EPS))
    first = BETA_ONE * moment1 + (1.0 - BETA_ONE) * clipped
    second = BETA_TWO * moment2 + (1.0 - BETA_TWO) * clipped * clipped
    steps_done = step_count[0].astype(jnp.float32)
    position = index * share + jnp.arange(share)
    rate = jnp.where(position < ENC_PARAMS, block_rates[0], block_rates[1])
    update = (
        first
        / (1.0 - BETA_ONE**steps_done)
        / (jnp.sqrt(second / (1.0 - BETA_TWO**steps_done)) + ADAM_EPS)
    )
    master_new = master - rate * (update + DECAY * master)
    return (loss.reshape(1), grad_norm.reshape(1), first, second, master_new)


def solution(mesh):
    in_specs = (
        P(("dp", "pair"), None, None),
        P(("dp", "pair"), None),
        P(("dp", "pair")),
        P(("dp", "pair")),
        P(("dp", "pair")),
        P(("dp", "pair")),
        P(),
        P(),
        P(),
    )
    out_specs = (P(), P(), P(("dp", "pair")), P(("dp", "pair")), P(("dp", "pair")))
    return jax.shard_map(functools.partial(body, mesh.shape["dp"], mesh.shape["pair"]), mesh=mesh, in_specs=in_specs, out_specs=out_specs, check_vma=False)
```

```python
import functools

import jax
import jax.numpy as jnp
from jax import lax
from jax.experimental import pallas as pl
from jax.experimental.pallas import tpu as pltpu
from jax.sharding import PartitionSpec as P

MESH = pl.DeviceIdType.MESH
LANES = 128
TILE = 16 * LANES


def place():
    dp, pair = lax.axis_index("dp"), lax.axis_index("pair")
    return dp // 2, dp % 2, pair // 2, pair % 2


def slot_of(z, x, y, c):
    return (z * 2 + x) * 4 + y * 2 + c


def partners(z, x, y, c):
    return {
        "x": {"dp": z * 2 + (1 - x)},
        "y": {"pair": (1 - y) * 2 + c},
        "c": {"pair": y * 2 + (1 - c)},
        "up": {"dp": (z + 1) * 2 + x},
        "down": {"dp": (z - 1) * 2 + x},
    }


def greet(n_z, z, to):
    barrier = pltpu.get_barrier_semaphore()
    for name in ("x", "y", "c"):
        pl.semaphore_signal(barrier, inc=1, device_id=to[name], device_id_type=MESH)

    @pl.when(z < n_z - 1)
    def _():
        pl.semaphore_signal(barrier, inc=1, device_id=to["up"], device_id_type=MESH)

    @pl.when(z > 0)
    def _():
        pl.semaphore_signal(barrier, inc=1, device_id=to["down"], device_id_type=MESH)

    pl.semaphore_wait(barrier, 3 + jnp.where(z < n_z - 1, 1, 0) + jnp.where(z > 0, 1, 0))


def gather_kernel(n_z, slab_ref, out_ref, own_sem, send_sem, recv_sem):
    half = slab_ref.shape[0] // 2
    z, x, y, c = place()
    to = partners(z, x, y, c)
    me = slot_of(z, x, y, c)
    local = pltpu.make_async_copy(slab_ref, out_ref.at[me], own_sem)
    local.start()
    greet(n_z, z, to)
    local.wait()
    pending = []

    def copy(slot, part, name, index):
        rows = pl.ds(part * half, half)
        return pltpu.make_async_remote_copy(
            out_ref.at[slot, rows],
            out_ref.at[slot, rows],
            send_sem.at[index],
            recv_sem.at[slot, part],
            device_id=to[name],
            device_id_type=MESH,
        )

    def send(slot, part, name, where):
        index = len(pending)
        pending.append((slot, part, name, index, where))
        if where is None:
            copy(slot, part, name, index).start()
        else:
            pl.when(where)(lambda: copy(slot, part, name, index).start())

    def arrived(slot, part, where):
        if where is None:
            copy(slot, part, "c", 0).wait_recv()
        else:
            pl.when(where)(lambda: copy(slot, part, "c", 0).wait_recv())

    def both(one, two):
        return two if one is None else jnp.logical_and(one, two)

    levels = [[(z, None, None)]]
    for t in range(1, n_z):
        levels.append([(z - t, z >= t, "up"), (z + t, z + t < n_z, "down")])

    def first(level):
        for zz, where, onward in level:
            slot = slot_of(zz, x, y, c)
            for part in (0, 1):
                if onward is None:
                    send(slot, part, "up", z < n_z - 1)
                    send(slot, part, "down", z > 0)
                else:
                    arrived(slot, part, where)
                    more = z < n_z - 1 if onward == "up" else z > 0
                    send(slot, part, onward, both(where, more))
            for part in (0, 1):
                send(slot, part, ("x", "y")[part], where)
            for part in (0, 1):
                send(slot, part, ("y", "x")[part], where)
            for part in (0, 1):
                send(slot, part, "c", where)

    def second(level):
        for zz, where, _ in level:
            for part, slot in ((0, slot_of(zz, 1 - x, y, c)), (1, slot_of(zz, x, 1 - y, c))):
                arrived(slot, part, where)
                send(slot, part, ("y", "x")[part], where)
                send(slot, part, "c", where)

    def third(level):
        for zz, where, _ in level:
            for part, ox, oy in ((0, x, 1 - y), (1, 1 - x, y), (0, 1 - x, 1 - y), (1, 1 - x, 1 - y)):
                slot = slot_of(zz, ox, oy, c)
                arrived(slot, part, where)
                send(slot, part, "c", where)

    for t in range(n_z + 2):
        if t < n_z:
            first(levels[t])
        if 1 <= t < n_z + 1:
            second(levels[t - 1])
        if t >= 2:
            third(levels[t - 2])
    for level in levels:
        for zz, where, _ in level:
            for ox in (0, 1):
                for oy in (0, 1):
                    for part in (0, 1):
                        arrived(slot_of(zz, ox, oy, 1 - c), part, where)
    for slot, part, name, index, where in pending:
        if where is None:
            copy(slot, part, name, index).wait_send()
        else:
            pl.when(where)(lambda s=slot, p=part, n=name, i=index: copy(s, p, n, i).wait_send())


def gather(slab, n_dp, n_pair):
    n_z = n_dp // 2
    n = n_dp * n_pair
    sends = (2 * n_z - 1) * 16 + 8
    return pl.pallas_call(
        functools.partial(gather_kernel, n_z),
        name="gather",
        out_shape=jax.ShapeDtypeStruct((n,) + slab.shape, slab.dtype),
        in_specs=[pl.BlockSpec(memory_space=pl.ANY)],
        out_specs=pl.BlockSpec(memory_space=pl.ANY),
        scratch_shapes=[
            pltpu.SemaphoreType.DMA,
            pltpu.SemaphoreType.DMA((sends,)),
            pltpu.SemaphoreType.DMA((n, 2)),
        ],
        compiler_params=pltpu.CompilerParams(collective_id=0, has_side_effects=True),
    )(slab)


PIX, HEADS, F, DHEADS, FD, GRID, KEEP, D, DD, PATCHES = 768, 12, 3072, 16, 2048, 14, 64, 768, 512, 196
SHAPES = [(PIX, D), (D, 3 * D), (D, D), (D, F), (F, D), (6, D), (D, DD), (DD, 3 * DD), (DD, DD), (DD, FD), (FD, DD), (DD, PIX), (7, DD)]
SMALL = (5, 12)
ENC_PARAMS = 7672320
MB = 1 << 20
CELL = 8 * LANES
BLOCK = 96


def make_entries():
    entries, row, tile = [], 0, 0
    for number, (rows, width) in enumerate(SHAPES):
        lines = rows * width // LANES
        cols = 1 if number in SMALL else width // LANES
        groups = -(-lines // (8 * cols))
        entries.append((row, lines, cols, tile, groups))
        row += lines
        tile += groups * cols
    return entries, row, tile


ENTRIES, ROWS, TILES = make_entries()
MARGIN = 8 * max(cols for _, _, cols, _, _ in ENTRIES)


def first_tile(share, k):
    lo = share * k
    total = 0
    for row, lines, cols, tile, _ in ENTRIES:
        inside = jnp.logical_and(lo >= row * LANES, lo < (row + lines) * LANES)
        total = total + jnp.where(inside, tile + (lo - row * LANES) // (CELL * cols) * cols, 0)
    return total


def ranges(share, n):
    found = []
    for k in range(n):
        lo, hi = share * k, share * (k + 1)
        spans = []
        for row, lines, cols, tile, _ in ENTRIES:
            low, high = max(lo, row * LANES), min(hi, (row + lines) * LANES)
            if low < high:
                size = CELL * cols
                spans.append((tile + (low - row * LANES) // size * cols, tile + -(-(high - row * LANES) // size) * cols))
        found.append((spans[0][0], spans[-1][1]))
    return found


def slab_tiles(share, n):
    longest = max(b - a for a, b in ranges(share, n))
    return -(-longest // 24) * 24


def line_span(share, k):
    return share * k // LANES, (share * (k + 1) + LANES - 1) // LANES


def tiled(share, k, body):
    lo, hi = line_span(share, k)
    begin = first_tile(share, k)
    for number in SMALL + tuple(i for i in range(len(ENTRIES)) if i not in SMALL):
        row, lines, cols, tile, _ = ENTRIES[number]
        low = jnp.maximum(lo, row) - row
        high = jnp.minimum(hi, row + lines) - row
        size = 8 * cols

        def group(g, _, row=row, cols=cols, tile=tile, size=size):
            body(row + g * size - lo + MARGIN, tile + g * cols - begin, cols)
            return 0

        lax.fori_loop(jnp.where(low < high, low // size, 0), jnp.where(low < high, (high + size - 1) // size, 0), group, 0)


def tile_kernel(share, n_pair, lines_ref, extra_ref, out_ref, wide):
    k = lax.axis_index("dp") * n_pair + lax.axis_index("pair")
    rows = lines_ref.shape[0]
    wide[0:MARGIN, :] = jnp.zeros((MARGIN, LANES), jnp.float32)
    wide[MARGIN + rows :, :] = jnp.zeros((wide.shape[0] - MARGIN - rows, LANES), jnp.float32)
    wide[MARGIN : MARGIN + rows, :] = lines_ref[...]

    def body(line, tile, cols):
        for col in range(cols):
            out_ref[tile + col] = wide[pl.ds(line + col, 8, stride=cols), :].astype(out_ref.dtype)

    tiled(share, k, body)
    out_ref[out_ref.shape[0] - 2] = extra_ref[...].astype(out_ref.dtype)


def wide_rows(rows):
    return -(-(rows + 2 * MARGIN) // 8) * 8


def to_tiles(lines, extra, share, n, n_pair):
    rows = lines.shape[0]
    count = slab_tiles(share, n) + 2
    spec = pl.BlockSpec(memory_space=pltpu.VMEM)
    return pl.pallas_call(
        functools.partial(tile_kernel, share, n_pair),
        name="to_tiles",
        out_shape=jax.ShapeDtypeStruct((count, 8, LANES), jnp.bfloat16),
        in_specs=[spec, spec],
        out_specs=spec,
        scratch_shapes=[pltpu.VMEM((wide_rows(rows), LANES), jnp.float32)],
    )(lines, extra)


def line_kernel(share, n_pair, slab_ref, out_ref, wide):
    k = lax.axis_index("dp") * n_pair + lax.axis_index("pair")

    def body(line, tile, cols):
        for col in range(cols):
            wide[pl.ds(line + col, 8, stride=cols), :] = slab_ref[pl.ds(pl.multiple_of((tile + col) * 8, 8), 8), :]

    tiled(share, k, body)
    out_ref[...] = wide[MARGIN : MARGIN + out_ref.shape[0], :]


def to_lines(slab, rows, share, n_pair):
    spec = pl.BlockSpec(memory_space=pltpu.VMEM)
    return pl.pallas_call(
        functools.partial(line_kernel, share, n_pair),
        name="to_lines",
        out_shape=jax.ShapeDtypeStruct((rows, LANES), jnp.float32),
        in_specs=[spec],
        out_specs=spec,
        scratch_shapes=[pltpu.VMEM((wide_rows(rows), LANES), jnp.float32)],
    )(slab)


def pieces(share, n):
    spans = ranges(share, n)
    shared = [spans[k][1] > spans[k + 1][0] for k in range(n - 1)]
    plain, seams = [], []
    for number, (_, _, cols, tile, groups) in enumerate(ENTRIES):
        end = tile + groups * cols
        for k, (a, b) in enumerate(spans):
            low, high = max(a, tile), min(b, end)
            if low >= high:
                continue
            inner_low, inner_high = low, high
            if k > 0 and spans[k - 1][1] > low:
                inner_low = spans[k - 1][1]
            if k < n - 1 and spans[k + 1][0] < high:
                inner_high = spans[k + 1][0]
                seams.append((number, k, inner_high, high))
            if inner_low < inner_high:
                plain.append((number, k, inner_low, inner_high))
    return spans, plain, seams


def assemble_kernel(share, n, slots_ref, *refs):
    outs = refs[: len(ENTRIES)]
    whole, right, plain_sem, left_sem, right_sem, out_sem = refs[len(ENTRIES) :]
    spans, plain, seams = pieces(share, n)
    waits = [[] for _ in ENTRIES]
    for i, (number, k, low, high) in enumerate(plain):
        copy = pltpu.make_async_copy(slots_ref.at[k, pl.ds(low - spans[k][0], high - low)], whole.at[pl.ds(low, high - low)], plain_sem.at[i])
        copy.start()
        waits[number].append(copy)
    for i, (number, k, low, high) in enumerate(seams):
        one = pltpu.make_async_copy(slots_ref.at[k, pl.ds(low - spans[k][0], high - low)], whole.at[pl.ds(low, high - low)], left_sem.at[i])
        two = pltpu.make_async_copy(
            slots_ref.at[k + 1, pl.ds(low - spans[k + 1][0], high - low)], right.at[i, pl.ds(0, high - low)], right_sem.at[i]
        )
        one.start()
        two.start()
        waits[number] += [one, two]
    ended = []
    for number, (_, _, cols, tile, groups) in enumerate(ENTRIES):
        for copy in waits[number]:
            copy.wait()
        for i, (owner, k, low, high) in enumerate(seams):
            if owner == number:
                total = whole[low:high].astype(jnp.float32) + right[i, 0 : high - low].astype(jnp.float32)
                whole[low:high] = total.astype(jnp.bfloat16)
        copy = pltpu.make_async_copy(whole.at[pl.ds(tile, groups * cols)], outs[number], out_sem.at[number])
        copy.start()
        ended.append(copy)
    for copy in ended:
        copy.wait()


def assemble(slots, share):
    n = slots.shape[0]
    _, plain, seams = pieces(share, n)
    anyspec = pl.BlockSpec(memory_space=pl.ANY)
    dma = pltpu.SemaphoreType.DMA
    return pl.pallas_call(
        functools.partial(assemble_kernel, share, n),
        name="assemble",
        out_shape=[jax.ShapeDtypeStruct((groups * cols, 8, LANES), jnp.bfloat16) for _, _, cols, _, groups in ENTRIES],
        in_specs=[anyspec],
        out_specs=[anyspec] * len(ENTRIES),
        scratch_shapes=[
            pltpu.VMEM((TILES, 8, LANES), jnp.bfloat16),
            pltpu.VMEM((len(seams), MARGIN // 8, 8, LANES), jnp.bfloat16),
            dma((len(plain),)),
            dma((len(seams),)),
            dma((len(seams),)),
            dma((len(ENTRIES),)),
        ],
        compiler_params=pltpu.CompilerParams(vmem_limit_bytes=40 * MB),
    )(slots)


def matrix(tiles_, number):
    rows, width = SHAPES[number]
    cols = width // LANES
    return tiles_.reshape(rows // 8, cols, 8, LANES).transpose(0, 2, 1, 3).reshape(rows, width)


def matrix_tiles(value):
    rows, width = value.shape
    cols = width // LANES
    return value.reshape(rows // 8, 8, cols, LANES).transpose(0, 2, 1, 3).reshape(rows * cols, LANES)


def reduce_kernel(n_z, share, grad_ref, out_ref, sib_ref, gbuf, rbuf, keep, q1s, q1r, q2s, q2r, zs, zr, t1s, t1r, t2s, t2r, tzs, tzr, sib_sem, load_sem, s1_sem, s2_sem, z_sem):
    z, x, y, c = place()
    to = partners(z, x, y, c)
    rows = out_ref.shape[0]
    half = rows // 2
    count = half // BLOCK

    def start_of(k):
        return pl.multiple_of(first_tile(share, k) * 8, 8)

    def order(j):
        low = z < n_z // 2
        far = jnp.where(low, n_z - 1 - j, j)
        moved = jnp.where(low, jnp.where(far > z, far, far - 1), jnp.where(far < z, far, far + 1))
        return jnp.where(j == n_z - 1, z, moved)

    def sibling(j, xx, yy, core):
        k = slot_of(order(j), xx, yy, core)
        return pltpu.make_async_remote_copy(
            grad_ref.at[pl.ds(start_of(k), rows)],
            sib_ref.at[j, xx * 2 + yy],
            sib_sem.at[0, j, xx * 2 + yy],
            sib_sem.at[1, j, xx * 2 + yy],
            device_id=to["c"],
            device_id_type=MESH,
        )

    def loads(j, s, q):
        k = slot_of(order(j), q // 2, q % 2, c)
        return (
            pltpu.make_async_copy(grad_ref.at[pl.ds(start_of(k), rows)], gbuf.at[s, q], load_sem.at[0, s, q]),
            pltpu.make_async_copy(sib_ref.at[j, q], rbuf.at[s, q], load_sem.at[1, s, q]),
        )

    def load(j):
        s = lax.rem(j, 2)
        for q in range(4):
            sibling(j, q // 2, q % 2, 1 - c).wait_recv()
            for one in loads(j, s, q):
                one.start()

    def pack(value, q_ref, t_ref, b):
        top = jnp.max(jnp.abs(value), axis=0, keepdims=True)
        inverse = jnp.where(top > 1e-30, 32767.0 / jnp.maximum(top, 1e-30), 0.0)
        q_ref[pl.ds(pl.multiple_of(b * BLOCK, BLOCK), BLOCK), :] = jnp.round(value * inverse).astype(jnp.int32).astype(jnp.int16)
        t_ref[pl.ds(b, 1), :] = top * (1.0 / 32767.0)

    def unpack(q_ref, t_ref, b):
        return q_ref[pl.ds(pl.multiple_of(b * BLOCK, BLOCK), BLOCK), :].astype(jnp.int32).astype(jnp.float32) * t_ref[pl.ds(b, 1), :]

    def each(body):
        def one(b, _):
            body(b)
            return 0

        lax.fori_loop(0, count, one, 0)

    def own(s, q, part, b):
        at = pl.ds(pl.multiple_of(part * half + b * BLOCK, BLOCK), BLOCK)
        return gbuf[s, q, at, :] + rbuf[s, q, at, :]

    def message(qs, ts, qr, tr, sem, name):
        return (
            pltpu.make_async_remote_copy(qs, qr, sem.at[0, 0], sem.at[0, 1], device_id=to[name], device_id_type=MESH),
            pltpu.make_async_remote_copy(ts, tr, sem.at[1, 0], sem.at[1, 1], device_id=to[name], device_id_type=MESH),
        )

    def first_message(j, part, other):
        i = part * 2 + other
        return message(q1s.at[j, i], t1s.at[j, i], q1r.at[j, i], t1r.at[j, i], s1_sem.at[j, i], ("x", "y")[part])

    def second_message(j, part):
        return message(q2s.at[j, part], t2s.at[j, part], q2r.at[j, part], t2r.at[j, part], s2_sem.at[j, part], ("y", "x")[part])

    def z_message(zz, part, name):
        d = 0 if name == "up" else 1
        return message(zs.at[zz, part], tzs.at[zz, part], zr.at[d, zz, part], tzr.at[d, zz, part], z_sem.at[d, zz, part], name)

    def quarter(part, other, mine):
        if part == 0:
            return (x if mine else 1 - x) * 2 + other
        return other * 2 + (y if mine else 1 - y)

    def stage_one(j):
        s = lax.rem(j, 2)
        for q in range(4):
            for one in loads(j, s, q):
                one.wait()
        for part in (0, 1):
            for other in (0, 1):
                q = quarter(part, other, False)
                i = part * 2 + other
                each(lambda b: pack(own(s, q, part, b), q1s.at[j, i], t1s.at[j, i], b))
                for one in first_message(j, part, other):
                    one.start()

    def stage_two(j):
        s = lax.rem(j, 2)
        for part in (0, 1):
            for other in (0, 1):
                for one in first_message(j, part, other):
                    one.wait_recv()
            here = (y, x)[part]
            away = quarter(part, 1 - here, True)
            i = part * 2 + 1 - here
            each(lambda b: pack(own(s, away, part, b) + unpack(q1r.at[j, i], t1r.at[j, i], b), q2s.at[j, part], t2s.at[j, part], b))
            for one in second_message(j, part):
                one.start()
        for part in (0, 1):
            here = (y, x)[part]
            mine = x * 2 + y
            k = part * 2 + here

            def store(b, part=part, k=k):
                at = pl.ds(pl.multiple_of(part * half + b * BLOCK, BLOCK), BLOCK)
                keep[j, at, :] = own(s, mine, part, b) + unpack(q1r.at[j, k], t1r.at[j, k], b)

            each(store)

    def add_to_keep(j, part, q_ref, t_ref):
        def body(b):
            at = pl.ds(pl.multiple_of(part * half + b * BLOCK, BLOCK), BLOCK)
            keep[j, at, :] += unpack(q_ref, t_ref, b)

        each(body)

    def stage_three(j):
        for part in (0, 1):
            for one in second_message(j, part):
                one.wait_recv()
            add_to_keep(j, part, q2r.at[j, part], t2r.at[j, part])

    def pass_on(j, zz, part, name):
        def body(b):
            at = pl.ds(pl.multiple_of(part * half + b * BLOCK, BLOCK), BLOCK)
            pack(keep[j, at, :], zs.at[zz, part], tzs.at[zz, part], b)

        each(body)
        for one in z_message(zz, part, name):
            one.start()

    def stage_four(j):
        zz = order(j)
        for part in (0, 1):
            for d, name, has, onward in ((0, "up", z > 0, zz > z), (1, "down", z < n_z - 1, zz < z)):
                back = zz >= z if d == 0 else zz <= z

                @pl.when(jnp.logical_and(has, back))
                def _():
                    for one in z_message(zz, part, name):
                        one.wait_recv()
                    add_to_keep(j, part, zr.at[d, zz, part], tzr.at[d, zz, part])

                @pl.when(onward)
                def _():
                    pass_on(j, zz, part, name)

    greet(n_z, z, to)

    def begin(j, _):
        for q in range(4):
            sibling(j, q // 2, q % 2, 1 - c).start()
        return 0

    lax.fori_loop(0, n_z, begin, 0)
    load(0)

    def turn(t, _):
        pl.when(t < n_z)(lambda: stage_one(t))
        pl.when(jnp.logical_and(t >= 1, t <= n_z))(lambda: stage_two(t - 1))
        pl.when(t + 1 < n_z)(lambda: load(t + 1))
        pl.when(jnp.logical_and(t >= 2, t <= n_z + 1))(lambda: stage_three(t - 2))
        pl.when(t >= 3)(lambda: stage_four(t - 3))
        return 0

    lax.fori_loop(0, n_z + 3, turn, 0)
    out_ref[...] = keep[n_z - 1]

    def finish(j, _):
        zz = order(j)
        for q in range(4):
            sibling(j, q // 2, q % 2, 1 - c).wait_send()
        for part in (0, 1):
            for other in (0, 1):
                for one in first_message(j, part, other):
                    one.wait_send()
            for one in second_message(j, part):
                one.wait_send()

            @pl.when(zz > z)
            def _():
                for one in z_message(zz, part, "up"):
                    one.wait_send()

            @pl.when(zz < z)
            def _():
                for one in z_message(zz, part, "down"):
                    one.wait_send()

        return 0

    lax.fori_loop(0, n_z, finish, 0)


def reduce(flat, share, n_dp, n_pair):
    n_z, n = n_dp // 2, n_dp * n_pair
    rows = slab_tiles(share, n) * 8
    half = rows // 2
    marks = (half // BLOCK + 7) // 8 * 8
    anyspec = pl.BlockSpec(memory_space=pl.ANY)

    def q(*lead):
        return pltpu.VMEM(lead + (half, LANES), jnp.int16)

    def t(*lead):
        return pltpu.VMEM(lead + (marks, LANES), jnp.float32)

    dma = pltpu.SemaphoreType.DMA
    return pl.pallas_call(
        functools.partial(reduce_kernel, n_z, share),
        name="reduce_scatter",
        out_shape=[jax.ShapeDtypeStruct((rows, LANES), jnp.float32), jax.ShapeDtypeStruct((n_z, 4, rows, LANES), jnp.float32)],
        in_specs=[anyspec],
        out_specs=[pl.BlockSpec(memory_space=pltpu.VMEM), anyspec],
        scratch_shapes=[
            pltpu.VMEM((2, 4, rows, LANES), jnp.float32),
            pltpu.VMEM((2, 4, rows, LANES), jnp.float32),
            pltpu.VMEM((n_z, rows, LANES), jnp.float32),
            q(n_z, 4), q(n_z, 4), q(n_z, 2), q(n_z, 2), q(n_z, 2), q(2, n_z, 2),
            t(n_z, 4), t(n_z, 4), t(n_z, 2), t(n_z, 2), t(n_z, 2), t(2, n_z, 2),
            dma((2, n_z, 4)), dma((2, 2, 4)), dma((n_z, 4, 2, 2)), dma((n_z, 2, 2, 2)), dma((2, n_z, 2, 2, 2)),
        ],
        compiler_params=pltpu.CompilerParams(collective_id=1, has_side_effects=True, vmem_limit_bytes=60 * MB),
    )(flat)[0]


def share_kernel(n_dp, n_pair, in_ref, out_ref, send_sem, recv_sem):
    n = n_dp * n_pair
    me = lax.axis_index("dp") * n_pair + lax.axis_index("pair")
    barrier = pltpu.get_barrier_semaphore()

    def other(d):
        k = lax.rem(me + d, n)
        return {"dp": k // n_pair, "pair": lax.rem(k, n_pair)}

    def hello(d, _):
        pl.semaphore_signal(barrier, inc=1, device_id=other(d), device_id_type=MESH)
        return 0

    lax.fori_loop(1, n, hello, 0)
    pl.semaphore_wait(barrier, n - 1)
    out_ref[me] = in_ref[...]

    def copy(d):
        return pltpu.make_async_remote_copy(in_ref, out_ref.at[me], send_sem.at[d], recv_sem.at[d], device_id=other(d), device_id_type=MESH)

    def go(d, _):
        copy(d).start()
        return 0

    def stop(d, _):
        copy(d).wait()
        return 0

    lax.fori_loop(1, n, go, 0)
    lax.fori_loop(1, n, stop, 0)


def share_all(value, n_dp, n_pair, ident):
    n = n_dp * n_pair
    spec = pl.BlockSpec(memory_space=pltpu.VMEM)
    return pl.pallas_call(
        functools.partial(share_kernel, n_dp, n_pair),
        name="share_all",
        out_shape=jax.ShapeDtypeStruct((n,) + value.shape, value.dtype),
        in_specs=[spec],
        out_specs=spec,
        scratch_shapes=[pltpu.SemaphoreType.DMA((n,)), pltpu.SemaphoreType.DMA((n,))],
        compiler_params=pltpu.CompilerParams(collective_id=ident, has_side_effects=True),
    )(value)


NORM_EPS = 1e-06
NEG_FILL = -1000000000.0
P_ROWS = 208
BF = jnp.bfloat16
F32 = jnp.float32


def dot_nn(left, right):
    return lax.dot_general(left, right, (((1,), (0,)), ((), ())), preferred_element_type=F32)


def dot_nt(left, right):
    return lax.dot_general(left, right, (((1,), (1,)), ((), ())), preferred_element_type=F32)


def loop(count, body, unroll=1):
    def step(i, _):
        body(i)
        return 0

    lax.fori_loop(0, count, step, 0, unroll=unroll)


def rows_at(i, size):
    return pl.ds(pl.multiple_of(i * size, size), size)


def norm(x):
    centered = x - jnp.mean(x, axis=-1, keepdims=True)
    scale = lax.rsqrt(jnp.mean(centered * centered, axis=-1, keepdims=True) + NORM_EPS)
    return centered * scale, scale


def norm_grad(grad, plain, scale, gain):
    inner = grad * gain
    back = scale * (inner - jnp.mean(inner, axis=-1, keepdims=True) - plain * jnp.mean(inner * plain, axis=-1, keepdims=True))
    return back, jnp.sum(grad * plain, axis=0, keepdims=True), jnp.sum(grad, axis=0, keepdims=True)


def gelu_pair(h):
    cumulative = 0.5 * (1.0 + lax.erf(h * 0.7071067811865476))
    density = jnp.exp(-0.5 * h * h) * 0.3989422804014327
    return h * cumulative, cumulative + h * density


def head_masks(size):
    lane = lax.broadcasted_iota(jnp.int32, (1, LANES), 1)
    shift = size.bit_length() - 1
    return [jnp.where((lane >> shift) == h, 1.0, 0.0).astype(BF) for h in range(LANES // size)]


def three(value):
    top = value.astype(BF)
    rest = value - top.astype(F32)
    mid = rest.astype(BF)
    return top, mid, (rest - mid.astype(F32)).astype(BF)


def block_forward(x, rows, images, length, heads, weights, norms, key_bias, saved):
    triple_w, proj_w, up_w, down_w = weights
    entry, plain1, scale1, triple, probs, mixed, plain2, scale2, inner, act, slope = saved
    width = x.shape[1]
    size = width // heads
    per = LANES // size
    groups = width // LANES
    hidden = up_w.shape[1]

    def first(i):
        at = rows_at(i, rows)
        plain, scale = norm(x[at, :])
        plain1[at, :] = plain
        scale1[at, :] = scale
        entry[at, :] = (plain * norms[0:1, :] + norms[1:2, :]).astype(BF)

    loop(images, first)

    def project(j):
        at = rows_at(j, 256)
        triple[:, at] = dot_nn(entry[...], triple_w[:, at]).astype(BF)

    loop(3 * width // 256, project)
    masks = head_masks(size)

    def attend(i):
        at = rows_at(i, rows)
        bias = key_bias(i)
        for g in range(groups):
            q = triple[at, g * LANES : (g + 1) * LANES]
            k = triple[at, width + g * LANES : width + (g + 1) * LANES]
            v = triple[at, 2 * width + g * LANES : 2 * width + (g + 1) * LANES]
            v_side = v.T
            parts = []
            for h in range(per):
                s = dot_nt(k * masks[h], q) * size ** (-0.5) + bias
                e = jnp.exp(s - jnp.max(s, axis=0, keepdims=True))
                p = e * (1.0 / jnp.sum(e, axis=0, keepdims=True))
                probs[i * groups + g, h * rows : (h + 1) * rows, :] = p
                parts.append(dot_nn(v_side[h * size : (h + 1) * size, :], p.astype(BF)))
            mixed[at, g * LANES : (g + 1) * LANES] = jnp.concatenate(parts, axis=0).T.astype(BF)

    loop(images, attend)

    def middle(j):
        at = rows_at(j, 256)
        x[:, at] += dot_nn(mixed[...], proj_w[:, at])

    loop(width // 256, middle)

    def second(i):
        at = rows_at(i, rows)
        plain, scale = norm(x[at, :])
        plain2[at, :] = plain
        scale2[at, :] = scale
        inner[at, :] = (plain * norms[2:3, :] + norms[3:4, :]).astype(BF)

    loop(images, second)

    def up(j):
        at = rows_at(j, 256)
        value, gradient = gelu_pair(dot_nn(inner[...], up_w[:, at]))
        act[:, at] = value.astype(BF)
        slope[:, at] = gradient

    loop(hidden // 256, up)

    def down(j):
        at = rows_at(j, 256)
        x[:, at] += dot_nn(act[...], down_w[:, at])

    loop(width // 256, down)


class Writer:
    def __init__(self, flat, stage, sem):
        self.flat, self.stage, self.sem = flat, stage, sem

    def outer(self, number, left, right, chunk=256):
        _, _, cols, tile, _ = ENTRIES[number]
        rows = left.shape[1]
        count = rows // chunk
        tall = chunk // 8

        def copy(i, s):
            return pltpu.make_async_copy(
                self.stage.at[s, pl.ds(0, tall * cols)], self.flat.at[pl.ds(tile + i * tall * cols, tall * cols)], self.sem.at[s]
            )

        def body(i):
            s = lax.rem(i, 2)

            @pl.when(i >= 2)
            def _():
                copy(i - 2, s).wait()

            side = left[:, rows_at(i, chunk)].T
            for c in range(0, cols, 2):
                value = dot_nn(side, right[:, c * LANES : (c + 2) * LANES])
                for d in range(2):
                    self.stage[s, pl.ds(c + d, tall, stride=cols)] = value[:, d * LANES : (d + 1) * LANES].reshape(tall, 8, LANES)
            copy(i, s).start()

        loop(count, body)
        for i in range(max(0, count - 2), count):
            copy(i, i % 2).wait()


def block_backward(grad, rows, images, length, heads, weights, norms, norm_sums, saved, extra, writer, numbers):
    triple_w, proj_w, up_w, down_w = weights
    entry, plain1, scale1, triple, probs, mixed, plain2, scale2, inner, act, slope = saved
    low, grad_hidden, side, low_mixed, grad_triple = extra
    width = grad.shape[1]
    size = width // heads
    per = LANES // size
    groups = width // LANES
    hidden = up_w.shape[1]
    low[...] = grad[...].astype(BF)

    def back_up(j):
        at = rows_at(j, 256)
        grad_hidden[:, at] = (dot_nt(low[...], down_w[at, :]) * slope[:, at]).astype(BF)

    loop(hidden // 256, back_up)
    writer.outer(numbers[3], act, low)
    writer.outer(numbers[2], inner, grad_hidden)

    def back_inner(j):
        at = rows_at(j, 256)
        side[:, at] = dot_nt(grad_hidden[...], up_w[at, :])

    loop(width // 256, back_inner)

    def second(i):
        at = rows_at(i, rows)
        back, gain, shift = norm_grad(side[at, :], plain2[at, :], scale2[at, :], norms[2:3, :])
        norm_sums[2:3, :] += gain
        norm_sums[3:4, :] += shift
        total = grad[at, :] + back
        grad[at, :] = total
        low[at, :] = total.astype(BF)

    loop(images, second)
    writer.outer(numbers[1], mixed, low)

    def back_mixed(j):
        at = rows_at(j, 256)
        low_mixed[:, at] = dot_nt(low[...], proj_w[at, :]).astype(BF)

    loop(width // 256, back_mixed)
    masks = head_masks(size)

    def attend(i):
        at = rows_at(i, rows)
        for g in range(groups):
            lanes = [slice(t * width + g * LANES, t * width + (g + 1) * LANES) for t in range(3)]
            q, k, v = (triple[at, lane] for lane in lanes)
            dm = low_mixed[at, g * LANES : (g + 1) * LANES]
            k_side = k.T
            parts, dk, dv = [], 0.0, 0.0
            for h in range(per):
                p = probs[i * groups + g, h * rows : (h + 1) * rows, :]
                dp = dot_nt(v * masks[h], dm)
                ds = (p * (dp - jnp.sum(p * dp, axis=0, keepdims=True))).astype(BF)
                dv = dv + dot_nn(p.astype(BF), dm * masks[h])
                dk = dk + dot_nn(ds, q * masks[h])
                parts.append(dot_nn(k_side[h * size : (h + 1) * size, :], ds))
            dq = jnp.concatenate(parts, axis=0).T
            grad_triple[at, lanes[0]] = (dq * size ** (-0.5)).astype(BF)
            grad_triple[at, lanes[1]] = (dk * size ** (-0.5)).astype(BF)
            grad_triple[at, lanes[2]] = dv.astype(BF)

    loop(images, attend)
    writer.outer(numbers[0], entry, grad_triple)

    def back_entry(j):
        at = rows_at(j, 256)
        side[:, at] = dot_nt(grad_triple[...], triple_w[at, :])

    loop(width // 256, back_entry)

    def first(i):
        at = rows_at(i, rows)
        back, gain, shift = norm_grad(side[at, :], plain1[at, :], scale1[at, :], norms[0:1, :])
        norm_sums[0:1, :] += gain
        norm_sums[1:2, :] += shift
        grad[at, :] += back

    loop(images, first)


def write_small(number, norm_sums, count, flat, stage, sem):
    _, lines, _, tile, groups = ENTRIES[number]
    per = SHAPES[number][1] // LANES
    stage[0, 0:groups] = jnp.zeros((groups, 8, LANES), F32)
    for r in range(count):
        for c in range(per):
            line = r * per + c
            stage[0, line // 8, line % 8 : line % 8 + 1, :] = norm_sums[r : r + 1, c * LANES : (c + 1) * LANES]
    copy = pltpu.make_async_copy(stage.at[0, pl.ds(0, groups)], flat.at[pl.ds(tile, groups)], sem.at[0])
    copy.start()
    copy.wait()


def encoder_kernel(images, counts_ref, patches_ref, cols_ref, pos_ref, embed_ref, triple_ref, proj_ref, up_ref, down_ref, norms_ref, dec_embed_ref,
                   seen, entry, plain1, scale1, triple, probs, mixed, plain2, scale2, inner, act, slope, plain3, scale3, encoded, entering, x, place, pos_split):
    spots = lax.broadcasted_iota(jnp.int32, (KEEP, P_ROWS), 1)
    for t, part in enumerate(three(pos_ref[...])):
        pos_split[t] = part

    def select(i):
        at = rows_at(i, KEEP)
        pick = jnp.where(spots == cols_ref[i], 1.0, 0.0).astype(BF)
        seen[at, :] = dot_nn(pick, patches_ref[rows_at(i, P_ROWS), :]).astype(BF)
        place[at, :] = dot_nn(pick, pos_split[0]) + dot_nn(pick, pos_split[1]) + dot_nn(pick, pos_split[2])

    loop(images, select)

    def embed(j):
        at = rows_at(j, 256)
        x[:, at] = dot_nn(seen[...], embed_ref[:, at]) + place[:, at]

    loop(D // 256, embed)
    slot = lax.broadcasted_iota(jnp.int32, (KEEP, 1), 0)

    def key_bias(i):
        return jnp.where(slot < counts_ref[i], 0.0, NEG_FILL)

    block_forward(x, KEEP, images, KEEP, HEADS, (triple_ref, proj_ref, up_ref, down_ref), norms_ref, key_bias,
                  (entry, plain1, scale1, triple, probs, mixed, plain2, scale2, inner, act, slope))

    def last(i):
        at = rows_at(i, KEEP)
        plain, scale = norm(x[at, :])
        plain3[at, :] = plain
        scale3[at, :] = scale
        encoded[at, :] = (plain * norms_ref[4:5, :] + norms_ref[5:6, :]).astype(BF)

    loop(images, last)
    entering[...] = dot_nn(encoded[...], dec_embed_ref[...])


def encoder(counts, patches, cols, pos, weights, norms, dec_embed):
    images = counts.shape[0]
    rows = images * KEEP
    vmem = pl.BlockSpec(memory_space=pltpu.VMEM)

    def s(shape, kind):
        return jax.ShapeDtypeStruct(shape, kind)

    return pl.pallas_call(
        functools.partial(encoder_kernel, images),
        name="encoder",
        out_shape=[
            s((rows, D), BF), s((rows, D), BF), s((rows, D), F32), s((rows, 1), F32), s((rows, 3 * D), BF),
            s((images * D // LANES, LANES, KEEP), F32), s((rows, D), BF), s((rows, D), F32), s((rows, 1), F32), s((rows, D), BF),
            s((rows, F), BF), s((rows, F), F32), s((rows, D), F32), s((rows, 1), F32), s((rows, D), BF), s((rows, DD), F32),
        ],
        in_specs=[pl.BlockSpec(memory_space=pltpu.SMEM)] + [vmem] * 10,
        out_specs=[vmem] * 16,
        scratch_shapes=[pltpu.VMEM((rows, D), F32), pltpu.VMEM((rows, D), F32), pltpu.VMEM((3, P_ROWS, D), BF)],
        compiler_params=pltpu.CompilerParams(vmem_limit_bytes=60 * MB),
    )(counts, patches, cols, pos, *weights, norms, dec_embed)


def decoder_kernel(images, counts_ref, masked_ref, patches_ref, cols_ref, rows_ref, pos_ref, entering_ref, triple_ref, proj_ref, up_ref, down_ref, head_ref, norms_ref,
                   flat, grad_entering, loss_ref,
                   x, hide, entry, plain1, scale1, triple, probs, mixed, plain2, scale2, inner, act, slope, plain3, scale3, final, grad_pred,
                   low, grad_hidden, side, low_mixed, grad_triple, norm_sums, stage, sem):
    lane = lax.broadcasted_iota(jnp.int32, (P_ROWS, KEEP), 1)
    spot = lax.broadcasted_iota(jnp.int32, (P_ROWS, KEEP), 0)
    line = lax.broadcasted_iota(jnp.int32, (P_ROWS, 1), 0)

    def start(i):
        at = rows_at(i, P_ROWS)
        hit = jnp.where(jnp.logical_and(spot == rows_ref[pl.ds(i, 1), 0:KEEP], lane < counts_ref[i]), 1.0, 0.0)
        shown = jnp.max(hit, axis=1, keepdims=True)
        pick = hit.astype(BF)
        top, mid, end = three(entering_ref[rows_at(i, KEEP), :])
        picked = dot_nn(pick, top) + dot_nn(pick, mid) + dot_nn(pick, end)
        x[at, :] = jnp.where(shown > 0.0, picked, norms_ref[6:7, :]) + pos_ref[...]
        hide[at, :] = jnp.where(jnp.logical_and(line < PATCHES, shown == 0.0), 1.0, 0.0)

    loop(images, start)
    bias = jnp.where(line < PATCHES, 0.0, NEG_FILL)
    weights = (triple_ref, proj_ref, up_ref, down_ref)
    saved = (entry, plain1, scale1, triple, probs, mixed, plain2, scale2, inner, act, slope)
    block_forward(x, P_ROWS, images, PATCHES, DHEADS, weights, norms_ref, lambda i: bias, saved)

    def last(i):
        at = rows_at(i, P_ROWS)
        plain, scale = norm(x[at, :])
        plain3[at, :] = plain
        scale3[at, :] = scale
        final[at, :] = (plain * norms_ref[4:5, :] + norms_ref[5:6, :]).astype(BF)

    loop(images, last)
    loss_ref[...] = jnp.zeros_like(loss_ref)
    masked = masked_ref[0:1, 0:1]

    def score(i):
        at = rows_at(i, P_ROWS)
        target, _ = norm(patches_ref[at, :].astype(F32))
        diff = dot_nn(final[at, :], head_ref[...]) - target
        hidden = hide[at, :]
        loss_ref[...] += jnp.sum(jnp.mean(diff * diff, axis=-1, keepdims=True) * hidden, axis=0, keepdims=True)
        grad_pred[at, :] = (diff * (hidden * (2.0 / PIX)) / masked).astype(BF)

    loop(images, score)
    writer = Writer(flat, stage, sem)
    writer.outer(11, final, grad_pred)
    norm_sums[...] = jnp.zeros_like(norm_sums)

    def back_final(i):
        at = rows_at(i, P_ROWS)
        back, gain, shift = norm_grad(dot_nt(grad_pred[at, :], head_ref[...]), plain3[at, :], scale3[at, :], norms_ref[4:5, :])
        norm_sums[4:5, :] += gain
        norm_sums[5:6, :] += shift
        x[at, :] = back

    loop(images, back_final)
    block_backward(x, P_ROWS, images, PATCHES, DHEADS, weights, norms_ref, norm_sums, saved, (low, grad_hidden, side, low_mixed, grad_triple), writer, (7, 8, 9, 10))
    spots = lax.broadcasted_iota(jnp.int32, (KEEP, P_ROWS), 1)
    slot = lax.broadcasted_iota(jnp.int32, (KEEP, P_ROWS), 0)

    def finish(i):
        at = rows_at(i, P_ROWS)
        grad = x[at, :]
        norm_sums[6:7, :] += jnp.sum(grad * hide[at, :], axis=0, keepdims=True)
        pick = jnp.where(jnp.logical_and(spots == cols_ref[i], slot < counts_ref[i]), 1.0, 0.0).astype(BF)
        grad_entering[rows_at(i, KEEP), :] = dot_nn(pick, grad.astype(BF)).astype(BF)

    loop(images, finish)
    write_small(12, norm_sums, 7, flat, stage, sem)
    extra = flat.shape[0] - TILES
    if extra > 0:
        stage[0, 0:extra] = jnp.zeros((extra, 8, LANES), F32)
        copy = pltpu.make_async_copy(stage.at[0, pl.ds(0, extra)], flat.at[pl.ds(TILES, extra)], sem.at[0])
        copy.start()
        copy.wait()


def decoder(total, counts, masked, patches, cols, order, pos, entering, weights, head, norms):
    images = counts.shape[0]
    rows = images * P_ROWS
    vmem = pl.BlockSpec(memory_space=pltpu.VMEM)

    def v(shape, kind=F32):
        return pltpu.VMEM(shape, kind)

    return pl.pallas_call(
        functools.partial(decoder_kernel, images),
        name="decoder",
        out_shape=[
            jax.ShapeDtypeStruct((total, 8, LANES), F32),
            jax.ShapeDtypeStruct((images * KEEP, DD), BF),
            jax.ShapeDtypeStruct((1, 1), F32),
        ],
        in_specs=[pl.BlockSpec(memory_space=pltpu.SMEM)] + [vmem] * 12,
        out_specs=[pl.BlockSpec(memory_space=pl.ANY), vmem, vmem],
        scratch_shapes=[
            v((rows, DD)), v((rows, 1)), v((rows, DD), BF), v((rows, DD)), v((rows, 1)), v((rows, 3 * DD), BF),
            v((images * DD // LANES, 4 * P_ROWS, P_ROWS)), v((rows, DD), BF), v((rows, DD)), v((rows, 1)), v((rows, DD), BF),
            v((rows, FD), BF), v((rows, FD)), v((rows, DD)), v((rows, 1)), v((rows, DD), BF), v((rows, PIX), BF),
            v((rows, DD), BF), v((rows, FD), BF), v((rows, DD)), v((rows, DD), BF), v((rows, 3 * DD), BF),
            v((8, DD)), v((2, 32 * 16, 8, LANES)), pltpu.SemaphoreType.DMA((2,)),
        ],
        compiler_params=pltpu.CompilerParams(vmem_limit_bytes=63 * MB),
    )(counts, masked, patches, cols, order, pos, entering, *weights, head, norms)


def encoder_back_kernel(images, flat_in, grad_entering, seen, entry, plain1, scale1, triple, probs, mixed, plain2, scale2, inner, act, slope, plain3, scale3, encoded,
                        triple_ref, proj_ref, up_ref, down_ref, norms_ref, dec_embed_ref, flat, x, low, grad_hidden, side, low_mixed, grad_triple, norm_sums, stage, sem):
    writer = Writer(flat, stage, sem)
    writer.outer(6, encoded, grad_entering)
    norm_sums[...] = jnp.zeros_like(norm_sums)
    side[...] = dot_nt(grad_entering[...], dec_embed_ref[...])

    def last(i):
        at = rows_at(i, KEEP)
        back, gain, shift = norm_grad(side[at, :], plain3[at, :], scale3[at, :], norms_ref[4:5, :])
        norm_sums[4:5, :] += gain
        norm_sums[5:6, :] += shift
        x[at, :] = back

    loop(images, last)
    block_backward(x, KEEP, images, KEEP, HEADS, (triple_ref, proj_ref, up_ref, down_ref), norms_ref, norm_sums,
                   (entry, plain1, scale1, triple, probs, mixed, plain2, scale2, inner, act, slope), (low, grad_hidden, side, low_mixed, grad_triple), writer, (1, 2, 3, 4))
    low[...] = x[...].astype(BF)
    writer.outer(0, seen, low)
    write_small(5, norm_sums, 6, flat, stage, sem)


def encoder_back(flat, grad_entering, saved, weights, norms, dec_embed):
    rows = grad_entering.shape[0]
    images = rows // KEEP
    vmem = pl.BlockSpec(memory_space=pltpu.VMEM)
    anyspec = pl.BlockSpec(memory_space=pl.ANY)

    def v(shape, kind=F32):
        return pltpu.VMEM(shape, kind)

    return pl.pallas_call(
        functools.partial(encoder_back_kernel, images),
        name="encoder_back",
        out_shape=jax.ShapeDtypeStruct(flat.shape, flat.dtype),
        in_specs=[anyspec] + [vmem] * (1 + len(saved) + 6),
        out_specs=anyspec,
        scratch_shapes=[
            v((rows, D)), v((rows, D), BF), v((rows, F), BF), v((rows, D)), v((rows, D), BF), v((rows, 3 * D), BF),
            v((8, D)), v((2, 32 * 24, 8, LANES)), pltpu.SemaphoreType.DMA((2,)),
        ],
        input_output_aliases={0: 0},
        compiler_params=pltpu.CompilerParams(vmem_limit_bytes=60 * MB),
    )(flat, grad_entering, *saved, *weights, norms, dec_embed)


def positions(width):
    index = jnp.arange(PATCHES)
    quarter = width // 4
    freq = 10000.0 ** (-jnp.arange(quarter).astype(jnp.float32) / quarter)
    row = (index // GRID).astype(jnp.float32)[:, None] * freq[None, :]
    column = (index % GRID).astype(jnp.float32)[:, None] * freq[None, :]
    return jnp.concatenate([jnp.sin(row), jnp.cos(row), jnp.sin(column), jnp.cos(column)], axis=1)


ADAM_EPS = 1e-08
BETA_ONE = 0.9
BETA_TWO = 0.95
DECAY = 0.05


def own_lines(flat, share, index):
    if share % LANES == 0:
        return flat.reshape(-1, LANES)
    rows = (share + LANES - 1) // LANES + 1
    return lax.dynamic_update_slice(jnp.zeros((rows * LANES,), flat.dtype), flat, (share * index % LANES,)).reshape(rows, LANES)


def own_flat(lines, share, index):
    if share % LANES == 0:
        return lines.reshape(-1)
    return lax.dynamic_slice(lines.reshape(-1), (share * index % LANES,), (share,))


def body(n_dp, n_pair, patches, patch_order, counts, master, moment1, moment2, block_rates, clip_limit, step_count):
    n = n_dp * n_pair
    share = master.shape[0]
    images = counts.shape[0]
    index = lax.axis_index("dp") * n_pair + lax.axis_index("pair")
    extra = jnp.zeros((8, LANES), F32).at[0, :images].set((PATCHES - counts).astype(F32))
    slab = to_tiles(own_lines(master, share, index), extra, share, n, n_pair)
    slots = gather(slab, n_dp, n_pair)
    masked = jnp.sum(slots[:, slab.shape[0] - 2, 0, :].astype(F32))
    held = assemble(slots, share)
    parts = [held[i].reshape(-1)[: SHAPES[i][0] * SHAPES[i][1]].reshape(SHAPES[i]).astype(F32) if i in SMALL else matrix(held[i], i) for i in range(len(SHAPES))]
    padded = jnp.pad(patches, ((0, 0), (0, P_ROWS - PATCHES), (0, 0))).reshape(images * P_ROWS, PIX)
    slots_at = patch_order[:, :KEEP]
    cols = slots_at[:, :, None]
    pos_e = jnp.pad(positions(D), ((0, P_ROWS - PATCHES), (0, 0)))
    pos_d = jnp.pad(positions(DD), ((0, P_ROWS - PATCHES), (0, 0)))
    enc_weights = parts[1:5]
    *saved, entering = encoder(counts, padded, cols, pos_e, [parts[0]] + enc_weights, parts[5], parts[6])
    total = max(a for a, _ in ranges(share, n)) + slab_tiles(share, n)
    flat, grad_entering, loss_local = decoder(
        total, counts, masked.reshape(1, 1), padded, cols, slots_at, pos_d, entering, parts[7:11], parts[11], parts[12]
    )
    flat = encoder_back(flat, grad_entering, saved, enc_weights, parts[5], parts[6])
    slab_sum = reduce(flat.reshape(-1, LANES), share, n_dp, n_pair)
    rows = share // LANES if share % LANES == 0 else (share + LANES - 1) // LANES + 1
    grad_share = own_flat(to_lines(slab_sum, rows, share, n_pair), share, index)
    scalars = jnp.stack([jnp.sum(grad_share * grad_share), loss_local[0, 0]])
    shared = share_all(jnp.zeros((8, LANES), F32).at[0, :2].set(scalars), n_dp, n_pair, 2)
    squares, loss_sum = jnp.sum(shared[:, 0, 0]), jnp.sum(shared[:, 0, 1])
    grad_norm = jnp.sqrt(squares)
    loss = loss_sum / masked
    clipped = grad_share * (clip_limit[0] / (grad_norm + NORM_EPS))
    first = BETA_ONE * moment1 + (1.0 - BETA_ONE) * clipped
    second = BETA_TWO * moment2 + (1.0 - BETA_TWO) * clipped * clipped
    steps_done = step_count[0].astype(F32)
    position = index * share + jnp.arange(share)
    rate = jnp.where(position < ENC_PARAMS, block_rates[0], block_rates[1])
    update = first / (1.0 - BETA_ONE**steps_done) / (jnp.sqrt(second / (1.0 - BETA_TWO**steps_done)) + ADAM_EPS)
    master_new = master - rate * (update + DECAY * master)
    return (loss.reshape(1), grad_norm.reshape(1), first, second, master_new)


def solution(mesh):
    whole = P(("dp", "pair"))
    in_specs = (P(("dp", "pair"), None, None), P(("dp", "pair"), None), whole, whole, whole, whole, P(), P(), P())
    out_specs = (P(), P(), whole, whole, whole)
    step = functools.partial(body, mesh.shape["dp"], mesh.shape["pair"])
    return jax.shard_map(step, mesh=mesh, in_specs=in_specs, out_specs=out_specs, check_vma=False)
```

```python
import functools

import jax
import jax.numpy as jnp
import numpy as np
from jax import lax
from jax.experimental import pallas as pl
from jax.experimental.pallas import tpu as pltpu
from jax.sharding import PartitionSpec as P

MESH = pl.DeviceIdType.MESH
LANES = 128
TILE = 16 * LANES


def place():
    dp, pair = lax.axis_index("dp"), lax.axis_index("pair")
    return dp // 2, dp % 2, pair // 2, pair % 2


def slot_of(z, x, y, c):
    return (z * 2 + x) * 4 + y * 2 + c


def partners(z, x, y, c):
    return {
        "x": {"dp": z * 2 + (1 - x)},
        "y": {"pair": (1 - y) * 2 + c},
        "c": {"pair": y * 2 + (1 - c)},
        "up": {"dp": (z + 1) * 2 + x},
        "down": {"dp": (z - 1) * 2 + x},
    }


def greet(n_z, z, to):
    barrier = pltpu.get_barrier_semaphore()
    for name in ("x", "y", "c"):
        pl.semaphore_signal(barrier, inc=1, device_id=to[name], device_id_type=MESH)

    @pl.when(z < n_z - 1)
    def _():
        pl.semaphore_signal(barrier, inc=1, device_id=to["up"], device_id_type=MESH)

    @pl.when(z > 0)
    def _():
        pl.semaphore_signal(barrier, inc=1, device_id=to["down"], device_id_type=MESH)

    pl.semaphore_wait(barrier, 3 + jnp.where(z < n_z - 1, 1, 0) + jnp.where(z > 0, 1, 0))


def both(*conditions):
    total = conditions[0]
    for one in conditions[1:]:
        total = jnp.logical_and(total, one)
    return total


def gather_kernel(n_z, chunks, slab_ref, out_ref, own_sem, z_sem, plane_sem, second_sem, third_sem, recv_sem):
    piece = slab_ref.shape[0] // (2 * chunks)
    z, x, y, c = place()
    to = partners(z, x, y, c)
    me = slot_of(z, x, y, c)
    local = pltpu.make_async_copy(slab_ref, out_ref.at[me], own_sem)
    local.start()
    greet(n_z, z, to)
    local.wait()
    steps = n_z * chunks

    def copy(slot, chunk, part, name, sem):
        rows = pl.ds((chunk * 2 + part) * piece, piece)
        return pltpu.make_async_remote_copy(
            out_ref.at[slot, rows],
            out_ref.at[slot, rows],
            sem,
            recv_sem.at[slot, chunk, part],
            device_id=to[name],
            device_id_type=MESH,
        )

    def arrived(slot, chunk, part):
        copy(slot, chunk, part, "c", own_sem).wait_recv()

    def lines(s):
        t, chunk = s // chunks, lax.rem(s, chunks)
        for d in (0, 1):
            zz = z - t if d == 0 else z + t
            inside = zz >= 0 if d == 0 else zz < n_z
            more = z < n_z - 1 if d == 0 else z > 0
            fresh = both(t > 0, inside)
            held = jnp.logical_or(fresh, t == 0) if d == 0 else fresh
            onward = both(jnp.logical_or(fresh, t == 0), more)
            yield d, zz, chunk, fresh, held, onward

    def first_sends(d, zz, chunk, held, onward, s, act):
        slot = slot_of(zz, x, y, c)
        for part in (0, 1):
            pl.when(onward)(lambda part=part: act(copy(slot, chunk, part, ("up", "down")[d], z_sem.at[s, d, part])))

        @pl.when(held)
        def _():
            for i, (part, name) in enumerate(((0, "x"), (1, "y"), (0, "y"), (1, "x"), (0, "c"), (1, "c"))):
                act(copy(slot, chunk, part, name, plane_sem.at[s, d, i]))

    def first(s):
        for d, zz, chunk, fresh, held, onward in lines(s):

            @pl.when(fresh)
            def _():
                for part in (0, 1):
                    arrived(slot_of(zz, x, y, c), chunk, part)

            first_sends(d, zz, chunk, held, onward, s, lambda one: one.start())

    def second_items(zz):
        return ((0, slot_of(zz, 1 - x, y, c), "y"), (1, slot_of(zz, x, 1 - y, c), "x"))

    def second(s):
        for d, zz, chunk, _, held, _ in lines(s):

            @pl.when(held)
            def _():
                for part, slot, name in second_items(zz):
                    arrived(slot, chunk, part)
                    copy(slot, chunk, part, name, second_sem.at[s, d, part, 0]).start()
                    copy(slot, chunk, part, "c", second_sem.at[s, d, part, 1]).start()

    def third_items(zz):
        return ((0, slot_of(zz, x, 1 - y, c)), (1, slot_of(zz, 1 - x, y, c)), (0, slot_of(zz, 1 - x, 1 - y, c)), (1, slot_of(zz, 1 - x, 1 - y, c)))

    def third(s):
        for d, zz, chunk, _, held, _ in lines(s):

            @pl.when(held)
            def _():
                for i, (part, slot) in enumerate(third_items(zz)):
                    arrived(slot, chunk, part)
                    copy(slot, chunk, part, "c", third_sem.at[s, d, i]).start()

    def turn(s, _):
        pl.when(s < steps)(lambda: first(s))
        pl.when(both(s >= 1, s < steps + 1))(lambda: second(s - 1))
        pl.when(s >= 2)(lambda: third(s - 2))
        return 0

    lax.fori_loop(0, steps + 2, turn, 0)

    def finish(s, _):
        for d, zz, chunk, _, held, onward in lines(s):
            first_sends(d, zz, chunk, held, onward, s, lambda one: one.wait_send())

            @pl.when(held)
            def _():
                for part, slot, name in second_items(zz):
                    copy(slot, chunk, part, name, second_sem.at[s, d, part, 0]).wait_send()
                    copy(slot, chunk, part, "c", second_sem.at[s, d, part, 1]).wait_send()
                for i, (part, slot) in enumerate(third_items(zz)):
                    copy(slot, chunk, part, "c", third_sem.at[s, d, i]).wait_send()
                for ox in (0, 1):
                    for oy in (0, 1):
                        for part in (0, 1):
                            arrived(slot_of(zz, ox, oy, 1 - c), chunk, part)

        return 0

    lax.fori_loop(0, steps, finish, 0)


def gather(slab, n_dp, n_pair, chunks):
    n_z = n_dp // 2
    n = n_dp * n_pair
    steps = n_z * chunks
    dma = pltpu.SemaphoreType.DMA
    return pl.pallas_call(
        functools.partial(gather_kernel, n_z, chunks),
        name="gather",
        out_shape=jax.ShapeDtypeStruct((n,) + slab.shape, slab.dtype),
        in_specs=[pl.BlockSpec(memory_space=pltpu.VMEM)],
        out_specs=pl.BlockSpec(memory_space=pl.ANY),
        scratch_shapes=[dma, dma((steps, 2, 2)), dma((steps, 2, 6)), dma((steps, 2, 2, 2)), dma((steps, 2, 4)), dma((n, chunks, 2))],
        compiler_params=pltpu.CompilerParams(collective_id=0, has_side_effects=True),
    )(slab)


PIX, HEADS, F, DHEADS, FD, GRID, KEEP, D, DD, PATCHES = 768, 12, 3072, 16, 2048, 14, 64, 768, 512, 196
SHAPES = [(PIX, D), (D, 3 * D), (D, D), (D, F), (F, D), (6, D), (D, DD), (DD, 3 * DD), (DD, DD), (DD, FD), (FD, DD), (DD, PIX), (7, DD)]
SMALL = (5, 12)
ENC_PARAMS = 7672320
MB = 1 << 20
CELL = 8 * LANES
BLOCK = 96


def make_entries():
    entries, row, tile = [], 0, 0
    for number, (rows, width) in enumerate(SHAPES):
        lines = rows * width // LANES
        cols = 1 if number in SMALL else width // LANES
        groups = -(-lines // (8 * cols))
        entries.append((row, lines, cols, tile, groups))
        row += lines
        tile += groups * cols
    return entries, row, tile


ENTRIES, ROWS, TILES = make_entries()
MARGIN = 8 * max(cols for _, _, cols, _, _ in ENTRIES)


def first_tile(share, k):
    lo = share * k
    total = 0
    for row, lines, cols, tile, _ in ENTRIES:
        inside = jnp.logical_and(lo >= row * LANES, lo < (row + lines) * LANES)
        total = total + jnp.where(inside, tile + (lo - row * LANES) // (CELL * cols) * cols, 0)
    return total


def ranges(share, n):
    found = []
    for k in range(n):
        lo, hi = share * k, share * (k + 1)
        spans = []
        for row, lines, cols, tile, _ in ENTRIES:
            low, high = max(lo, row * LANES), min(hi, (row + lines) * LANES)
            if low < high:
                size = CELL * cols
                spans.append((tile + (low - row * LANES) // size * cols, tile + -(-(high - row * LANES) // size) * cols))
        found.append((spans[0][0], spans[-1][1]))
    return found


def slab_tiles(share, n):
    longest = max(b - a for a, b in ranges(share, n))
    return -(-longest // 24) * 24


def line_span(share, k):
    return share * k // LANES, (share * (k + 1) + LANES - 1) // LANES


def tiled(share, k, body):
    lo, hi = line_span(share, k)
    begin = first_tile(share, k)
    for number in SMALL + tuple(i for i in range(len(ENTRIES)) if i not in SMALL):
        row, lines, cols, tile, _ = ENTRIES[number]
        low = jnp.maximum(lo, row) - row
        high = jnp.minimum(hi, row + lines) - row
        size = 8 * cols

        def group(g, _, row=row, cols=cols, tile=tile, size=size):
            body(row + g * size - lo + MARGIN, tile + g * cols - begin, cols)
            return 0

        lax.fori_loop(jnp.where(low < high, low // size, 0), jnp.where(low < high, (high + size - 1) // size, 0), group, 0)


def tile_kernel(share, n_pair, lines_ref, extra_ref, out_ref, wide):
    k = lax.axis_index("dp") * n_pair + lax.axis_index("pair")
    rows = lines_ref.shape[0]
    wide[0:MARGIN, :] = jnp.zeros((MARGIN, LANES), jnp.float32)
    wide[MARGIN + rows :, :] = jnp.zeros((wide.shape[0] - MARGIN - rows, LANES), jnp.float32)
    wide[MARGIN : MARGIN + rows, :] = lines_ref[...]

    def body(line, tile, cols):
        for col in range(cols):
            out_ref[tile + col] = wide[pl.ds(line + col, 8, stride=cols), :].astype(out_ref.dtype)

    tiled(share, k, body)
    out_ref[out_ref.shape[0] - 2] = extra_ref[...].astype(out_ref.dtype)


def wide_rows(rows):
    return -(-(rows + 2 * MARGIN) // 8) * 8


def to_tiles(lines, extra, share, n, n_pair):
    rows = lines.shape[0]
    count = slab_tiles(share, n) + 2
    spec = pl.BlockSpec(memory_space=pltpu.VMEM)
    return pl.pallas_call(
        functools.partial(tile_kernel, share, n_pair),
        name="to_tiles",
        out_shape=jax.ShapeDtypeStruct((count, 8, LANES), jnp.bfloat16),
        in_specs=[spec, spec],
        out_specs=spec,
        scratch_shapes=[pltpu.VMEM((wide_rows(rows), LANES), jnp.float32)],
    )(lines, extra)


def line_kernel(share, n_pair, slab_ref, out_ref, wide):
    k = lax.axis_index("dp") * n_pair + lax.axis_index("pair")

    def body(line, tile, cols):
        for col in range(cols):
            wide[pl.ds(line + col, 8, stride=cols), :] = slab_ref[pl.ds(pl.multiple_of((tile + col) * 8, 8), 8), :]

    tiled(share, k, body)
    out_ref[...] = wide[MARGIN : MARGIN + out_ref.shape[0], :]


def to_lines(slab, rows, share, n_pair):
    spec = pl.BlockSpec(memory_space=pltpu.VMEM)
    return pl.pallas_call(
        functools.partial(line_kernel, share, n_pair),
        name="to_lines",
        out_shape=jax.ShapeDtypeStruct((rows, LANES), jnp.float32),
        in_specs=[spec],
        out_specs=spec,
        scratch_shapes=[pltpu.VMEM((wide_rows(rows), LANES), jnp.float32)],
    )(slab)


def pieces(share, n):
    spans = ranges(share, n)
    shared = [spans[k][1] > spans[k + 1][0] for k in range(n - 1)]
    plain, seams = [], []
    for number, (_, _, cols, tile, groups) in enumerate(ENTRIES):
        end = tile + groups * cols
        for k, (a, b) in enumerate(spans):
            low, high = max(a, tile), min(b, end)
            if low >= high:
                continue
            inner_low, inner_high = low, high
            if k > 0 and spans[k - 1][1] > low:
                inner_low = spans[k - 1][1]
            if k < n - 1 and spans[k + 1][0] < high:
                inner_high = spans[k + 1][0]
                seams.append((number, k, inner_high, high))
            if inner_low < inner_high:
                plain.append((number, k, inner_low, inner_high))
    return spans, plain, seams


def assemble_kernel(share, n, slots_ref, *refs):
    outs = refs[: len(ENTRIES)]
    whole, right, plain_sem, left_sem, right_sem, out_sem = refs[len(ENTRIES) :]
    spans, plain, seams = pieces(share, n)
    waits = [[] for _ in ENTRIES]
    for i, (number, k, low, high) in enumerate(plain):
        copy = pltpu.make_async_copy(slots_ref.at[k, pl.ds(low - spans[k][0], high - low)], whole.at[pl.ds(low, high - low)], plain_sem.at[i])
        copy.start()
        waits[number].append(copy)
    for i, (number, k, low, high) in enumerate(seams):
        one = pltpu.make_async_copy(slots_ref.at[k, pl.ds(low - spans[k][0], high - low)], whole.at[pl.ds(low, high - low)], left_sem.at[i])
        two = pltpu.make_async_copy(
            slots_ref.at[k + 1, pl.ds(low - spans[k + 1][0], high - low)], right.at[i, pl.ds(0, high - low)], right_sem.at[i]
        )
        one.start()
        two.start()
        waits[number] += [one, two]
    ended = []
    for number, (_, _, cols, tile, groups) in enumerate(ENTRIES):
        for copy in waits[number]:
            copy.wait()
        for i, (owner, k, low, high) in enumerate(seams):
            if owner == number:
                total = whole[low:high].astype(jnp.float32) + right[i, 0 : high - low].astype(jnp.float32)
                whole[low:high] = total.astype(jnp.bfloat16)
        copy = pltpu.make_async_copy(whole.at[pl.ds(tile, groups * cols)], outs[number], out_sem.at[number])
        copy.start()
        ended.append(copy)
    for copy in ended:
        copy.wait()


def assemble(slots, share):
    n = slots.shape[0]
    _, plain, seams = pieces(share, n)
    anyspec = pl.BlockSpec(memory_space=pl.ANY)
    dma = pltpu.SemaphoreType.DMA
    return pl.pallas_call(
        functools.partial(assemble_kernel, share, n),
        name="assemble",
        out_shape=[jax.ShapeDtypeStruct((groups * cols, 8, LANES), jnp.bfloat16) for _, _, cols, _, groups in ENTRIES],
        in_specs=[anyspec],
        out_specs=[anyspec] * len(ENTRIES),
        scratch_shapes=[
            pltpu.VMEM((TILES, 8, LANES), jnp.bfloat16),
            pltpu.VMEM((len(seams), MARGIN // 8, 8, LANES), jnp.bfloat16),
            dma((len(plain),)),
            dma((len(seams),)),
            dma((len(seams),)),
            dma((len(ENTRIES),)),
        ],
        compiler_params=pltpu.CompilerParams(vmem_limit_bytes=60 * MB),
    )(slots)


def matrix(tiles_, number):
    rows, width = SHAPES[number]
    cols = width // LANES
    return tiles_.reshape(rows // 8, cols, 8, LANES).transpose(0, 2, 1, 3).reshape(rows, width)


def matrix_tiles(value):
    rows, width = value.shape
    cols = width // LANES
    return value.reshape(rows // 8, 8, cols, LANES).transpose(0, 2, 1, 3).reshape(rows * cols, LANES)


def reduce_kernel(n_z, chunks, share, grad_ref, out_ref, sib_ref, gbuf, rbuf, keep, q1s, q1r, q2s, q2r, zs, zr, t1s, t1r, t2s, t2r, tzs, tzr, sib_sem, load_sem, s1_sem, s2_sem, z_sem):
    z, x, y, c = place()
    to = partners(z, x, y, c)
    rows = out_ref.shape[0] // chunks
    half = rows // 2
    steps = n_z * chunks
    count = half // BLOCK

    def start_of(k):
        return pl.multiple_of(first_tile(share, k) * 8, 8)

    def order(j):
        low = z < n_z // 2
        far = jnp.where(low, n_z - 1 - j, j)
        moved = jnp.where(low, jnp.where(far > z, far, far - 1), jnp.where(far < z, far, far + 1))
        return jnp.where(j == n_z - 1, z, moved)

    def lines_of(s, xx, yy, core):
        k = slot_of(order(s // chunks), xx, yy, core)
        return pl.ds(pl.multiple_of(start_of(k) + lax.rem(s, chunks) * rows, 8), rows)

    def kept(s, part, b):
        return s // chunks, pl.ds(pl.multiple_of(lax.rem(s, chunks) * rows + part * half + b * BLOCK, BLOCK), BLOCK)

    def sibling(s, xx, yy, core):
        return pltpu.make_async_remote_copy(
            grad_ref.at[lines_of(s, xx, yy, core)],
            sib_ref.at[s, xx * 2 + yy],
            sib_sem.at[0, s, xx * 2 + yy],
            sib_sem.at[1, s, xx * 2 + yy],
            device_id=to["c"],
            device_id_type=MESH,
        )

    def loads(j, s, q):
        return (
            pltpu.make_async_copy(grad_ref.at[lines_of(j, q // 2, q % 2, c)], gbuf.at[s, q], load_sem.at[0, s, q]),
            pltpu.make_async_copy(sib_ref.at[j, q], rbuf.at[s, q], load_sem.at[1, s, q]),
        )

    def load(j):
        s = lax.rem(j, 2)
        for q in range(4):
            sibling(j, q // 2, q % 2, 1 - c).wait_recv()
            for one in loads(j, s, q):
                one.start()

    def pack(value, q_ref, t_ref, b):
        top = jnp.max(jnp.abs(value), axis=0, keepdims=True)
        inverse = jnp.where(top > 1e-30, 32767.0 / jnp.maximum(top, 1e-30), 0.0)
        q_ref[pl.ds(pl.multiple_of(b * BLOCK, BLOCK), BLOCK), :] = jnp.round(value * inverse).astype(jnp.int32).astype(jnp.int16)
        t_ref[pl.ds(b, 1), :] = top * (1.0 / 32767.0)

    def unpack(q_ref, t_ref, b):
        return q_ref[pl.ds(pl.multiple_of(b * BLOCK, BLOCK), BLOCK), :].astype(jnp.int32).astype(jnp.float32) * t_ref[pl.ds(b, 1), :]

    def each(body):
        def one(b, _):
            body(b)
            return 0

        lax.fori_loop(0, count, one, 0)

    def own(s, q, part, b):
        at = pl.ds(pl.multiple_of(part * half + b * BLOCK, BLOCK), BLOCK)
        return gbuf[s, q, at, :] + rbuf[s, q, at, :]

    def message(qs, ts, qr, tr, sem, name):
        return (
            pltpu.make_async_remote_copy(qs, qr, sem.at[0, 0], sem.at[0, 1], device_id=to[name], device_id_type=MESH),
            pltpu.make_async_remote_copy(ts, tr, sem.at[1, 0], sem.at[1, 1], device_id=to[name], device_id_type=MESH),
        )

    def first_message(j, part, other):
        i = part * 2 + other
        return message(q1s.at[j, i], t1s.at[j, i], q1r.at[j, i], t1r.at[j, i], s1_sem.at[j, i], ("x", "y")[part])

    def second_message(j, part):
        return message(q2s.at[j, part], t2s.at[j, part], q2r.at[j, part], t2r.at[j, part], s2_sem.at[j, part], ("y", "x")[part])

    def z_message(zz, part, name):
        d = 0 if name == "up" else 1
        return message(zs.at[zz, part], tzs.at[zz, part], zr.at[d, zz, part], tzr.at[d, zz, part], z_sem.at[d, zz, part], name)

    def quarter(part, other, mine):
        if part == 0:
            return (x if mine else 1 - x) * 2 + other
        return other * 2 + (y if mine else 1 - y)

    def stage_one(j):
        s = lax.rem(j, 2)
        for q in range(4):
            for one in loads(j, s, q):
                one.wait()
        for part in (0, 1):
            for other in (0, 1):
                q = quarter(part, other, False)
                i = part * 2 + other
                each(lambda b: pack(own(s, q, part, b), q1s.at[j, i], t1s.at[j, i], b))
                for one in first_message(j, part, other):
                    one.start()

    def stage_two(j):
        s = lax.rem(j, 2)
        for part in (0, 1):
            for other in (0, 1):
                for one in first_message(j, part, other):
                    one.wait_recv()
            here = (y, x)[part]
            away = quarter(part, 1 - here, True)
            i = part * 2 + 1 - here
            each(lambda b: pack(own(s, away, part, b) + unpack(q1r.at[j, i], t1r.at[j, i], b), q2s.at[j, part], t2s.at[j, part], b))
            for one in second_message(j, part):
                one.start()
        for part in (0, 1):
            here = (y, x)[part]
            mine = x * 2 + y
            k = part * 2 + here

            def store(b, part=part, k=k):
                group, at = kept(j, part, b)
                keep[group, at, :] = own(s, mine, part, b) + unpack(q1r.at[j, k], t1r.at[j, k], b)

            each(store)

    def add_to_keep(j, part, q_ref, t_ref):
        def body(b):
            group, at = kept(j, part, b)
            keep[group, at, :] += unpack(q_ref, t_ref, b)

        each(body)

    def stage_three(j):
        for part in (0, 1):
            for one in second_message(j, part):
                one.wait_recv()
            add_to_keep(j, part, q2r.at[j, part], t2r.at[j, part])

    def pass_on(j, zz, part, name):
        def body(b):
            group, at = kept(j, part, b)
            pack(keep[group, at, :], zs.at[zz, part], tzs.at[zz, part], b)

        each(body)
        for one in z_message(zz, part, name):
            one.start()

    def stage_four(j):
        zz = order(j // chunks)
        zc = zz * chunks + lax.rem(j, chunks)
        for part in (0, 1):
            for d, name, has, onward in ((0, "up", z > 0, zz > z), (1, "down", z < n_z - 1, zz < z)):
                back = zz >= z if d == 0 else zz <= z

                @pl.when(jnp.logical_and(has, back))
                def _():
                    for one in z_message(zc, part, name):
                        one.wait_recv()
                    add_to_keep(j, part, zr.at[d, zc, part], tzr.at[d, zc, part])

                @pl.when(onward)
                def _():
                    pass_on(j, zc, part, name)

    greet(n_z, z, to)

    def begin(j, _):
        for q in range(4):
            sibling(j, q // 2, q % 2, 1 - c).start()
        return 0

    lax.fori_loop(0, steps, begin, 0)
    load(0)

    def turn(t, _):
        pl.when(t < steps)(lambda: stage_one(t))
        pl.when(jnp.logical_and(t >= 1, t <= steps))(lambda: stage_two(t - 1))
        pl.when(t + 1 < steps)(lambda: load(t + 1))
        pl.when(jnp.logical_and(t >= 2, t <= steps + 1))(lambda: stage_three(t - 2))
        pl.when(t >= 3)(lambda: stage_four(t - 3))
        return 0

    lax.fori_loop(0, steps + 3, turn, 0)
    out_ref[...] = keep[n_z - 1]

    def finish(j, _):
        zz = order(j // chunks)
        zc = zz * chunks + lax.rem(j, chunks)
        for q in range(4):
            sibling(j, q // 2, q % 2, 1 - c).wait_send()
        for part in (0, 1):
            for other in (0, 1):
                for one in first_message(j, part, other):
                    one.wait_send()
            for one in second_message(j, part):
                one.wait_send()

            @pl.when(zz > z)
            def _():
                for one in z_message(zc, part, "up"):
                    one.wait_send()

            @pl.when(zz < z)
            def _():
                for one in z_message(zc, part, "down"):
                    one.wait_send()

        return 0

    lax.fori_loop(0, steps, finish, 0)


def reduce_chunks(share, n):
    rows = slab_tiles(share, n) * 8
    return max(d for d in (1, 2, 4) if rows % (2 * BLOCK * d) == 0)


def reduce(flat, share, n_dp, n_pair):
    chunks = reduce_chunks(share, n_dp * n_pair)
    n_z, n = n_dp // 2, n_dp * n_pair
    rows = slab_tiles(share, n) * 8
    part = rows // chunks
    half = part // 2
    steps = n_z * chunks
    marks = (half // BLOCK + 7) // 8 * 8
    anyspec = pl.BlockSpec(memory_space=pl.ANY)

    def q(*lead):
        return pltpu.VMEM(lead + (half, LANES), jnp.int16)

    def t(*lead):
        return pltpu.VMEM(lead + (marks, LANES), jnp.float32)

    dma = pltpu.SemaphoreType.DMA
    return pl.pallas_call(
        functools.partial(reduce_kernel, n_z, chunks, share),
        name="reduce_scatter",
        out_shape=[jax.ShapeDtypeStruct((rows, LANES), jnp.float32), jax.ShapeDtypeStruct((steps, 4, part, LANES), jnp.float32)],
        in_specs=[anyspec],
        out_specs=[pl.BlockSpec(memory_space=pltpu.VMEM), anyspec],
        scratch_shapes=[
            pltpu.VMEM((2, 4, part, LANES), jnp.float32),
            pltpu.VMEM((2, 4, part, LANES), jnp.float32),
            pltpu.VMEM((n_z, rows, LANES), jnp.float32),
            q(steps, 4), q(steps, 4), q(steps, 2), q(steps, 2), q(steps, 2), q(2, steps, 2),
            t(steps, 4), t(steps, 4), t(steps, 2), t(steps, 2), t(steps, 2), t(2, steps, 2),
            dma((2, steps, 4)), dma((2, 2, 4)), dma((steps, 4, 2, 2)), dma((steps, 2, 2, 2)), dma((2, steps, 2, 2, 2)),
        ],
        compiler_params=pltpu.CompilerParams(collective_id=1, has_side_effects=True, vmem_limit_bytes=60 * MB),
    )(flat)[0]


def share_kernel(n_dp, n_pair, in_ref, out_ref, send_sem, recv_sem):
    n = n_dp * n_pair
    me = lax.axis_index("dp") * n_pair + lax.axis_index("pair")
    barrier = pltpu.get_barrier_semaphore()

    def other(d):
        k = lax.rem(me + d, n)
        return {"dp": k // n_pair, "pair": lax.rem(k, n_pair)}

    def hello(d, _):
        pl.semaphore_signal(barrier, inc=1, device_id=other(d), device_id_type=MESH)
        return 0

    lax.fori_loop(1, n, hello, 0)
    pl.semaphore_wait(barrier, n - 1)
    out_ref[me] = in_ref[...]

    def copy(d):
        return pltpu.make_async_remote_copy(in_ref, out_ref.at[me], send_sem.at[d], recv_sem.at[d], device_id=other(d), device_id_type=MESH)

    def go(d, _):
        copy(d).start()
        return 0

    def stop(d, _):
        copy(d).wait()
        return 0

    lax.fori_loop(1, n, go, 0)
    lax.fori_loop(1, n, stop, 0)


def share_all(value, n_dp, n_pair, ident):
    n = n_dp * n_pair
    spec = pl.BlockSpec(memory_space=pltpu.VMEM)
    return pl.pallas_call(
        functools.partial(share_kernel, n_dp, n_pair),
        name="share_all",
        out_shape=jax.ShapeDtypeStruct((n,) + value.shape, value.dtype),
        in_specs=[spec],
        out_specs=spec,
        scratch_shapes=[pltpu.SemaphoreType.DMA((n,)), pltpu.SemaphoreType.DMA((n,))],
        compiler_params=pltpu.CompilerParams(collective_id=ident, has_side_effects=True),
    )(value)


NORM_EPS = 1e-06
NEG_FILL = -1000000000.0
P_ROWS = 208
BF = jnp.bfloat16
F32 = jnp.float32


def dot_nn(left, right):
    return lax.dot_general(left, right, (((1,), (0,)), ((), ())), preferred_element_type=F32)


def dot_nt(left, right):
    return lax.dot_general(left, right, (((1,), (1,)), ((), ())), preferred_element_type=F32)


def loop(count, body, unroll=1):
    def step(i, _):
        body(i)
        return 0

    lax.fori_loop(0, count, step, 0, unroll=unroll)


def rows_at(i, size):
    return pl.ds(pl.multiple_of(i * size, size), size)


def norm(x):
    centered = x - jnp.mean(x, axis=-1, keepdims=True)
    scale = lax.rsqrt(jnp.mean(centered * centered, axis=-1, keepdims=True) + NORM_EPS)
    return centered * scale, scale


def norm_grad(grad, plain, scale, gain):
    inner = grad * gain
    back = scale * (inner - jnp.mean(inner, axis=-1, keepdims=True) - plain * jnp.mean(inner * plain, axis=-1, keepdims=True))
    return back, jnp.sum(grad * plain, axis=0, keepdims=True), jnp.sum(grad, axis=0, keepdims=True)


def gelu_pair(h):
    cumulative = 0.5 * (1.0 + lax.erf(h * 0.7071067811865476))
    density = jnp.exp(-0.5 * h * h) * 0.3989422804014327
    return h * cumulative, cumulative + h * density


def head_masks(size):
    lane = lax.broadcasted_iota(jnp.int32, (1, LANES), 1)
    shift = size.bit_length() - 1
    return [jnp.where((lane >> shift) == h, 1.0, 0.0).astype(BF) for h in range(LANES // size)]


def three(value):
    top = value.astype(BF)
    rest = value - top.astype(F32)
    mid = rest.astype(BF)
    return top, mid, (rest - mid.astype(F32)).astype(BF)


class Moves:
    def __init__(self, names, sources, targets, sems):
        self.targets = dict(zip(names, targets))
        self.copies = {name: pltpu.make_async_copy(a, b, sems.at[i]) for i, (name, a, b) in enumerate(zip(names, sources, targets))}
        self.open = []

    def start(self, *names):
        for name in names or self.copies:
            self.copies[name].start()
            self.open.append(name)

    def __call__(self, name):
        if name in self.open:
            self.copies[name].wait()
            self.open.remove(name)
        return self.targets[name]

    def close(self):
        for name in list(self.open):
            self(name)


def wide_attention(width, heads, rows, triple, bias, probs, mixed):
    size = width // heads
    per = LANES // size
    masks = head_masks(size)
    for g in range(width // LANES):
        q, k, v = (triple[:, t * width + g * LANES : t * width + (g + 1) * LANES] for t in range(3))
        v_side = v.T
        parts = []
        for h in range(per):
            s = dot_nt(k * masks[h], q) * size ** (-0.5) + bias[...]
            e = jnp.exp(s - jnp.max(s, axis=0, keepdims=True))
            p = e * (1.0 / jnp.sum(e, axis=0, keepdims=True))
            probs[g * per + h] = p
            parts.append(dot_nn(v_side[h * size : (h + 1) * size, :], p.astype(BF)))
        mixed[:, g * LANES : (g + 1) * LANES] = jnp.concatenate(parts, axis=0).T.astype(BF)


def wide_attention_back(width, heads, triple, probs, low_mixed, grad_triple):
    size = width // heads
    per = LANES // size
    masks = head_masks(size)
    for g in range(width // LANES):
        lanes = [slice(t * width + g * LANES, t * width + (g + 1) * LANES) for t in range(3)]
        q, k, v = (triple[:, lane] for lane in lanes)
        dm = low_mixed[:, g * LANES : (g + 1) * LANES]
        k_side = k.T
        parts, dk, dv = [], 0.0, 0.0
        for h in range(per):
            p = probs[g * per + h]
            dp = dot_nt(v * masks[h], dm)
            ds = (p * (dp - jnp.sum(p * dp, axis=0, keepdims=True))).astype(BF)
            dv = dv + dot_nn(p.astype(BF), dm * masks[h])
            dk = dk + dot_nn(ds, q * masks[h])
            parts.append(dot_nn(k_side[h * size : (h + 1) * size, :], ds))
        grad_triple[:, lanes[0]] = (jnp.concatenate(parts, axis=0).T * size ** (-0.5)).astype(BF)
        grad_triple[:, lanes[1]] = (dk * size ** (-0.5)).astype(BF)
        grad_triple[:, lanes[2]] = dv.astype(BF)


def block_forward(x, rows, images, heads, need, norms, key_bias, saved, done=lambda *names: None):
    entry, plain1, scale1, triple, probs, mixed, plain2, scale2, inner, act, slope = saved
    width = x.shape[1]
    size = width // heads
    per = LANES // size
    groups = width // LANES

    def first(i):
        at = rows_at(i, rows)
        plain, scale = norm(x[at, :])
        plain1[at, :] = plain
        scale1[at, :] = scale
        entry[at, :] = (plain * norms[0:1, :] + norms[1:2, :]).astype(BF)

    loop(images, first)

    done("entry", "plain1", "scale1")
    triple_w = need("triple_w")

    def project(j):
        at = rows_at(j, 256)
        triple[:, at] = dot_nn(entry[...], triple_w[:, at]).astype(BF)

    loop(3 * width // 256, project)
    done("triple")
    masks = head_masks(size)

    def attend(i):
        at = rows_at(i, rows)
        bias = key_bias(i)
        for g in range(groups):
            q = triple[at, g * LANES : (g + 1) * LANES]
            k = triple[at, width + g * LANES : width + (g + 1) * LANES]
            v = triple[at, 2 * width + g * LANES : 2 * width + (g + 1) * LANES]
            v_side = v.T
            parts = []
            for h in range(per):
                s = dot_nt(k * masks[h], q) * size ** (-0.5) + bias
                e = jnp.exp(s - jnp.max(s, axis=0, keepdims=True))
                p = e * (1.0 / jnp.sum(e, axis=0, keepdims=True))
                probs[i * groups + g, h * rows : (h + 1) * rows, :] = p
                parts.append(dot_nn(v_side[h * size : (h + 1) * size, :], p.astype(BF)))
            mixed[at, g * LANES : (g + 1) * LANES] = jnp.concatenate(parts, axis=0).T.astype(BF)

    if callable(key_bias):
        loop(images, attend)
    else:
        wide_attention(width, heads, rows, triple, key_bias, probs, mixed)
    done("probs", "mixed")
    proj_w = need("proj_w")

    def middle(j):
        at = rows_at(j, 256)
        x[:, at] += dot_nn(mixed[...], proj_w[:, at])

    loop(width // 256, middle)

    def second(i):
        at = rows_at(i, rows)
        plain, scale = norm(x[at, :])
        plain2[at, :] = plain
        scale2[at, :] = scale
        inner[at, :] = (plain * norms[2:3, :] + norms[3:4, :]).astype(BF)

    loop(images, second)
    done("plain2", "scale2", "inner")
    up_w = need("up_w")
    hidden = up_w.shape[1]

    def up(j):
        at = rows_at(j, 256)
        value, gradient = gelu_pair(dot_nn(inner[...], up_w[:, at]))
        act[:, at] = value.astype(BF)
        slope[:, at] = gradient

    loop(hidden // 256, up)
    done("act", "slope")
    down_w = need("down_w")

    def down(j):
        at = rows_at(j, 256)
        x[:, at] += dot_nn(act[...], down_w[:, at])

    loop(width // 256, down)


class Writer:
    def __init__(self, flat, stage, sem):
        self.flat, self.stage, self.sem = flat, stage, sem
        self.pending = {}

    def settle(self, s):
        if s in self.pending:
            self.pending.pop(s).wait()

    def outer(self, number, left, right, chunk=256):
        _, _, cols, tile, _ = ENTRIES[number]
        rows = left.shape[1]
        count = rows // chunk
        tall = chunk // 8
        before = dict(self.pending)

        def copy(i, s):
            return pltpu.make_async_copy(
                self.stage.at[s, pl.ds(0, tall * cols)], self.flat.at[pl.ds(tile + i * tall * cols, tall * cols)], self.sem.at[s]
            )

        def body(i):
            s = lax.rem(i, 2)
            for early in before:
                pl.when(i == early)(before[early].wait)

            @pl.when(i >= 2)
            def _():
                copy(i - 2, s).wait()

            side = left[:, rows_at(i, chunk)].T
            for c in range(0, cols, 2):
                value = dot_nn(side, right[:, c * LANES : (c + 2) * LANES])
                for d in range(2):
                    self.stage[s, pl.ds(c + d, tall, stride=cols)] = value[:, d * LANES : (d + 1) * LANES].reshape(tall, 8, LANES)
            copy(i, s).start()

        loop(count, body)
        self.pending = {(count - 2) % 2: copy(count - 2, (count - 2) % 2), (count - 1) % 2: copy(count - 1, (count - 1) % 2)}

    def small(self, number, norm_sums, count, extra=0):
        _, _, _, tile, groups = ENTRIES[number]
        per = SHAPES[number][1] // LANES
        self.settle(0)
        self.stage[0, 0 : groups + extra] = jnp.zeros((groups + extra, 8, LANES), F32)
        for r in range(count):
            for c in range(per):
                line = r * per + c
                self.stage[0, line // 8, line % 8 : line % 8 + 1, :] = norm_sums[r : r + 1, c * LANES : (c + 1) * LANES]
        copy = pltpu.make_async_copy(self.stage.at[0, pl.ds(0, groups + extra)], self.flat.at[pl.ds(tile, groups + extra)], self.sem.at[0])
        copy.start()
        copy.wait()
        self.settle(1)


def block_backward(grad, rows, images, heads, need, norms, norm_sums, extra, writer, numbers):
    low, grad_hidden, side, low_mixed, grad_triple = extra
    width = grad.shape[1]
    size = width // heads
    per = LANES // size
    groups = width // LANES
    low[...] = grad[...].astype(BF)
    down_w, slope = need("down_w"), need("slope")
    hidden = down_w.shape[0]

    def back_up(j):
        at = rows_at(j, 256)
        grad_hidden[:, at] = (dot_nt(low[...], down_w[at, :]) * slope[:, at]).astype(BF)

    loop(hidden // 256, back_up)
    writer.outer(numbers[3], need("act"), low)
    writer.outer(numbers[2], need("inner"), grad_hidden)
    up_w = need("up_w")

    def back_inner(j):
        at = rows_at(j, 256)
        side[:, at] = dot_nt(grad_hidden[...], up_w[at, :])

    loop(width // 256, back_inner)
    plain2, scale2 = need("plain2"), need("scale2")

    def second(i):
        at = rows_at(i, rows)
        back, gain, shift = norm_grad(side[at, :], plain2[at, :], scale2[at, :], norms[2:3, :])
        norm_sums[2:3, :] += gain
        norm_sums[3:4, :] += shift
        total = grad[at, :] + back
        grad[at, :] = total
        low[at, :] = total.astype(BF)

    loop(images, second)
    writer.outer(numbers[1], need("mixed"), low)
    proj_w = need("proj_w")

    def back_mixed(j):
        at = rows_at(j, 256)
        low_mixed[:, at] = dot_nt(low[...], proj_w[at, :]).astype(BF)

    loop(width // 256, back_mixed)
    triple, probs = need("triple"), need("probs")
    masks = head_masks(size)

    def attend(i):
        at = rows_at(i, rows)
        for g in range(groups):
            lanes = [slice(t * width + g * LANES, t * width + (g + 1) * LANES) for t in range(3)]
            q, k, v = (triple[at, lane] for lane in lanes)
            dm = low_mixed[at, g * LANES : (g + 1) * LANES]
            k_side = k.T
            parts, dk, dv = [], 0.0, 0.0
            for h in range(per):
                p = probs[i * groups + g, h * rows : (h + 1) * rows, :]
                dp = dot_nt(v * masks[h], dm)
                ds = (p * (dp - jnp.sum(p * dp, axis=0, keepdims=True))).astype(BF)
                dv = dv + dot_nn(p.astype(BF), dm * masks[h])
                dk = dk + dot_nn(ds, q * masks[h])
                parts.append(dot_nn(k_side[h * size : (h + 1) * size, :], ds))
            dq = jnp.concatenate(parts, axis=0).T
            grad_triple[at, lanes[0]] = (dq * size ** (-0.5)).astype(BF)
            grad_triple[at, lanes[1]] = (dk * size ** (-0.5)).astype(BF)
            grad_triple[at, lanes[2]] = dv.astype(BF)

    if probs.shape[1] == probs.shape[2] and probs.shape[0] == heads:
        wide_attention_back(width, heads, triple, probs, low_mixed, grad_triple)
    else:
        loop(images, attend)
    writer.outer(numbers[0], need("entry"), grad_triple)
    triple_w = need("triple_w")

    def back_entry(j):
        at = rows_at(j, 256)
        side[:, at] = dot_nt(grad_triple[...], triple_w[at, :])

    loop(width // 256, back_entry)
    plain1, scale1 = need("plain1"), need("scale1")

    def first(i):
        at = rows_at(i, rows)
        back, gain, shift = norm_grad(side[at, :], plain1[at, :], scale1[at, :], norms[0:1, :])
        norm_sums[0:1, :] += gain
        norm_sums[1:2, :] += shift
        grad[at, :] += back

    loop(images, first)


SAVED = ("seen", "entry", "plain1", "scale1", "triple", "probs", "mixed", "plain2", "scale2", "inner", "act", "slope", "plain3", "scale3", "encoded")
ENC_NAMES = ("embed_w", "triple_w", "proj_w", "up_w", "down_w", "dec_embed_w")
DEC_NAMES = ("triple_w", "proj_w", "up_w", "down_w", "head_w")


def saved_shapes(rows):
    s = jax.ShapeDtypeStruct
    return [
        s((rows, D), BF), s((rows, D), BF), s((rows, D), F32), s((rows, 1), F32), s((rows, 3 * D), BF),
        s((HEADS, rows, rows), F32), s((rows, D), BF), s((rows, D), F32), s((rows, 1), F32), s((rows, D), BF),
        s((rows, F), BF), s((rows, F), F32), s((rows, D), F32), s((rows, 1), F32), s((rows, D), BF),
    ]


def like(shape):
    return pltpu.VMEM(shape.shape, shape.dtype)


def pad_patches(patches, padded, images):
    padded[...] = jnp.zeros_like(padded)
    for i in range(images):
        padded[i * P_ROWS : i * P_ROWS + PATCHES, :] = patches[i]


def encoder_kernel(images, counts_ref, cols_ref, norms_ref, *refs):
    pos_hbm, patches_hbm, *weights_hbm = refs[:8]
    outs = refs[8:23]
    entering = refs[23]
    pos, patches, *weights = refs[24:32]
    saved = dict(zip(SAVED, refs[32:47]))
    x, place_, pos_split, padded, bias, in_sem, out_sem = refs[47:]
    need = Moves(("pos", "patches") + ENC_NAMES, [pos_hbm, patches_hbm] + weights_hbm, [pos, patches] + weights, in_sem)
    need.start()
    put = Moves(SAVED, [saved[name] for name in SAVED], outs, out_sem)
    rows = images * KEEP
    key = lax.broadcasted_iota(jnp.int32, (KEEP, rows), 0)
    query = lax.broadcasted_iota(jnp.int32, (KEEP, rows), 1)
    for i in range(images):
        inside = jnp.logical_and(jnp.logical_and(query >= i * KEEP, query < (i + 1) * KEEP), key < counts_ref[i])
        bias[i * KEEP : (i + 1) * KEEP, :] = jnp.where(inside, 0.0, NEG_FILL)
    need("pos")
    for t, part in enumerate(three(pos[...])):
        pos_split[t] = part
    pad_patches(need("patches"), padded, images)
    spots = lax.broadcasted_iota(jnp.int32, (KEEP, P_ROWS), 1)
    seen = saved["seen"]

    def select(i):
        at = rows_at(i, KEEP)
        pick = jnp.where(spots == cols_ref[i], 1.0, 0.0).astype(BF)
        seen[at, :] = dot_nn(pick, padded[rows_at(i, P_ROWS), :]).astype(BF)
        place_[at, :] = dot_nn(pick, pos_split[0]) + dot_nn(pick, pos_split[1]) + dot_nn(pick, pos_split[2])

    loop(images, select)
    put.start("seen")
    embed_w = need("embed_w")

    def embed(j):
        at = rows_at(j, 256)
        x[:, at] = dot_nn(seen[...], embed_w[:, at]) + place_[:, at]

    loop(D // 256, embed)
    block_forward(x, KEEP, images, HEADS, need, norms_ref, bias, [saved[name] for name in SAVED[1:12]], put.start)
    plain3, scale3, encoded = (saved[name] for name in SAVED[12:])

    def last(i):
        at = rows_at(i, KEEP)
        plain, scale = norm(x[at, :])
        plain3[at, :] = plain
        scale3[at, :] = scale
        encoded[at, :] = (plain * norms_ref[4:5, :] + norms_ref[5:6, :]).astype(BF)

    loop(images, last)
    put.start("plain3", "scale3", "encoded")
    entering[...] = dot_nn(encoded[...], need("dec_embed_w")[...])
    put.close()


def encoder(counts, patches, cols, pos, weights, norms):
    images = counts.shape[0]
    rows = images * KEEP
    vmem = pl.BlockSpec(memory_space=pltpu.VMEM)
    anyspec = pl.BlockSpec(memory_space=pl.ANY)
    shapes = saved_shapes(rows)
    return pl.pallas_call(
        functools.partial(encoder_kernel, images),
        name="encoder",
        out_shape=shapes + [jax.ShapeDtypeStruct((rows, DD), F32)],
        in_specs=[pl.BlockSpec(memory_space=pltpu.SMEM), vmem, vmem] + [anyspec] * 8,
        out_specs=[anyspec] * 15 + [vmem],
        scratch_shapes=[like(one) for one in [pos, patches] + weights + shapes]
        + [
            pltpu.VMEM((rows, D), F32), pltpu.VMEM((rows, D), F32), pltpu.VMEM((3, P_ROWS, D), BF), pltpu.VMEM((images * P_ROWS, PIX), BF),
            pltpu.VMEM((rows, rows), F32), pltpu.SemaphoreType.DMA((8,)), pltpu.SemaphoreType.DMA((15,)),
        ],
        compiler_params=pltpu.CompilerParams(vmem_limit_bytes=60 * MB),
    )(counts, cols, norms, pos, patches, *weights)


def decoder_kernel(images, counts_ref, masked_ref, cols_ref, rows_ref, entering_ref, norms_ref, *refs):
    pos_hbm, patches_hbm, *weights_hbm = refs[:7]
    flat, grad_entering, loss_ref = refs[7:10]
    pos, patches, *weights = refs[10:17]
    (x, hide, entry, plain1, scale1, triple, probs, mixed, plain2, scale2, inner, act, slope, plain3, scale3, final, grad_pred,
     low, grad_hidden, side, low_mixed, grad_triple, norm_sums, padded, stage, sem, in_sem) = refs[17:]
    need = Moves(("pos", "patches") + DEC_NAMES, [pos_hbm, patches_hbm] + weights_hbm, [pos, patches] + weights, in_sem)
    need.start()
    saved = (entry, plain1, scale1, triple, probs, mixed, plain2, scale2, inner, act, slope)
    need.targets.update(zip(SAVED[1:12], saved))
    lane = lax.broadcasted_iota(jnp.int32, (P_ROWS, KEEP), 1)
    spot = lax.broadcasted_iota(jnp.int32, (P_ROWS, KEEP), 0)
    line = lax.broadcasted_iota(jnp.int32, (P_ROWS, 1), 0)
    need("pos")

    def start(i):
        at = rows_at(i, P_ROWS)
        hit = jnp.where(jnp.logical_and(spot == rows_ref[pl.ds(i, 1), 0:KEEP], lane < counts_ref[i]), 1.0, 0.0)
        shown = jnp.max(hit, axis=1, keepdims=True)
        pick = hit.astype(BF)
        top, mid, end = three(entering_ref[rows_at(i, KEEP), :])
        picked = dot_nn(pick, top) + dot_nn(pick, mid) + dot_nn(pick, end)
        x[at, :] = jnp.where(shown > 0.0, picked, norms_ref[6:7, :]) + pos[...]
        hide[at, :] = jnp.where(jnp.logical_and(line < PATCHES, shown == 0.0), 1.0, 0.0)

    loop(images, start)
    bias = jnp.where(line < PATCHES, 0.0, NEG_FILL)
    block_forward(x, P_ROWS, images, DHEADS, need, norms_ref, lambda i: bias, saved)

    def last(i):
        at = rows_at(i, P_ROWS)
        plain, scale = norm(x[at, :])
        plain3[at, :] = plain
        scale3[at, :] = scale
        final[at, :] = (plain * norms_ref[4:5, :] + norms_ref[5:6, :]).astype(BF)

    loop(images, last)
    loss_ref[...] = jnp.zeros_like(loss_ref)
    masked = masked_ref[0:1, 0:1]
    head_w = need("head_w")
    pad_patches(need("patches"), padded, images)

    def score(i):
        at = rows_at(i, P_ROWS)
        target, _ = norm(padded[at, :].astype(F32))
        diff = dot_nn(final[at, :], head_w[...]) - target
        hidden = hide[at, :]
        loss_ref[...] += jnp.sum(jnp.mean(diff * diff, axis=-1, keepdims=True) * hidden, axis=0, keepdims=True)
        grad_pred[at, :] = (diff * (hidden * (2.0 / PIX)) / masked).astype(BF)

    loop(images, score)
    writer = Writer(flat, stage, sem)
    writer.outer(11, final, grad_pred)
    norm_sums[...] = jnp.zeros_like(norm_sums)

    def back_final(i):
        at = rows_at(i, P_ROWS)
        back, gain, shift = norm_grad(dot_nt(grad_pred[at, :], head_w[...]), plain3[at, :], scale3[at, :], norms_ref[4:5, :])
        norm_sums[4:5, :] += gain
        norm_sums[5:6, :] += shift
        x[at, :] = back

    loop(images, back_final)
    block_backward(x, P_ROWS, images, DHEADS, need, norms_ref, norm_sums, (low, grad_hidden, side, low_mixed, grad_triple), writer, (7, 8, 9, 10))
    spots = lax.broadcasted_iota(jnp.int32, (KEEP, P_ROWS), 1)
    slot = lax.broadcasted_iota(jnp.int32, (KEEP, P_ROWS), 0)

    def finish(i):
        at = rows_at(i, P_ROWS)
        grad = x[at, :]
        norm_sums[6:7, :] += jnp.sum(grad * hide[at, :], axis=0, keepdims=True)
        pick = jnp.where(jnp.logical_and(spots == cols_ref[i], slot < counts_ref[i]), 1.0, 0.0).astype(BF)
        grad_entering[rows_at(i, KEEP), :] = dot_nn(pick, grad.astype(BF)).astype(BF)

    loop(images, finish)
    writer.small(12, norm_sums, 7, flat.shape[0] - TILES)


def decoder(total, counts, masked, patches, cols, order, pos, entering, weights, norms):
    images = counts.shape[0]
    rows = images * P_ROWS
    vmem = pl.BlockSpec(memory_space=pltpu.VMEM)
    anyspec = pl.BlockSpec(memory_space=pl.ANY)

    def v(shape, kind=F32):
        return pltpu.VMEM(shape, kind)

    return pl.pallas_call(
        functools.partial(decoder_kernel, images),
        name="decoder",
        out_shape=[
            jax.ShapeDtypeStruct((total, 8, LANES), F32),
            jax.ShapeDtypeStruct((images * KEEP, DD), BF),
            jax.ShapeDtypeStruct((1, 1), F32),
        ],
        in_specs=[pl.BlockSpec(memory_space=pltpu.SMEM)] + [vmem] * 5 + [anyspec] * 7,
        out_specs=[anyspec, vmem, vmem],
        scratch_shapes=[like(one) for one in [pos, patches] + weights]
        + [
            v((rows, DD)), v((rows, 1)), v((rows, DD), BF), v((rows, DD)), v((rows, 1)), v((rows, 3 * DD), BF),
            v((images * DD // LANES, 4 * P_ROWS, P_ROWS)), v((rows, DD), BF), v((rows, DD)), v((rows, 1)), v((rows, DD), BF),
            v((rows, FD), BF), v((rows, FD)), v((rows, DD)), v((rows, 1)), v((rows, DD), BF), v((rows, PIX), BF),
            v((rows, DD), BF), v((rows, FD), BF), v((rows, DD)), v((rows, DD), BF), v((rows, 3 * DD), BF),
            v((8, DD)), v((rows, PIX), BF), v((2, 32 * 16, 8, LANES)), pltpu.SemaphoreType.DMA((2,)), pltpu.SemaphoreType.DMA((7,)),
        ],
        compiler_params=pltpu.CompilerParams(vmem_limit_bytes=63 * MB),
    )(counts, masked, cols, order, entering, norms, pos, patches, *weights)


def encoder_back_kernel(images, flat_in, grad_entering, norms_ref, *refs):
    names = SAVED + ENC_NAMES[1:]
    sources = refs[:20]
    flat = refs[20]
    targets = refs[21:41]
    x, low, grad_hidden, side, low_mixed, grad_triple, norm_sums, stage, sem, in_sem = refs[41:]
    need = Moves(names, sources, targets, in_sem)
    need.start(
        "encoded", "dec_embed_w", "plain3", "scale3", "down_w", "slope", "act", "inner", "up_w", "plain2", "scale2",
        "mixed", "proj_w", "triple", "probs", "entry", "triple_w", "plain1", "scale1", "seen",
    )
    writer = Writer(flat, stage, sem)
    writer.outer(6, need("encoded"), grad_entering)
    norm_sums[...] = jnp.zeros_like(norm_sums)
    side[...] = dot_nt(grad_entering[...], need("dec_embed_w")[...])
    plain3, scale3 = need("plain3"), need("scale3")

    def last(i):
        at = rows_at(i, KEEP)
        back, gain, shift = norm_grad(side[at, :], plain3[at, :], scale3[at, :], norms_ref[4:5, :])
        norm_sums[4:5, :] += gain
        norm_sums[5:6, :] += shift
        x[at, :] = back

    loop(images, last)
    block_backward(x, KEEP, images, HEADS, need, norms_ref, norm_sums, (low, grad_hidden, side, low_mixed, grad_triple), writer, (1, 2, 3, 4))
    low[...] = x[...].astype(BF)
    writer.outer(0, need("seen"), low)
    writer.small(5, norm_sums, 6)


def encoder_back(flat, grad_entering, saved, weights, norms):
    rows = grad_entering.shape[0]
    images = rows // KEEP
    vmem = pl.BlockSpec(memory_space=pltpu.VMEM)
    anyspec = pl.BlockSpec(memory_space=pl.ANY)

    def v(shape, kind=F32):
        return pltpu.VMEM(shape, kind)

    return pl.pallas_call(
        functools.partial(encoder_back_kernel, images),
        name="encoder_back",
        out_shape=jax.ShapeDtypeStruct(flat.shape, flat.dtype),
        in_specs=[anyspec, vmem, vmem] + [anyspec] * 20,
        out_specs=anyspec,
        scratch_shapes=[like(one) for one in saved + weights]
        + [
            v((rows, D)), v((rows, D), BF), v((rows, F), BF), v((rows, D)), v((rows, D), BF), v((rows, 3 * D), BF),
            v((8, D)), v((2, 32 * 24, 8, LANES)), pltpu.SemaphoreType.DMA((2,)), pltpu.SemaphoreType.DMA((20,)),
        ],
        input_output_aliases={0: 0},
        compiler_params=pltpu.CompilerParams(vmem_limit_bytes=60 * MB),
    )(flat, grad_entering, norms, *saved, *weights)


def positions(width):
    index = np.arange(PATCHES)
    quarter = width // 4
    freq = 10000.0 ** (-np.arange(quarter).astype(np.float32) / np.float32(quarter))
    row = (index // GRID).astype(np.float32)[:, None] * freq[None, :].astype(np.float32)
    column = (index % GRID).astype(np.float32)[:, None] * freq[None, :].astype(np.float32)
    table = np.concatenate([np.sin(row), np.cos(row), np.sin(column), np.cos(column)], axis=1).astype(np.float32)
    return jnp.asarray(np.pad(table, ((0, P_ROWS - PATCHES), (0, 0))))


ADAM_EPS = 1e-08
BETA_ONE = 0.9
BETA_TWO = 0.95
DECAY = 0.05


def own_lines(flat, share, index):
    if share % LANES == 0:
        return flat.reshape(-1, LANES)
    rows = (share + LANES - 1) // LANES + 1
    return lax.dynamic_update_slice(jnp.zeros((rows * LANES,), flat.dtype), flat, (share * index % LANES,)).reshape(rows, LANES)


def own_flat(lines, share, index):
    if share % LANES == 0:
        return lines.reshape(-1)
    return lax.dynamic_slice(lines.reshape(-1), (share * index % LANES,), (share,))


def body(n_dp, n_pair, patches, patch_order, counts, master, moment1, moment2, block_rates, clip_limit, step_count):
    n = n_dp * n_pair
    share = master.shape[0]
    images = counts.shape[0]
    index = lax.axis_index("dp") * n_pair + lax.axis_index("pair")
    extra = jnp.zeros((8, LANES), F32).at[0, :images].set((PATCHES - counts).astype(F32))
    slab = to_tiles(own_lines(master, share, index), extra, share, n, n_pair)
    slots = gather(slab, n_dp, n_pair, 1)
    masked = jnp.sum(slots[:, slab.shape[0] - 2, 0, :].astype(F32))
    held = assemble(slots, share)
    parts = [held[i].reshape(-1)[: SHAPES[i][0] * SHAPES[i][1]].reshape(SHAPES[i]).astype(F32) if i in SMALL else matrix(held[i], i) for i in range(len(SHAPES))]
    slots_at = patch_order[:, :KEEP]
    cols = slots_at[:, :, None]
    enc_weights = parts[1:5] + [parts[6]]
    *saved, entering = encoder(counts, patches, cols, positions(D), [parts[0]] + enc_weights, parts[5])
    total = max(a for a, _ in ranges(share, n)) + slab_tiles(share, n)
    flat, grad_entering, loss_local = decoder(
        total, counts, masked.reshape(1, 1), patches, cols, slots_at, positions(DD), entering, parts[7:12], parts[12]
    )
    flat = encoder_back(flat, grad_entering, saved, enc_weights, parts[5])
    slab_sum = reduce(flat.reshape(-1, LANES), share, n_dp, n_pair)
    rows = share // LANES if share % LANES == 0 else (share + LANES - 1) // LANES + 1
    grad_share = own_flat(to_lines(slab_sum, rows, share, n_pair), share, index)
    scalars = jnp.stack([jnp.sum(grad_share * grad_share), loss_local[0, 0]])
    shared = share_all(jnp.zeros((8, LANES), F32).at[0, :2].set(scalars), n_dp, n_pair, 2)
    squares, loss_sum = jnp.sum(shared[:, 0, 0]), jnp.sum(shared[:, 0, 1])
    grad_norm = jnp.sqrt(squares)
    loss = loss_sum / masked
    clipped = grad_share * (clip_limit[0] / (grad_norm + NORM_EPS))
    first = BETA_ONE * moment1 + (1.0 - BETA_ONE) * clipped
    second = BETA_TWO * moment2 + (1.0 - BETA_TWO) * clipped * clipped
    steps_done = step_count[0].astype(F32)
    position = index * share + jnp.arange(share)
    rate = jnp.where(position < ENC_PARAMS, block_rates[0], block_rates[1])
    update = first / (1.0 - BETA_ONE**steps_done) / (jnp.sqrt(second / (1.0 - BETA_TWO**steps_done)) + ADAM_EPS)
    master_new = master - rate * (update + DECAY * master)
    return (loss.reshape(1), grad_norm.reshape(1), first, second, master_new)


def solution(mesh):
    whole = P(("dp", "pair"))
    in_specs = (P(("dp", "pair"), None, None), P(("dp", "pair"), None), whole, whole, whole, whole, P(), P(), P())
    out_specs = (P(), P(), whole, whole, whole)
    step = functools.partial(body, mesh.shape["dp"], mesh.shape["pair"])
    return jax.shard_map(step, mesh=mesh, in_specs=in_specs, out_specs=out_specs, check_vma=False)
```

```python
import functools

import jax
import jax.numpy as jnp
import numpy as np
from jax import lax
from jax.experimental import pallas as pl
from jax.experimental.pallas import tpu as pltpu
from jax.sharding import PartitionSpec as P

MESH = pl.DeviceIdType.MESH
LANES = 128
TILE = 16 * LANES


def place():
    dp, pair = lax.axis_index("dp"), lax.axis_index("pair")
    return dp // 2, dp % 2, pair // 2, pair % 2


def slot_of(z, x, y, c):
    return (z * 2 + x) * 4 + y * 2 + c


def partners(z, x, y, c):
    return {
        "x": {"dp": z * 2 + (1 - x)},
        "y": {"pair": (1 - y) * 2 + c},
        "c": {"pair": y * 2 + (1 - c)},
        "up": {"dp": (z + 1) * 2 + x},
        "down": {"dp": (z - 1) * 2 + x},
    }


def greet(n_z, z, to):
    barrier = pltpu.get_barrier_semaphore()
    for name in ("x", "y", "c"):
        pl.semaphore_signal(barrier, inc=1, device_id=to[name], device_id_type=MESH)

    @pl.when(z < n_z - 1)
    def _():
        pl.semaphore_signal(barrier, inc=1, device_id=to["up"], device_id_type=MESH)

    @pl.when(z > 0)
    def _():
        pl.semaphore_signal(barrier, inc=1, device_id=to["down"], device_id_type=MESH)

    pl.semaphore_wait(barrier, 3 + jnp.where(z < n_z - 1, 1, 0) + jnp.where(z > 0, 1, 0))


def both(*conditions):
    total = conditions[0]
    for one in conditions[1:]:
        total = jnp.logical_and(total, one)
    return total


PIX, HEADS, F, DHEADS, FD, GRID, KEEP, D, DD, PATCHES = 768, 12, 3072, 16, 2048, 14, 64, 768, 512, 196
SHAPES = [(PIX, D), (D, 3 * D), (D, D), (D, F), (F, D), (6, D), (D, DD), (DD, 3 * DD), (DD, DD), (DD, FD), (FD, DD), (DD, PIX), (7, DD)]
SMALL = (5, 12)
ENC_PARAMS = 7672320
NORM_EPS = 1e-06
ADAM_EPS = 1e-08
BETA_ONE = 0.9
BETA_TWO = 0.95
DECAY = 0.05
MB = 1 << 20
CELL = 8 * LANES
BLOCK = 96


def make_entries():
    entries, row, tile = [], 0, 0
    for number, (rows, width) in enumerate(SHAPES):
        lines = rows * width // LANES
        cols = 1 if number in SMALL else width // LANES
        groups = -(-lines // (8 * cols))
        entries.append((row, lines, cols, tile, groups))
        row += lines
        tile += groups * cols
    return entries, row, tile


ENTRIES, ROWS, TILES = make_entries()
BIG = tuple(i for i in range(len(SHAPES)) if i not in SMALL)
MARGIN = 8 * max(cols for _, _, cols, _, _ in ENTRIES)


def first_tile(share, k):
    lo = share * k
    total = 0
    for row, lines, cols, tile, _ in ENTRIES:
        inside = jnp.logical_and(lo >= row * LANES, lo < (row + lines) * LANES)
        total = total + jnp.where(inside, tile + (lo - row * LANES) // (CELL * cols) * cols, 0)
    return total


def ranges(share, n):
    found = []
    for k in range(n):
        lo, hi = share * k, share * (k + 1)
        spans = []
        for row, lines, cols, tile, _ in ENTRIES:
            low, high = max(lo, row * LANES), min(hi, (row + lines) * LANES)
            if low < high:
                size = CELL * cols
                spans.append((tile + (low - row * LANES) // size * cols, tile + -(-(high - row * LANES) // size) * cols))
        found.append((spans[0][0], spans[-1][1]))
    return found


def slab_tiles(share, n):
    longest = max(b - a for a, b in ranges(share, n))
    return -(-longest // 24) * 24


def line_span(share, k):
    return share * k // LANES, (share * (k + 1) + LANES - 1) // LANES


def tiled(share, k, body):
    lo, hi = line_span(share, k)
    begin = first_tile(share, k)
    for number in SMALL + tuple(i for i in range(len(ENTRIES)) if i not in SMALL):
        row, lines, cols, tile, _ = ENTRIES[number]
        low = jnp.maximum(lo, row) - row
        high = jnp.minimum(hi, row + lines) - row
        size = 8 * cols

        def group(g, _, row=row, cols=cols, tile=tile, size=size):
            body(row + g * size - lo + MARGIN, tile + g * cols - begin, cols)
            return 0

        lax.fori_loop(jnp.where(low < high, low // size, 0), jnp.where(low < high, (high + size - 1) // size, 0), group, 0)


def wide_rows(rows):
    return -(-(rows + 2 * MARGIN) // 8) * 8


def pieces(share, n):
    spans = ranges(share, n)
    shared = [spans[k][1] > spans[k + 1][0] for k in range(n - 1)]
    plain, seams = [], []
    for number, (_, _, cols, tile, groups) in enumerate(ENTRIES):
        end = tile + groups * cols
        for k, (a, b) in enumerate(spans):
            low, high = max(a, tile), min(b, end)
            if low >= high:
                continue
            inner_low, inner_high = low, high
            if k > 0 and spans[k - 1][1] > low:
                inner_low = spans[k - 1][1]
            if k < n - 1 and spans[k + 1][0] < high:
                inner_high = spans[k + 1][0]
                seams.append((number, k, inner_high, high))
            if inner_low < inner_high:
                plain.append((number, k, inner_low, inner_high))
    return spans, plain, seams


def matrix(tiles_, number):
    rows, width = SHAPES[number]
    cols = width // LANES
    return tiles_.reshape(rows // 8, cols, 8, LANES).transpose(0, 2, 1, 3).reshape(rows, width)


def matrix_tiles(value):
    rows, width = value.shape
    cols = width // LANES
    return value.reshape(rows // 8, 8, cols, LANES).transpose(0, 2, 1, 3).reshape(rows * cols, LANES)


def gather_kernel(n_z, n_pair, chunks, share, lines_ref, extra_ref, *refs):
    outs = dict(zip(BIG, refs[: len(BIG)]))
    enc_norms, dec_norms, masked_ref = refs[len(BIG) : len(BIG) + 3]
    wide, out_ref, own_sem, z_sem, plane_sem, second_sem, third_sem, recv_sem, put_sem = refs[len(BIG) + 3 :]
    n = n_z * 2 * n_pair
    piece = out_ref.shape[1] // (2 * chunks)
    z, x, y, c = place()
    to = partners(z, x, y, c)
    me = slot_of(z, x, y, c)
    rows = lines_ref.shape[0]
    wide[0:MARGIN, :] = jnp.zeros((MARGIN, LANES), jnp.float32)
    wide[MARGIN + rows :, :] = jnp.zeros((wide.shape[0] - MARGIN - rows, LANES), jnp.float32)
    wide[MARGIN : MARGIN + rows, :] = lines_ref[...]

    def fill(line, tile, cols):
        for col in range(cols):
            out_ref[me, tile + col] = wide[pl.ds(line + col, 8, stride=cols), :].astype(out_ref.dtype)

    tiled(share, me, fill)
    out_ref[me, out_ref.shape[1] - 2] = extra_ref[...].astype(out_ref.dtype)
    greet(n_z, z, to)
    steps = n_z * chunks

    def copy(slot, chunk, part, name, sem):
        rows = pl.ds((chunk * 2 + part) * piece, piece)
        return pltpu.make_async_remote_copy(
            out_ref.at[slot, rows],
            out_ref.at[slot, rows],
            sem,
            recv_sem.at[slot, chunk, part],
            device_id=to[name],
            device_id_type=MESH,
        )

    def arrived(slot, chunk, part):
        copy(slot, chunk, part, "c", own_sem).wait_recv()

    def lines(s):
        t, chunk = s // chunks, lax.rem(s, chunks)
        for d in (0, 1):
            zz = z - t if d == 0 else z + t
            inside = zz >= 0 if d == 0 else zz < n_z
            more = z < n_z - 1 if d == 0 else z > 0
            fresh = both(t > 0, inside)
            held = jnp.logical_or(fresh, t == 0) if d == 0 else fresh
            onward = both(jnp.logical_or(fresh, t == 0), more)
            yield d, zz, chunk, fresh, held, onward

    def first_sends(d, zz, chunk, held, onward, s, act):
        slot = slot_of(zz, x, y, c)
        for part in (0, 1):
            pl.when(onward)(lambda part=part: act(copy(slot, chunk, part, ("up", "down")[d], z_sem.at[s, d, part])))

        @pl.when(held)
        def _():
            for i, (part, name) in enumerate(((0, "x"), (1, "y"), (0, "y"), (1, "x"), (0, "c"), (1, "c"))):
                act(copy(slot, chunk, part, name, plane_sem.at[s, d, i]))

    def first(s):
        for d, zz, chunk, fresh, held, onward in lines(s):

            @pl.when(fresh)
            def _():
                for part in (0, 1):
                    arrived(slot_of(zz, x, y, c), chunk, part)

            first_sends(d, zz, chunk, held, onward, s, lambda one: one.start())

    def second_items(zz):
        return ((0, slot_of(zz, 1 - x, y, c), "y"), (1, slot_of(zz, x, 1 - y, c), "x"))

    def second(s):
        for d, zz, chunk, _, held, _ in lines(s):

            @pl.when(held)
            def _():
                for part, slot, name in second_items(zz):
                    arrived(slot, chunk, part)
                    copy(slot, chunk, part, name, second_sem.at[s, d, part, 0]).start()
                    copy(slot, chunk, part, "c", second_sem.at[s, d, part, 1]).start()

    def third_items(zz):
        return ((0, slot_of(zz, x, 1 - y, c)), (1, slot_of(zz, 1 - x, y, c)), (0, slot_of(zz, 1 - x, 1 - y, c)), (1, slot_of(zz, 1 - x, 1 - y, c)))

    def third(s):
        for d, zz, chunk, _, held, _ in lines(s):

            @pl.when(held)
            def _():
                for i, (part, slot) in enumerate(third_items(zz)):
                    arrived(slot, chunk, part)
                    copy(slot, chunk, part, "c", third_sem.at[s, d, i]).start()

    def turn(s, _):
        pl.when(s < steps)(lambda: first(s))
        pl.when(both(s >= 1, s < steps + 1))(lambda: second(s - 1))
        pl.when(s >= 2)(lambda: third(s - 2))
        return 0

    lax.fori_loop(0, steps + 2, turn, 0)

    def finish(s, _):
        for d, zz, chunk, _, held, onward in lines(s):
            first_sends(d, zz, chunk, held, onward, s, lambda one: one.wait_send())

            @pl.when(held)
            def _():
                for part, slot, name in second_items(zz):
                    copy(slot, chunk, part, name, second_sem.at[s, d, part, 0]).wait_send()
                    copy(slot, chunk, part, "c", second_sem.at[s, d, part, 1]).wait_send()
                for i, (part, slot) in enumerate(third_items(zz)):
                    copy(slot, chunk, part, "c", third_sem.at[s, d, i]).wait_send()
                for ox in (0, 1):
                    for oy in (0, 1):
                        for part in (0, 1):
                            arrived(slot_of(zz, ox, oy, 1 - c), chunk, part)

        return 0

    lax.fori_loop(0, steps, finish, 0)

    spans, plain, seams = pieces(share, n)
    puts = []

    def put(number, k, low, high):
        copy = pltpu.make_async_copy(
            out_ref.at[k, pl.ds(low - spans[k][0], high - low)], outs[number].at[pl.ds(low - ENTRIES[number][3], high - low)], put_sem.at[len(puts)]
        )
        copy.start()
        puts.append(copy)

    home = {}
    for number, k, low, high in plain + seams:
        if number in SMALL:
            home.update({tile: (k, tile - spans[k][0]) for tile in range(low, high)})
        elif (number, k, low, high) in plain:
            put(number, k, low, high)
    for number, k, low, high in seams:
        left = pl.ds(low - spans[k][0], high - low)
        right = pl.ds(low - spans[k + 1][0], high - low)
        total = out_ref[k, left].astype(jnp.float32) + out_ref[k + 1, right].astype(jnp.float32)
        out_ref[k, left] = total.astype(out_ref.dtype)
        if number not in SMALL:
            put(number, k, low, high)
    for number, target in zip(SMALL, (enc_norms, dec_norms)):
        row, lines_, _, tile, groups = ENTRIES[number]
        per = SHAPES[number][1] // LANES
        for group in range(groups):
            k, at = home[tile + group]
            value = out_ref[k, at].astype(jnp.float32)
            for line in range(group * 8, min(group * 8 + 8, lines_)):
                target[line // per : line // per + 1, line % per * LANES : (line % per + 1) * LANES] = value[line % 8 : line % 8 + 1, :]
    masked_ref[...] = jnp.zeros_like(masked_ref)

    def count(k, _):
        masked_ref[...] += jnp.sum(out_ref[k, out_ref.shape[1] - 2].astype(jnp.float32)[0:1, :], axis=1, keepdims=True)
        return 0

    lax.fori_loop(0, n, count, 0)
    for copy in puts:
        copy.wait()


def gather(lines, extra, share, n_dp, n_pair, chunks):
    n_z = n_dp // 2
    n = n_dp * n_pair
    steps = n_z * chunks
    tiles_ = slab_tiles(share, n) + 2
    _, plain, seams = pieces(share, n)
    dma = pltpu.SemaphoreType.DMA
    anyspec = pl.BlockSpec(memory_space=pl.ANY)
    vmem = pl.BlockSpec(memory_space=pltpu.VMEM)

    def s(shape, kind=jnp.float32):
        return jax.ShapeDtypeStruct(shape, kind)

    return pl.pallas_call(
        functools.partial(gather_kernel, n_z, n_pair, chunks, share),
        name="gather",
        out_shape=[s((ENTRIES[i][4] * ENTRIES[i][2], 8, LANES), jnp.bfloat16) for i in BIG] + [s(SHAPES[5]), s(SHAPES[12]), s((1, 1))],
        in_specs=[vmem, vmem],
        out_specs=[anyspec] * len(BIG) + [vmem] * 3,
        scratch_shapes=[
            pltpu.VMEM((wide_rows(lines.shape[0]), LANES), jnp.float32),
            pltpu.VMEM((n, tiles_, 8, LANES), jnp.bfloat16),
            dma, dma((steps, 2, 2)), dma((steps, 2, 6)), dma((steps, 2, 2, 2)), dma((steps, 2, 4)), dma((n, chunks, 2)), dma((len(plain) + len(seams),)),
        ],
        compiler_params=pltpu.CompilerParams(collective_id=0, has_side_effects=True, vmem_limit_bytes=60 * MB),
    )(lines, extra)


def reduce_kernel(n_z, n_pair, chunks, share, grad_ref, loss_in, params, master, moment1, moment2, first_ref, second_ref, master_ref, total_ref, sib_ref, wide, mine, shared, send_sem, recv_sem, gbuf, rbuf, keep, q1s, q1r, q2s, q2r, zs, zr, t1s, t1r, t2s, t2r, tzs, tzr, sib_sem, load_sem, s1_sem, s2_sem, z_sem):
    z, x, y, c = place()
    to = partners(z, x, y, c)
    n = n_z * 2 * n_pair
    me = slot_of(z, x, y, c)
    rows = keep.shape[1] // chunks
    half = rows // 2
    steps = n_z * chunks
    count = half // BLOCK

    def start_of(k):
        return pl.multiple_of(first_tile(share, k) * 8, 8)

    def order(j):
        low = z < n_z // 2
        far = jnp.where(low, n_z - 1 - j, j)
        moved = jnp.where(low, jnp.where(far > z, far, far - 1), jnp.where(far < z, far, far + 1))
        return jnp.where(j == n_z - 1, z, moved)

    def lines_of(s, xx, yy, core):
        k = slot_of(order(s // chunks), xx, yy, core)
        return pl.ds(pl.multiple_of(start_of(k) + lax.rem(s, chunks) * rows, 8), rows)

    def kept(s, part, b):
        return s // chunks, pl.ds(pl.multiple_of(lax.rem(s, chunks) * rows + part * half + b * BLOCK, BLOCK), BLOCK)

    def sibling(s, xx, yy, core):
        return pltpu.make_async_remote_copy(
            grad_ref.at[lines_of(s, xx, yy, core)],
            sib_ref.at[s, xx * 2 + yy],
            sib_sem.at[0, s, xx * 2 + yy],
            sib_sem.at[1, s, xx * 2 + yy],
            device_id=to["c"],
            device_id_type=MESH,
        )

    def loads(j, s, q):
        return (
            pltpu.make_async_copy(grad_ref.at[lines_of(j, q // 2, q % 2, c)], gbuf.at[s, q], load_sem.at[0, s, q]),
            pltpu.make_async_copy(sib_ref.at[j, q], rbuf.at[s, q], load_sem.at[1, s, q]),
        )

    def load(j):
        s = lax.rem(j, 2)
        for q in range(4):
            sibling(j, q // 2, q % 2, 1 - c).wait_recv()
            for one in loads(j, s, q):
                one.start()

    def pack(value, q_ref, t_ref, b):
        top = jnp.max(jnp.abs(value), axis=0, keepdims=True)
        inverse = jnp.where(top > 1e-30, 32767.0 / jnp.maximum(top, 1e-30), 0.0)
        q_ref[pl.ds(pl.multiple_of(b * BLOCK, BLOCK), BLOCK), :] = jnp.round(value * inverse).astype(jnp.int32).astype(jnp.int16)
        t_ref[pl.ds(b, 1), :] = top * (1.0 / 32767.0)

    def unpack(q_ref, t_ref, b):
        return q_ref[pl.ds(pl.multiple_of(b * BLOCK, BLOCK), BLOCK), :].astype(jnp.int32).astype(jnp.float32) * t_ref[pl.ds(b, 1), :]

    def each(body):
        def one(b, _):
            body(b)
            return 0

        lax.fori_loop(0, count, one, 0)

    def own(s, q, part, b):
        at = pl.ds(pl.multiple_of(part * half + b * BLOCK, BLOCK), BLOCK)
        return gbuf[s, q, at, :] + rbuf[s, q, at, :]

    def message(qs, ts, qr, tr, sem, name):
        return (
            pltpu.make_async_remote_copy(qs, qr, sem.at[0, 0], sem.at[0, 1], device_id=to[name], device_id_type=MESH),
            pltpu.make_async_remote_copy(ts, tr, sem.at[1, 0], sem.at[1, 1], device_id=to[name], device_id_type=MESH),
        )

    def first_message(j, part, other):
        i = part * 2 + other
        return message(q1s.at[j, i], t1s.at[j, i], q1r.at[j, i], t1r.at[j, i], s1_sem.at[j, i], ("x", "y")[part])

    def second_message(j, part):
        return message(q2s.at[j, part], t2s.at[j, part], q2r.at[j, part], t2r.at[j, part], s2_sem.at[j, part], ("y", "x")[part])

    def z_message(zz, part, name):
        d = 0 if name == "up" else 1
        return message(zs.at[zz, part], tzs.at[zz, part], zr.at[d, zz, part], tzr.at[d, zz, part], z_sem.at[d, zz, part], name)

    def quarter(part, other, mine):
        if part == 0:
            return (x if mine else 1 - x) * 2 + other
        return other * 2 + (y if mine else 1 - y)

    def stage_one(j):
        s = lax.rem(j, 2)
        for q in range(4):
            for one in loads(j, s, q):
                one.wait()
        for part in (0, 1):
            for other in (0, 1):
                q = quarter(part, other, False)
                i = part * 2 + other
                each(lambda b: pack(own(s, q, part, b), q1s.at[j, i], t1s.at[j, i], b))
                for one in first_message(j, part, other):
                    one.start()

    def stage_two(j):
        s = lax.rem(j, 2)
        for part in (0, 1):
            for other in (0, 1):
                for one in first_message(j, part, other):
                    one.wait_recv()
            here = (y, x)[part]
            away = quarter(part, 1 - here, True)
            i = part * 2 + 1 - here
            each(lambda b: pack(own(s, away, part, b) + unpack(q1r.at[j, i], t1r.at[j, i], b), q2s.at[j, part], t2s.at[j, part], b))
            for one in second_message(j, part):
                one.start()
        for part in (0, 1):
            here = (y, x)[part]
            mine = x * 2 + y
            k = part * 2 + here

            def store(b, part=part, k=k):
                group, at = kept(j, part, b)
                keep[group, at, :] = own(s, mine, part, b) + unpack(q1r.at[j, k], t1r.at[j, k], b)

            each(store)

    def add_to_keep(j, part, q_ref, t_ref):
        def body(b):
            group, at = kept(j, part, b)
            keep[group, at, :] += unpack(q_ref, t_ref, b)

        each(body)

    def stage_three(j):
        for part in (0, 1):
            for one in second_message(j, part):
                one.wait_recv()
            add_to_keep(j, part, q2r.at[j, part], t2r.at[j, part])

    def pass_on(j, zz, part, name):
        def body(b):
            group, at = kept(j, part, b)
            pack(keep[group, at, :], zs.at[zz, part], tzs.at[zz, part], b)

        each(body)
        for one in z_message(zz, part, name):
            one.start()

    def stage_four(j):
        zz = order(j // chunks)
        zc = zz * chunks + lax.rem(j, chunks)
        for part in (0, 1):
            for d, name, has, onward in ((0, "up", z > 0, zz > z), (1, "down", z < n_z - 1, zz < z)):
                back = zz >= z if d == 0 else zz <= z

                @pl.when(jnp.logical_and(has, back))
                def _():
                    for one in z_message(zc, part, name):
                        one.wait_recv()
                    add_to_keep(j, part, zr.at[d, zc, part], tzr.at[d, zc, part])

                @pl.when(onward)
                def _():
                    pass_on(j, zc, part, name)

    def spread_lines(line, tile, cols):
        for col in range(cols):
            wide[pl.ds(line + col, 8, stride=cols), :] = keep[n_z - 1, pl.ds(pl.multiple_of((tile + col) * 8, 8), 8), :]

    count_lines = master.shape[0]
    tall = 128

    def by_lines(body):
        def one(i, _):
            body(pl.multiple_of(i * tall, tall), tall)
            return 0

        lax.fori_loop(0, count_lines // tall, one, 0)
        if count_lines % tall:
            body(count_lines // tall * tall, count_lines % tall)

    def send(d):
        return pltpu.make_async_remote_copy(mine, shared.at[me], send_sem.at[d], recv_sem.at[d], device_id=peer(d), device_id_type=MESH)

    def update():
        tiled(share, me, spread_lines)
        lo, _ = line_span(share, me)
        mine[...] = jnp.zeros_like(mine)

        def squares(start, size):
            value = wide[pl.ds(MARGIN + start, size), :]
            if share % LANES:
                line = lax.broadcasted_iota(jnp.int32, (size, LANES), 0) + lo + start
                spot = line * LANES + lax.broadcasted_iota(jnp.int32, (size, LANES), 1)
                inside = jnp.logical_and(spot >= share * me, spot < share * (me + 1))
                value = jnp.where(inside, value, 0.0)
            mine[0:1, :] += jnp.sum(value * value, axis=0, keepdims=True)

        by_lines(squares)
        lane = lax.broadcasted_iota(jnp.int32, (1, LANES), 1)
        mine[1:2, :] = jnp.where(lane == 0, loss_in[0:1, 0:1], 0.0)
        shared[me] = mine[...]

        def go(d, _):
            send(d).start()
            return 0

        def stop(d, _):
            send(d).wait()
            return 0

        lax.fori_loop(1, n, go, 0)
        lax.fori_loop(1, n, stop, 0)

        def add(k, total):
            return total + shared[k]

        total = lax.fori_loop(0, n, add, jnp.zeros((8, LANES), jnp.float32))
        norm_ = jnp.sqrt(jnp.sum(total[0:1, :], axis=1, keepdims=True))
        loss_sum = jnp.sum(total[1:2, :], axis=1, keepdims=True)
        total_ref[...] = jnp.where(lax.broadcasted_iota(jnp.int32, (8, LANES), 0) == 0, norm_, loss_sum)
        factor = params[2] / (norm_ + NORM_EPS)

        def adam(start, size):
            at = pl.ds(start, size)
            clipped = wide[pl.ds(MARGIN + start, size), :] * factor
            one = BETA_ONE * moment1[at, :] + (1.0 - BETA_ONE) * clipped
            two = BETA_TWO * moment2[at, :] + (1.0 - BETA_TWO) * clipped * clipped
            line = lax.broadcasted_iota(jnp.int32, (size, 1), 0) + lo + start
            rate = jnp.where(line < ENC_PARAMS // LANES, params[0], params[1])
            step = one / params[3] / (jnp.sqrt(two / params[4]) + ADAM_EPS)
            first_ref[at, :] = one
            second_ref[at, :] = two
            master_ref[at, :] = master[at, :] - rate * (step + DECAY * master[at, :])

        by_lines(adam)

    barrier = pltpu.get_barrier_semaphore()

    def peer(d):
        k = lax.rem(me + d, n)
        return {"dp": k // n_pair, "pair": lax.rem(k, n_pair)}

    def hello(d, _):
        pl.semaphore_signal(barrier, inc=1, device_id=peer(d), device_id_type=MESH)
        return 0

    lax.fori_loop(1, n, hello, 0)
    pl.semaphore_wait(barrier, n - 1)

    def begin(j, _):
        for q in range(4):
            sibling(j, q // 2, q % 2, 1 - c).start()
        return 0

    lax.fori_loop(0, steps, begin, 0)
    load(0)

    def turn(t, _):
        pl.when(t < steps)(lambda: stage_one(t))
        pl.when(jnp.logical_and(t >= 1, t <= steps))(lambda: stage_two(t - 1))
        pl.when(t + 1 < steps)(lambda: load(t + 1))
        pl.when(jnp.logical_and(t >= 2, t <= steps + 1))(lambda: stage_three(t - 2))
        pl.when(t >= 3)(lambda: stage_four(t - 3))
        return 0

    lax.fori_loop(0, steps + 3, turn, 0)
    update()

    def finish(j, _):
        zz = order(j // chunks)
        zc = zz * chunks + lax.rem(j, chunks)
        for q in range(4):
            sibling(j, q // 2, q % 2, 1 - c).wait_send()
        for part in (0, 1):
            for other in (0, 1):
                for one in first_message(j, part, other):
                    one.wait_send()
            for one in second_message(j, part):
                one.wait_send()

            @pl.when(zz > z)
            def _():
                for one in z_message(zc, part, "up"):
                    one.wait_send()

            @pl.when(zz < z)
            def _():
                for one in z_message(zc, part, "down"):
                    one.wait_send()

        return 0

    lax.fori_loop(0, steps, finish, 0)


def reduce_chunks(share, n):
    rows = slab_tiles(share, n) * 8
    return max(d for d in (1, 2, 4) if rows % (2 * BLOCK * d) == 0)


def reduce(flat, loss, params, lines, share, n_dp, n_pair):
    chunks = reduce_chunks(share, n_dp * n_pair)
    n_z, n = n_dp // 2, n_dp * n_pair
    rows = slab_tiles(share, n) * 8
    part = rows // chunks
    half = part // 2
    steps = n_z * chunks
    marks = (half // BLOCK + 7) // 8 * 8
    anyspec = pl.BlockSpec(memory_space=pl.ANY)
    vmem = pl.BlockSpec(memory_space=pltpu.VMEM)
    line = jax.ShapeDtypeStruct(lines[0].shape, jnp.float32)

    def q(*lead):
        return pltpu.VMEM(lead + (half, LANES), jnp.int16)

    def t(*lead):
        return pltpu.VMEM(lead + (marks, LANES), jnp.float32)

    dma = pltpu.SemaphoreType.DMA
    return pl.pallas_call(
        functools.partial(reduce_kernel, n_z, n_pair, chunks, share),
        name="reduce_scatter",
        out_shape=[line, line, line, jax.ShapeDtypeStruct((8, LANES), jnp.float32), jax.ShapeDtypeStruct((steps, 4, part, LANES), jnp.float32)],
        in_specs=[anyspec, vmem, pl.BlockSpec(memory_space=pltpu.SMEM)] + [vmem] * 3,
        out_specs=[vmem] * 4 + [anyspec],
        scratch_shapes=[
            pltpu.VMEM((wide_rows(lines[0].shape[0]), LANES), jnp.float32),
            pltpu.VMEM((8, LANES), jnp.float32),
            pltpu.VMEM((n, 8, LANES), jnp.float32),
            dma((n,)),
            dma((n,)),
            pltpu.VMEM((2, 4, part, LANES), jnp.float32),
            pltpu.VMEM((2, 4, part, LANES), jnp.float32),
            pltpu.VMEM((n_z, rows, LANES), jnp.float32),
            q(steps, 4), q(steps, 4), q(steps, 2), q(steps, 2), q(steps, 2), q(2, steps, 2),
            t(steps, 4), t(steps, 4), t(steps, 2), t(steps, 2), t(steps, 2), t(2, steps, 2),
            dma((2, steps, 4)), dma((2, 2, 4)), dma((steps, 4, 2, 2)), dma((steps, 2, 2, 2)), dma((2, steps, 2, 2, 2)),
        ],
        compiler_params=pltpu.CompilerParams(collective_id=1, has_side_effects=True, vmem_limit_bytes=60 * MB),
    )(flat, loss, params, *lines)[:4]


NEG_FILL = -1000000000.0
P_ROWS = 208
BF = jnp.bfloat16
F32 = jnp.float32


def dot_nn(left, right):
    return lax.dot_general(left, right, (((1,), (0,)), ((), ())), preferred_element_type=F32)


def dot_nt(left, right):
    return lax.dot_general(left, right, (((1,), (1,)), ((), ())), preferred_element_type=F32)


def loop(count, body, unroll=1):
    def step(i, _):
        body(i)
        return 0

    lax.fori_loop(0, count, step, 0, unroll=unroll)


def rows_at(i, size):
    return pl.ds(pl.multiple_of(i * size, size), size)


def norm(x):
    centered = x - jnp.mean(x, axis=-1, keepdims=True)
    scale = lax.rsqrt(jnp.mean(centered * centered, axis=-1, keepdims=True) + NORM_EPS)
    return centered * scale, scale


def norm_grad(grad, plain, scale, gain):
    inner = grad * gain
    back = scale * (inner - jnp.mean(inner, axis=-1, keepdims=True) - plain * jnp.mean(inner * plain, axis=-1, keepdims=True))
    return back, jnp.sum(grad * plain, axis=0, keepdims=True), jnp.sum(grad, axis=0, keepdims=True)


def gelu_pair(h):
    cumulative = 0.5 * (1.0 + lax.erf(h * 0.7071067811865476))
    density = jnp.exp(-0.5 * h * h) * 0.3989422804014327
    return h * cumulative, cumulative + h * density


def head_masks(size):
    lane = lax.broadcasted_iota(jnp.int32, (1, LANES), 1)
    shift = size.bit_length() - 1
    return [jnp.where((lane >> shift) == h, 1.0, 0.0).astype(BF) for h in range(LANES // size)]


def three(value):
    top = value.astype(BF)
    rest = value - top.astype(F32)
    mid = rest.astype(BF)
    return top, mid, (rest - mid.astype(F32)).astype(BF)


class Moves:
    def __init__(self, names, sources, targets, sems):
        self.targets = dict(zip(names, targets))
        self.copies = {name: pltpu.make_async_copy(a, b, sems.at[i]) for i, (name, a, b) in enumerate(zip(names, sources, targets))}
        self.open = []

    def start(self, *names):
        for name in names or self.copies:
            self.copies[name].start()
            self.open.append(name)

    def __call__(self, name):
        if name in self.open:
            self.copies[name].wait()
            self.open.remove(name)
        return self.targets[name]

    def close(self):
        for name in list(self.open):
            self(name)


def wide_attention(width, heads, rows, triple, bias, probs, mixed):
    size = width // heads
    per = LANES // size
    masks = head_masks(size)
    for g in range(width // LANES):
        q, k, v = (triple[:, t * width + g * LANES : t * width + (g + 1) * LANES] for t in range(3))
        v_side = v.T
        parts = []
        for h in range(per):
            s = dot_nt(k * masks[h], q) * size ** (-0.5) + bias[...]
            e = jnp.exp(s - jnp.max(s, axis=0, keepdims=True))
            p = e * (1.0 / jnp.sum(e, axis=0, keepdims=True))
            probs[g * per + h] = p
            parts.append(dot_nn(v_side[h * size : (h + 1) * size, :], p.astype(BF)))
        mixed[:, g * LANES : (g + 1) * LANES] = jnp.concatenate(parts, axis=0).T.astype(BF)


def wide_attention_back(width, heads, triple, probs, low_mixed, grad_triple):
    size = width // heads
    per = LANES // size
    masks = head_masks(size)
    for g in range(width // LANES):
        lanes = [slice(t * width + g * LANES, t * width + (g + 1) * LANES) for t in range(3)]
        q, k, v = (triple[:, lane] for lane in lanes)
        dm = low_mixed[:, g * LANES : (g + 1) * LANES]
        k_side = k.T
        parts, dk, dv = [], 0.0, 0.0
        for h in range(per):
            p = probs[g * per + h]
            dp = dot_nt(v * masks[h], dm)
            ds = (p * (dp - jnp.sum(p * dp, axis=0, keepdims=True))).astype(BF)
            dv = dv + dot_nn(p.astype(BF), dm * masks[h])
            dk = dk + dot_nn(ds, q * masks[h])
            parts.append(dot_nn(k_side[h * size : (h + 1) * size, :], ds))
        grad_triple[:, lanes[0]] = (jnp.concatenate(parts, axis=0).T * size ** (-0.5)).astype(BF)
        grad_triple[:, lanes[1]] = (dk * size ** (-0.5)).astype(BF)
        grad_triple[:, lanes[2]] = dv.astype(BF)


def block_forward(x, rows, images, heads, need, norms, key_bias, saved, done=lambda *names: None):
    entry, plain1, scale1, triple, probs, mixed, plain2, scale2, inner, act, slope = saved
    width = x.shape[1]
    size = width // heads
    per = LANES // size
    groups = width // LANES

    def first(i):
        at = rows_at(i, rows)
        plain, scale = norm(x[at, :])
        plain1[at, :] = plain
        scale1[at, :] = scale
        entry[at, :] = (plain * norms[0:1, :] + norms[1:2, :]).astype(BF)

    loop(images, first)

    done("entry", "plain1", "scale1")
    triple_w = need("triple_w")

    def project(j):
        at = rows_at(j, 256)
        triple[:, at] = dot_nn(entry[...], triple_w[:, at]).astype(BF)

    loop(3 * width // 256, project)
    done("triple")
    masks = head_masks(size)

    def attend(i):
        at = rows_at(i, rows)
        bias = key_bias(i)
        for g in range(groups):
            q = triple[at, g * LANES : (g + 1) * LANES]
            k = triple[at, width + g * LANES : width + (g + 1) * LANES]
            v = triple[at, 2 * width + g * LANES : 2 * width + (g + 1) * LANES]
            v_side = v.T
            parts = []
            for h in range(per):
                s = dot_nt(k * masks[h], q) * size ** (-0.5) + bias
                e = jnp.exp(s - jnp.max(s, axis=0, keepdims=True))
                p = e * (1.0 / jnp.sum(e, axis=0, keepdims=True))
                probs[i * groups + g, h * rows : (h + 1) * rows, :] = p
                parts.append(dot_nn(v_side[h * size : (h + 1) * size, :], p.astype(BF)))
            mixed[at, g * LANES : (g + 1) * LANES] = jnp.concatenate(parts, axis=0).T.astype(BF)

    if callable(key_bias):
        loop(images, attend)
    else:
        wide_attention(width, heads, rows, triple, key_bias, probs, mixed)
    done("probs", "mixed")
    proj_w = need("proj_w")

    def middle(j):
        at = rows_at(j, 256)
        x[:, at] += dot_nn(mixed[...], proj_w[:, at])

    loop(width // 256, middle)

    def second(i):
        at = rows_at(i, rows)
        plain, scale = norm(x[at, :])
        plain2[at, :] = plain
        scale2[at, :] = scale
        inner[at, :] = (plain * norms[2:3, :] + norms[3:4, :]).astype(BF)

    loop(images, second)
    done("plain2", "scale2", "inner")
    up_w = need("up_w")
    hidden = up_w.shape[1]

    def up(j):
        at = rows_at(j, 256)
        value, gradient = gelu_pair(dot_nn(inner[...], up_w[:, at]))
        act[:, at] = value.astype(BF)
        slope[:, at] = gradient

    loop(hidden // 256, up)
    done("act", "slope")
    down_w = need("down_w")

    def down(j):
        at = rows_at(j, 256)
        x[:, at] += dot_nn(act[...], down_w[:, at])

    loop(width // 256, down)


class Writer:
    def __init__(self, flat, stage, sem):
        self.flat, self.stage, self.sem = flat, stage, sem
        self.pending = {}

    def settle(self, s):
        if s in self.pending:
            self.pending.pop(s).wait()

    def outer(self, number, left, right, chunk=256):
        _, _, cols, tile, _ = ENTRIES[number]
        rows = left.shape[1]
        count = rows // chunk
        tall = chunk // 8
        before = dict(self.pending)

        def copy(i, s):
            return pltpu.make_async_copy(
                self.stage.at[s, pl.ds(0, tall * cols)], self.flat.at[pl.ds(tile + i * tall * cols, tall * cols)], self.sem.at[s]
            )

        def body(i):
            s = lax.rem(i, 2)
            for early in before:
                pl.when(i == early)(before[early].wait)

            @pl.when(i >= 2)
            def _():
                copy(i - 2, s).wait()

            side = left[:, rows_at(i, chunk)].T
            for c in range(0, cols, 2):
                value = dot_nn(side, right[:, c * LANES : (c + 2) * LANES])
                for d in range(2):
                    self.stage[s, pl.ds(c + d, tall, stride=cols)] = value[:, d * LANES : (d + 1) * LANES].reshape(tall, 8, LANES)
            copy(i, s).start()

        loop(count, body)
        self.pending = {(count - 2) % 2: copy(count - 2, (count - 2) % 2), (count - 1) % 2: copy(count - 1, (count - 1) % 2)}

    def small(self, number, norm_sums, count, extra=0):
        _, _, _, tile, groups = ENTRIES[number]
        per = SHAPES[number][1] // LANES
        self.settle(0)
        self.stage[0, 0 : groups + extra] = jnp.zeros((groups + extra, 8, LANES), F32)
        for r in range(count):
            for c in range(per):
                line = r * per + c
                self.stage[0, line // 8, line % 8 : line % 8 + 1, :] = norm_sums[r : r + 1, c * LANES : (c + 1) * LANES]
        copy = pltpu.make_async_copy(self.stage.at[0, pl.ds(0, groups + extra)], self.flat.at[pl.ds(tile, groups + extra)], self.sem.at[0])
        copy.start()
        copy.wait()
        self.settle(1)


def block_backward(grad, rows, images, heads, need, norms, norm_sums, extra, writer, numbers):
    low, grad_hidden, side, low_mixed, grad_triple = extra
    width = grad.shape[1]
    size = width // heads
    per = LANES // size
    groups = width // LANES
    low[...] = grad[...].astype(BF)
    down_w, slope = need("down_w"), need("slope")
    hidden = down_w.shape[0]

    def back_up(j):
        at = rows_at(j, 256)
        grad_hidden[:, at] = (dot_nt(low[...], down_w[at, :]) * slope[:, at]).astype(BF)

    loop(hidden // 256, back_up)
    writer.outer(numbers[3], need("act"), low)
    writer.outer(numbers[2], need("inner"), grad_hidden)
    up_w = need("up_w")

    def back_inner(j):
        at = rows_at(j, 256)
        side[:, at] = dot_nt(grad_hidden[...], up_w[at, :])

    loop(width // 256, back_inner)
    plain2, scale2 = need("plain2"), need("scale2")

    def second(i):
        at = rows_at(i, rows)
        back, gain, shift = norm_grad(side[at, :], plain2[at, :], scale2[at, :], norms[2:3, :])
        norm_sums[2:3, :] += gain
        norm_sums[3:4, :] += shift
        total = grad[at, :] + back
        grad[at, :] = total
        low[at, :] = total.astype(BF)

    loop(images, second)
    writer.outer(numbers[1], need("mixed"), low)
    proj_w = need("proj_w")

    def back_mixed(j):
        at = rows_at(j, 256)
        low_mixed[:, at] = dot_nt(low[...], proj_w[at, :]).astype(BF)

    loop(width // 256, back_mixed)
    triple, probs = need("triple"), need("probs")
    masks = head_masks(size)

    def attend(i):
        at = rows_at(i, rows)
        for g in range(groups):
            lanes = [slice(t * width + g * LANES, t * width + (g + 1) * LANES) for t in range(3)]
            q, k, v = (triple[at, lane] for lane in lanes)
            dm = low_mixed[at, g * LANES : (g + 1) * LANES]
            k_side = k.T
            parts, dk, dv = [], 0.0, 0.0
            for h in range(per):
                p = probs[i * groups + g, h * rows : (h + 1) * rows, :]
                dp = dot_nt(v * masks[h], dm)
                ds = (p * (dp - jnp.sum(p * dp, axis=0, keepdims=True))).astype(BF)
                dv = dv + dot_nn(p.astype(BF), dm * masks[h])
                dk = dk + dot_nn(ds, q * masks[h])
                parts.append(dot_nn(k_side[h * size : (h + 1) * size, :], ds))
            dq = jnp.concatenate(parts, axis=0).T
            grad_triple[at, lanes[0]] = (dq * size ** (-0.5)).astype(BF)
            grad_triple[at, lanes[1]] = (dk * size ** (-0.5)).astype(BF)
            grad_triple[at, lanes[2]] = dv.astype(BF)

    if probs.shape[1] == probs.shape[2] and probs.shape[0] == heads:
        wide_attention_back(width, heads, triple, probs, low_mixed, grad_triple)
    else:
        loop(images, attend)
    writer.outer(numbers[0], need("entry"), grad_triple)
    triple_w = need("triple_w")

    def back_entry(j):
        at = rows_at(j, 256)
        side[:, at] = dot_nt(grad_triple[...], triple_w[at, :])

    loop(width // 256, back_entry)
    plain1, scale1 = need("plain1"), need("scale1")

    def first(i):
        at = rows_at(i, rows)
        back, gain, shift = norm_grad(side[at, :], plain1[at, :], scale1[at, :], norms[0:1, :])
        norm_sums[0:1, :] += gain
        norm_sums[1:2, :] += shift
        grad[at, :] += back

    loop(images, first)


SAVED = ("seen", "entry", "plain1", "scale1", "triple", "probs", "mixed", "plain2", "scale2", "inner", "act", "slope", "plain3", "scale3", "encoded")
ENC_NAMES = ("embed_w", "triple_w", "proj_w", "up_w", "down_w", "dec_embed_w")
DEC_NAMES = ("triple_w", "proj_w", "up_w", "down_w", "head_w")


def saved_shapes(rows):
    s = jax.ShapeDtypeStruct
    return [
        s((rows, D), BF), s((rows, D), BF), s((rows, D), F32), s((rows, 1), F32), s((rows, 3 * D), BF),
        s((HEADS, rows, rows), F32), s((rows, D), BF), s((rows, D), F32), s((rows, 1), F32), s((rows, D), BF),
        s((rows, F), BF), s((rows, F), F32), s((rows, D), F32), s((rows, 1), F32), s((rows, D), BF),
    ]


def like(shape):
    return pltpu.VMEM(shape.shape, shape.dtype)


def pad_patches(patches, padded, images):
    padded[...] = jnp.zeros_like(padded)
    for i in range(images):
        padded[i * P_ROWS : i * P_ROWS + PATCHES, :] = patches[i]


def encoder_kernel(images, counts_ref, cols_ref, norms_ref, *refs):
    pos_hbm, patches_hbm, *weights_hbm = refs[:8]
    outs = refs[8:23]
    entering = refs[23]
    pos, patches, *weights = refs[24:32]
    saved = dict(zip(SAVED, refs[32:47]))
    x, place_, pos_split, padded, bias, in_sem, out_sem = refs[47:]
    need = Moves(("pos", "patches") + ENC_NAMES, [pos_hbm, patches_hbm] + weights_hbm, [pos, patches] + weights, in_sem)
    need.start()
    put = Moves(SAVED, [saved[name] for name in SAVED], outs, out_sem)
    rows = images * KEEP
    key = lax.broadcasted_iota(jnp.int32, (KEEP, rows), 0)
    query = lax.broadcasted_iota(jnp.int32, (KEEP, rows), 1)
    for i in range(images):
        inside = jnp.logical_and(jnp.logical_and(query >= i * KEEP, query < (i + 1) * KEEP), key < counts_ref[i])
        bias[i * KEEP : (i + 1) * KEEP, :] = jnp.where(inside, 0.0, NEG_FILL)
    need("pos")
    for t, part in enumerate(three(pos[...])):
        pos_split[t] = part
    pad_patches(need("patches"), padded, images)
    spots = lax.broadcasted_iota(jnp.int32, (KEEP, P_ROWS), 1)
    seen = saved["seen"]

    def select(i):
        at = rows_at(i, KEEP)
        pick = jnp.where(spots == cols_ref[i], 1.0, 0.0).astype(BF)
        seen[at, :] = dot_nn(pick, padded[rows_at(i, P_ROWS), :]).astype(BF)
        place_[at, :] = dot_nn(pick, pos_split[0]) + dot_nn(pick, pos_split[1]) + dot_nn(pick, pos_split[2])

    loop(images, select)
    put.start("seen")
    embed_w = need("embed_w")

    def embed(j):
        at = rows_at(j, 256)
        x[:, at] = dot_nn(seen[...], embed_w[:, at]) + place_[:, at]

    loop(D // 256, embed)
    block_forward(x, KEEP, images, HEADS, need, norms_ref, bias, [saved[name] for name in SAVED[1:12]], put.start)
    plain3, scale3, encoded = (saved[name] for name in SAVED[12:])

    def last(i):
        at = rows_at(i, KEEP)
        plain, scale = norm(x[at, :])
        plain3[at, :] = plain
        scale3[at, :] = scale
        encoded[at, :] = (plain * norms_ref[4:5, :] + norms_ref[5:6, :]).astype(BF)

    loop(images, last)
    put.start("plain3", "scale3", "encoded")
    entering[...] = dot_nn(encoded[...], need("dec_embed_w")[...])
    put.close()


def encoder(counts, patches, cols, pos, weights, norms):
    images = counts.shape[0]
    rows = images * KEEP
    vmem = pl.BlockSpec(memory_space=pltpu.VMEM)
    anyspec = pl.BlockSpec(memory_space=pl.ANY)
    shapes = saved_shapes(rows)
    return pl.pallas_call(
        functools.partial(encoder_kernel, images),
        name="encoder",
        out_shape=shapes + [jax.ShapeDtypeStruct((rows, DD), F32)],
        in_specs=[pl.BlockSpec(memory_space=pltpu.SMEM), vmem, vmem] + [anyspec] * 8,
        out_specs=[anyspec] * 15 + [vmem],
        scratch_shapes=[like(one) for one in [pos, patches] + weights + shapes]
        + [
            pltpu.VMEM((rows, D), F32), pltpu.VMEM((rows, D), F32), pltpu.VMEM((3, P_ROWS, D), BF), pltpu.VMEM((images * P_ROWS, PIX), BF),
            pltpu.VMEM((rows, rows), F32), pltpu.SemaphoreType.DMA((8,)), pltpu.SemaphoreType.DMA((15,)),
        ],
        compiler_params=pltpu.CompilerParams(vmem_limit_bytes=60 * MB),
    )(counts, cols, norms, pos, patches, *weights)


def decoder_kernel(images, counts_ref, masked_ref, cols_ref, rows_ref, entering_ref, norms_ref, *refs):
    pos_hbm, patches_hbm, *weights_hbm = refs[:7]
    flat, grad_entering, loss_ref = refs[7:10]
    pos, patches, *weights = refs[10:17]
    (x, hide, entry, plain1, scale1, triple, probs, mixed, plain2, scale2, inner, act, slope, plain3, scale3, final, grad_pred,
     low, grad_hidden, side, low_mixed, grad_triple, norm_sums, padded, stage, sem, in_sem) = refs[17:]
    need = Moves(("pos", "patches") + DEC_NAMES, [pos_hbm, patches_hbm] + weights_hbm, [pos, patches] + weights, in_sem)
    need.start()
    saved = (entry, plain1, scale1, triple, probs, mixed, plain2, scale2, inner, act, slope)
    need.targets.update(zip(SAVED[1:12], saved))
    lane = lax.broadcasted_iota(jnp.int32, (P_ROWS, KEEP), 1)
    spot = lax.broadcasted_iota(jnp.int32, (P_ROWS, KEEP), 0)
    line = lax.broadcasted_iota(jnp.int32, (P_ROWS, 1), 0)
    need("pos")

    def start(i):
        at = rows_at(i, P_ROWS)
        hit = jnp.where(jnp.logical_and(spot == rows_ref[pl.ds(i, 1), 0:KEEP], lane < counts_ref[i]), 1.0, 0.0)
        shown = jnp.max(hit, axis=1, keepdims=True)
        pick = hit.astype(BF)
        top, mid, end = three(entering_ref[rows_at(i, KEEP), :])
        picked = dot_nn(pick, top) + dot_nn(pick, mid) + dot_nn(pick, end)
        x[at, :] = jnp.where(shown > 0.0, picked, norms_ref[6:7, :]) + pos[...]
        hide[at, :] = jnp.where(jnp.logical_and(line < PATCHES, shown == 0.0), 1.0, 0.0)

    loop(images, start)
    bias = jnp.where(line < PATCHES, 0.0, NEG_FILL)
    block_forward(x, P_ROWS, images, DHEADS, need, norms_ref, lambda i: bias, saved)

    def last(i):
        at = rows_at(i, P_ROWS)
        plain, scale = norm(x[at, :])
        plain3[at, :] = plain
        scale3[at, :] = scale
        final[at, :] = (plain * norms_ref[4:5, :] + norms_ref[5:6, :]).astype(BF)

    loop(images, last)
    loss_ref[...] = jnp.zeros_like(loss_ref)
    masked = masked_ref[0:1, 0:1]
    head_w = need("head_w")
    pad_patches(need("patches"), padded, images)

    def score(i):
        at = rows_at(i, P_ROWS)
        target, _ = norm(padded[at, :].astype(F32))
        diff = dot_nn(final[at, :], head_w[...]) - target
        hidden = hide[at, :]
        loss_ref[...] += jnp.sum(jnp.mean(diff * diff, axis=-1, keepdims=True) * hidden, axis=0, keepdims=True)
        grad_pred[at, :] = (diff * (hidden * (2.0 / PIX)) / masked).astype(BF)

    loop(images, score)
    writer = Writer(flat, stage, sem)
    writer.outer(11, final, grad_pred)
    norm_sums[...] = jnp.zeros_like(norm_sums)

    def back_final(i):
        at = rows_at(i, P_ROWS)
        back, gain, shift = norm_grad(dot_nt(grad_pred[at, :], head_w[...]), plain3[at, :], scale3[at, :], norms_ref[4:5, :])
        norm_sums[4:5, :] += gain
        norm_sums[5:6, :] += shift
        x[at, :] = back

    loop(images, back_final)
    block_backward(x, P_ROWS, images, DHEADS, need, norms_ref, norm_sums, (low, grad_hidden, side, low_mixed, grad_triple), writer, (7, 8, 9, 10))
    spots = lax.broadcasted_iota(jnp.int32, (KEEP, P_ROWS), 1)
    slot = lax.broadcasted_iota(jnp.int32, (KEEP, P_ROWS), 0)

    def finish(i):
        at = rows_at(i, P_ROWS)
        grad = x[at, :]
        norm_sums[6:7, :] += jnp.sum(grad * hide[at, :], axis=0, keepdims=True)
        pick = jnp.where(jnp.logical_and(spots == cols_ref[i], slot < counts_ref[i]), 1.0, 0.0).astype(BF)
        grad_entering[rows_at(i, KEEP), :] = dot_nn(pick, grad.astype(BF)).astype(BF)

    loop(images, finish)
    writer.small(12, norm_sums, 7, flat.shape[0] - TILES)


def decoder(total, counts, masked, patches, cols, order, pos, entering, weights, norms):
    images = counts.shape[0]
    rows = images * P_ROWS
    vmem = pl.BlockSpec(memory_space=pltpu.VMEM)
    anyspec = pl.BlockSpec(memory_space=pl.ANY)

    def v(shape, kind=F32):
        return pltpu.VMEM(shape, kind)

    return pl.pallas_call(
        functools.partial(decoder_kernel, images),
        name="decoder",
        out_shape=[
            jax.ShapeDtypeStruct((total, 8, LANES), F32),
            jax.ShapeDtypeStruct((images * KEEP, DD), BF),
            jax.ShapeDtypeStruct((1, 1), F32),
        ],
        in_specs=[pl.BlockSpec(memory_space=pltpu.SMEM)] + [vmem] * 5 + [anyspec] * 7,
        out_specs=[anyspec, vmem, vmem],
        scratch_shapes=[like(one) for one in [pos, patches] + weights]
        + [
            v((rows, DD)), v((rows, 1)), v((rows, DD), BF), v((rows, DD)), v((rows, 1)), v((rows, 3 * DD), BF),
            v((images * DD // LANES, 4 * P_ROWS, P_ROWS)), v((rows, DD), BF), v((rows, DD)), v((rows, 1)), v((rows, DD), BF),
            v((rows, FD), BF), v((rows, FD)), v((rows, DD)), v((rows, 1)), v((rows, DD), BF), v((rows, PIX), BF),
            v((rows, DD), BF), v((rows, FD), BF), v((rows, DD)), v((rows, DD), BF), v((rows, 3 * DD), BF),
            v((8, DD)), v((rows, PIX), BF), v((2, 32 * 16, 8, LANES)), pltpu.SemaphoreType.DMA((2,)), pltpu.SemaphoreType.DMA((7,)),
        ],
        compiler_params=pltpu.CompilerParams(vmem_limit_bytes=63 * MB),
    )(counts, masked, cols, order, entering, norms, pos, patches, *weights)


def encoder_back_kernel(images, flat_in, grad_entering, norms_ref, *refs):
    names = SAVED + ENC_NAMES[1:]
    sources = refs[:20]
    flat = refs[20]
    targets = refs[21:41]
    x, low, grad_hidden, side, low_mixed, grad_triple, norm_sums, stage, sem, in_sem = refs[41:]
    need = Moves(names, sources, targets, in_sem)
    need.start(
        "encoded", "dec_embed_w", "plain3", "scale3", "down_w", "slope", "act", "inner", "up_w", "plain2", "scale2",
        "mixed", "proj_w", "triple", "probs", "entry", "triple_w", "plain1", "scale1", "seen",
    )
    writer = Writer(flat, stage, sem)
    writer.outer(6, need("encoded"), grad_entering)
    norm_sums[...] = jnp.zeros_like(norm_sums)
    side[...] = dot_nt(grad_entering[...], need("dec_embed_w")[...])
    plain3, scale3 = need("plain3"), need("scale3")

    def last(i):
        at = rows_at(i, KEEP)
        back, gain, shift = norm_grad(side[at, :], plain3[at, :], scale3[at, :], norms_ref[4:5, :])
        norm_sums[4:5, :] += gain
        norm_sums[5:6, :] += shift
        x[at, :] = back

    loop(images, last)
    block_backward(x, KEEP, images, HEADS, need, norms_ref, norm_sums, (low, grad_hidden, side, low_mixed, grad_triple), writer, (1, 2, 3, 4))
    low[...] = x[...].astype(BF)
    writer.outer(0, need("seen"), low)
    writer.small(5, norm_sums, 6)


def encoder_back(flat, grad_entering, saved, weights, norms):
    rows = grad_entering.shape[0]
    images = rows // KEEP
    vmem = pl.BlockSpec(memory_space=pltpu.VMEM)
    anyspec = pl.BlockSpec(memory_space=pl.ANY)

    def v(shape, kind=F32):
        return pltpu.VMEM(shape, kind)

    return pl.pallas_call(
        functools.partial(encoder_back_kernel, images),
        name="encoder_back",
        out_shape=jax.ShapeDtypeStruct(flat.shape, flat.dtype),
        in_specs=[anyspec, vmem, vmem] + [anyspec] * 20,
        out_specs=anyspec,
        scratch_shapes=[like(one) for one in saved + weights]
        + [
            v((rows, D)), v((rows, D), BF), v((rows, F), BF), v((rows, D)), v((rows, D), BF), v((rows, 3 * D), BF),
            v((8, D)), v((2, 32 * 24, 8, LANES)), pltpu.SemaphoreType.DMA((2,)), pltpu.SemaphoreType.DMA((20,)),
        ],
        input_output_aliases={0: 0},
        compiler_params=pltpu.CompilerParams(vmem_limit_bytes=60 * MB),
    )(flat, grad_entering, norms, *saved, *weights)


def positions(width):
    index = np.arange(PATCHES)
    quarter = width // 4
    freq = 10000.0 ** (-np.arange(quarter).astype(np.float32) / np.float32(quarter))
    row = (index // GRID).astype(np.float32)[:, None] * freq[None, :].astype(np.float32)
    column = (index % GRID).astype(np.float32)[:, None] * freq[None, :].astype(np.float32)
    table = np.concatenate([np.sin(row), np.cos(row), np.sin(column), np.cos(column)], axis=1).astype(np.float32)
    return jnp.asarray(np.pad(table, ((0, P_ROWS - PATCHES), (0, 0))))


def own_lines(flat, share, index):
    if share % LANES == 0:
        return flat.reshape(-1, LANES)
    rows = (share + LANES - 1) // LANES + 1
    return lax.dynamic_update_slice(jnp.zeros((rows * LANES,), flat.dtype), flat, (share * index % LANES,)).reshape(rows, LANES)


def own_flat(lines, share, index):
    if share % LANES == 0:
        return lines.reshape(-1)
    return lax.dynamic_slice(lines.reshape(-1), (share * index % LANES,), (share,))


def body(n_dp, n_pair, patches, patch_order, counts, master, moment1, moment2, block_rates, clip_limit, step_count):
    n = n_dp * n_pair
    share = master.shape[0]
    images = counts.shape[0]
    index = lax.axis_index("dp") * n_pair + lax.axis_index("pair")
    extra = jnp.zeros((8, LANES), F32).at[0, :images].set((PATCHES - counts).astype(F32))
    lines = [own_lines(one, share, index) for one in (master, moment1, moment2)]
    steps_done = step_count[0].astype(F32)
    params = jnp.stack([block_rates[0], block_rates[1], clip_limit[0], 1.0 - BETA_ONE**steps_done, 1.0 - BETA_TWO**steps_done])
    *held, enc_norms, dec_norms, masked = gather(lines[0], extra, share, n_dp, n_pair, 1)
    parts = {i: matrix(one, i) for i, one in zip(BIG, held)}
    slots_at = patch_order[:, :KEEP]
    cols = slots_at[:, :, None]
    enc_weights = [parts[i] for i in (1, 2, 3, 4, 6)]
    *saved, entering = encoder(counts, patches, cols, positions(D), [parts[0]] + enc_weights, enc_norms)
    total = max(a for a, _ in ranges(share, n)) + slab_tiles(share, n)
    dec_weights = [parts[i] for i in (7, 8, 9, 10, 11)]
    flat, grad_entering, loss_local = decoder(total, counts, masked, patches, cols, slots_at, positions(DD), entering, dec_weights, dec_norms)
    flat = encoder_back(flat, grad_entering, saved, enc_weights, enc_norms)
    first, second, master_new, totals = reduce(flat.reshape(-1, LANES), loss_local, params, lines, share, n_dp, n_pair)
    loss = totals[1, 0:1] / masked[0]
    first, second, master_new = (own_flat(one, share, index) for one in (first, second, master_new))
    return (loss, totals[0, 0:1], first, second, master_new)


def solution(mesh):
    whole = P(("dp", "pair"))
    in_specs = (P(("dp", "pair"), None, None), P(("dp", "pair"), None), whole, whole, whole, whole, P(), P(), P())
    out_specs = (P(), P(), whole, whole, whole)
    step = functools.partial(body, mesh.shape["dp"], mesh.shape["pair"])
    return jax.shard_map(step, mesh=mesh, in_specs=in_specs, out_specs=out_specs, check_vma=False)
```

```python
import functools

import jax
import jax.numpy as jnp
import numpy as np
from jax import lax
from jax.experimental import pallas as pl
from jax.experimental.pallas import tpu as pltpu
from jax.sharding import PartitionSpec as P

MESH = pl.DeviceIdType.MESH
LANES = 128
TILE = 16 * LANES


def place():
    dp, pair = lax.axis_index("dp"), lax.axis_index("pair")
    return dp // 2, dp % 2, pair // 2, pair % 2


def slot_of(z, x, y, c):
    return (z * 2 + x) * 4 + y * 2 + c


def partners(z, x, y, c):
    return {
        "x": {"dp": z * 2 + (1 - x)},
        "y": {"pair": (1 - y) * 2 + c},
        "c": {"pair": y * 2 + (1 - c)},
        "up": {"dp": (z + 1) * 2 + x},
        "down": {"dp": (z - 1) * 2 + x},
    }


def greet(n_z, z, to):
    barrier = pltpu.get_barrier_semaphore()
    for name in ("x", "y", "c"):
        pl.semaphore_signal(barrier, inc=1, device_id=to[name], device_id_type=MESH)

    @pl.when(z < n_z - 1)
    def _():
        pl.semaphore_signal(barrier, inc=1, device_id=to["up"], device_id_type=MESH)

    @pl.when(z > 0)
    def _():
        pl.semaphore_signal(barrier, inc=1, device_id=to["down"], device_id_type=MESH)

    pl.semaphore_wait(barrier, 3 + jnp.where(z < n_z - 1, 1, 0) + jnp.where(z > 0, 1, 0))


def both(*conditions):
    total = conditions[0]
    for one in conditions[1:]:
        total = jnp.logical_and(total, one)
    return total


PIX, HEADS, F, DHEADS, FD, GRID, KEEP, D, DD, PATCHES = 768, 12, 3072, 16, 2048, 14, 64, 768, 512, 196
SHAPES = [(PIX, D), (D, 3 * D), (D, D), (D, F), (F, D), (6, D), (D, DD), (DD, 3 * DD), (DD, DD), (DD, FD), (FD, DD), (DD, PIX), (7, DD)]
SMALL = (5, 12)
ENC_PARAMS = 7672320
NORM_EPS = 1e-06
ADAM_EPS = 1e-08
BETA_ONE = 0.9
BETA_TWO = 0.95
DECAY = 0.05
MB = 1 << 20
CELL = 8 * LANES
BLOCK = 96


def make_entries():
    entries, row, tile = [], 0, 0
    for number, (rows, width) in enumerate(SHAPES):
        lines = rows * width // LANES
        cols = 1 if number in SMALL else width // LANES
        groups = -(-lines // (8 * cols))
        entries.append((row, lines, cols, tile, groups))
        row += lines
        tile += groups * cols
    return entries, row, tile


ENTRIES, ROWS, TILES = make_entries()
BIG = tuple(i for i in range(len(SHAPES)) if i not in SMALL)
MARGIN = 8 * max(cols for _, _, cols, _, _ in ENTRIES)


def first_tile(share, k):
    lo = share * k
    total = 0
    for row, lines, cols, tile, _ in ENTRIES:
        inside = jnp.logical_and(lo >= row * LANES, lo < (row + lines) * LANES)
        total = total + jnp.where(inside, tile + (lo - row * LANES) // (CELL * cols) * cols, 0)
    return total


def ranges(share, n):
    found = []
    for k in range(n):
        lo, hi = share * k, share * (k + 1)
        spans = []
        for row, lines, cols, tile, _ in ENTRIES:
            low, high = max(lo, row * LANES), min(hi, (row + lines) * LANES)
            if low < high:
                size = CELL * cols
                spans.append((tile + (low - row * LANES) // size * cols, tile + -(-(high - row * LANES) // size) * cols))
        found.append((spans[0][0], spans[-1][1]))
    return found


def slab_tiles(share, n):
    longest = max(b - a for a, b in ranges(share, n))
    return -(-longest // 24) * 24


def line_span(share, k):
    return share * k // LANES, (share * (k + 1) + LANES - 1) // LANES


def tiled(share, k, body):
    lo, hi = line_span(share, k)
    begin = first_tile(share, k)
    for number in SMALL + tuple(i for i in range(len(ENTRIES)) if i not in SMALL):
        row, lines, cols, tile, _ = ENTRIES[number]
        low = jnp.maximum(lo, row) - row
        high = jnp.minimum(hi, row + lines) - row
        size = 8 * cols

        def group(g, _, row=row, cols=cols, tile=tile, size=size):
            body(row + g * size - lo + MARGIN, tile + g * cols - begin, cols)
            return 0

        lax.fori_loop(jnp.where(low < high, low // size, 0), jnp.where(low < high, (high + size - 1) // size, 0), group, 0)


def wide_rows(rows):
    return -(-(rows + 2 * MARGIN) // 8) * 8


def pieces(share, n):
    spans = ranges(share, n)
    shared = [spans[k][1] > spans[k + 1][0] for k in range(n - 1)]
    plain, seams = [], []
    for number, (_, _, cols, tile, groups) in enumerate(ENTRIES):
        end = tile + groups * cols
        for k, (a, b) in enumerate(spans):
            low, high = max(a, tile), min(b, end)
            if low >= high:
                continue
            inner_low, inner_high = low, high
            if k > 0 and spans[k - 1][1] > low:
                inner_low = spans[k - 1][1]
            if k < n - 1 and spans[k + 1][0] < high:
                inner_high = spans[k + 1][0]
                seams.append((number, k, inner_high, high))
            if inner_low < inner_high:
                plain.append((number, k, inner_low, inner_high))
    return spans, plain, seams


def matrix(tiles_, number):
    rows, width = SHAPES[number]
    cols = width // LANES
    return tiles_.reshape(rows // 8, cols, 8, LANES).transpose(0, 2, 1, 3).reshape(rows, width)


def matrix_tiles(value):
    rows, width = value.shape
    cols = width // LANES
    return value.reshape(rows // 8, 8, cols, LANES).transpose(0, 2, 1, 3).reshape(rows * cols, LANES)


def gather_kernel(n_z, n_pair, share, lines_ref, extra_ref, *refs):
    outs = dict(zip(BIG, refs[: len(BIG)]))
    enc_norms, dec_norms, masked_ref = refs[len(BIG) : len(BIG) + 3]
    wide, out_ref, z_sem, plane_sem, second_sem, third_sem, flat_sem, line_sem, core_sem, recv_sem, put_sem = refs[len(BIG) + 3 :]
    n = n_z * 2 * n_pair
    total_tiles = out_ref.shape[1]
    small = total_tiles // 2 * 2 // 9
    large = total_tiles // 2 - small
    spans_of = ((0, large), (large, large), (2 * large, small), (2 * large + small, small), (2 * large, 2 * small))
    z, x, y, c = place()
    to = partners(z, x, y, c)
    me = slot_of(z, x, y, c)
    rows = lines_ref.shape[0]
    wide[0:MARGIN, :] = jnp.zeros((MARGIN, LANES), jnp.float32)
    wide[MARGIN + rows :, :] = jnp.zeros((wide.shape[0] - MARGIN - rows, LANES), jnp.float32)
    wide[MARGIN : MARGIN + rows, :] = lines_ref[...]

    def fill(line, tile, cols):
        for col in range(cols):
            out_ref[me, tile + col] = wide[pl.ds(line + col, 8, stride=cols), :].astype(out_ref.dtype)

    tiled(share, me, fill)
    out_ref[me, total_tiles - 2] = extra_ref[...].astype(out_ref.dtype)
    greet(n_z, z, to)

    def copy(slot, part, name, sem):
        at = pl.ds(*spans_of[part])
        return pltpu.make_async_remote_copy(
            out_ref.at[slot, at], out_ref.at[slot, at], sem, recv_sem.at[slot, 2 if part == 4 else part], device_id=to[name], device_id_type=MESH
        )

    def arrived(slot, part):
        copy(slot, part, "c", plane_sem.at[0, 0, 0]).wait_recv()

    def start(one):
        one.start()

    def stop(one):
        one.wait_send()

    def lines(t):
        for d in (0, 1):
            zz = z - t if d == 0 else z + t
            inside = zz >= 0 if d == 0 else zz < n_z
            more = z < n_z - 1 if d == 0 else z > 0
            fresh = both(t > 0, inside)
            held = jnp.logical_or(fresh, t == 0) if d == 0 else fresh
            yield d, zz, fresh, held, more

    def own_z(act):
        for d, more in ((0, z < n_z - 1), (1, z > 0)):
            for part in (0, 1):
                pl.when(more)(lambda d=d, part=part: act(copy(me, part, ("up", "down")[d], z_sem.at[0, d, part])))

    def onward_z(t, d, zz, fresh, more, act):
        for part in (0, 1):
            pl.when(both(fresh, more))(lambda part=part: act(copy(slot_of(zz, x, y, c), part, ("up", "down")[d], z_sem.at[t, d, part])))

    def plane_sends(t, d, zz, held, act):
        @pl.when(held)
        def _():
            for i, (part, name) in enumerate(((0, "x"), (1, "y"), (0, "y"), (1, "x"), (0, "c"), (1, "c"))):
                act(copy(slot_of(zz, x, y, c), part, name, plane_sem.at[t, d, i]))

    def first(t):
        for d, zz, fresh, held, more in lines(t):

            @pl.when(fresh)
            def _():
                for part in (0, 1):
                    arrived(slot_of(zz, x, y, c), part)

            onward_z(t, d, zz, fresh, more, start)
            plane_sends(t, d, zz, held, start)

    def second_items(zz):
        return ((0, slot_of(zz, 1 - x, y, c), "y"), (1, slot_of(zz, x, 1 - y, c), "x"))

    def second(t):
        for d, zz, _, held, _ in lines(t):

            @pl.when(held)
            def _():
                for part, slot, name in second_items(zz):
                    arrived(slot, part)
                    copy(slot, part, name, second_sem.at[t, d, part, 0]).start()
                    copy(slot, part, "c", second_sem.at[t, d, part, 1]).start()

    def third_items(zz):
        return ((0, slot_of(zz, x, 1 - y, c)), (1, slot_of(zz, 1 - x, y, c)), (0, slot_of(zz, 1 - x, 1 - y, c)), (1, slot_of(zz, 1 - x, 1 - y, c)))

    def third(t):
        for d, zz, _, held, _ in lines(t):

            @pl.when(held)
            def _():
                for i, (part, slot) in enumerate(third_items(zz)):
                    arrived(slot, part)
                    copy(slot, part, "c", third_sem.at[t, d, i]).start()

    near = ((2, me, "x"), (3, me, "y"), (2, me, "y"), (3, me, "x"), (2, me, "c"), (3, me, "c"))
    beside = ((2, slot_of(z, 1 - x, y, c), "y"), (3, slot_of(z, x, 1 - y, c), "x"))
    across = ((2, slot_of(z, x, 1 - y, c)), (3, slot_of(z, 1 - x, y, c)), (2, slot_of(z, 1 - x, 1 - y, c)), (3, slot_of(z, 1 - x, 1 - y, c)))

    def flat_sends(act, which):
        for i, (part, slot, name) in enumerate(near):
            if which == 0:
                act(copy(slot, part, name, flat_sem.at[i]))
        for i, (part, slot, name) in enumerate(beside):
            if which == 1:
                act(copy(slot, part, name, flat_sem.at[6 + i]))
                act(copy(slot, part, "c", flat_sem.at[8 + i]))
        for i, (part, slot) in enumerate(across):
            if which == 2:
                act(copy(slot, part, "c", flat_sem.at[10 + i]))

    def corner(zz, i):
        return slot_of(zz, i // 2, i % 2, c)

    def line_sends(t, act):
        for d, zz, fresh, _, more in lines(t):
            for i in range(4):
                go = jnp.logical_or(fresh, t == 0)
                pl.when(both(go, more))(lambda d=d, zz=zz, i=i: act(copy(corner(zz, i), 4, ("up", "down")[d], line_sem.at[t, d, i])))
                pl.when(fresh)(lambda d=d, zz=zz, i=i: act(copy(corner(zz, i), 4, "c", core_sem.at[t, d, i])))

    def along(t):
        for d, zz, fresh, _, _ in lines(t):

            @pl.when(fresh)
            def _():
                for i in range(4):
                    arrived(corner(zz, i), 4)

        @pl.when(t == 0)
        def _():
            for part, slot in across:
                arrived(slot, part)
            flat_sends(start, 2)

        line_sends(t, start)

    own_z(start)
    flat_sends(start, 0)
    for part, slot, _ in beside:
        arrived(slot, part)
    flat_sends(start, 1)

    def turn(t, _):
        pl.when(t < n_z)(lambda: first(t))
        pl.when(both(t >= 1, t < n_z + 1))(lambda: second(t - 1))
        pl.when(both(t >= 1, t < n_z + 1))(lambda: along(t - 1))
        pl.when(t >= 2)(lambda: third(t - 2))
        return 0

    lax.fori_loop(0, n_z + 2, turn, 0)
    own_z(stop)
    for which in range(3):
        flat_sends(stop, which)

    def finish(t, _):
        line_sends(t, stop)
        for d, zz, fresh, held, more in lines(t):
            onward_z(t, d, zz, fresh, more, stop)
            plane_sends(t, d, zz, held, stop)

            @pl.when(held)
            def _():
                for part, slot, name in second_items(zz):
                    copy(slot, part, name, second_sem.at[t, d, part, 0]).wait_send()
                    copy(slot, part, "c", second_sem.at[t, d, part, 1]).wait_send()
                for i, (part, slot) in enumerate(third_items(zz)):
                    copy(slot, part, "c", third_sem.at[t, d, i]).wait_send()
                for i in range(4):
                    for part in (0, 1):
                        arrived(slot_of(zz, i // 2, i % 2, 1 - c), part)

            @pl.when(fresh)
            def _():
                for i in range(4):
                    arrived(slot_of(zz, i // 2, i % 2, 1 - c), 4)

        return 0

    lax.fori_loop(0, n_z, finish, 0)
    for i in range(4):
        for part in (2, 3):
            arrived(slot_of(z, i // 2, i % 2, 1 - c), part)
    spans, plain, seams = pieces(share, n)
    puts = []

    def put(number, k, low, high):
        copy = pltpu.make_async_copy(
            out_ref.at[k, pl.ds(low - spans[k][0], high - low)], outs[number].at[pl.ds(low - ENTRIES[number][3], high - low)], put_sem.at[len(puts)]
        )
        copy.start()
        puts.append(copy)

    home = {}
    for number, k, low, high in plain + seams:
        if number in SMALL:
            home.update({tile: (k, tile - spans[k][0]) for tile in range(low, high)})
        elif (number, k, low, high) in plain:
            put(number, k, low, high)
    for number, k, low, high in seams:
        left = pl.ds(low - spans[k][0], high - low)
        right = pl.ds(low - spans[k + 1][0], high - low)
        total = out_ref[k, left].astype(jnp.float32) + out_ref[k + 1, right].astype(jnp.float32)
        out_ref[k, left] = total.astype(out_ref.dtype)
        if number not in SMALL:
            put(number, k, low, high)
    for number, target in zip(SMALL, (enc_norms, dec_norms)):
        row, lines_, _, tile, groups = ENTRIES[number]
        per = SHAPES[number][1] // LANES
        for group in range(groups):
            k, at = home[tile + group]
            value = out_ref[k, at].astype(jnp.float32)
            for line in range(group * 8, min(group * 8 + 8, lines_)):
                target[line // per : line // per + 1, line % per * LANES : (line % per + 1) * LANES] = value[line % 8 : line % 8 + 1, :]
    masked_ref[...] = jnp.zeros_like(masked_ref)

    def count(k, _):
        masked_ref[...] += jnp.sum(out_ref[k, out_ref.shape[1] - 2].astype(jnp.float32)[0:1, :], axis=1, keepdims=True)
        return 0

    lax.fori_loop(0, n, count, 0)
    for copy in puts:
        copy.wait()


def gather(lines, extra, share, n_dp, n_pair):
    n_z = n_dp // 2
    n = n_dp * n_pair
    tiles_ = slab_tiles(share, n) + 2
    _, plain, seams = pieces(share, n)
    dma = pltpu.SemaphoreType.DMA
    anyspec = pl.BlockSpec(memory_space=pl.ANY)
    vmem = pl.BlockSpec(memory_space=pltpu.VMEM)

    def s(shape, kind=jnp.float32):
        return jax.ShapeDtypeStruct(shape, kind)

    return pl.pallas_call(
        functools.partial(gather_kernel, n_z, n_pair, share),
        name="gather",
        out_shape=[s((ENTRIES[i][4] * ENTRIES[i][2], 8, LANES), jnp.bfloat16) for i in BIG] + [s(SHAPES[5]), s(SHAPES[12]), s((1, 1))],
        in_specs=[vmem, vmem],
        out_specs=[anyspec] * len(BIG) + [vmem] * 3,
        scratch_shapes=[
            pltpu.VMEM((wide_rows(lines.shape[0]), LANES), jnp.float32),
            pltpu.VMEM((n, tiles_, 8, LANES), jnp.bfloat16),
            dma((n_z, 2, 2)), dma((n_z, 2, 6)), dma((n_z, 2, 2, 2)), dma((n_z, 2, 4)), dma((14,)), dma((n_z, 2, 4)), dma((n_z, 2, 4)), dma((n, 4)),
            dma((len(plain) + len(seams),)),
        ],
        compiler_params=pltpu.CompilerParams(collective_id=0, has_side_effects=True, vmem_limit_bytes=60 * MB),
    )(lines, extra)


def reduce_chunks(share, n):
    rows = slab_tiles(share, n) * 8
    return max(d for d in (1, 2, 4) if rows % (2 * BLOCK * d) == 0)


def late_cut(share):
    return -(-ENTRIES[7][0] * LANES // (share * 8))


def pack(value, q_ref, t_ref, b):
    top = jnp.max(jnp.abs(value), axis=0, keepdims=True)
    inverse = jnp.where(top > 1e-30, 32767.0 / jnp.maximum(top, 1e-30), 0.0)
    q_ref[pl.ds(pl.multiple_of(b * BLOCK, BLOCK), BLOCK), :] = jnp.round(value * inverse).astype(jnp.int32).astype(jnp.int16)
    t_ref[pl.ds(b, 1), :] = top * (1.0 / 32767.0)


def unpack(q_ref, t_ref, b):
    return q_ref[pl.ds(pl.multiple_of(b * BLOCK, BLOCK), BLOCK), :].astype(jnp.int32).astype(jnp.float32) * t_ref[pl.ds(b, 1), :]


def message(qs, ts, qr, tr, sem, to):
    return (
        pltpu.make_async_remote_copy(qs, qr, sem.at[0, 0], sem.at[0, 1], device_id=to, device_id_type=MESH),
        pltpu.make_async_remote_copy(ts, tr, sem.at[1, 0], sem.at[1, 1], device_id=to, device_id_type=MESH),
    )


class Plane:
    def __init__(self, share, chunks, steps, plane_of, grad, sib, keep, base, scratch):
        self.share, self.chunks, self.steps, self.plane_of = share, chunks, steps, plane_of
        self.grad, self.sib, self.keep, self.base = grad, sib, keep, base
        (self.gbuf, self.rbuf, self.q1s, self.q1r, self.q2s, self.q2r, self.t1s, self.t1r, self.t2s, self.t2r,
         self.sib_sem, self.load_sem, self.s1_sem, self.s2_sem) = scratch
        self.z, self.x, self.y, self.c = place()
        self.to = partners(self.z, self.x, self.y, self.c)
        self.rows = keep.shape[1] // chunks
        self.half = self.rows // 2

    def tiles_of(self, s, xx, yy, core):
        k = slot_of(self.plane_of(s // self.chunks), xx, yy, core)
        return pl.ds(first_tile(self.share, k) + s % self.chunks * (self.rows // 8), self.rows // 8)

    def kept(self, s, part, b):
        return self.base + s // self.chunks, pl.ds(pl.multiple_of(s % self.chunks * self.rows + part * self.half + b * BLOCK, BLOCK), BLOCK)

    def sibling(self, s, q, core):
        return pltpu.make_async_remote_copy(
            self.grad.at[self.tiles_of(s, q // 2, q % 2, core)],
            self.sib.at[s, q],
            self.sib_sem.at[0, s, q],
            self.sib_sem.at[1, s, q],
            device_id=self.to["c"],
            device_id_type=MESH,
        )

    def begin(self):
        def one(s, _):
            for q in range(4):
                self.sibling(s, q, 1 - self.c).start()
            return 0

        lax.fori_loop(0, self.steps, one, 0)
        self.load(0)

    def loads(self, s, q):
        slot = s % 2
        return (
            pltpu.make_async_copy(self.grad.at[self.tiles_of(s, q // 2, q % 2, self.c)], self.gbuf.at[slot, q], self.load_sem.at[0, slot, q]),
            pltpu.make_async_copy(self.sib.at[s, q], self.rbuf.at[slot, q], self.load_sem.at[1, slot, q]),
        )

    def load(self, s):
        for q in range(4):
            self.sibling(s, q, 1 - self.c).wait_recv()
            for one in self.loads(s, q):
                one.start()

    def each(self, body):
        def one(b, _):
            body(b)
            return 0

        lax.fori_loop(0, self.half // BLOCK, one, 0, unroll=self.half // BLOCK)

    def own(self, slot, q, part, b):
        at = pl.ds(part * (self.half // 8) + b * (BLOCK // 8), BLOCK // 8)
        return (self.gbuf[slot, q, at] + self.rbuf[slot, q, at]).reshape(BLOCK, LANES)

    def first_message(self, s, part, other):
        i = part * 2 + other
        return message(self.q1s.at[s, i], self.t1s.at[s, i], self.q1r.at[s, i], self.t1r.at[s, i], self.s1_sem.at[s, i], self.to[("x", "y")[part]])

    def second_message(self, s, part):
        return message(
            self.q2s.at[s, part], self.t2s.at[s, part], self.q2r.at[s, part], self.t2r.at[s, part], self.s2_sem.at[s, part], self.to[("y", "x")[part]]
        )

    def quarter(self, part, other, mine):
        if part == 0:
            return (self.x if mine else 1 - self.x) * 2 + other
        return other * 2 + (self.y if mine else 1 - self.y)

    def stage_one(self, s):
        slot = s % 2
        for q in range(4):
            for one in self.loads(s, q):
                one.wait()
        for part in (0, 1):
            for other in (0, 1):
                q = self.quarter(part, other, False)
                i = part * 2 + other
                self.each(lambda b: pack(self.own(slot, q, part, b), self.q1s.at[s, i], self.t1s.at[s, i], b))
                for one in self.first_message(s, part, other):
                    one.start()

    def stage_two(self, s):
        slot = s % 2
        for part in (0, 1):
            for other in (0, 1):
                for one in self.first_message(s, part, other):
                    one.wait_recv()
            here = (self.y, self.x)[part]
            away = self.quarter(part, 1 - here, True)
            i = part * 2 + 1 - here
            self.each(
                lambda b: pack(
                    self.own(slot, away, part, b) + unpack(self.q1r.at[s, i], self.t1r.at[s, i], b), self.q2s.at[s, part], self.t2s.at[s, part], b
                )
            )
            for one in self.second_message(s, part):
                one.start()
        for part in (0, 1):
            here = (self.y, self.x)[part]
            k = part * 2 + here

            def store(b, part=part, k=k):
                group, at = self.kept(s, part, b)
                self.keep[group, at, :] = self.own(slot, self.x * 2 + self.y, part, b) + unpack(self.q1r.at[s, k], self.t1r.at[s, k], b)

            self.each(store)

    def stage_three(self, s):
        for part in (0, 1):
            for one in self.second_message(s, part):
                one.wait_recv()

            def body(b, part=part):
                group, at = self.kept(s, part, b)
                self.keep[group, at, :] += unpack(self.q2r.at[s, part], self.t2r.at[s, part], b)

            self.each(body)

    def finish(self):
        def one(s, _):
            for q in range(4):
                self.sibling(s, q, 1 - self.c).wait_send()
            for part in (0, 1):
                for other in (0, 1):
                    for two in self.first_message(s, part, other):
                        two.wait_send()
                for two in self.second_message(s, part):
                    two.wait_send()
            return 0

        lax.fori_loop(0, self.steps, one, 0)


def message_scratch(part, *leads):
    half = part // 2
    marks = (half // BLOCK + 7) // 8 * 8
    return [pltpu.VMEM(lead + (half, LANES), jnp.int16) for lead in leads] + [pltpu.VMEM(lead + (marks, LANES), jnp.float32) for lead in leads]


def plane_scratch(steps, part):
    dma = pltpu.SemaphoreType.DMA
    return [
        pltpu.VMEM((2, 4, part // 8, 8, LANES), jnp.float32),
        pltpu.VMEM((2, 4, part // 8, 8, LANES), jnp.float32),
        *message_scratch(part, (steps, 4), (steps, 4), (steps, 2), (steps, 2)),
        dma((2, steps, 4)), dma((2, 2, 4)), dma((steps, 4, 2, 2)), dma((steps, 2, 2, 2)),
    ]


def reduce_kernel(n_z, n_pair, chunks, share, grad_ref, late_ref, loss_in, params, master, moment1, moment2, first_ref, second_ref, master_ref, total_ref, sib_ref,
                  wide, mine, shared, send_sem, recv_sem, keep, late_sem, zs, zr, tzs, tzr, z_sem, *scratch):
    z, x, y, c = place()
    to = partners(z, x, y, c)
    n = n_z * 2 * n_pair
    me = slot_of(z, x, y, c)
    cut = late_cut(share)
    steps, late = cut * chunks, (n_z - cut) * chunks
    home = jnp.where(z < cut, cut - 1, z)

    def order(j):
        low = z < cut // 2
        far = jnp.where(low, cut - 1 - j, j)
        moved = jnp.where(low, jnp.where(far > z, far, far - 1), jnp.where(far < z, far, far + 1))
        return jnp.where(z >= cut, j, jnp.where(j == cut - 1, z, moved))

    plane = Plane(share, chunks, steps, order, grad_ref, sib_ref, keep, 0, scratch)

    def z_message(spot, part, name):
        d = 0 if name == "up" else 1
        return message(zs.at[spot, part], tzs.at[spot, part], zr.at[d, spot, part], tzr.at[d, spot, part], z_sem.at[d, spot, part], to[name])

    def stage_four(group, chunk, zz):
        spot = zz * chunks + chunk
        for part in (0, 1):

            def lines(b, part=part):
                return pl.ds(pl.multiple_of(chunk * plane.rows + part * plane.half + b * BLOCK, BLOCK), BLOCK)

            for d, name, has, onward in ((0, "up", z > 0, zz > z), (1, "down", z < n_z - 1, zz < z)):
                back = zz >= z if d == 0 else zz <= z

                @pl.when(both(has, back))
                def _():
                    for one in z_message(spot, part, name):
                        one.wait_recv()

                    def add(b):
                        keep[group, lines(b), :] += unpack(zr.at[d, spot, part], tzr.at[d, spot, part], b)

                    plane.each(add)

                @pl.when(onward)
                def _():
                    plane.each(lambda b: pack(keep[group, lines(b), :], zs.at[spot, part], tzs.at[spot, part], b))
                    for one in z_message(spot, part, name):
                        one.start()

    def spread_lines(line, tile, cols):
        for col in range(cols):
            wide[pl.ds(line + col, 8, stride=cols), :] = keep[home, pl.ds(pl.multiple_of((tile + col) * 8, 8), 8), :]

    count_lines = master.shape[0]
    tall = 128

    def by_lines(body):
        def one(i, _):
            body(pl.multiple_of(i * tall, tall), tall)
            return 0

        lax.fori_loop(0, count_lines // tall, one, 0)
        if count_lines % tall:
            body(count_lines // tall * tall, count_lines % tall)

    barrier = pltpu.get_barrier_semaphore()

    def peer(d):
        k = lax.rem(me + d, n)
        return {"dp": k // n_pair, "pair": lax.rem(k, n_pair)}

    def hello(d, _):
        pl.semaphore_signal(barrier, inc=1, device_id=peer(d), device_id_type=MESH)
        return 0

    lax.fori_loop(1, n, hello, 0)
    kept = pltpu.make_async_copy(late_ref, keep.at[pl.ds(cut, n_z - cut)], late_sem)
    kept.start()
    pl.semaphore_wait(barrier, n - 1)
    plane.begin()
    kept.wait()
    lag = 0

    def turn(t, _):
        pl.when(t < steps)(lambda: plane.stage_one(t))
        pl.when(both(t >= 1, t <= steps))(lambda: plane.stage_two(t - 1))
        pl.when(t + 1 < steps)(lambda: plane.load(t + 1))
        pl.when(both(t >= 2, t <= steps + 1))(lambda: plane.stage_three(t - 2))
        early, main = t - z, t - 3 - lag
        pl.when(both(early >= 0, early < late))(lambda: stage_four(cut + early // chunks, lax.rem(early, chunks), cut + early // chunks))
        pl.when(both(main >= 0, main < steps))(lambda: stage_four(main // chunks, lax.rem(main, chunks), order(main // chunks)))
        return 0

    lax.fori_loop(0, max(steps + 3, late + n_z), turn, 0)
    tiled(share, me, spread_lines)
    lo, _ = line_span(share, me)
    mine[...] = jnp.zeros_like(mine)

    def squares(start, size):
        value = wide[pl.ds(MARGIN + start, size), :]
        if share % LANES:
            line = lax.broadcasted_iota(jnp.int32, (size, LANES), 0) + lo + start
            spot = line * LANES + lax.broadcasted_iota(jnp.int32, (size, LANES), 1)
            inside = jnp.logical_and(spot >= share * me, spot < share * (me + 1))
            value = jnp.where(inside, value, 0.0)
        mine[0:1, :] += jnp.sum(value * value, axis=0, keepdims=True)

    by_lines(squares)
    lane = lax.broadcasted_iota(jnp.int32, (1, LANES), 1)
    mine[1:2, :] = jnp.where(lane == 0, loss_in[0:1, 0:1], 0.0)
    shared[me] = mine[...]

    def send(d):
        return pltpu.make_async_remote_copy(mine, shared.at[me], send_sem.at[d], recv_sem.at[d], device_id=peer(d), device_id_type=MESH)

    def go(d, _):
        send(d).start()
        return 0

    def stop(d, _):
        send(d).wait()
        return 0

    lax.fori_loop(1, n, go, 0)
    plane.finish()

    def finish(spot, _):
        zz = spot // chunks
        for part in (0, 1):
            for name, sent in (("up", zz > z), ("down", zz < z)):

                @pl.when(sent)
                def _():
                    for one in z_message(spot, part, name):
                        one.wait_send()

        return 0

    lax.fori_loop(0, n_z * chunks, finish, 0)
    lax.fori_loop(1, n, stop, 0)

    def add(k, total):
        return total + shared[k]

    total = lax.fori_loop(0, n, add, jnp.zeros((8, LANES), jnp.float32))
    norm_ = jnp.sqrt(jnp.sum(total[0:1, :], axis=1, keepdims=True))
    loss_sum = jnp.sum(total[1:2, :], axis=1, keepdims=True)
    total_ref[...] = jnp.where(lax.broadcasted_iota(jnp.int32, (8, LANES), 0) == 0, norm_, loss_sum)
    factor = params[2] / (norm_ + NORM_EPS)

    def adam(start, size):
        at = pl.ds(start, size)
        clipped = wide[pl.ds(MARGIN + start, size), :] * factor
        one = BETA_ONE * moment1[at, :] + (1.0 - BETA_ONE) * clipped
        two = BETA_TWO * moment2[at, :] + (1.0 - BETA_TWO) * clipped * clipped
        line = lax.broadcasted_iota(jnp.int32, (size, 1), 0) + lo + start
        rate = jnp.where(line < ENC_PARAMS // LANES, params[0], params[1])
        step = one / params[3] / (jnp.sqrt(two / params[4]) + ADAM_EPS)
        first_ref[at, :] = one
        second_ref[at, :] = two
        master_ref[at, :] = master[at, :] - rate * (step + DECAY * master[at, :])

    by_lines(adam)


def reduce(flat, late, loss, params, lines, share, n_dp, n_pair):
    n_z, n = n_dp // 2, n_dp * n_pair
    chunks = reduce_chunks(share, n)
    rows = slab_tiles(share, n) * 8
    part = rows // chunks
    steps = late_cut(share) * chunks
    spots = n_z * chunks
    anyspec = pl.BlockSpec(memory_space=pl.ANY)
    vmem = pl.BlockSpec(memory_space=pltpu.VMEM)
    line = jax.ShapeDtypeStruct(lines[0].shape, jnp.float32)
    dma = pltpu.SemaphoreType.DMA
    return pl.pallas_call(
        functools.partial(reduce_kernel, n_z, n_pair, chunks, share),
        name="reduce_scatter",
        out_shape=[line, line, line, jax.ShapeDtypeStruct((8, LANES), jnp.float32), jax.ShapeDtypeStruct((steps, 4, part // 8, 8, LANES), jnp.float32)],
        in_specs=[anyspec, anyspec, vmem, pl.BlockSpec(memory_space=pltpu.SMEM)] + [vmem] * 3,
        out_specs=[vmem] * 4 + [anyspec],
        scratch_shapes=[
            pltpu.VMEM((wide_rows(lines[0].shape[0]), LANES), jnp.float32),
            pltpu.VMEM((8, LANES), jnp.float32),
            pltpu.VMEM((n, 8, LANES), jnp.float32),
            dma((n,)),
            dma((n,)),
            pltpu.VMEM((n_z, rows, LANES), jnp.float32),
            dma,
            *message_scratch(part, (spots, 2), (2, spots, 2)),
            dma((2, spots, 2, 2, 2)),
            *plane_scratch(steps, part),
        ],
        compiler_params=pltpu.CompilerParams(collective_id=1, has_side_effects=True, vmem_limit_bytes=60 * MB),
    )(flat, late, loss, params, *lines)[:4]


NEG_FILL = -1000000000.0
P_ROWS = 208
BF = jnp.bfloat16
F32 = jnp.float32


def dot_nn(left, right):
    return lax.dot_general(left, right, (((1,), (0,)), ((), ())), preferred_element_type=F32)


def dot_nt(left, right):
    return lax.dot_general(left, right, (((1,), (1,)), ((), ())), preferred_element_type=F32)


def loop(count, body, unroll=1):
    def step(i, _):
        body(i)
        return 0

    lax.fori_loop(0, count, step, 0, unroll=unroll)


def rows_at(i, size):
    return pl.ds(pl.multiple_of(i * size, size), size)


def norm(x):
    centered = x - jnp.mean(x, axis=-1, keepdims=True)
    scale = lax.rsqrt(jnp.mean(centered * centered, axis=-1, keepdims=True) + NORM_EPS)
    return centered * scale, scale


def norm_grad(grad, plain, scale, gain):
    inner = grad * gain
    back = scale * (inner - jnp.mean(inner, axis=-1, keepdims=True) - plain * jnp.mean(inner * plain, axis=-1, keepdims=True))
    return back, jnp.sum(grad * plain, axis=0, keepdims=True), jnp.sum(grad, axis=0, keepdims=True)


def gelu_pair(h):
    cumulative = 0.5 * (1.0 + lax.erf(h * 0.7071067811865476))
    density = jnp.exp(-0.5 * h * h) * 0.3989422804014327
    return h * cumulative, cumulative + h * density


def head_masks(size):
    lane = lax.broadcasted_iota(jnp.int32, (1, LANES), 1)
    shift = size.bit_length() - 1
    return [jnp.where((lane >> shift) == h, 1.0, 0.0).astype(BF) for h in range(LANES // size)]


def three(value):
    top = value.astype(BF)
    rest = value - top.astype(F32)
    mid = rest.astype(BF)
    return top, mid, (rest - mid.astype(F32)).astype(BF)


class Moves:
    def __init__(self, names, sources, targets, sems):
        self.targets = dict(zip(names, targets))
        self.copies = {name: pltpu.make_async_copy(a, b, sems.at[i]) for i, (name, a, b) in enumerate(zip(names, sources, targets))}
        self.open = []

    def start(self, *names):
        for name in names or self.copies:
            self.copies[name].start()
            self.open.append(name)

    def __call__(self, name):
        if name in self.open:
            self.copies[name].wait()
            self.open.remove(name)
        return self.targets[name]

    def close(self):
        for name in list(self.open):
            self(name)


def wide_attention(width, heads, rows, triple, bias, probs, mixed):
    size = width // heads
    per = LANES // size
    masks = head_masks(size)
    for g in range(width // LANES):
        q, k, v = (triple[:, t * width + g * LANES : t * width + (g + 1) * LANES] for t in range(3))
        v_side = v.T
        parts = []
        for h in range(per):
            s = dot_nt(k * masks[h], q) * size ** (-0.5) + bias[...]
            e = jnp.exp(s - jnp.max(s, axis=0, keepdims=True))
            p = e * (1.0 / jnp.sum(e, axis=0, keepdims=True))
            probs[g * per + h] = p
            parts.append(dot_nn(v_side[h * size : (h + 1) * size, :], p.astype(BF)))
        mixed[:, g * LANES : (g + 1) * LANES] = jnp.concatenate(parts, axis=0).T.astype(BF)


def wide_attention_back(width, heads, triple, probs, low_mixed, grad_triple):
    size = width // heads
    per = LANES // size
    masks = head_masks(size)
    for g in range(width // LANES):
        lanes = [slice(t * width + g * LANES, t * width + (g + 1) * LANES) for t in range(3)]
        q, k, v = (triple[:, lane] for lane in lanes)
        dm = low_mixed[:, g * LANES : (g + 1) * LANES]
        k_side = k.T
        parts, dk, dv = [], 0.0, 0.0
        for h in range(per):
            p = probs[g * per + h]
            dp = dot_nt(v * masks[h], dm)
            ds = (p * (dp - jnp.sum(p * dp, axis=0, keepdims=True))).astype(BF)
            dv = dv + dot_nn(p.astype(BF), dm * masks[h])
            dk = dk + dot_nn(ds, q * masks[h])
            parts.append(dot_nn(k_side[h * size : (h + 1) * size, :], ds))
        grad_triple[:, lanes[0]] = (jnp.concatenate(parts, axis=0).T * size ** (-0.5)).astype(BF)
        grad_triple[:, lanes[1]] = (dk * size ** (-0.5)).astype(BF)
        grad_triple[:, lanes[2]] = dv.astype(BF)


def block_forward(x, rows, images, heads, need, norms, key_bias, saved, done=lambda *names: None):
    entry, plain1, scale1, triple, probs, mixed, plain2, scale2, inner, act, slope = saved
    width = x.shape[1]
    size = width // heads
    per = LANES // size
    groups = width // LANES

    def first(i):
        at = rows_at(i, rows)
        plain, scale = norm(x[at, :])
        plain1[at, :] = plain
        scale1[at, :] = scale
        entry[at, :] = (plain * norms[0:1, :] + norms[1:2, :]).astype(BF)

    loop(images, first)

    done("entry", "plain1", "scale1")
    triple_w = need("triple_w")

    def project(j):
        at = rows_at(j, 256)
        triple[:, at] = dot_nn(entry[...], triple_w[:, at]).astype(BF)

    loop(3 * width // 256, project)
    done("triple")
    masks = head_masks(size)

    def attend(i):
        at = rows_at(i, rows)
        bias = key_bias(i)
        for g in range(groups):
            q = triple[at, g * LANES : (g + 1) * LANES]
            k = triple[at, width + g * LANES : width + (g + 1) * LANES]
            v = triple[at, 2 * width + g * LANES : 2 * width + (g + 1) * LANES]
            v_side = v.T
            parts = []
            for h in range(per):
                s = dot_nt(k * masks[h], q) * size ** (-0.5) + bias
                e = jnp.exp(s - jnp.max(s, axis=0, keepdims=True))
                p = e * (1.0 / jnp.sum(e, axis=0, keepdims=True))
                probs[i * groups + g, h * rows : (h + 1) * rows, :] = p
                parts.append(dot_nn(v_side[h * size : (h + 1) * size, :], p.astype(BF)))
            mixed[at, g * LANES : (g + 1) * LANES] = jnp.concatenate(parts, axis=0).T.astype(BF)

    if callable(key_bias):
        loop(images, attend)
    else:
        wide_attention(width, heads, rows, triple, key_bias, probs, mixed)
    done("probs", "mixed")
    proj_w = need("proj_w")

    def middle(j):
        at = rows_at(j, 256)
        x[:, at] += dot_nn(mixed[...], proj_w[:, at])

    loop(width // 256, middle)

    def second(i):
        at = rows_at(i, rows)
        plain, scale = norm(x[at, :])
        plain2[at, :] = plain
        scale2[at, :] = scale
        inner[at, :] = (plain * norms[2:3, :] + norms[3:4, :]).astype(BF)

    loop(images, second)
    done("plain2", "scale2", "inner")
    up_w = need("up_w")
    hidden = up_w.shape[1]

    def up(j):
        at = rows_at(j, 256)
        value, gradient = gelu_pair(dot_nn(inner[...], up_w[:, at]))
        act[:, at] = value.astype(BF)
        slope[:, at] = gradient

    loop(hidden // 256, up)
    done("act", "slope")
    down_w = need("down_w")

    def down(j):
        at = rows_at(j, 256)
        x[:, at] += dot_nn(act[...], down_w[:, at])

    loop(width // 256, down)


class Writer:
    def __init__(self, flat, stage, sem):
        self.flat, self.stage, self.sem = flat, stage, sem
        self.pending = {}

    def settle(self, s):
        if s in self.pending:
            self.pending.pop(s).wait()

    def outer(self, number, left, right, chunk=256):
        _, _, cols, tile, _ = ENTRIES[number]
        rows = left.shape[1]
        count = rows // chunk
        tall = chunk // 8
        before = dict(self.pending)

        def copy(i, s):
            return pltpu.make_async_copy(
                self.stage.at[s, pl.ds(0, tall * cols)], self.flat.at[pl.ds(tile + i * tall * cols, tall * cols)], self.sem.at[s]
            )

        def body(i):
            s = lax.rem(i, 2)
            for early in before:
                pl.when(i == early)(before[early].wait)

            @pl.when(i >= 2)
            def _():
                copy(i - 2, s).wait()

            side = left[:, rows_at(i, chunk)].T
            for c in range(0, cols, 2):
                value = dot_nn(side, right[:, c * LANES : (c + 2) * LANES])
                for d in range(2):
                    self.stage[s, pl.ds(c + d, tall, stride=cols)] = value[:, d * LANES : (d + 1) * LANES].reshape(tall, 8, LANES)
            copy(i, s).start()

        loop(count, body)
        self.pending = {(count - 2) % 2: copy(count - 2, (count - 2) % 2), (count - 1) % 2: copy(count - 1, (count - 1) % 2)}

    def small(self, number, norm_sums, count, extra=0):
        _, _, _, tile, groups = ENTRIES[number]
        per = SHAPES[number][1] // LANES
        self.settle(0)
        self.stage[0, 0 : groups + extra] = jnp.zeros((groups + extra, 8, LANES), F32)
        for r in range(count):
            for c in range(per):
                line = r * per + c
                self.stage[0, line // 8, line % 8 : line % 8 + 1, :] = norm_sums[r : r + 1, c * LANES : (c + 1) * LANES]
        copy = pltpu.make_async_copy(self.stage.at[0, pl.ds(0, groups + extra)], self.flat.at[pl.ds(tile, groups + extra)], self.sem.at[0])
        copy.start()
        copy.wait()
        self.settle(1)


def block_backward(grad, rows, images, heads, need, norms, norm_sums, extra, writer, numbers, tick=lambda: None):
    low, grad_hidden, side, low_mixed, grad_triple = extra
    width = grad.shape[1]
    size = width // heads
    per = LANES // size
    groups = width // LANES
    low[...] = grad[...].astype(BF)
    down_w, slope = need("down_w"), need("slope")
    hidden = down_w.shape[0]

    def back_up(j):
        at = rows_at(j, 256)
        grad_hidden[:, at] = (dot_nt(low[...], down_w[at, :]) * slope[:, at]).astype(BF)

    loop(hidden // 256, back_up)
    tick()
    writer.outer(numbers[3], need("act"), low)
    tick()
    writer.outer(numbers[2], need("inner"), grad_hidden)
    tick()
    up_w = need("up_w")

    def back_inner(j):
        at = rows_at(j, 256)
        side[:, at] = dot_nt(grad_hidden[...], up_w[at, :])

    loop(width // 256, back_inner)
    tick()
    plain2, scale2 = need("plain2"), need("scale2")

    def second(i):
        at = rows_at(i, rows)
        back, gain, shift = norm_grad(side[at, :], plain2[at, :], scale2[at, :], norms[2:3, :])
        norm_sums[2:3, :] += gain
        norm_sums[3:4, :] += shift
        total = grad[at, :] + back
        grad[at, :] = total
        low[at, :] = total.astype(BF)

    loop(images, second)
    writer.outer(numbers[1], need("mixed"), low)
    proj_w = need("proj_w")

    def back_mixed(j):
        at = rows_at(j, 256)
        low_mixed[:, at] = dot_nt(low[...], proj_w[at, :]).astype(BF)

    loop(width // 256, back_mixed)
    tick()
    triple, probs = need("triple"), need("probs")
    masks = head_masks(size)

    def attend(i):
        at = rows_at(i, rows)
        for g in range(groups):
            lanes = [slice(t * width + g * LANES, t * width + (g + 1) * LANES) for t in range(3)]
            q, k, v = (triple[at, lane] for lane in lanes)
            dm = low_mixed[at, g * LANES : (g + 1) * LANES]
            k_side = k.T
            parts, dk, dv = [], 0.0, 0.0
            for h in range(per):
                p = probs[i * groups + g, h * rows : (h + 1) * rows, :]
                dp = dot_nt(v * masks[h], dm)
                ds = (p * (dp - jnp.sum(p * dp, axis=0, keepdims=True))).astype(BF)
                dv = dv + dot_nn(p.astype(BF), dm * masks[h])
                dk = dk + dot_nn(ds, q * masks[h])
                parts.append(dot_nn(k_side[h * size : (h + 1) * size, :], ds))
            dq = jnp.concatenate(parts, axis=0).T
            grad_triple[at, lanes[0]] = (dq * size ** (-0.5)).astype(BF)
            grad_triple[at, lanes[1]] = (dk * size ** (-0.5)).astype(BF)
            grad_triple[at, lanes[2]] = dv.astype(BF)

    if probs.shape[1] == probs.shape[2] and probs.shape[0] == heads:
        wide_attention_back(width, heads, triple, probs, low_mixed, grad_triple)
    else:
        loop(images, attend)
    tick()
    writer.outer(numbers[0], need("entry"), grad_triple)
    tick()
    triple_w = need("triple_w")

    def back_entry(j):
        at = rows_at(j, 256)
        side[:, at] = dot_nt(grad_triple[...], triple_w[at, :])

    loop(width // 256, back_entry)
    tick()
    plain1, scale1 = need("plain1"), need("scale1")

    def first(i):
        at = rows_at(i, rows)
        back, gain, shift = norm_grad(side[at, :], plain1[at, :], scale1[at, :], norms[0:1, :])
        norm_sums[0:1, :] += gain
        norm_sums[1:2, :] += shift
        grad[at, :] += back

    loop(images, first)


TICKS = 11
SAVED = ("seen", "entry", "plain1", "scale1", "triple", "probs", "mixed", "plain2", "scale2", "inner", "act", "slope", "plain3", "scale3", "encoded")
ENC_NAMES = ("embed_w", "triple_w", "proj_w", "up_w", "down_w", "dec_embed_w")
DEC_NAMES = ("triple_w", "proj_w", "up_w", "down_w", "head_w")


def saved_shapes(rows):
    s = jax.ShapeDtypeStruct
    return [
        s((rows, D), BF), s((rows, D), BF), s((rows, D), F32), s((rows, 1), F32), s((rows, 3 * D), BF),
        s((HEADS, rows, rows), F32), s((rows, D), BF), s((rows, D), F32), s((rows, 1), F32), s((rows, D), BF),
        s((rows, F), BF), s((rows, F), F32), s((rows, D), F32), s((rows, 1), F32), s((rows, D), BF),
    ]


def like(shape):
    return pltpu.VMEM(shape.shape, shape.dtype)


def pad_patches(patches, padded, images):
    padded[...] = jnp.zeros_like(padded)
    for i in range(images):
        padded[i * P_ROWS : i * P_ROWS + PATCHES, :] = patches[i]


def encoder_kernel(images, counts_ref, cols_ref, norms_ref, *refs):
    pos_hbm, patches_hbm, *weights_hbm = refs[:8]
    outs = refs[8:23]
    entering = refs[23]
    pos, patches, *weights = refs[24:32]
    saved = dict(zip(SAVED, refs[32:47]))
    x, place_, pos_split, padded, bias, in_sem, out_sem = refs[47:]
    need = Moves(("pos", "patches") + ENC_NAMES, [pos_hbm, patches_hbm] + weights_hbm, [pos, patches] + weights, in_sem)
    need.start()
    put = Moves(SAVED, [saved[name] for name in SAVED], outs, out_sem)
    rows = images * KEEP
    key = lax.broadcasted_iota(jnp.int32, (KEEP, rows), 0)
    query = lax.broadcasted_iota(jnp.int32, (KEEP, rows), 1)
    for i in range(images):
        inside = jnp.logical_and(jnp.logical_and(query >= i * KEEP, query < (i + 1) * KEEP), key < counts_ref[i])
        bias[i * KEEP : (i + 1) * KEEP, :] = jnp.where(inside, 0.0, NEG_FILL)
    need("pos")
    for t, part in enumerate(three(pos[...])):
        pos_split[t] = part
    pad_patches(need("patches"), padded, images)
    spots = lax.broadcasted_iota(jnp.int32, (KEEP, P_ROWS), 1)
    seen = saved["seen"]

    def select(i):
        at = rows_at(i, KEEP)
        pick = jnp.where(spots == cols_ref[i], 1.0, 0.0).astype(BF)
        seen[at, :] = dot_nn(pick, padded[rows_at(i, P_ROWS), :]).astype(BF)
        place_[at, :] = dot_nn(pick, pos_split[0]) + dot_nn(pick, pos_split[1]) + dot_nn(pick, pos_split[2])

    loop(images, select)
    put.start("seen")
    embed_w = need("embed_w")

    def embed(j):
        at = rows_at(j, 256)
        x[:, at] = dot_nn(seen[...], embed_w[:, at]) + place_[:, at]

    loop(D // 256, embed)
    block_forward(x, KEEP, images, HEADS, need, norms_ref, bias, [saved[name] for name in SAVED[1:12]], put.start)
    plain3, scale3, encoded = (saved[name] for name in SAVED[12:])

    def last(i):
        at = rows_at(i, KEEP)
        plain, scale = norm(x[at, :])
        plain3[at, :] = plain
        scale3[at, :] = scale
        encoded[at, :] = (plain * norms_ref[4:5, :] + norms_ref[5:6, :]).astype(BF)

    loop(images, last)
    put.start("plain3", "scale3", "encoded")
    entering[...] = dot_nn(encoded[...], need("dec_embed_w")[...])
    put.close()


def encoder(counts, patches, cols, pos, weights, norms):
    images = counts.shape[0]
    rows = images * KEEP
    vmem = pl.BlockSpec(memory_space=pltpu.VMEM)
    anyspec = pl.BlockSpec(memory_space=pl.ANY)
    shapes = saved_shapes(rows)
    return pl.pallas_call(
        functools.partial(encoder_kernel, images),
        name="encoder",
        out_shape=shapes + [jax.ShapeDtypeStruct((rows, DD), F32)],
        in_specs=[pl.BlockSpec(memory_space=pltpu.SMEM), vmem, vmem] + [anyspec] * 8,
        out_specs=[anyspec] * 15 + [vmem],
        scratch_shapes=[like(one) for one in [pos, patches] + weights + shapes]
        + [
            pltpu.VMEM((rows, D), F32), pltpu.VMEM((rows, D), F32), pltpu.VMEM((3, P_ROWS, D), BF), pltpu.VMEM((images * P_ROWS, PIX), BF),
            pltpu.VMEM((rows, rows), F32), pltpu.SemaphoreType.DMA((8,)), pltpu.SemaphoreType.DMA((15,)),
        ],
        compiler_params=pltpu.CompilerParams(vmem_limit_bytes=60 * MB),
    )(counts, cols, norms, pos, patches, *weights)


def decoder_kernel(images, counts_ref, masked_ref, cols_ref, rows_ref, entering_ref, norms_ref, *refs):
    pos_hbm, patches_hbm, *weights_hbm = refs[:7]
    flat, grad_entering, loss_ref = refs[7:10]
    pos, patches, *weights = refs[10:17]
    (x, hide, entry, plain1, scale1, triple, probs, mixed, plain2, scale2, inner, act, slope, plain3, scale3, final, grad_pred,
     low, grad_hidden, side, low_mixed, grad_triple, norm_sums, padded, stage, sem, in_sem) = refs[17:]
    need = Moves(("pos", "patches") + DEC_NAMES, [pos_hbm, patches_hbm] + weights_hbm, [pos, patches] + weights, in_sem)
    need.start()
    saved = (entry, plain1, scale1, triple, probs, mixed, plain2, scale2, inner, act, slope)
    need.targets.update(zip(SAVED[1:12], saved))
    lane = lax.broadcasted_iota(jnp.int32, (P_ROWS, KEEP), 1)
    spot = lax.broadcasted_iota(jnp.int32, (P_ROWS, KEEP), 0)
    line = lax.broadcasted_iota(jnp.int32, (P_ROWS, 1), 0)
    need("pos")

    def start(i):
        at = rows_at(i, P_ROWS)
        hit = jnp.where(jnp.logical_and(spot == rows_ref[pl.ds(i, 1), 0:KEEP], lane < counts_ref[i]), 1.0, 0.0)
        shown = jnp.max(hit, axis=1, keepdims=True)
        pick = hit.astype(BF)
        top, mid, end = three(entering_ref[rows_at(i, KEEP), :])
        picked = dot_nn(pick, top) + dot_nn(pick, mid) + dot_nn(pick, end)
        x[at, :] = jnp.where(shown > 0.0, picked, norms_ref[6:7, :]) + pos[...]
        hide[at, :] = jnp.where(jnp.logical_and(line < PATCHES, shown == 0.0), 1.0, 0.0)

    loop(images, start)
    bias = jnp.where(line < PATCHES, 0.0, NEG_FILL)
    block_forward(x, P_ROWS, images, DHEADS, need, norms_ref, lambda i: bias, saved)

    def last(i):
        at = rows_at(i, P_ROWS)
        plain, scale = norm(x[at, :])
        plain3[at, :] = plain
        scale3[at, :] = scale
        final[at, :] = (plain * norms_ref[4:5, :] + norms_ref[5:6, :]).astype(BF)

    loop(images, last)
    loss_ref[...] = jnp.zeros_like(loss_ref)
    masked = masked_ref[0:1, 0:1]
    head_w = need("head_w")
    pad_patches(need("patches"), padded, images)

    def score(i):
        at = rows_at(i, P_ROWS)
        target, _ = norm(padded[at, :].astype(F32))
        diff = dot_nn(final[at, :], head_w[...]) - target
        hidden = hide[at, :]
        loss_ref[...] += jnp.sum(jnp.mean(diff * diff, axis=-1, keepdims=True) * hidden, axis=0, keepdims=True)
        grad_pred[at, :] = (diff * (hidden * (2.0 / PIX)) / masked).astype(BF)

    loop(images, score)
    writer = Writer(flat, stage, sem)
    writer.outer(11, final, grad_pred)
    norm_sums[...] = jnp.zeros_like(norm_sums)

    def back_final(i):
        at = rows_at(i, P_ROWS)
        back, gain, shift = norm_grad(dot_nt(grad_pred[at, :], head_w[...]), plain3[at, :], scale3[at, :], norms_ref[4:5, :])
        norm_sums[4:5, :] += gain
        norm_sums[5:6, :] += shift
        x[at, :] = back

    loop(images, back_final)
    block_backward(x, P_ROWS, images, DHEADS, need, norms_ref, norm_sums, (low, grad_hidden, side, low_mixed, grad_triple), writer, (7, 8, 9, 10))
    spots = lax.broadcasted_iota(jnp.int32, (KEEP, P_ROWS), 1)
    slot = lax.broadcasted_iota(jnp.int32, (KEEP, P_ROWS), 0)

    def finish(i):
        at = rows_at(i, P_ROWS)
        grad = x[at, :]
        norm_sums[6:7, :] += jnp.sum(grad * hide[at, :], axis=0, keepdims=True)
        pick = jnp.where(jnp.logical_and(spots == cols_ref[i], slot < counts_ref[i]), 1.0, 0.0).astype(BF)
        grad_entering[rows_at(i, KEEP), :] = dot_nn(pick, grad.astype(BF)).astype(BF)

    loop(images, finish)
    writer.small(12, norm_sums, 7, flat.shape[0] - TILES)


def decoder(total, counts, masked, patches, cols, order, pos, entering, weights, norms):
    images = counts.shape[0]
    rows = images * P_ROWS
    vmem = pl.BlockSpec(memory_space=pltpu.VMEM)
    anyspec = pl.BlockSpec(memory_space=pl.ANY)

    def v(shape, kind=F32):
        return pltpu.VMEM(shape, kind)

    return pl.pallas_call(
        functools.partial(decoder_kernel, images),
        name="decoder",
        out_shape=[
            jax.ShapeDtypeStruct((total, 8, LANES), F32),
            jax.ShapeDtypeStruct((images * KEEP, DD), BF),
            jax.ShapeDtypeStruct((1, 1), F32),
        ],
        in_specs=[pl.BlockSpec(memory_space=pltpu.SMEM)] + [vmem] * 5 + [anyspec] * 7,
        out_specs=[anyspec, vmem, vmem],
        scratch_shapes=[like(one) for one in [pos, patches] + weights]
        + [
            v((rows, DD)), v((rows, 1)), v((rows, DD), BF), v((rows, DD)), v((rows, 1)), v((rows, 3 * DD), BF),
            v((images * DD // LANES, 4 * P_ROWS, P_ROWS)), v((rows, DD), BF), v((rows, DD)), v((rows, 1)), v((rows, DD), BF),
            v((rows, FD), BF), v((rows, FD)), v((rows, DD)), v((rows, 1)), v((rows, DD), BF), v((rows, PIX), BF),
            v((rows, DD), BF), v((rows, FD), BF), v((rows, DD)), v((rows, DD), BF), v((rows, 3 * DD), BF),
            v((8, DD)), v((rows, PIX), BF), v((2, 32 * 16, 8, LANES)), pltpu.SemaphoreType.DMA((2,)), pltpu.SemaphoreType.DMA((7,)),
        ],
        compiler_params=pltpu.CompilerParams(vmem_limit_bytes=63 * MB),
    )(counts, masked, cols, order, entering, norms, pos, patches, *weights)


def encoder_back_kernel(images, share, chunks, flat_in, grad_entering, norms_ref, *refs):
    names = SAVED + ENC_NAMES[1:]
    sources = refs[:20]
    flat, late_ref, sib_ref = refs[20:23]
    targets = refs[23:43]
    x, low, grad_hidden, side, low_mixed, grad_triple, norm_sums, stage, sem, in_sem = refs[43:53]
    cut = late_cut(share)
    steps = late_ref.shape[0] * chunks
    plane = Plane(share, chunks, steps, lambda group: cut + group, flat, sib_ref, late_ref, 0, refs[53:])
    barrier = pltpu.get_barrier_semaphore()
    for name in ("x", "y", "c"):
        pl.semaphore_signal(barrier, inc=1, device_id=plane.to[name], device_id_type=MESH)
    need = Moves(names, sources, targets, in_sem)
    need.start(
        "encoded", "dec_embed_w", "plain3", "scale3", "down_w", "slope", "act", "inner", "up_w", "plain2", "scale2",
        "mixed", "proj_w", "triple", "probs", "entry", "triple_w", "plain1", "scale1", "seen",
    )
    pl.semaphore_wait(barrier, 3)
    plane.begin()
    turns = []
    for t in range(steps + 2):
        if t < steps:
            turns.append((t, plane.stage_one, t))
        if 1 <= t <= steps:
            turns.append((t, plane.stage_two, t - 1))
        if t + 1 < steps:
            turns.append((t, plane.load, t + 1))
        if t >= 2:
            turns.append((t, plane.stage_three, t - 2))
    ticks = [0]

    def tick():
        ticks[0] += 1
        while turns and turns[0][0] * TICKS < (ticks[0] - 1) * (steps + 2):
            _, stage_, s = turns.pop(0)
            stage_(s)

    writer = Writer(flat, stage, sem)
    writer.outer(6, need("encoded"), grad_entering)
    norm_sums[...] = jnp.zeros_like(norm_sums)
    side[...] = dot_nt(grad_entering[...], need("dec_embed_w")[...])
    plain3, scale3 = need("plain3"), need("scale3")

    def last(i):
        at = rows_at(i, KEEP)
        back, gain, shift = norm_grad(side[at, :], plain3[at, :], scale3[at, :], norms_ref[4:5, :])
        norm_sums[4:5, :] += gain
        norm_sums[5:6, :] += shift
        x[at, :] = back

    loop(images, last)
    tick()
    block_backward(x, KEEP, images, HEADS, need, norms_ref, norm_sums, (low, grad_hidden, side, low_mixed, grad_triple), writer, (1, 2, 3, 4), tick)
    low[...] = x[...].astype(BF)
    tick()
    writer.outer(0, need("seen"), low)
    tick()
    writer.small(5, norm_sums, 6)
    for _, stage_, s in turns:
        stage_(s)
    plane.finish()


def encoder_back(flat, grad_entering, saved, weights, norms, share, n_dp, n_pair):
    chunks = reduce_chunks(share, n_dp * n_pair)
    slab = slab_tiles(share, n_dp * n_pair) * 8
    groups = n_dp // 2 - late_cut(share)
    part = slab // chunks
    rows = grad_entering.shape[0]
    images = rows // KEEP
    vmem = pl.BlockSpec(memory_space=pltpu.VMEM)
    anyspec = pl.BlockSpec(memory_space=pl.ANY)

    def v(shape, kind=F32):
        return pltpu.VMEM(shape, kind)

    return pl.pallas_call(
        functools.partial(encoder_back_kernel, images, share, chunks),
        name="encoder_back",
        out_shape=[
            jax.ShapeDtypeStruct(flat.shape, flat.dtype),
            jax.ShapeDtypeStruct((groups, slab, LANES), F32),
            jax.ShapeDtypeStruct((groups * chunks, 4, part // 8, 8, LANES), F32),
        ],
        in_specs=[anyspec, vmem, vmem] + [anyspec] * 20,
        out_specs=[anyspec, vmem, anyspec],
        scratch_shapes=[like(one) for one in saved + weights]
        + [
            v((rows, D)), v((rows, D), BF), v((rows, F), BF), v((rows, D)), v((rows, D), BF), v((rows, 3 * D), BF),
            v((8, D)), v((2, 32 * 24, 8, LANES)), pltpu.SemaphoreType.DMA((2,)), pltpu.SemaphoreType.DMA((20,)),
        ]
        + plane_scratch(groups * chunks, part),
        input_output_aliases={0: 0},
        compiler_params=pltpu.CompilerParams(collective_id=2, has_side_effects=True, vmem_limit_bytes=63 * MB),
    )(flat, grad_entering, norms, *saved, *weights)[:2]


def positions(width):
    index = np.arange(PATCHES)
    quarter = width // 4
    freq = 10000.0 ** (-np.arange(quarter).astype(np.float32) / np.float32(quarter))
    row = (index // GRID).astype(np.float32)[:, None] * freq[None, :].astype(np.float32)
    column = (index % GRID).astype(np.float32)[:, None] * freq[None, :].astype(np.float32)
    table = np.concatenate([np.sin(row), np.cos(row), np.sin(column), np.cos(column)], axis=1).astype(np.float32)
    return jnp.asarray(np.pad(table, ((0, P_ROWS - PATCHES), (0, 0))))


def own_lines(flat, share, index):
    if share % LANES == 0:
        return flat.reshape(-1, LANES)
    rows = (share + LANES - 1) // LANES + 1
    return lax.dynamic_update_slice(jnp.zeros((rows * LANES,), flat.dtype), flat, (share * index % LANES,)).reshape(rows, LANES)


def own_flat(lines, share, index):
    if share % LANES == 0:
        return lines.reshape(-1)
    return lax.dynamic_slice(lines.reshape(-1), (share * index % LANES,), (share,))


def body(n_dp, n_pair, patches, patch_order, counts, master, moment1, moment2, block_rates, clip_limit, step_count):
    n = n_dp * n_pair
    share = master.shape[0]
    images = counts.shape[0]
    index = lax.axis_index("dp") * n_pair + lax.axis_index("pair")
    extra = jnp.zeros((8, LANES), F32).at[0, :images].set((PATCHES - counts).astype(F32))
    lines = [own_lines(one, share, index) for one in (master, moment1, moment2)]
    steps_done = step_count[0].astype(F32)
    params = jnp.stack([block_rates[0], block_rates[1], clip_limit[0], 1.0 - BETA_ONE**steps_done, 1.0 - BETA_TWO**steps_done])
    *held, enc_norms, dec_norms, masked = gather(lines[0], extra, share, n_dp, n_pair)
    parts = {i: matrix(one, i) for i, one in zip(BIG, held)}
    slots_at = patch_order[:, :KEEP]
    cols = slots_at[:, :, None]
    enc_weights = [parts[i] for i in (1, 2, 3, 4, 6)]
    *saved, entering = encoder(counts, patches, cols, positions(D), [parts[0]] + enc_weights, enc_norms)
    total = max(a for a, _ in ranges(share, n)) + slab_tiles(share, n)
    dec_weights = [parts[i] for i in (7, 8, 9, 10, 11)]
    flat, grad_entering, loss_local = decoder(total, counts, masked, patches, cols, slots_at, positions(DD), entering, dec_weights, dec_norms)
    flat, late = encoder_back(flat, grad_entering, saved, enc_weights, enc_norms, share, n_dp, n_pair)
    first, second, master_new, totals = reduce(flat, late, loss_local, params, lines, share, n_dp, n_pair)
    loss = totals[1, 0:1] / masked[0]
    first, second, master_new = (own_flat(one, share, index) for one in (first, second, master_new))
    return (loss, totals[0, 0:1], first, second, master_new)


def solution(mesh):
    whole = P(("dp", "pair"))
    in_specs = (P(("dp", "pair"), None, None), P(("dp", "pair"), None), whole, whole, whole, whole, P(), P(), P())
    out_specs = (P(), P(), whole, whole, whole)
    step = functools.partial(body, mesh.shape["dp"], mesh.shape["pair"])
    return jax.shard_map(step, mesh=mesh, in_specs=in_specs, out_specs=out_specs, check_vma=False)
```

```python
import functools

import jax
import jax.numpy as jnp
import numpy as np
from jax import lax
from jax.experimental import pallas as pl
from jax.experimental.pallas import tpu as pltpu
from jax.sharding import PartitionSpec as P

MESH = pl.DeviceIdType.MESH
LANES = 128
TILE = 16 * LANES


def place():
    dp, pair = lax.axis_index("dp"), lax.axis_index("pair")
    return dp // 2, dp % 2, pair // 2, pair % 2


def slot_of(z, x, y, c):
    return (z * 2 + x) * 4 + y * 2 + c


def partners(z, x, y, c):
    return {
        "x": {"dp": z * 2 + (1 - x)},
        "y": {"pair": (1 - y) * 2 + c},
        "c": {"pair": y * 2 + (1 - c)},
        "up": {"dp": (z + 1) * 2 + x},
        "down": {"dp": (z - 1) * 2 + x},
    }


def greet(n_z, z, to):
    barrier = pltpu.get_barrier_semaphore()
    for name in ("x", "y", "c"):
        pl.semaphore_signal(barrier, inc=1, device_id=to[name], device_id_type=MESH)

    @pl.when(z < n_z - 1)
    def _():
        pl.semaphore_signal(barrier, inc=1, device_id=to["up"], device_id_type=MESH)

    @pl.when(z > 0)
    def _():
        pl.semaphore_signal(barrier, inc=1, device_id=to["down"], device_id_type=MESH)

    pl.semaphore_wait(barrier, 3 + jnp.where(z < n_z - 1, 1, 0) + jnp.where(z > 0, 1, 0))


def both(*conditions):
    total = conditions[0]
    for one in conditions[1:]:
        total = jnp.logical_and(total, one)
    return total


PIX, HEADS, F, DHEADS, FD, GRID, KEEP, D, DD, PATCHES = 768, 12, 3072, 16, 2048, 14, 64, 768, 512, 196
SHAPES = [(PIX, D), (D, 3 * D), (D, D), (D, F), (F, D), (6, D), (D, DD), (DD, 3 * DD), (DD, DD), (DD, FD), (FD, DD), (DD, PIX), (7, DD)]
SMALL = (5, 12)
ENC_PARAMS = 7672320
NORM_EPS = 1e-06
ADAM_EPS = 1e-08
BETA_ONE = 0.9
BETA_TWO = 0.95
DECAY = 0.05
MB = 1 << 20
CELL = 8 * LANES
BLOCK = 96


def make_entries():
    entries, row, tile = [], 0, 0
    for number, (rows, width) in enumerate(SHAPES):
        lines = rows * width // LANES
        cols = 1 if number in SMALL else width // LANES
        groups = -(-lines // (8 * cols))
        entries.append((row, lines, cols, tile, groups))
        row += lines
        tile += groups * cols
    return entries, row, tile


ENTRIES, ROWS, TILES = make_entries()
BIG = tuple(i for i in range(len(SHAPES)) if i not in SMALL)
MARGIN = 8 * max(cols for _, _, cols, _, _ in ENTRIES)


def first_tile(share, k):
    lo = share * k
    total = 0
    for row, lines, cols, tile, _ in ENTRIES:
        inside = jnp.logical_and(lo >= row * LANES, lo < (row + lines) * LANES)
        total = total + jnp.where(inside, tile + (lo - row * LANES) // (CELL * cols) * cols, 0)
    return total


def ranges(share, n):
    found = []
    for k in range(n):
        lo, hi = share * k, share * (k + 1)
        spans = []
        for row, lines, cols, tile, _ in ENTRIES:
            low, high = max(lo, row * LANES), min(hi, (row + lines) * LANES)
            if low < high:
                size = CELL * cols
                spans.append((tile + (low - row * LANES) // size * cols, tile + -(-(high - row * LANES) // size) * cols))
        found.append((spans[0][0], spans[-1][1]))
    return found


def slab_tiles(share, n):
    longest = max(b - a for a, b in ranges(share, n))
    return -(-longest // 24) * 24


def line_span(share, k):
    return share * k // LANES, (share * (k + 1) + LANES - 1) // LANES


def tiled(share, k, body):
    lo, hi = line_span(share, k)
    begin = first_tile(share, k)
    for number in SMALL + tuple(i for i in range(len(ENTRIES)) if i not in SMALL):
        row, lines, cols, tile, _ = ENTRIES[number]
        low = jnp.maximum(lo, row) - row
        high = jnp.minimum(hi, row + lines) - row
        size = 8 * cols

        def group(g, _, row=row, cols=cols, tile=tile, size=size):
            body(row + g * size - lo + MARGIN, tile + g * cols - begin, cols)
            return 0

        lax.fori_loop(jnp.where(low < high, low // size, 0), jnp.where(low < high, (high + size - 1) // size, 0), group, 0)


def wide_rows(rows):
    return -(-(rows + 2 * MARGIN) // 8) * 8


def pieces(share, n):
    spans = ranges(share, n)
    shared = [spans[k][1] > spans[k + 1][0] for k in range(n - 1)]
    plain, seams = [], []
    for number, (_, _, cols, tile, groups) in enumerate(ENTRIES):
        end = tile + groups * cols
        for k, (a, b) in enumerate(spans):
            low, high = max(a, tile), min(b, end)
            if low >= high:
                continue
            inner_low, inner_high = low, high
            if k > 0 and spans[k - 1][1] > low:
                inner_low = spans[k - 1][1]
            if k < n - 1 and spans[k + 1][0] < high:
                inner_high = spans[k + 1][0]
                seams.append((number, k, inner_high, high))
            if inner_low < inner_high:
                plain.append((number, k, inner_low, inner_high))
    return spans, plain, seams


def matrix(tiles_, number):
    rows, width = SHAPES[number]
    cols = width // LANES
    return tiles_.reshape(rows // 8, cols, 8, LANES).transpose(0, 2, 1, 3).reshape(rows, width)


def matrix_tiles(value):
    rows, width = value.shape
    cols = width // LANES
    return value.reshape(rows // 8, 8, cols, LANES).transpose(0, 2, 1, 3).reshape(rows * cols, LANES)


def gather_kernel(n_z, n_pair, share, lines_ref, extra_ref, *refs):
    outs = dict(zip(BIG, refs[: len(BIG)]))
    enc_norms, dec_norms, masked_ref = refs[len(BIG) : len(BIG) + 3]
    wide, out_ref, z_sem, plane_sem, second_sem, third_sem, flat_sem, line_sem, core_sem, recv_sem, put_sem = refs[len(BIG) + 3 :]
    n = n_z * 2 * n_pair
    total_tiles = out_ref.shape[1]
    small = total_tiles // 2 * 2 // 9
    large = total_tiles // 2 - small
    spans_of = ((0, large), (large, large), (2 * large, small), (2 * large + small, small), (2 * large, 2 * small))
    z, x, y, c = place()
    to = partners(z, x, y, c)
    me = slot_of(z, x, y, c)
    rows = lines_ref.shape[0]
    wide[0:MARGIN, :] = jnp.zeros((MARGIN, LANES), jnp.float32)
    wide[MARGIN + rows :, :] = jnp.zeros((wide.shape[0] - MARGIN - rows, LANES), jnp.float32)
    wide[MARGIN : MARGIN + rows, :] = lines_ref[...]

    def fill(line, tile, cols):
        for col in range(cols):
            out_ref[me, tile + col] = wide[pl.ds(line + col, 8, stride=cols), :].astype(out_ref.dtype)

    tiled(share, me, fill)
    out_ref[me, total_tiles - 2] = extra_ref[...].astype(out_ref.dtype)
    greet(n_z, z, to)

    def copy(slot, part, name, sem):
        at = pl.ds(*spans_of[part])
        return pltpu.make_async_remote_copy(
            out_ref.at[slot, at], out_ref.at[slot, at], sem, recv_sem.at[slot, 2 if part == 4 else part], device_id=to[name], device_id_type=MESH
        )

    def arrived(slot, part):
        copy(slot, part, "c", plane_sem.at[0, 0, 0]).wait_recv()

    def start(one):
        one.start()

    def stop(one):
        one.wait_send()

    def lines(t):
        for d in (0, 1):
            zz = z - t if d == 0 else z + t
            inside = zz >= 0 if d == 0 else zz < n_z
            more = z < n_z - 1 if d == 0 else z > 0
            fresh = both(t > 0, inside)
            held = jnp.logical_or(fresh, t == 0) if d == 0 else fresh
            yield d, zz, fresh, held, more

    def own_z(act):
        for d, more in ((0, z < n_z - 1), (1, z > 0)):
            for part in (0, 1):
                pl.when(more)(lambda d=d, part=part: act(copy(me, part, ("up", "down")[d], z_sem.at[0, d, part])))

    def onward_z(t, d, zz, fresh, more, act):
        for part in (0, 1):
            pl.when(both(fresh, more))(lambda part=part: act(copy(slot_of(zz, x, y, c), part, ("up", "down")[d], z_sem.at[t, d, part])))

    def plane_sends(t, d, zz, held, act):
        @pl.when(held)
        def _():
            for i, (part, name) in enumerate(((0, "x"), (1, "y"), (0, "y"), (1, "x"), (0, "c"), (1, "c"))):
                act(copy(slot_of(zz, x, y, c), part, name, plane_sem.at[t, d, i]))

    def first(t):
        for d, zz, fresh, held, more in lines(t):

            @pl.when(fresh)
            def _():
                for part in (0, 1):
                    arrived(slot_of(zz, x, y, c), part)

            onward_z(t, d, zz, fresh, more, start)
            plane_sends(t, d, zz, held, start)

    def second_items(zz):
        return ((0, slot_of(zz, 1 - x, y, c), "y"), (1, slot_of(zz, x, 1 - y, c), "x"))

    def second(t):
        for d, zz, _, held, _ in lines(t):

            @pl.when(held)
            def _():
                for part, slot, name in second_items(zz):
                    arrived(slot, part)
                    copy(slot, part, name, second_sem.at[t, d, part, 0]).start()
                    copy(slot, part, "c", second_sem.at[t, d, part, 1]).start()

    def third_items(zz):
        return ((0, slot_of(zz, x, 1 - y, c)), (1, slot_of(zz, 1 - x, y, c)), (0, slot_of(zz, 1 - x, 1 - y, c)), (1, slot_of(zz, 1 - x, 1 - y, c)))

    def third(t):
        for d, zz, _, held, _ in lines(t):

            @pl.when(held)
            def _():
                for i, (part, slot) in enumerate(third_items(zz)):
                    arrived(slot, part)
                    copy(slot, part, "c", third_sem.at[t, d, i]).start()

    near = ((2, me, "x"), (3, me, "y"), (2, me, "y"), (3, me, "x"), (2, me, "c"), (3, me, "c"))
    beside = ((2, slot_of(z, 1 - x, y, c), "y"), (3, slot_of(z, x, 1 - y, c), "x"))
    across = ((2, slot_of(z, x, 1 - y, c)), (3, slot_of(z, 1 - x, y, c)), (2, slot_of(z, 1 - x, 1 - y, c)), (3, slot_of(z, 1 - x, 1 - y, c)))

    def flat_sends(act, which):
        for i, (part, slot, name) in enumerate(near):
            if which == 0:
                act(copy(slot, part, name, flat_sem.at[i]))
        for i, (part, slot, name) in enumerate(beside):
            if which == 1:
                act(copy(slot, part, name, flat_sem.at[6 + i]))
                act(copy(slot, part, "c", flat_sem.at[8 + i]))
        for i, (part, slot) in enumerate(across):
            if which == 2:
                act(copy(slot, part, "c", flat_sem.at[10 + i]))

    def corner(zz, i):
        return slot_of(zz, i // 2, i % 2, c)

    def line_sends(t, act):
        for d, zz, fresh, _, more in lines(t):
            for i in range(4):
                go = jnp.logical_or(fresh, t == 0)
                pl.when(both(go, more))(lambda d=d, zz=zz, i=i: act(copy(corner(zz, i), 4, ("up", "down")[d], line_sem.at[t, d, i])))
                pl.when(fresh)(lambda d=d, zz=zz, i=i: act(copy(corner(zz, i), 4, "c", core_sem.at[t, d, i])))

    def along(t):
        for d, zz, fresh, _, _ in lines(t):

            @pl.when(fresh)
            def _():
                for i in range(4):
                    arrived(corner(zz, i), 4)

        @pl.when(t == 0)
        def _():
            for part, slot in across:
                arrived(slot, part)
            flat_sends(start, 2)

        line_sends(t, start)

    own_z(start)
    flat_sends(start, 0)
    for part, slot, _ in beside:
        arrived(slot, part)
    flat_sends(start, 1)

    def turn(t, _):
        pl.when(t < n_z)(lambda: first(t))
        pl.when(both(t >= 1, t < n_z + 1))(lambda: second(t - 1))
        pl.when(both(t >= 1, t < n_z + 1))(lambda: along(t - 1))
        pl.when(t >= 2)(lambda: third(t - 2))
        return 0

    lax.fori_loop(0, n_z + 2, turn, 0)
    own_z(stop)
    for which in range(3):
        flat_sends(stop, which)

    def finish(t, _):
        line_sends(t, stop)
        for d, zz, fresh, held, more in lines(t):
            onward_z(t, d, zz, fresh, more, stop)
            plane_sends(t, d, zz, held, stop)

            @pl.when(held)
            def _():
                for part, slot, name in second_items(zz):
                    copy(slot, part, name, second_sem.at[t, d, part, 0]).wait_send()
                    copy(slot, part, "c", second_sem.at[t, d, part, 1]).wait_send()
                for i, (part, slot) in enumerate(third_items(zz)):
                    copy(slot, part, "c", third_sem.at[t, d, i]).wait_send()
                for i in range(4):
                    for part in (0, 1):
                        arrived(slot_of(zz, i // 2, i % 2, 1 - c), part)

            @pl.when(fresh)
            def _():
                for i in range(4):
                    arrived(slot_of(zz, i // 2, i % 2, 1 - c), 4)

        return 0

    lax.fori_loop(0, n_z, finish, 0)
    for i in range(4):
        for part in (2, 3):
            arrived(slot_of(z, i // 2, i % 2, 1 - c), part)
    spans, plain, seams = pieces(share, n)
    puts = []

    def put(number, k, low, high):
        copy = pltpu.make_async_copy(
            out_ref.at[k, pl.ds(low - spans[k][0], high - low)], outs[number].at[pl.ds(low - ENTRIES[number][3], high - low)], put_sem.at[len(puts)]
        )
        copy.start()
        puts.append(copy)

    home = {}
    for number, k, low, high in plain + seams:
        if number in SMALL:
            home.update({tile: (k, tile - spans[k][0]) for tile in range(low, high)})
        elif (number, k, low, high) in plain:
            put(number, k, low, high)
    for number, k, low, high in seams:
        left = pl.ds(low - spans[k][0], high - low)
        right = pl.ds(low - spans[k + 1][0], high - low)
        total = out_ref[k, left].astype(jnp.float32) + out_ref[k + 1, right].astype(jnp.float32)
        out_ref[k, left] = total.astype(out_ref.dtype)
        if number not in SMALL:
            put(number, k, low, high)
    for number, target in zip(SMALL, (enc_norms, dec_norms)):
        row, lines_, _, tile, groups = ENTRIES[number]
        per = SHAPES[number][1] // LANES
        for group in range(groups):
            k, at = home[tile + group]
            value = out_ref[k, at].astype(jnp.float32)
            for line in range(group * 8, min(group * 8 + 8, lines_)):
                target[line // per : line // per + 1, line % per * LANES : (line % per + 1) * LANES] = value[line % 8 : line % 8 + 1, :]
    masked_ref[...] = jnp.zeros_like(masked_ref)

    def count(k, _):
        masked_ref[...] += jnp.sum(out_ref[k, out_ref.shape[1] - 2].astype(jnp.float32)[0:1, :], axis=1, keepdims=True)
        return 0

    lax.fori_loop(0, n, count, 0)
    for copy in puts:
        copy.wait()


def gather(lines, extra, share, n_dp, n_pair):
    n_z = n_dp // 2
    n = n_dp * n_pair
    tiles_ = slab_tiles(share, n) + 2
    _, plain, seams = pieces(share, n)
    dma = pltpu.SemaphoreType.DMA
    anyspec = pl.BlockSpec(memory_space=pl.ANY)
    vmem = pl.BlockSpec(memory_space=pltpu.VMEM)

    def s(shape, kind=jnp.float32):
        return jax.ShapeDtypeStruct(shape, kind)

    return pl.pallas_call(
        functools.partial(gather_kernel, n_z, n_pair, share),
        name="gather",
        out_shape=[s((ENTRIES[i][4] * ENTRIES[i][2], 8, LANES), jnp.bfloat16) for i in BIG] + [s(SHAPES[5]), s(SHAPES[12]), s((1, 1))],
        in_specs=[vmem, vmem],
        out_specs=[anyspec] * len(BIG) + [vmem] * 3,
        scratch_shapes=[
            pltpu.VMEM((wide_rows(lines.shape[0]), LANES), jnp.float32),
            pltpu.VMEM((n, tiles_, 8, LANES), jnp.bfloat16),
            dma((n_z, 2, 2)), dma((n_z, 2, 6)), dma((n_z, 2, 2, 2)), dma((n_z, 2, 4)), dma((14,)), dma((n_z, 2, 4)), dma((n_z, 2, 4)), dma((n, 4)),
            dma((len(plain) + len(seams),)),
        ],
        compiler_params=pltpu.CompilerParams(collective_id=0, has_side_effects=True, vmem_limit_bytes=60 * MB),
    )(lines, extra)


def reduce_chunks(share, n):
    rows = slab_tiles(share, n) * 8
    return max(d for d in (1, 2, 4) if rows % (2 * BLOCK * d) == 0)


def late_cut(share):
    return -(-ENTRIES[7][0] * LANES // (share * 8))


def pack(value, q_ref, t_ref, b):
    top = jnp.max(jnp.abs(value), axis=0, keepdims=True)
    inverse = jnp.where(top > 1e-30, 32767.0 / jnp.maximum(top, 1e-30), 0.0)
    q_ref[pl.ds(pl.multiple_of(b * BLOCK, BLOCK), BLOCK), :] = jnp.round(value * inverse).astype(jnp.int32).astype(jnp.int16)
    t_ref[pl.ds(b, 1), :] = top * (1.0 / 32767.0)


def unpack(q_ref, t_ref, b):
    return q_ref[pl.ds(pl.multiple_of(b * BLOCK, BLOCK), BLOCK), :].astype(jnp.int32).astype(jnp.float32) * t_ref[pl.ds(b, 1), :]


def message(qs, ts, qr, tr, sem, to):
    return (
        pltpu.make_async_remote_copy(qs, qr, sem.at[0, 0], sem.at[0, 1], device_id=to, device_id_type=MESH),
        pltpu.make_async_remote_copy(ts, tr, sem.at[1, 0], sem.at[1, 1], device_id=to, device_id_type=MESH),
    )


def slab_start(share, n, k):
    if n > 64:
        return first_tile(share, k)
    starts = [a for a, _ in ranges(share, n)]
    found = starts[0]
    for i in range(1, n):
        found = jnp.where(k >= i, starts[i], found)
    return found


class Plane:
    def __init__(self, share, n, chunks, steps, plane_of, grad, sib, keep, base, scratch):
        self.share, self.n, self.chunks, self.steps, self.plane_of = share, n, chunks, steps, plane_of
        self.grad, self.sib, self.keep, self.base = grad, sib, keep, base
        (self.gbuf, self.rbuf, self.q1s, self.q1r, self.q2s, self.q2r, self.t1s, self.t1r, self.t2s, self.t2r,
         self.sib_sem, self.load_sem, self.s1_sem, self.s2_sem) = scratch
        self.z, self.x, self.y, self.c = place()
        self.to = partners(self.z, self.x, self.y, self.c)
        self.rows = keep.shape[1] // chunks
        self.half = self.rows // 2

    def tiles_of(self, s, xx, yy, core):
        k = slot_of(self.plane_of(s // self.chunks), xx, yy, core)
        return pl.ds(slab_start(self.share, self.n, k) + s % self.chunks * (self.rows // 8), self.rows // 8)

    def kept(self, s, part, b):
        return self.base + s // self.chunks, pl.ds(pl.multiple_of(s % self.chunks * self.rows + part * self.half + b * BLOCK, BLOCK), BLOCK)

    def sibling(self, s, q, at=None):
        return pltpu.make_async_remote_copy(
            self.grad.at[at if at is not None else pl.ds(0, self.rows // 8)],
            self.sib.at[s, q],
            self.sib_sem.at[0, s, q],
            self.sib_sem.at[1, s, q],
            device_id=self.to["c"],
            device_id_type=MESH,
        )

    def begin(self):
        def one(s, _):
            for q in range(4):
                self.sibling(s, q, self.tiles_of(s, q // 2, q % 2, 1 - self.c)).start()
            return 0

        lax.fori_loop(0, self.steps, one, 0)

    def loads(self, s, q, at=None):
        slot = s % 2
        return pltpu.make_async_copy(self.grad.at[at if at is not None else pl.ds(0, self.rows // 8)], self.gbuf.at[slot, q], self.load_sem.at[slot, q])

    def other(self, s):
        return pltpu.make_async_copy(self.sib.at[s], self.rbuf.at[s % 2], self.load_sem.at[s % 2, 4])

    def load(self, s):
        for q in range(4):
            self.loads(s, q, self.tiles_of(s, q // 2, q % 2, self.c)).start()
        for q in range(4):
            self.sibling(s, q).wait_recv()
        self.other(s).start()

    def each(self, body):
        def one(b, _):
            body(b)
            return 0

        lax.fori_loop(0, self.half // BLOCK, one, 0, unroll=self.half // BLOCK)

    def own(self, slot, q, part, b):
        at = pl.ds(part * (self.half // 8) + b * (BLOCK // 8), BLOCK // 8)
        return (self.gbuf[slot, q, at] + self.rbuf[slot, q, at]).reshape(BLOCK, LANES)

    def first_message(self, s, part):
        i = pl.ds(part * 2, 2)
        return message(self.q1s.at[s, i], self.t1s.at[s, i], self.q1r.at[s, i], self.t1r.at[s, i], self.s1_sem.at[s, part], self.to[("x", "y")[part]])

    def second_message(self, s, part):
        return message(
            self.q2s.at[s, part], self.t2s.at[s, part], self.q2r.at[s, part], self.t2r.at[s, part], self.s2_sem.at[s, part], self.to[("y", "x")[part]]
        )

    def quarter(self, part, other, mine):
        if part == 0:
            return (self.x if mine else 1 - self.x) * 2 + other
        return other * 2 + (self.y if mine else 1 - self.y)

    def stage_one(self, s):
        slot = s % 2
        for q in range(4):
            self.loads(s, q).wait()
        self.other(s).wait()
        for part in (0, 1):
            for other in (0, 1):
                q = self.quarter(part, other, False)
                i = part * 2 + other
                self.each(lambda b: pack(self.own(slot, q, part, b), self.q1s.at[s, i], self.t1s.at[s, i], b))
            for one in self.first_message(s, part):
                one.start()

    def stage_two(self, s):
        slot = s % 2
        for part in (0, 1):
            for one in self.first_message(s, part):
                one.wait_recv()
            here = (self.y, self.x)[part]
            away = self.quarter(part, 1 - here, True)
            i = part * 2 + 1 - here
            self.each(
                lambda b: pack(
                    self.own(slot, away, part, b) + unpack(self.q1r.at[s, i], self.t1r.at[s, i], b), self.q2s.at[s, part], self.t2s.at[s, part], b
                )
            )
            for one in self.second_message(s, part):
                one.start()
        for part in (0, 1):
            here = (self.y, self.x)[part]
            k = part * 2 + here

            def store(b, part=part, k=k):
                group, at = self.kept(s, part, b)
                self.keep[group, at, :] = self.own(slot, self.x * 2 + self.y, part, b) + unpack(self.q1r.at[s, k], self.t1r.at[s, k], b)

            self.each(store)

    def stage_three(self, s):
        for part in (0, 1):
            for one in self.second_message(s, part):
                one.wait_recv()

            def body(b, part=part):
                group, at = self.kept(s, part, b)
                self.keep[group, at, :] += unpack(self.q2r.at[s, part], self.t2r.at[s, part], b)

            self.each(body)

    def finish(self):
        def one(s, _):
            for q in range(4):
                self.sibling(s, q).wait_send()
            for part in (0, 1):
                for two in self.first_message(s, part):
                    two.wait_send()
                for two in self.second_message(s, part):
                    two.wait_send()
            return 0

        lax.fori_loop(0, self.steps, one, 0)


def message_scratch(part, *leads):
    half = part // 2
    marks = (half // BLOCK + 7) // 8 * 8
    return [pltpu.VMEM(lead + (half, LANES), jnp.int16) for lead in leads] + [pltpu.VMEM(lead + (marks, LANES), jnp.float32) for lead in leads]


def plane_scratch(steps, part):
    dma = pltpu.SemaphoreType.DMA
    return [
        pltpu.VMEM((2, 4, part // 8, 8, LANES), jnp.float32),
        pltpu.VMEM((2, 4, part // 8, 8, LANES), jnp.float32),
        *message_scratch(part, (steps, 4), (steps, 4), (steps, 2), (steps, 2)),
        dma((2, steps, 4)), dma((2, 5)), dma((steps, 2, 2, 2)), dma((steps, 2, 2, 2)),
    ]


def reduce_kernel(n_z, n_pair, chunks, share, grad_ref, late_ref, loss_in, lines_ref, total_ref, sib_ref,
                  wide, mine, shared, send_sem, recv_sem, keep, late_sem, zs, zr, tzs, tzr, z_sem, *scratch):
    z, x, y, c = place()
    to = partners(z, x, y, c)
    n = n_z * 2 * n_pair
    me = slot_of(z, x, y, c)
    cut = late_cut(share)
    steps, late = cut * chunks, (n_z - cut) * chunks
    home = jnp.where(z < cut, cut - 1, z)

    def order(j):
        low = z < cut // 2
        far = jnp.where(low, cut - 1 - j, j)
        moved = jnp.where(low, jnp.where(far > z, far, far - 1), jnp.where(far < z, far, far + 1))
        return jnp.where(z >= cut, j, jnp.where(j == cut - 1, z, moved))

    plane = Plane(share, n, chunks, steps, order, grad_ref, sib_ref, keep, 0, scratch)

    def z_message(spot, name):
        d = 0 if name == "up" else 1
        return message(zs.at[spot], tzs.at[spot], zr.at[d, spot], tzr.at[d, spot], z_sem.at[d, spot], to[name])

    def stage_four(group, chunk, zz):
        spot = zz * chunks + chunk

        def lines(part, b):
            return pl.ds(pl.multiple_of(chunk * plane.rows + part * plane.half + b * BLOCK, BLOCK), BLOCK)

        for d, name, has, onward in ((0, "up", z > 0, zz > z), (1, "down", z < n_z - 1, zz < z)):
            back = zz >= z if d == 0 else zz <= z

            @pl.when(both(has, back))
            def _():
                for one in z_message(spot, name):
                    one.wait_recv()
                for part in (0, 1):

                    def add(b, part=part):
                        keep[group, lines(part, b), :] += unpack(zr.at[d, spot, part], tzr.at[d, spot, part], b)

                    plane.each(add)

            @pl.when(onward)
            def _():
                for part in (0, 1):
                    plane.each(lambda b, part=part: pack(keep[group, lines(part, b), :], zs.at[spot, part], tzs.at[spot, part], b))
                for one in z_message(spot, name):
                    one.start()

    def spread_lines(line, tile, cols):
        for col in range(cols):
            wide[pl.ds(line + col, 8, stride=cols), :] = keep[home, pl.ds(pl.multiple_of((tile + col) * 8, 8), 8), :]

    count_lines = lines_ref.shape[0]
    tall = 128

    def by_lines(body):
        def one(i, _):
            body(pl.multiple_of(i * tall, tall), tall)
            return 0

        lax.fori_loop(0, count_lines // tall, one, 0)
        if count_lines % tall:
            body(count_lines // tall * tall, count_lines % tall)

    barrier = pltpu.get_barrier_semaphore()

    def peer(d):
        k = lax.rem(me + d, n)
        return {"dp": k // n_pair, "pair": lax.rem(k, n_pair)}

    def hello(d, _):
        pl.semaphore_signal(barrier, inc=1, device_id=peer(d), device_id_type=MESH)
        return 0

    lax.fori_loop(1, n, hello, 0)
    kept = pltpu.make_async_copy(late_ref, keep.at[pl.ds(cut, n_z - cut)], late_sem)
    kept.start()
    pl.semaphore_wait(barrier, n - 1)
    plane.begin()
    plane.load(0)
    kept.wait()
    lag = 0

    def turn(t, _):
        pl.when(t < steps)(lambda: plane.stage_one(t))
        pl.when(both(t >= 1, t <= steps))(lambda: plane.stage_two(t - 1))
        pl.when(t + 1 < steps)(lambda: plane.load(t + 1))
        pl.when(both(t >= 2, t <= steps + 1))(lambda: plane.stage_three(t - 2))
        early, main = t - z, t - 3 - lag
        pl.when(both(early >= 0, early < late))(lambda: stage_four(cut + early // chunks, lax.rem(early, chunks), cut + early // chunks))
        pl.when(both(main >= 0, main < steps))(lambda: stage_four(main // chunks, lax.rem(main, chunks), order(main // chunks)))
        return 0

    lax.fori_loop(0, max(steps + 3, late + n_z), turn, 0)
    tiled(share, me, spread_lines)
    lo, _ = line_span(share, me)
    mine[...] = jnp.zeros_like(mine)

    def squares(start, size):
        value = wide[pl.ds(MARGIN + start, size), :]
        if share % LANES:
            line = lax.broadcasted_iota(jnp.int32, (size, LANES), 0) + lo + start
            spot = line * LANES + lax.broadcasted_iota(jnp.int32, (size, LANES), 1)
            inside = jnp.logical_and(spot >= share * me, spot < share * (me + 1))
            value = jnp.where(inside, value, 0.0)
        lines_ref[pl.ds(start, size), :] = value
        mine[0:1, :] += jnp.sum(value * value, axis=0, keepdims=True)

    by_lines(squares)
    lane = lax.broadcasted_iota(jnp.int32, (1, LANES), 1)
    mine[1:2, :] = jnp.where(lane == 0, loss_in[0:1, 0:1], 0.0)
    shared[me] = mine[...]

    def send(d):
        return pltpu.make_async_remote_copy(mine, shared.at[me], send_sem.at[d], recv_sem.at[d], device_id=peer(d), device_id_type=MESH)

    def go(d, _):
        send(d).start()
        return 0

    def stop(d, _):
        send(d).wait()
        return 0

    lax.fori_loop(1, n, go, 0)
    plane.finish()

    def finish(spot, _):
        zz = spot // chunks
        for name, sent in (("up", zz > z), ("down", zz < z)):

            @pl.when(sent)
            def _():
                for one in z_message(spot, name):
                    one.wait_send()

        return 0

    lax.fori_loop(0, n_z * chunks, finish, 0)
    lax.fori_loop(1, n, stop, 0)

    def add(k, total):
        return total + shared[k]

    total = lax.fori_loop(0, n, add, jnp.zeros((8, LANES), jnp.float32))
    norm_ = jnp.sqrt(jnp.sum(total[0:1, :], axis=1, keepdims=True))
    loss_sum = jnp.sum(total[1:2, :], axis=1, keepdims=True)
    total_ref[...] = jnp.where(lax.broadcasted_iota(jnp.int32, (8, LANES), 0) == 0, norm_, loss_sum)


def reduce(flat, late, loss, shape, share, n_dp, n_pair):
    n_z, n = n_dp // 2, n_dp * n_pair
    chunks = reduce_chunks(share, n)
    rows = slab_tiles(share, n) * 8
    part = rows // chunks
    steps = late_cut(share) * chunks
    spots = n_z * chunks
    anyspec = pl.BlockSpec(memory_space=pl.ANY)
    vmem = pl.BlockSpec(memory_space=pltpu.VMEM)
    line = jax.ShapeDtypeStruct(shape, jnp.float32)
    dma = pltpu.SemaphoreType.DMA
    return pl.pallas_call(
        functools.partial(reduce_kernel, n_z, n_pair, chunks, share),
        name="reduce_scatter",
        out_shape=[line, jax.ShapeDtypeStruct((8, LANES), jnp.float32), jax.ShapeDtypeStruct((steps, 4, part // 8, 8, LANES), jnp.float32)],
        in_specs=[anyspec, anyspec, vmem],
        out_specs=[vmem, vmem, anyspec],
        scratch_shapes=[
            pltpu.VMEM((wide_rows(shape[0]), LANES), jnp.float32),
            pltpu.VMEM((8, LANES), jnp.float32),
            pltpu.VMEM((n, 8, LANES), jnp.float32),
            dma((n,)),
            dma((n,)),
            pltpu.VMEM((n_z, rows, LANES), jnp.float32),
            dma,
            *message_scratch(part, (spots, 2), (2, spots, 2)),
            dma((2, spots, 2, 2)),
            *plane_scratch(steps, part),
        ],
        compiler_params=pltpu.CompilerParams(collective_id=1, has_side_effects=True, vmem_limit_bytes=60 * MB),
    )(flat, late, loss)[:2]


NEG_FILL = -1000000000.0
P_ROWS = 208
BF = jnp.bfloat16
F32 = jnp.float32


def dot_nn(left, right):
    return lax.dot_general(left, right, (((1,), (0,)), ((), ())), preferred_element_type=F32)


def dot_nt(left, right):
    return lax.dot_general(left, right, (((1,), (1,)), ((), ())), preferred_element_type=F32)


def loop(count, body, unroll=1):
    def step(i, _):
        body(i)
        return 0

    lax.fori_loop(0, count, step, 0, unroll=unroll)


def rows_at(i, size):
    return pl.ds(pl.multiple_of(i * size, size), size)


def norm(x):
    centered = x - jnp.mean(x, axis=-1, keepdims=True)
    scale = lax.rsqrt(jnp.mean(centered * centered, axis=-1, keepdims=True) + NORM_EPS)
    return centered * scale, scale


def norm_grad(grad, plain, scale, gain):
    inner = grad * gain
    back = scale * (inner - jnp.mean(inner, axis=-1, keepdims=True) - plain * jnp.mean(inner * plain, axis=-1, keepdims=True))
    return back, jnp.sum(grad * plain, axis=0, keepdims=True), jnp.sum(grad, axis=0, keepdims=True)


def gelu_pair(h):
    cumulative = 0.5 * (1.0 + lax.erf(h * 0.7071067811865476))
    density = jnp.exp(-0.5 * h * h) * 0.3989422804014327
    return h * cumulative, cumulative + h * density


def head_masks(size):
    lane = lax.broadcasted_iota(jnp.int32, (1, LANES), 1)
    shift = size.bit_length() - 1
    return [jnp.where((lane >> shift) == h, 1.0, 0.0).astype(BF) for h in range(LANES // size)]


def three(value):
    top = value.astype(BF)
    rest = value - top.astype(F32)
    mid = rest.astype(BF)
    return top, mid, (rest - mid.astype(F32)).astype(BF)


class Moves:
    def __init__(self, names, sources, targets, sems):
        self.targets = dict(zip(names, targets))
        self.copies = {name: pltpu.make_async_copy(a, b, sems.at[i]) for i, (name, a, b) in enumerate(zip(names, sources, targets))}
        self.open = []

    def start(self, *names):
        for name in names or self.copies:
            self.copies[name].start()
            self.open.append(name)

    def __call__(self, name):
        if name in self.open:
            self.copies[name].wait()
            self.open.remove(name)
        return self.targets[name]

    def close(self):
        for name in list(self.open):
            self(name)


def wide_attention(width, heads, rows, triple, bias, probs, mixed):
    size = width // heads
    per = LANES // size
    masks = head_masks(size)
    for g in range(width // LANES):
        q, k, v = (triple[:, t * width + g * LANES : t * width + (g + 1) * LANES] for t in range(3))
        v_side = v.T
        parts = []
        for h in range(per):
            s = dot_nt(k * masks[h], q) * size ** (-0.5) + bias[...]
            e = jnp.exp(s - jnp.max(s, axis=0, keepdims=True))
            p = e * (1.0 / jnp.sum(e, axis=0, keepdims=True))
            probs[g * per + h] = p
            parts.append(dot_nn(v_side[h * size : (h + 1) * size, :], p.astype(BF)))
        mixed[:, g * LANES : (g + 1) * LANES] = jnp.concatenate(parts, axis=0).T.astype(BF)


def wide_attention_back(width, heads, triple, probs, low_mixed, grad_triple):
    size = width // heads
    per = LANES // size
    masks = head_masks(size)
    for g in range(width // LANES):
        lanes = [slice(t * width + g * LANES, t * width + (g + 1) * LANES) for t in range(3)]
        q, k, v = (triple[:, lane] for lane in lanes)
        dm = low_mixed[:, g * LANES : (g + 1) * LANES]
        k_side = k.T
        parts, dk, dv = [], 0.0, 0.0
        for h in range(per):
            p = probs[g * per + h]
            dp = dot_nt(v * masks[h], dm)
            ds = (p * (dp - jnp.sum(p * dp, axis=0, keepdims=True))).astype(BF)
            dv = dv + dot_nn(p.astype(BF), dm * masks[h])
            dk = dk + dot_nn(ds, q * masks[h])
            parts.append(dot_nn(k_side[h * size : (h + 1) * size, :], ds))
        grad_triple[:, lanes[0]] = (jnp.concatenate(parts, axis=0).T * size ** (-0.5)).astype(BF)
        grad_triple[:, lanes[1]] = (dk * size ** (-0.5)).astype(BF)
        grad_triple[:, lanes[2]] = dv.astype(BF)


def block_forward(x, rows, images, heads, need, norms, key_bias, saved, done=lambda *names: None):
    entry, plain1, scale1, triple, probs, mixed, plain2, scale2, inner, act, slope = saved
    width = x.shape[1]
    size = width // heads
    per = LANES // size
    groups = width // LANES

    def first(i):
        at = rows_at(i, rows)
        plain, scale = norm(x[at, :])
        plain1[at, :] = plain
        scale1[at, :] = scale
        entry[at, :] = (plain * norms[0:1, :] + norms[1:2, :]).astype(BF)

    loop(images, first)

    done("entry", "plain1", "scale1")
    triple_w = need("triple_w")

    def project(j):
        at = rows_at(j, 256)
        triple[:, at] = dot_nn(entry[...], triple_w[:, at]).astype(BF)

    loop(3 * width // 256, project)
    done("triple")
    masks = head_masks(size)

    def attend(i):
        at = rows_at(i, rows)
        bias = key_bias(i)
        for g in range(groups):
            q = triple[at, g * LANES : (g + 1) * LANES]
            k = triple[at, width + g * LANES : width + (g + 1) * LANES]
            v = triple[at, 2 * width + g * LANES : 2 * width + (g + 1) * LANES]
            v_side = v.T
            parts = []
            for h in range(per):
                s = dot_nt(k * masks[h], q) * size ** (-0.5) + bias
                e = jnp.exp(s - jnp.max(s, axis=0, keepdims=True))
                p = e * (1.0 / jnp.sum(e, axis=0, keepdims=True))
                probs[i * groups + g, h * rows : (h + 1) * rows, :] = p
                parts.append(dot_nn(v_side[h * size : (h + 1) * size, :], p.astype(BF)))
            mixed[at, g * LANES : (g + 1) * LANES] = jnp.concatenate(parts, axis=0).T.astype(BF)

    if callable(key_bias):
        loop(images, attend)
    else:
        wide_attention(width, heads, rows, triple, key_bias, probs, mixed)
    done("probs", "mixed")
    proj_w = need("proj_w")

    def middle(j):
        at = rows_at(j, 256)
        x[:, at] += dot_nn(mixed[...], proj_w[:, at])

    loop(width // 256, middle)

    def second(i):
        at = rows_at(i, rows)
        plain, scale = norm(x[at, :])
        plain2[at, :] = plain
        scale2[at, :] = scale
        inner[at, :] = (plain * norms[2:3, :] + norms[3:4, :]).astype(BF)

    loop(images, second)
    done("plain2", "scale2", "inner")
    up_w = need("up_w")
    hidden = up_w.shape[1]

    def up(j):
        at = rows_at(j, 256)
        value, gradient = gelu_pair(dot_nn(inner[...], up_w[:, at]))
        act[:, at] = value.astype(BF)
        slope[:, at] = gradient

    loop(hidden // 256, up)
    done("act", "slope")
    down_w = need("down_w")

    def down(j):
        at = rows_at(j, 256)
        x[:, at] += dot_nn(act[...], down_w[:, at])

    loop(width // 256, down)


class Writer:
    def __init__(self, flat, stage, sem):
        self.flat, self.stage, self.sem = flat, stage, sem
        self.pending = {}

    def settle(self, s):
        if s in self.pending:
            self.pending.pop(s).wait()

    def outer(self, number, left, right, chunk=256):
        _, _, cols, tile, _ = ENTRIES[number]
        rows = left.shape[1]
        count = rows // chunk
        tall = chunk // 8
        before = dict(self.pending)

        def copy(i, s):
            return pltpu.make_async_copy(
                self.stage.at[s, pl.ds(0, tall * cols)], self.flat.at[pl.ds(tile + i * tall * cols, tall * cols)], self.sem.at[s]
            )

        def body(i):
            s = lax.rem(i, 2)
            for early in before:
                pl.when(i == early)(before[early].wait)

            @pl.when(i >= 2)
            def _():
                copy(i - 2, s).wait()

            side = left[:, rows_at(i, chunk)].T
            for c in range(0, cols, 2):
                value = dot_nn(side, right[:, c * LANES : (c + 2) * LANES])
                for d in range(2):
                    self.stage[s, pl.ds(c + d, tall, stride=cols)] = value[:, d * LANES : (d + 1) * LANES].reshape(tall, 8, LANES)
            copy(i, s).start()

        loop(count, body)
        self.pending = {(count - 2) % 2: copy(count - 2, (count - 2) % 2), (count - 1) % 2: copy(count - 1, (count - 1) % 2)}

    def small(self, number, norm_sums, count, extra=0):
        _, _, _, tile, groups = ENTRIES[number]
        per = SHAPES[number][1] // LANES
        self.settle(0)
        self.stage[0, 0 : groups + extra] = jnp.zeros((groups + extra, 8, LANES), F32)
        for r in range(count):
            for c in range(per):
                line = r * per + c
                self.stage[0, line // 8, line % 8 : line % 8 + 1, :] = norm_sums[r : r + 1, c * LANES : (c + 1) * LANES]
        copy = pltpu.make_async_copy(self.stage.at[0, pl.ds(0, groups + extra)], self.flat.at[pl.ds(tile, groups + extra)], self.sem.at[0])
        copy.start()
        copy.wait()
        self.settle(1)


def block_backward(grad, rows, images, heads, need, norms, norm_sums, extra, writer, numbers, tick=lambda: None):
    low, grad_hidden, side, low_mixed, grad_triple = extra
    width = grad.shape[1]
    size = width // heads
    per = LANES // size
    groups = width // LANES
    low[...] = grad[...].astype(BF)
    down_w, slope = need("down_w"), need("slope")
    hidden = down_w.shape[0]

    def back_up(j):
        at = rows_at(j, 256)
        grad_hidden[:, at] = (dot_nt(low[...], down_w[at, :]) * slope[:, at]).astype(BF)

    loop(hidden // 256, back_up)
    tick()
    writer.outer(numbers[3], need("act"), low)
    tick()
    writer.outer(numbers[2], need("inner"), grad_hidden)
    tick()
    up_w = need("up_w")

    def back_inner(j):
        at = rows_at(j, 256)
        side[:, at] = dot_nt(grad_hidden[...], up_w[at, :])

    loop(width // 256, back_inner)
    tick()
    plain2, scale2 = need("plain2"), need("scale2")

    def second(i):
        at = rows_at(i, rows)
        back, gain, shift = norm_grad(side[at, :], plain2[at, :], scale2[at, :], norms[2:3, :])
        norm_sums[2:3, :] += gain
        norm_sums[3:4, :] += shift
        total = grad[at, :] + back
        grad[at, :] = total
        low[at, :] = total.astype(BF)

    loop(images, second)
    writer.outer(numbers[1], need("mixed"), low)
    proj_w = need("proj_w")

    def back_mixed(j):
        at = rows_at(j, 256)
        low_mixed[:, at] = dot_nt(low[...], proj_w[at, :]).astype(BF)

    loop(width // 256, back_mixed)
    tick()
    triple, probs = need("triple"), need("probs")
    masks = head_masks(size)

    def attend(i):
        at = rows_at(i, rows)
        for g in range(groups):
            lanes = [slice(t * width + g * LANES, t * width + (g + 1) * LANES) for t in range(3)]
            q, k, v = (triple[at, lane] for lane in lanes)
            dm = low_mixed[at, g * LANES : (g + 1) * LANES]
            k_side = k.T
            parts, dk, dv = [], 0.0, 0.0
            for h in range(per):
                p = probs[i * groups + g, h * rows : (h + 1) * rows, :]
                dp = dot_nt(v * masks[h], dm)
                ds = (p * (dp - jnp.sum(p * dp, axis=0, keepdims=True))).astype(BF)
                dv = dv + dot_nn(p.astype(BF), dm * masks[h])
                dk = dk + dot_nn(ds, q * masks[h])
                parts.append(dot_nn(k_side[h * size : (h + 1) * size, :], ds))
            dq = jnp.concatenate(parts, axis=0).T
            grad_triple[at, lanes[0]] = (dq * size ** (-0.5)).astype(BF)
            grad_triple[at, lanes[1]] = (dk * size ** (-0.5)).astype(BF)
            grad_triple[at, lanes[2]] = dv.astype(BF)

    if probs.shape[1] == probs.shape[2] and probs.shape[0] == heads:
        wide_attention_back(width, heads, triple, probs, low_mixed, grad_triple)
    else:
        loop(images, attend)
    tick()
    writer.outer(numbers[0], need("entry"), grad_triple)
    tick()
    triple_w = need("triple_w")

    def back_entry(j):
        at = rows_at(j, 256)
        side[:, at] = dot_nt(grad_triple[...], triple_w[at, :])

    loop(width // 256, back_entry)
    tick()
    plain1, scale1 = need("plain1"), need("scale1")

    def first(i):
        at = rows_at(i, rows)
        back, gain, shift = norm_grad(side[at, :], plain1[at, :], scale1[at, :], norms[0:1, :])
        norm_sums[0:1, :] += gain
        norm_sums[1:2, :] += shift
        grad[at, :] += back

    loop(images, first)


TICKS = 11
SAVED = ("seen", "entry", "plain1", "scale1", "triple", "probs", "mixed", "plain2", "scale2", "inner", "act", "slope", "plain3", "scale3", "encoded")
ENC_NAMES = ("embed_w", "triple_w", "proj_w", "up_w", "down_w", "dec_embed_w")
DEC_NAMES = ("triple_w", "proj_w", "up_w", "down_w", "head_w")


def saved_shapes(rows):
    s = jax.ShapeDtypeStruct
    return [
        s((rows, D), BF), s((rows, D), BF), s((rows, D), F32), s((rows, 1), F32), s((rows, 3 * D), BF),
        s((HEADS, rows, rows), F32), s((rows, D), BF), s((rows, D), F32), s((rows, 1), F32), s((rows, D), BF),
        s((rows, F), BF), s((rows, F), F32), s((rows, D), F32), s((rows, 1), F32), s((rows, D), BF),
    ]


def like(shape):
    return pltpu.VMEM(shape.shape, shape.dtype)


def pad_patches(patches, padded, images):
    padded[...] = jnp.zeros_like(padded)
    for i in range(images):
        padded[i * P_ROWS : i * P_ROWS + PATCHES, :] = patches[i]


def encoder_kernel(images, counts_ref, cols_ref, norms_ref, *refs):
    pos_hbm, patches_hbm, *weights_hbm = refs[:8]
    outs = refs[8:23]
    entering = refs[23]
    pos, patches, *weights = refs[24:32]
    saved = dict(zip(SAVED, refs[32:47]))
    x, place_, pos_split, padded, bias, in_sem, out_sem = refs[47:]
    need = Moves(("pos", "patches") + ENC_NAMES, [pos_hbm, patches_hbm] + weights_hbm, [pos, patches] + weights, in_sem)
    need.start()
    put = Moves(SAVED, [saved[name] for name in SAVED], outs, out_sem)
    rows = images * KEEP
    key = lax.broadcasted_iota(jnp.int32, (KEEP, rows), 0)
    query = lax.broadcasted_iota(jnp.int32, (KEEP, rows), 1)
    for i in range(images):
        inside = jnp.logical_and(jnp.logical_and(query >= i * KEEP, query < (i + 1) * KEEP), key < counts_ref[i])
        bias[i * KEEP : (i + 1) * KEEP, :] = jnp.where(inside, 0.0, NEG_FILL)
    need("pos")
    for t, part in enumerate(three(pos[...])):
        pos_split[t] = part
    pad_patches(need("patches"), padded, images)
    spots = lax.broadcasted_iota(jnp.int32, (KEEP, P_ROWS), 1)
    seen = saved["seen"]

    def select(i):
        at = rows_at(i, KEEP)
        pick = jnp.where(spots == cols_ref[i], 1.0, 0.0).astype(BF)
        seen[at, :] = dot_nn(pick, padded[rows_at(i, P_ROWS), :]).astype(BF)
        place_[at, :] = dot_nn(pick, pos_split[0]) + dot_nn(pick, pos_split[1]) + dot_nn(pick, pos_split[2])

    loop(images, select)
    put.start("seen")
    embed_w = need("embed_w")

    def embed(j):
        at = rows_at(j, 256)
        x[:, at] = dot_nn(seen[...], embed_w[:, at]) + place_[:, at]

    loop(D // 256, embed)
    block_forward(x, KEEP, images, HEADS, need, norms_ref, bias, [saved[name] for name in SAVED[1:12]], put.start)
    plain3, scale3, encoded = (saved[name] for name in SAVED[12:])

    def last(i):
        at = rows_at(i, KEEP)
        plain, scale = norm(x[at, :])
        plain3[at, :] = plain
        scale3[at, :] = scale
        encoded[at, :] = (plain * norms_ref[4:5, :] + norms_ref[5:6, :]).astype(BF)

    loop(images, last)
    put.start("plain3", "scale3", "encoded")
    entering[...] = dot_nn(encoded[...], need("dec_embed_w")[...])
    put.close()


def encoder(counts, patches, cols, pos, weights, norms):
    images = counts.shape[0]
    rows = images * KEEP
    vmem = pl.BlockSpec(memory_space=pltpu.VMEM)
    anyspec = pl.BlockSpec(memory_space=pl.ANY)
    shapes = saved_shapes(rows)
    return pl.pallas_call(
        functools.partial(encoder_kernel, images),
        name="encoder",
        out_shape=shapes + [jax.ShapeDtypeStruct((rows, DD), F32)],
        in_specs=[pl.BlockSpec(memory_space=pltpu.SMEM), vmem, vmem] + [anyspec] * 8,
        out_specs=[anyspec] * 15 + [vmem],
        scratch_shapes=[like(one) for one in [pos, patches] + weights + shapes]
        + [
            pltpu.VMEM((rows, D), F32), pltpu.VMEM((rows, D), F32), pltpu.VMEM((3, P_ROWS, D), BF), pltpu.VMEM((images * P_ROWS, PIX), BF),
            pltpu.VMEM((rows, rows), F32), pltpu.SemaphoreType.DMA((8,)), pltpu.SemaphoreType.DMA((15,)),
        ],
        compiler_params=pltpu.CompilerParams(vmem_limit_bytes=60 * MB),
    )(counts, cols, norms, pos, patches, *weights)


def decoder_kernel(images, counts_ref, masked_ref, cols_ref, rows_ref, entering_ref, norms_ref, *refs):
    pos_hbm, patches_hbm, *weights_hbm = refs[:7]
    flat, grad_entering, loss_ref = refs[7:10]
    pos, patches, *weights = refs[10:17]
    (x, hide, entry, plain1, scale1, triple, probs, mixed, plain2, scale2, inner, act, slope, plain3, scale3, final, grad_pred,
     low, grad_hidden, side, low_mixed, grad_triple, norm_sums, padded, stage, sem, in_sem) = refs[17:]
    need = Moves(("pos", "patches") + DEC_NAMES, [pos_hbm, patches_hbm] + weights_hbm, [pos, patches] + weights, in_sem)
    need.start()
    saved = (entry, plain1, scale1, triple, probs, mixed, plain2, scale2, inner, act, slope)
    need.targets.update(zip(SAVED[1:12], saved))
    lane = lax.broadcasted_iota(jnp.int32, (P_ROWS, KEEP), 1)
    spot = lax.broadcasted_iota(jnp.int32, (P_ROWS, KEEP), 0)
    line = lax.broadcasted_iota(jnp.int32, (P_ROWS, 1), 0)
    need("pos")

    def start(i):
        at = rows_at(i, P_ROWS)
        hit = jnp.where(jnp.logical_and(spot == rows_ref[pl.ds(i, 1), 0:KEEP], lane < counts_ref[i]), 1.0, 0.0)
        shown = jnp.max(hit, axis=1, keepdims=True)
        pick = hit.astype(BF)
        top, mid, end = three(entering_ref[rows_at(i, KEEP), :])
        picked = dot_nn(pick, top) + dot_nn(pick, mid) + dot_nn(pick, end)
        x[at, :] = jnp.where(shown > 0.0, picked, norms_ref[6:7, :]) + pos[...]
        hide[at, :] = jnp.where(jnp.logical_and(line < PATCHES, shown == 0.0), 1.0, 0.0)

    loop(images, start)
    bias = jnp.where(line < PATCHES, 0.0, NEG_FILL)
    block_forward(x, P_ROWS, images, DHEADS, need, norms_ref, lambda i: bias, saved)

    def last(i):
        at = rows_at(i, P_ROWS)
        plain, scale = norm(x[at, :])
        plain3[at, :] = plain
        scale3[at, :] = scale
        final[at, :] = (plain * norms_ref[4:5, :] + norms_ref[5:6, :]).astype(BF)

    loop(images, last)
    loss_ref[...] = jnp.zeros_like(loss_ref)
    masked = masked_ref[0:1, 0:1]
    head_w = need("head_w")
    pad_patches(need("patches"), padded, images)

    def score(i):
        at = rows_at(i, P_ROWS)
        target, _ = norm(padded[at, :].astype(F32))
        diff = dot_nn(final[at, :], head_w[...]) - target
        hidden = hide[at, :]
        loss_ref[...] += jnp.sum(jnp.mean(diff * diff, axis=-1, keepdims=True) * hidden, axis=0, keepdims=True)
        grad_pred[at, :] = (diff * (hidden * (2.0 / PIX)) / masked).astype(BF)

    loop(images, score)
    writer = Writer(flat, stage, sem)
    writer.outer(11, final, grad_pred)
    norm_sums[...] = jnp.zeros_like(norm_sums)

    def back_final(i):
        at = rows_at(i, P_ROWS)
        back, gain, shift = norm_grad(dot_nt(grad_pred[at, :], head_w[...]), plain3[at, :], scale3[at, :], norms_ref[4:5, :])
        norm_sums[4:5, :] += gain
        norm_sums[5:6, :] += shift
        x[at, :] = back

    loop(images, back_final)
    block_backward(x, P_ROWS, images, DHEADS, need, norms_ref, norm_sums, (low, grad_hidden, side, low_mixed, grad_triple), writer, (7, 8, 9, 10))
    spots = lax.broadcasted_iota(jnp.int32, (KEEP, P_ROWS), 1)
    slot = lax.broadcasted_iota(jnp.int32, (KEEP, P_ROWS), 0)

    def finish(i):
        at = rows_at(i, P_ROWS)
        grad = x[at, :]
        norm_sums[6:7, :] += jnp.sum(grad * hide[at, :], axis=0, keepdims=True)
        pick = jnp.where(jnp.logical_and(spots == cols_ref[i], slot < counts_ref[i]), 1.0, 0.0).astype(BF)
        grad_entering[rows_at(i, KEEP), :] = dot_nn(pick, grad.astype(BF)).astype(BF)

    loop(images, finish)
    writer.small(12, norm_sums, 7, flat.shape[0] - TILES)


def decoder(total, counts, masked, patches, cols, order, pos, entering, weights, norms):
    images = counts.shape[0]
    rows = images * P_ROWS
    vmem = pl.BlockSpec(memory_space=pltpu.VMEM)
    anyspec = pl.BlockSpec(memory_space=pl.ANY)

    def v(shape, kind=F32):
        return pltpu.VMEM(shape, kind)

    return pl.pallas_call(
        functools.partial(decoder_kernel, images),
        name="decoder",
        out_shape=[
            jax.ShapeDtypeStruct((total, 8, LANES), F32),
            jax.ShapeDtypeStruct((images * KEEP, DD), BF),
            jax.ShapeDtypeStruct((1, 1), F32),
        ],
        in_specs=[pl.BlockSpec(memory_space=pltpu.SMEM)] + [vmem] * 5 + [anyspec] * 7,
        out_specs=[anyspec, vmem, vmem],
        scratch_shapes=[like(one) for one in [pos, patches] + weights]
        + [
            v((rows, DD)), v((rows, 1)), v((rows, DD), BF), v((rows, DD)), v((rows, 1)), v((rows, 3 * DD), BF),
            v((images * DD // LANES, 4 * P_ROWS, P_ROWS)), v((rows, DD), BF), v((rows, DD)), v((rows, 1)), v((rows, DD), BF),
            v((rows, FD), BF), v((rows, FD)), v((rows, DD)), v((rows, 1)), v((rows, DD), BF), v((rows, PIX), BF),
            v((rows, DD), BF), v((rows, FD), BF), v((rows, DD)), v((rows, DD), BF), v((rows, 3 * DD), BF),
            v((8, DD)), v((rows, PIX), BF), v((2, 32 * 16, 8, LANES)), pltpu.SemaphoreType.DMA((2,)), pltpu.SemaphoreType.DMA((7,)),
        ],
        compiler_params=pltpu.CompilerParams(vmem_limit_bytes=63 * MB),
    )(counts, masked, cols, order, entering, norms, pos, patches, *weights)


def encoder_back_kernel(images, share, n, chunks, flat_in, grad_entering, norms_ref, *refs):
    names = SAVED + ENC_NAMES[1:]
    sources = refs[:20]
    flat, late_ref, sib_ref = refs[20:23]
    targets = refs[23:43]
    x, low, grad_hidden, side, low_mixed, grad_triple, norm_sums, stage, sem, in_sem = refs[43:53]
    cut = late_cut(share)
    steps = late_ref.shape[0] * chunks
    plane = Plane(share, n, chunks, steps, lambda group: cut + group, flat, sib_ref, late_ref, 0, refs[53:])
    barrier = pltpu.get_barrier_semaphore()
    for name in ("x", "y", "c"):
        pl.semaphore_signal(barrier, inc=1, device_id=plane.to[name], device_id_type=MESH)
    need = Moves(names, sources, targets, in_sem)
    need.start(
        "encoded", "dec_embed_w", "plain3", "scale3", "down_w", "slope", "act", "inner", "up_w", "plain2", "scale2",
        "mixed", "proj_w", "triple", "probs", "entry", "triple_w", "plain1", "scale1", "seen",
    )
    pl.semaphore_wait(barrier, 3)
    plane.begin()
    one, two, three_, load = plane.stage_one, plane.stage_two, plane.stage_three, plane.load
    if steps == 4:
        plan = [
            [(load, 0)], [(one, 0), (load, 1)], [(one, 1)], [(two, 0), (load, 2)], [(one, 2), (two, 1), (load, 3)], [(one, 3)],
            [(two, 2), (three_, 0), (three_, 1)], [(two, 3), (three_, 2)], [], [], [(three_, 3)],
        ]
    else:
        flow = [(load, 0)]
        for t in range(steps + 2):
            flow += [(stage_, s) for stage_, s in ((one, t), (two, t - 1), (load, t + 1), (three_, t - 2)) if 0 <= s < steps]
        size = -(-len(flow) // TICKS)
        plan = [flow[i * size : (i + 1) * size] for i in range(TICKS)]

    def tick():
        for stage_, s in plan.pop(0):
            stage_(s)

    writer = Writer(flat, stage, sem)
    writer.outer(6, need("encoded"), grad_entering)
    norm_sums[...] = jnp.zeros_like(norm_sums)
    side[...] = dot_nt(grad_entering[...], need("dec_embed_w")[...])
    plain3, scale3 = need("plain3"), need("scale3")

    def last(i):
        at = rows_at(i, KEEP)
        back, gain, shift = norm_grad(side[at, :], plain3[at, :], scale3[at, :], norms_ref[4:5, :])
        norm_sums[4:5, :] += gain
        norm_sums[5:6, :] += shift
        x[at, :] = back

    loop(images, last)
    tick()
    block_backward(x, KEEP, images, HEADS, need, norms_ref, norm_sums, (low, grad_hidden, side, low_mixed, grad_triple), writer, (1, 2, 3, 4), tick)
    low[...] = x[...].astype(BF)
    tick()
    writer.outer(0, need("seen"), low)
    tick()
    writer.small(5, norm_sums, 6)
    plane.finish()


def encoder_back(flat, grad_entering, saved, weights, norms, share, n_dp, n_pair):
    chunks = reduce_chunks(share, n_dp * n_pair)
    slab = slab_tiles(share, n_dp * n_pair) * 8
    groups = n_dp // 2 - late_cut(share)
    part = slab // chunks
    rows = grad_entering.shape[0]
    images = rows // KEEP
    vmem = pl.BlockSpec(memory_space=pltpu.VMEM)
    anyspec = pl.BlockSpec(memory_space=pl.ANY)

    def v(shape, kind=F32):
        return pltpu.VMEM(shape, kind)

    return pl.pallas_call(
        functools.partial(encoder_back_kernel, images, share, n_dp * n_pair, chunks),
        name="encoder_back",
        out_shape=[
            jax.ShapeDtypeStruct(flat.shape, flat.dtype),
            jax.ShapeDtypeStruct((groups, slab, LANES), F32),
            jax.ShapeDtypeStruct((groups * chunks, 4, part // 8, 8, LANES), F32),
        ],
        in_specs=[anyspec, vmem, vmem] + [anyspec] * 20,
        out_specs=[anyspec, vmem, anyspec],
        scratch_shapes=[like(one) for one in saved + weights]
        + [
            v((rows, D)), v((rows, D), BF), v((rows, F), BF), v((rows, D)), v((rows, D), BF), v((rows, 3 * D), BF),
            v((8, D)), v((2, 32 * 24, 8, LANES)), pltpu.SemaphoreType.DMA((2,)), pltpu.SemaphoreType.DMA((20,)),
        ]
        + plane_scratch(groups * chunks, part),
        input_output_aliases={0: 0},
        compiler_params=pltpu.CompilerParams(collective_id=2, has_side_effects=True, vmem_limit_bytes=63 * MB),
    )(flat, grad_entering, norms, *saved, *weights)[:2]


def positions(width):
    index = np.arange(PATCHES)
    quarter = width // 4
    freq = 10000.0 ** (-np.arange(quarter).astype(np.float32) / np.float32(quarter))
    row = (index // GRID).astype(np.float32)[:, None] * freq[None, :].astype(np.float32)
    column = (index % GRID).astype(np.float32)[:, None] * freq[None, :].astype(np.float32)
    table = np.concatenate([np.sin(row), np.cos(row), np.sin(column), np.cos(column)], axis=1).astype(np.float32)
    return jnp.asarray(np.pad(table, ((0, P_ROWS - PATCHES), (0, 0))))


def own_lines(flat, share, index):
    if share % LANES == 0:
        return flat.reshape(-1, LANES)
    rows = (share + LANES - 1) // LANES + 1
    return lax.dynamic_update_slice(jnp.zeros((rows * LANES,), flat.dtype), flat, (share * index % LANES,)).reshape(rows, LANES)


def own_flat(lines, share, index):
    if share % LANES == 0:
        return lines.reshape(-1)
    return lax.dynamic_slice(lines.reshape(-1), (share * index % LANES,), (share,))


def body(n_dp, n_pair, patches, patch_order, counts, master, moment1, moment2, block_rates, clip_limit, step_count):
    n = n_dp * n_pair
    share = master.shape[0]
    images = counts.shape[0]
    index = lax.axis_index("dp") * n_pair + lax.axis_index("pair")
    extra = jnp.zeros((8, LANES), F32).at[0, :images].set((PATCHES - counts).astype(F32))
    lines = own_lines(master, share, index)
    *held, enc_norms, dec_norms, masked = gather(lines, extra, share, n_dp, n_pair)
    parts = {i: matrix(one, i) for i, one in zip(BIG, held)}
    slots_at = patch_order[:, :KEEP]
    cols = slots_at[:, :, None]
    enc_weights = [parts[i] for i in (1, 2, 3, 4, 6)]
    *saved, entering = encoder(counts, patches, cols, positions(D), [parts[0]] + enc_weights, enc_norms)
    total = max(a for a, _ in ranges(share, n)) + slab_tiles(share, n)
    dec_weights = [parts[i] for i in (7, 8, 9, 10, 11)]
    flat, grad_entering, loss_local = decoder(total, counts, masked, patches, cols, slots_at, positions(DD), entering, dec_weights, dec_norms)
    flat, late = encoder_back(flat, grad_entering, saved, enc_weights, enc_norms, share, n_dp, n_pair)
    grad_lines, totals = reduce(flat, late, loss_local, lines.shape, share, n_dp, n_pair)
    grad_norm = totals[0, 0:1]
    loss = totals[1, 0:1] / masked[0]
    clipped = own_flat(grad_lines, share, index) * (clip_limit[0] / (grad_norm[0] + NORM_EPS))
    first = BETA_ONE * moment1 + (1.0 - BETA_ONE) * clipped
    second = BETA_TWO * moment2 + (1.0 - BETA_TWO) * clipped * clipped
    steps_done = step_count[0].astype(F32)
    position = index * share + jnp.arange(share)
    rate = jnp.where(position < ENC_PARAMS, block_rates[0], block_rates[1])
    update = first / (1.0 - BETA_ONE**steps_done) / (jnp.sqrt(second / (1.0 - BETA_TWO**steps_done)) + ADAM_EPS)
    master_new = master - rate * (update + DECAY * master)
    return (loss, grad_norm, first, second, master_new)


def solution(mesh):
    whole = P(("dp", "pair"))
    in_specs = (P(("dp", "pair"), None, None), P(("dp", "pair"), None), whole, whole, whole, whole, P(), P(), P())
    out_specs = (P(), P(), whole, whole, whole)
    step = functools.partial(body, mesh.shape["dp"], mesh.shape["pair"])
    return jax.shard_map(step, mesh=mesh, in_specs=in_specs, out_specs=out_specs, check_vma=False)
```

```python
import functools

import jax
import jax.numpy as jnp
import numpy as np
from jax import lax
from jax.experimental import pallas as pl
from jax.experimental.pallas import tpu as pltpu
from jax.sharding import PartitionSpec as P

MESH = pl.DeviceIdType.MESH
LANES = 128
TILE = 16 * LANES


def place():
    dp, pair = lax.axis_index("dp"), lax.axis_index("pair")
    return dp // 2, dp % 2, pair // 2, pair % 2


def slot_of(z, x, y, c):
    return (z * 2 + x) * 4 + y * 2 + c


def partners(z, x, y, c):
    return {
        "x": {"dp": z * 2 + (1 - x)},
        "y": {"pair": (1 - y) * 2 + c},
        "c": {"pair": y * 2 + (1 - c)},
        "up": {"dp": (z + 1) * 2 + x},
        "down": {"dp": (z - 1) * 2 + x},
    }


def greet(n_z, z, to):
    barrier = pltpu.get_barrier_semaphore()
    for name in ("x", "y", "c"):
        pl.semaphore_signal(barrier, inc=1, device_id=to[name], device_id_type=MESH)

    @pl.when(z < n_z - 1)
    def _():
        pl.semaphore_signal(barrier, inc=1, device_id=to["up"], device_id_type=MESH)

    @pl.when(z > 0)
    def _():
        pl.semaphore_signal(barrier, inc=1, device_id=to["down"], device_id_type=MESH)

    pl.semaphore_wait(barrier, 3 + jnp.where(z < n_z - 1, 1, 0) + jnp.where(z > 0, 1, 0))


def both(*conditions):
    total = conditions[0]
    for one in conditions[1:]:
        total = jnp.logical_and(total, one)
    return total


PIX, HEADS, F, DHEADS, FD, GRID, KEEP, D, DD, PATCHES = 768, 12, 3072, 16, 2048, 14, 64, 768, 512, 196
SHAPES = [(PIX, D), (D, 3 * D), (D, D), (D, F), (F, D), (6, D), (D, DD), (DD, 3 * DD), (DD, DD), (DD, FD), (FD, DD), (DD, PIX), (7, DD)]
SMALL = (5, 12)
ENC_PARAMS = 7672320
NORM_EPS = 1e-06
ADAM_EPS = 1e-08
BETA_ONE = 0.9
BETA_TWO = 0.95
DECAY = 0.05
MB = 1 << 20
CELL = 8 * LANES
BLOCK = 96


def make_entries():
    entries, row, tile = [], 0, 0
    for number, (rows, width) in enumerate(SHAPES):
        lines = rows * width // LANES
        cols = 1 if number in SMALL else width // LANES
        groups = -(-lines // (8 * cols))
        entries.append((row, lines, cols, tile, groups))
        row += lines
        tile += groups * cols
    return entries, row, tile


ENTRIES, ROWS, TILES = make_entries()
BIG = tuple(i for i in range(len(SHAPES)) if i not in SMALL)
MARGIN = 8 * max(cols for _, _, cols, _, _ in ENTRIES)


def first_tile(share, k):
    lo = share * k
    total = 0
    for row, lines, cols, tile, _ in ENTRIES:
        inside = jnp.logical_and(lo >= row * LANES, lo < (row + lines) * LANES)
        total = total + jnp.where(inside, tile + (lo - row * LANES) // (CELL * cols) * cols, 0)
    return total


def ranges(share, n):
    found = []
    for k in range(n):
        lo, hi = share * k, share * (k + 1)
        spans = []
        for row, lines, cols, tile, _ in ENTRIES:
            low, high = max(lo, row * LANES), min(hi, (row + lines) * LANES)
            if low < high:
                size = CELL * cols
                spans.append((tile + (low - row * LANES) // size * cols, tile + -(-(high - row * LANES) // size) * cols))
        found.append((spans[0][0], spans[-1][1]))
    return found


def slab_tiles(share, n):
    longest = max(b - a for a, b in ranges(share, n))
    return -(-longest // 24) * 24


def line_span(share, k):
    return share * k // LANES, (share * (k + 1) + LANES - 1) // LANES


def tiled(share, k, body):
    lo, hi = line_span(share, k)
    begin = first_tile(share, k)
    for number in SMALL + tuple(i for i in range(len(ENTRIES)) if i not in SMALL):
        row, lines, cols, tile, _ = ENTRIES[number]
        low = jnp.maximum(lo, row) - row
        high = jnp.minimum(hi, row + lines) - row
        size = 8 * cols

        def group(g, _, row=row, cols=cols, tile=tile, size=size):
            body(row + g * size - lo + MARGIN, tile + g * cols - begin, cols)
            return 0

        lax.fori_loop(jnp.where(low < high, low // size, 0), jnp.where(low < high, (high + size - 1) // size, 0), group, 0)


def wide_rows(rows):
    return -(-(rows + 2 * MARGIN) // 8) * 8


def pieces(share, n):
    spans = ranges(share, n)
    shared = [spans[k][1] > spans[k + 1][0] for k in range(n - 1)]
    plain, seams = [], []
    for number, (_, _, cols, tile, groups) in enumerate(ENTRIES):
        end = tile + groups * cols
        for k, (a, b) in enumerate(spans):
            low, high = max(a, tile), min(b, end)
            if low >= high:
                continue
            inner_low, inner_high = low, high
            if k > 0 and spans[k - 1][1] > low:
                inner_low = spans[k - 1][1]
            if k < n - 1 and spans[k + 1][0] < high:
                inner_high = spans[k + 1][0]
                seams.append((number, k, inner_high, high))
            if inner_low < inner_high:
                plain.append((number, k, inner_low, inner_high))
    return spans, plain, seams


def matrix(tiles_, number):
    rows, width = SHAPES[number]
    cols = width // LANES
    return tiles_.reshape(rows // 8, cols, 8, LANES).transpose(0, 2, 1, 3).reshape(rows, width)


def matrix_tiles(value):
    rows, width = value.shape
    cols = width // LANES
    return value.reshape(rows // 8, 8, cols, LANES).transpose(0, 2, 1, 3).reshape(rows * cols, LANES)


def gather_kernel(n_z, n_pair, share, lines_ref, extra_ref, *refs):
    outs = dict(zip(BIG, refs[: len(BIG)]))
    enc_norms, dec_norms, masked_ref = refs[len(BIG) : len(BIG) + 3]
    wide, out_ref, z_sem, plane_sem, second_sem, third_sem, flat_sem, line_sem, core_sem, recv_sem, put_sem = refs[len(BIG) + 3 :]
    n = n_z * 2 * n_pair
    total_tiles = out_ref.shape[1]
    small = total_tiles // 2 * 2 // 9
    large = total_tiles // 2 - small
    spans_of = ((0, large), (large, large), (2 * large, small), (2 * large + small, small), (2 * large, 2 * small))
    z, x, y, c = place()
    to = partners(z, x, y, c)
    me = slot_of(z, x, y, c)
    rows = lines_ref.shape[0]
    wide[0:MARGIN, :] = jnp.zeros((MARGIN, LANES), jnp.float32)
    wide[MARGIN + rows :, :] = jnp.zeros((wide.shape[0] - MARGIN - rows, LANES), jnp.float32)
    wide[MARGIN : MARGIN + rows, :] = lines_ref[...]

    def fill(line, tile, cols):
        for col in range(cols):
            out_ref[me, tile + col] = wide[pl.ds(line + col, 8, stride=cols), :].astype(out_ref.dtype)

    tiled(share, me, fill)
    out_ref[me, total_tiles - 2] = extra_ref[...].astype(out_ref.dtype)
    greet(n_z, z, to)

    def copy(slot, part, name, sem):
        at = pl.ds(*spans_of[part])
        return pltpu.make_async_remote_copy(
            out_ref.at[slot, at], out_ref.at[slot, at], sem, recv_sem.at[slot, 2 if part == 4 else part], device_id=to[name], device_id_type=MESH
        )

    def arrived(slot, part):
        copy(slot, part, "c", plane_sem.at[0, 0, 0]).wait_recv()

    def start(one):
        one.start()

    def stop(one):
        one.wait_send()

    def lines(t):
        for d in (0, 1):
            zz = z - t if d == 0 else z + t
            inside = zz >= 0 if d == 0 else zz < n_z
            more = z < n_z - 1 if d == 0 else z > 0
            fresh = both(t > 0, inside)
            held = jnp.logical_or(fresh, t == 0) if d == 0 else fresh
            yield d, zz, fresh, held, more

    def own_z(act):
        for d, more in ((0, z < n_z - 1), (1, z > 0)):
            for part in (0, 1):
                pl.when(more)(lambda d=d, part=part: act(copy(me, part, ("up", "down")[d], z_sem.at[0, d, part])))

    def onward_z(t, d, zz, fresh, more, act):
        for part in (0, 1):
            pl.when(both(fresh, more))(lambda part=part: act(copy(slot_of(zz, x, y, c), part, ("up", "down")[d], z_sem.at[t, d, part])))

    def plane_sends(t, d, zz, held, act):
        @pl.when(held)
        def _():
            for i, (part, name) in enumerate(((0, "x"), (1, "y"), (0, "y"), (1, "x"), (0, "c"), (1, "c"))):
                act(copy(slot_of(zz, x, y, c), part, name, plane_sem.at[t, d, i]))

    def first(t):
        for d, zz, fresh, held, more in lines(t):

            @pl.when(fresh)
            def _():
                for part in (0, 1):
                    arrived(slot_of(zz, x, y, c), part)

            onward_z(t, d, zz, fresh, more, start)
            plane_sends(t, d, zz, held, start)

    def second_items(zz):
        return ((0, slot_of(zz, 1 - x, y, c), "y"), (1, slot_of(zz, x, 1 - y, c), "x"))

    def second(t):
        for d, zz, _, held, _ in lines(t):

            @pl.when(held)
            def _():
                for part, slot, name in second_items(zz):
                    arrived(slot, part)
                    copy(slot, part, name, second_sem.at[t, d, part, 0]).start()
                    copy(slot, part, "c", second_sem.at[t, d, part, 1]).start()

    def third_items(zz):
        return ((0, slot_of(zz, x, 1 - y, c)), (1, slot_of(zz, 1 - x, y, c)), (0, slot_of(zz, 1 - x, 1 - y, c)), (1, slot_of(zz, 1 - x, 1 - y, c)))

    def third(t):
        for d, zz, _, held, _ in lines(t):

            @pl.when(held)
            def _():
                for i, (part, slot) in enumerate(third_items(zz)):
                    arrived(slot, part)
                    copy(slot, part, "c", third_sem.at[t, d, i]).start()

    near = ((2, me, "x"), (3, me, "y"), (2, me, "y"), (3, me, "x"), (2, me, "c"), (3, me, "c"))
    beside = ((2, slot_of(z, 1 - x, y, c), "y"), (3, slot_of(z, x, 1 - y, c), "x"))
    across = ((2, slot_of(z, x, 1 - y, c)), (3, slot_of(z, 1 - x, y, c)), (2, slot_of(z, 1 - x, 1 - y, c)), (3, slot_of(z, 1 - x, 1 - y, c)))

    def flat_sends(act, which):
        for i, (part, slot, name) in enumerate(near):
            if which == 0:
                act(copy(slot, part, name, flat_sem.at[i]))
        for i, (part, slot, name) in enumerate(beside):
            if which == 1:
                act(copy(slot, part, name, flat_sem.at[6 + i]))
                act(copy(slot, part, "c", flat_sem.at[8 + i]))
        for i, (part, slot) in enumerate(across):
            if which == 2:
                act(copy(slot, part, "c", flat_sem.at[10 + i]))

    def corner(zz, i):
        return slot_of(zz, i // 2, i % 2, c)

    def line_sends(t, act):
        for d, zz, fresh, _, more in lines(t):
            for i in range(4):
                go = jnp.logical_or(fresh, t == 0)
                pl.when(both(go, more))(lambda d=d, zz=zz, i=i: act(copy(corner(zz, i), 4, ("up", "down")[d], line_sem.at[t, d, i])))
                pl.when(fresh)(lambda d=d, zz=zz, i=i: act(copy(corner(zz, i), 4, "c", core_sem.at[t, d, i])))

    def along(t):
        for d, zz, fresh, _, _ in lines(t):

            @pl.when(fresh)
            def _():
                for i in range(4):
                    arrived(corner(zz, i), 4)

        @pl.when(t == 0)
        def _():
            for part, slot in across:
                arrived(slot, part)
            flat_sends(start, 2)

        line_sends(t, start)

    own_z(start)
    flat_sends(start, 0)
    for part, slot, _ in beside:
        arrived(slot, part)
    flat_sends(start, 1)

    def turn(t, _):
        pl.when(t < n_z)(lambda: first(t))
        pl.when(both(t >= 1, t < n_z + 1))(lambda: second(t - 1))
        pl.when(both(t >= 1, t < n_z + 1))(lambda: along(t - 1))
        pl.when(t >= 2)(lambda: third(t - 2))
        return 0

    lax.fori_loop(0, n_z + 2, turn, 0)
    own_z(stop)
    for which in range(3):
        flat_sends(stop, which)

    def finish(t, _):
        line_sends(t, stop)
        for d, zz, fresh, held, more in lines(t):
            onward_z(t, d, zz, fresh, more, stop)
            plane_sends(t, d, zz, held, stop)

            @pl.when(held)
            def _():
                for part, slot, name in second_items(zz):
                    copy(slot, part, name, second_sem.at[t, d, part, 0]).wait_send()
                    copy(slot, part, "c", second_sem.at[t, d, part, 1]).wait_send()
                for i, (part, slot) in enumerate(third_items(zz)):
                    copy(slot, part, "c", third_sem.at[t, d, i]).wait_send()
                for i in range(4):
                    for part in (0, 1):
                        arrived(slot_of(zz, i // 2, i % 2, 1 - c), part)

            @pl.when(fresh)
            def _():
                for i in range(4):
                    arrived(slot_of(zz, i // 2, i % 2, 1 - c), 4)

        return 0

    lax.fori_loop(0, n_z, finish, 0)
    for i in range(4):
        for part in (2, 3):
            arrived(slot_of(z, i // 2, i % 2, 1 - c), part)
    spans, plain, seams = pieces(share, n)
    puts = []

    def put(number, k, low, high):
        copy = pltpu.make_async_copy(
            out_ref.at[k, pl.ds(low - spans[k][0], high - low)], outs[number].at[pl.ds(low - ENTRIES[number][3], high - low)], put_sem.at[len(puts)]
        )
        copy.start()
        puts.append(copy)

    home = {}
    for number, k, low, high in plain + seams:
        if number in SMALL:
            home.update({tile: (k, tile - spans[k][0]) for tile in range(low, high)})
        elif (number, k, low, high) in plain:
            put(number, k, low, high)
    for number, k, low, high in seams:
        left = pl.ds(low - spans[k][0], high - low)
        right = pl.ds(low - spans[k + 1][0], high - low)
        total = out_ref[k, left].astype(jnp.float32) + out_ref[k + 1, right].astype(jnp.float32)
        out_ref[k, left] = total.astype(out_ref.dtype)
        if number not in SMALL:
            put(number, k, low, high)
    for number, target in zip(SMALL, (enc_norms, dec_norms)):
        row, lines_, _, tile, groups = ENTRIES[number]
        per = SHAPES[number][1] // LANES
        for group in range(groups):
            k, at = home[tile + group]
            value = out_ref[k, at].astype(jnp.float32)
            for line in range(group * 8, min(group * 8 + 8, lines_)):
                target[line // per : line // per + 1, line % per * LANES : (line % per + 1) * LANES] = value[line % 8 : line % 8 + 1, :]
    masked_ref[...] = jnp.zeros_like(masked_ref)

    def count(k, _):
        masked_ref[...] += jnp.sum(out_ref[k, out_ref.shape[1] - 2].astype(jnp.float32)[0:1, :], axis=1, keepdims=True)
        return 0

    lax.fori_loop(0, n, count, 0)
    for copy in puts:
        copy.wait()


def gather(lines, extra, share, n_dp, n_pair):
    n_z = n_dp // 2
    n = n_dp * n_pair
    tiles_ = slab_tiles(share, n) + 2
    _, plain, seams = pieces(share, n)
    dma = pltpu.SemaphoreType.DMA
    anyspec = pl.BlockSpec(memory_space=pl.ANY)
    vmem = pl.BlockSpec(memory_space=pltpu.VMEM)

    def s(shape, kind=jnp.float32):
        return jax.ShapeDtypeStruct(shape, kind)

    return pl.pallas_call(
        functools.partial(gather_kernel, n_z, n_pair, share),
        name="gather",
        out_shape=[s((ENTRIES[i][4] * ENTRIES[i][2], 8, LANES), jnp.bfloat16) for i in BIG] + [s(SHAPES[5]), s(SHAPES[12]), s((1, 1))],
        in_specs=[vmem, vmem],
        out_specs=[anyspec] * len(BIG) + [vmem] * 3,
        scratch_shapes=[
            pltpu.VMEM((wide_rows(lines.shape[0]), LANES), jnp.float32),
            pltpu.VMEM((n, tiles_, 8, LANES), jnp.bfloat16),
            dma((n_z, 2, 2)), dma((n_z, 2, 6)), dma((n_z, 2, 2, 2)), dma((n_z, 2, 4)), dma((14,)), dma((n_z, 2, 4)), dma((n_z, 2, 4)), dma((n, 4)),
            dma((len(plain) + len(seams),)),
        ],
        compiler_params=pltpu.CompilerParams(collective_id=0, has_side_effects=True, vmem_limit_bytes=60 * MB),
    )(lines, extra)


def reduce_chunks(share, n):
    rows = slab_tiles(share, n) * 8
    return max(d for d in (1, 2, 4) if rows % (2 * BLOCK * d) == 0)


def late_cut(share):
    return -(-ENTRIES[7][0] * LANES // (share * 8))


def pack(value, q_ref, t_ref, b):
    top = jnp.max(jnp.abs(value), axis=0, keepdims=True)
    inverse = jnp.where(top > 1e-30, 32767.0 / jnp.maximum(top, 1e-30), 0.0)
    q_ref[pl.ds(pl.multiple_of(b * BLOCK, BLOCK), BLOCK), :] = jnp.round(value * inverse).astype(jnp.int32).astype(jnp.int16)
    t_ref[pl.ds(b, 1), :] = top * (1.0 / 32767.0)


def unpack(q_ref, t_ref, b):
    return q_ref[pl.ds(pl.multiple_of(b * BLOCK, BLOCK), BLOCK), :].astype(jnp.int32).astype(jnp.float32) * t_ref[pl.ds(b, 1), :]


def message(qs, ts, qr, tr, sem, to):
    return (
        pltpu.make_async_remote_copy(qs, qr, sem.at[0, 0], sem.at[0, 1], device_id=to, device_id_type=MESH),
        pltpu.make_async_remote_copy(ts, tr, sem.at[1, 0], sem.at[1, 1], device_id=to, device_id_type=MESH),
    )


def slab_start(share, n, k):
    if n > 64:
        return first_tile(share, k)
    starts = [a for a, _ in ranges(share, n)]
    found = starts[0]
    for i in range(1, n):
        found = jnp.where(k >= i, starts[i], found)
    return found


class Plane:
    def __init__(self, share, n, chunks, steps, plane_of, grad, sib, keep, base, scratch):
        self.share, self.n, self.chunks, self.steps, self.plane_of = share, n, chunks, steps, plane_of
        self.grad, self.sib, self.keep, self.base = grad, sib, keep, base
        (self.gbuf, self.rbuf, self.q1s, self.q1r, self.q2s, self.q2r, self.t1s, self.t1r, self.t2s, self.t2r,
         self.sib_sem, self.load_sem, self.s1_sem, self.s2_sem) = scratch
        self.z, self.x, self.y, self.c = place()
        self.to = partners(self.z, self.x, self.y, self.c)
        self.rows = keep.shape[1] // chunks
        self.half = self.rows // 2

    def tiles_of(self, s, xx, yy, core):
        k = slot_of(self.plane_of(s // self.chunks), xx, yy, core)
        return pl.ds(slab_start(self.share, self.n, k) + s % self.chunks * (self.rows // 8), self.rows // 8)

    def kept(self, s, part, b):
        return self.base + s // self.chunks, pl.ds(pl.multiple_of(s % self.chunks * self.rows + part * self.half + b * BLOCK, BLOCK), BLOCK)

    def sibling(self, s, q, at=None):
        return pltpu.make_async_remote_copy(
            self.grad.at[at if at is not None else pl.ds(0, self.rows // 8)],
            self.sib.at[s, q],
            self.sib_sem.at[0, s, q],
            self.sib_sem.at[1, s, q],
            device_id=self.to["c"],
            device_id_type=MESH,
        )

    def begin(self):
        def one(s, _):
            for q in range(4):
                self.sibling(s, q, self.tiles_of(s, q // 2, q % 2, 1 - self.c)).start()
            return 0

        lax.fori_loop(0, self.steps, one, 0)

    def loads(self, s, q, at=None):
        slot = s % 2
        return pltpu.make_async_copy(self.grad.at[at if at is not None else pl.ds(0, self.rows // 8)], self.gbuf.at[slot, q], self.load_sem.at[slot, q])

    def other(self, s):
        return pltpu.make_async_copy(self.sib.at[s], self.rbuf.at[s % 2], self.load_sem.at[s % 2, 4])

    def load(self, s):
        for q in range(4):
            self.loads(s, q, self.tiles_of(s, q // 2, q % 2, self.c)).start()
        for q in range(4):
            self.sibling(s, q).wait_recv()
        self.other(s).start()

    def each(self, body):
        def one(b, _):
            body(b)
            return 0

        lax.fori_loop(0, self.half // BLOCK, one, 0, unroll=self.half // BLOCK)

    def own(self, slot, q, part, b):
        at = pl.ds(part * (self.half // 8) + b * (BLOCK // 8), BLOCK // 8)
        return (self.gbuf[slot, q, at] + self.rbuf[slot, q, at]).reshape(BLOCK, LANES)

    def first_message(self, s, part):
        i = pl.ds(part * 2, 2)
        return message(self.q1s.at[s, i], self.t1s.at[s, i], self.q1r.at[s, i], self.t1r.at[s, i], self.s1_sem.at[s, part], self.to[("x", "y")[part]])

    def second_message(self, s, part):
        return message(
            self.q2s.at[s, part], self.t2s.at[s, part], self.q2r.at[s, part], self.t2r.at[s, part], self.s2_sem.at[s, part], self.to[("y", "x")[part]]
        )

    def quarter(self, part, other, mine):
        if part == 0:
            return (self.x if mine else 1 - self.x) * 2 + other
        return other * 2 + (self.y if mine else 1 - self.y)

    def stage_one(self, s):
        slot = s % 2
        for q in range(4):
            self.loads(s, q).wait()
        self.other(s).wait()
        for part in (0, 1):
            for other in (0, 1):
                q = self.quarter(part, other, False)
                i = part * 2 + other
                self.each(lambda b: pack(self.own(slot, q, part, b), self.q1s.at[s, i], self.t1s.at[s, i], b))
            for one in self.first_message(s, part):
                one.start()

    def stage_two(self, s):
        slot = s % 2
        for part in (0, 1):
            for one in self.first_message(s, part):
                one.wait_recv()
            here = (self.y, self.x)[part]
            away = self.quarter(part, 1 - here, True)
            i = part * 2 + 1 - here
            self.each(
                lambda b: pack(
                    self.own(slot, away, part, b) + unpack(self.q1r.at[s, i], self.t1r.at[s, i], b), self.q2s.at[s, part], self.t2s.at[s, part], b
                )
            )
            for one in self.second_message(s, part):
                one.start()
        for part in (0, 1):
            here = (self.y, self.x)[part]
            k = part * 2 + here

            def store(b, part=part, k=k):
                group, at = self.kept(s, part, b)
                self.keep[group, at, :] = self.own(slot, self.x * 2 + self.y, part, b) + unpack(self.q1r.at[s, k], self.t1r.at[s, k], b)

            self.each(store)

    def stage_three(self, s):
        for part in (0, 1):
            for one in self.second_message(s, part):
                one.wait_recv()

            def body(b, part=part):
                group, at = self.kept(s, part, b)
                self.keep[group, at, :] += unpack(self.q2r.at[s, part], self.t2r.at[s, part], b)

            self.each(body)

    def finish(self):
        def one(s, _):
            for q in range(4):
                self.sibling(s, q).wait_send()
            for part in (0, 1):
                for two in self.first_message(s, part):
                    two.wait_send()
                for two in self.second_message(s, part):
                    two.wait_send()
            return 0

        lax.fori_loop(0, self.steps, one, 0)


def message_scratch(part, *leads):
    half = part // 2
    marks = (half // BLOCK + 7) // 8 * 8
    return [pltpu.VMEM(lead + (half, LANES), jnp.int16) for lead in leads] + [pltpu.VMEM(lead + (marks, LANES), jnp.float32) for lead in leads]


def plane_scratch(steps, part):
    dma = pltpu.SemaphoreType.DMA
    return [
        pltpu.VMEM((2, 4, part // 8, 8, LANES), jnp.float32),
        pltpu.VMEM((2, 4, part // 8, 8, LANES), jnp.float32),
        *message_scratch(part, (steps, 4), (steps, 4), (steps, 2), (steps, 2)),
        dma((2, steps, 4)), dma((2, 5)), dma((steps, 2, 2, 2)), dma((steps, 2, 2, 2)),
    ]


def reduce_kernel(n_z, n_pair, chunks, share, grad_ref, late_ref, loss_in, lines_ref, total_ref, sib_ref,
                  wide, mine, shared, send_sem, recv_sem, keep, late_sem, zs, zr, tzs, tzr, z_sem, *scratch):
    z, x, y, c = place()
    to = partners(z, x, y, c)
    n = n_z * 2 * n_pair
    me = slot_of(z, x, y, c)
    cut = late_cut(share)
    steps, late = cut * chunks, (n_z - cut) * chunks
    home = jnp.where(z < cut, cut - 1, z)

    def order(j):
        low = z < cut // 2
        far = jnp.where(low, cut - 1 - j, j)
        moved = jnp.where(low, jnp.where(far > z, far, far - 1), jnp.where(far < z, far, far + 1))
        return jnp.where(z >= cut, j, jnp.where(j == cut - 1, z, moved))

    plane = Plane(share, n, chunks, steps, order, grad_ref, sib_ref, keep, 0, scratch)

    def z_message(spot, name):
        d = 0 if name == "up" else 1
        return message(zs.at[spot], tzs.at[spot], zr.at[d, spot], tzr.at[d, spot], z_sem.at[d, spot], to[name])

    def stage_four(group, chunk, zz):
        spot = zz * chunks + chunk

        def lines(part, b):
            return pl.ds(pl.multiple_of(chunk * plane.rows + part * plane.half + b * BLOCK, BLOCK), BLOCK)

        for d, name, has, onward in ((0, "up", z > 0, zz > z), (1, "down", z < n_z - 1, zz < z)):
            back = zz >= z if d == 0 else zz <= z

            @pl.when(both(has, back))
            def _():
                for one in z_message(spot, name):
                    one.wait_recv()
                for part in (0, 1):

                    def add(b, part=part):
                        keep[group, lines(part, b), :] += unpack(zr.at[d, spot, part], tzr.at[d, spot, part], b)

                    plane.each(add)

            @pl.when(onward)
            def _():
                for part in (0, 1):
                    plane.each(lambda b, part=part: pack(keep[group, lines(part, b), :], zs.at[spot, part], tzs.at[spot, part], b))
                for one in z_message(spot, name):
                    one.start()

    def spread_lines(line, tile, cols):
        for col in range(cols):
            wide[pl.ds(line + col, 8, stride=cols), :] = keep[home, pl.ds(pl.multiple_of((tile + col) * 8, 8), 8), :]

    count_lines = lines_ref.shape[0]
    tall = 128

    def by_lines(body):
        def one(i, _):
            body(pl.multiple_of(i * tall, tall), tall)
            return 0

        lax.fori_loop(0, count_lines // tall, one, 0)
        if count_lines % tall:
            body(count_lines // tall * tall, count_lines % tall)

    barrier = pltpu.get_barrier_semaphore()

    def peer(d):
        k = lax.rem(me + d, n)
        return {"dp": k // n_pair, "pair": lax.rem(k, n_pair)}

    def hello(d, _):
        pl.semaphore_signal(barrier, inc=1, device_id=peer(d), device_id_type=MESH)
        return 0

    lax.fori_loop(1, n, hello, 0)
    kept = pltpu.make_async_copy(late_ref, keep.at[pl.ds(cut, n_z - cut)], late_sem)
    kept.start()
    pl.semaphore_wait(barrier, n - 1)
    plane.begin()
    plane.load(0)
    kept.wait()
    lag = 0

    def turn(t, _):
        pl.when(t < steps)(lambda: plane.stage_one(t))
        pl.when(both(t >= 1, t <= steps))(lambda: plane.stage_two(t - 1))
        pl.when(t + 1 < steps)(lambda: plane.load(t + 1))
        pl.when(both(t >= 2, t <= steps + 1))(lambda: plane.stage_three(t - 2))
        early, main = t - z, t - 3 - lag
        pl.when(both(early >= 0, early < late))(lambda: stage_four(cut + early // chunks, lax.rem(early, chunks), cut + early // chunks))
        pl.when(both(main >= 0, main < steps))(lambda: stage_four(main // chunks, lax.rem(main, chunks), order(main // chunks)))
        return 0

    lax.fori_loop(0, max(steps + 3, late + n_z), turn, 0)
    tiled(share, me, spread_lines)
    lo, _ = line_span(share, me)
    mine[...] = jnp.zeros_like(mine)

    def squares(start, size):
        value = wide[pl.ds(MARGIN + start, size), :]
        if share % LANES:
            line = lax.broadcasted_iota(jnp.int32, (size, LANES), 0) + lo + start
            spot = line * LANES + lax.broadcasted_iota(jnp.int32, (size, LANES), 1)
            inside = jnp.logical_and(spot >= share * me, spot < share * (me + 1))
            value = jnp.where(inside, value, 0.0)
        lines_ref[pl.ds(start, size), :] = value
        mine[0:1, :] += jnp.sum(value * value, axis=0, keepdims=True)

    by_lines(squares)
    lane = lax.broadcasted_iota(jnp.int32, (1, LANES), 1)
    mine[1:2, :] = jnp.where(lane == 0, loss_in[0:1, 0:1], 0.0)
    shared[me] = mine[...]

    def send(d):
        return pltpu.make_async_remote_copy(mine, shared.at[me], send_sem.at[d], recv_sem.at[d], device_id=peer(d), device_id_type=MESH)

    def go(d, _):
        send(d).start()
        return 0

    def stop(d, _):
        send(d).wait()
        return 0

    lax.fori_loop(1, n, go, 0)
    plane.finish()

    def finish(spot, _):
        zz = spot // chunks
        for name, sent in (("up", zz > z), ("down", zz < z)):

            @pl.when(sent)
            def _():
                for one in z_message(spot, name):
                    one.wait_send()

        return 0

    lax.fori_loop(0, n_z * chunks, finish, 0)
    lax.fori_loop(1, n, stop, 0)

    def add(k, total):
        return total + shared[k]

    total = lax.fori_loop(0, n, add, jnp.zeros((8, LANES), jnp.float32))
    norm_ = jnp.sqrt(jnp.sum(total[0:1, :], axis=1, keepdims=True))
    loss_sum = jnp.sum(total[1:2, :], axis=1, keepdims=True)
    total_ref[...] = jnp.where(lax.broadcasted_iota(jnp.int32, (8, LANES), 0) == 0, norm_, loss_sum)


def reduce(flat, late, loss, shape, share, n_dp, n_pair):
    n_z, n = n_dp // 2, n_dp * n_pair
    chunks = reduce_chunks(share, n)
    rows = slab_tiles(share, n) * 8
    part = rows // chunks
    steps = late_cut(share) * chunks
    spots = n_z * chunks
    anyspec = pl.BlockSpec(memory_space=pl.ANY)
    vmem = pl.BlockSpec(memory_space=pltpu.VMEM)
    line = jax.ShapeDtypeStruct(shape, jnp.float32)
    dma = pltpu.SemaphoreType.DMA
    return pl.pallas_call(
        functools.partial(reduce_kernel, n_z, n_pair, chunks, share),
        name="reduce_scatter",
        out_shape=[line, jax.ShapeDtypeStruct((8, LANES), jnp.float32), jax.ShapeDtypeStruct((steps, 4, part // 8, 8, LANES), jnp.float32)],
        in_specs=[anyspec, anyspec, vmem],
        out_specs=[vmem, vmem, anyspec],
        scratch_shapes=[
            pltpu.VMEM((wide_rows(shape[0]), LANES), jnp.float32),
            pltpu.VMEM((8, LANES), jnp.float32),
            pltpu.VMEM((n, 8, LANES), jnp.float32),
            dma((n,)),
            dma((n,)),
            pltpu.VMEM((n_z, rows, LANES), jnp.float32),
            dma,
            *message_scratch(part, (spots, 2), (2, spots, 2)),
            dma((2, spots, 2, 2)),
            *plane_scratch(steps, part),
        ],
        compiler_params=pltpu.CompilerParams(collective_id=1, has_side_effects=True, vmem_limit_bytes=60 * MB),
    )(flat, late, loss)[:2]


NEG_FILL = -1000000000.0
P_ROWS = 208
BF = jnp.bfloat16
F32 = jnp.float32


def dot_nn(left, right):
    return lax.dot_general(left, right, (((1,), (0,)), ((), ())), preferred_element_type=F32)


def dot_nt(left, right):
    return lax.dot_general(left, right, (((1,), (1,)), ((), ())), preferred_element_type=F32)


def loop(count, body, unroll=1):
    def step(i, _):
        body(i)
        return 0

    lax.fori_loop(0, count, step, 0, unroll=unroll)


def rows_at(i, size):
    return pl.ds(pl.multiple_of(i * size, size), size)


def norm(x):
    centered = x - jnp.mean(x, axis=-1, keepdims=True)
    scale = lax.rsqrt(jnp.mean(centered * centered, axis=-1, keepdims=True) + NORM_EPS)
    return centered * scale, scale


def norm_grad(grad, plain, scale, gain):
    inner = grad * gain
    back = scale * (inner - jnp.mean(inner, axis=-1, keepdims=True) - plain * jnp.mean(inner * plain, axis=-1, keepdims=True))
    return back, jnp.sum(grad * plain, axis=0, keepdims=True), jnp.sum(grad, axis=0, keepdims=True)


def gelu_pair(h):
    cumulative = 0.5 * (1.0 + lax.erf(h * 0.7071067811865476))
    density = jnp.exp(-0.5 * h * h) * 0.3989422804014327
    return h * cumulative, cumulative + h * density


def head_masks(size):
    lane = lax.broadcasted_iota(jnp.int32, (1, LANES), 1)
    shift = size.bit_length() - 1
    return [jnp.where((lane >> shift) == h, 1.0, 0.0).astype(BF) for h in range(LANES // size)]


def three(value):
    top = value.astype(BF)
    rest = value - top.astype(F32)
    mid = rest.astype(BF)
    return top, mid, (rest - mid.astype(F32)).astype(BF)


class Moves:
    def __init__(self, names, sources, targets, sems):
        self.targets = dict(zip(names, targets))
        self.copies = {name: pltpu.make_async_copy(a, b, sems.at[i]) for i, (name, a, b) in enumerate(zip(names, sources, targets))}
        self.open = []

    def start(self, *names):
        for name in names or self.copies:
            self.copies[name].start()
            self.open.append(name)

    def __call__(self, name):
        if name in self.open:
            self.copies[name].wait()
            self.open.remove(name)
        return self.targets[name]

    def close(self):
        for name in list(self.open):
            self(name)


def wide_attention(width, heads, rows, triple, bias, probs, mixed):
    size = width // heads
    per = LANES // size
    masks = head_masks(size)
    for g in range(width // LANES):
        q, k, v = (triple[:, t * width + g * LANES : t * width + (g + 1) * LANES] for t in range(3))
        v_side = v.T
        parts = []
        for h in range(per):
            s = dot_nt(k * masks[h], q) * size ** (-0.5) + bias[...]
            e = jnp.exp(s - jnp.max(s, axis=0, keepdims=True))
            p = e * (1.0 / jnp.sum(e, axis=0, keepdims=True))
            probs[g * per + h] = p
            parts.append(dot_nn(v_side[h * size : (h + 1) * size, :], p.astype(BF)))
        mixed[:, g * LANES : (g + 1) * LANES] = jnp.concatenate(parts, axis=0).T.astype(BF)


def wide_attention_back(width, heads, triple, probs, low_mixed, grad_triple):
    size = width // heads
    per = LANES // size
    masks = head_masks(size)
    for g in range(width // LANES):
        lanes = [slice(t * width + g * LANES, t * width + (g + 1) * LANES) for t in range(3)]
        q, k, v = (triple[:, lane] for lane in lanes)
        dm = low_mixed[:, g * LANES : (g + 1) * LANES]
        k_side = k.T
        parts, dk, dv = [], 0.0, 0.0
        for h in range(per):
            p = probs[g * per + h]
            dp = dot_nt(v * masks[h], dm)
            ds = (p * (dp - jnp.sum(p * dp, axis=0, keepdims=True))).astype(BF)
            dv = dv + dot_nn(p.astype(BF), dm * masks[h])
            dk = dk + dot_nn(ds, q * masks[h])
            parts.append(dot_nn(k_side[h * size : (h + 1) * size, :], ds))
        grad_triple[:, lanes[0]] = (jnp.concatenate(parts, axis=0).T * size ** (-0.5)).astype(BF)
        grad_triple[:, lanes[1]] = (dk * size ** (-0.5)).astype(BF)
        grad_triple[:, lanes[2]] = dv.astype(BF)


def block_forward(x, rows, images, heads, need, norms, key_bias, saved, done=lambda *names: None):
    entry, plain1, scale1, triple, probs, mixed, plain2, scale2, inner, act, slope = saved
    width = x.shape[1]
    size = width // heads
    per = LANES // size
    groups = width // LANES

    def first(i):
        at = rows_at(i, rows)
        plain, scale = norm(x[at, :])
        plain1[at, :] = plain
        scale1[at, :] = scale
        entry[at, :] = (plain * norms[0:1, :] + norms[1:2, :]).astype(BF)

    loop(images, first, 2)

    done("entry", "plain1", "scale1")
    triple_w = need("triple_w")

    def project(j):
        at = rows_at(j, 256)
        triple[:, at] = dot_nn(entry[...], triple_w[:, at]).astype(BF)

    loop(3 * width // 256, project, 3)
    done("triple")
    masks = head_masks(size)

    def attend(i):
        at = rows_at(i, rows)
        bias = key_bias(i)
        for g in range(groups):
            q = triple[at, g * LANES : (g + 1) * LANES]
            k = triple[at, width + g * LANES : width + (g + 1) * LANES]
            v = triple[at, 2 * width + g * LANES : 2 * width + (g + 1) * LANES]
            v_side = v.T
            parts = []
            for h in range(per):
                s = dot_nt(k * masks[h], q) * size ** (-0.5) + bias
                e = jnp.exp(s - jnp.max(s, axis=0, keepdims=True))
                p = e * (1.0 / jnp.sum(e, axis=0, keepdims=True))
                probs[i * groups + g, h * rows : (h + 1) * rows, :] = p
                parts.append(dot_nn(v_side[h * size : (h + 1) * size, :], p.astype(BF)))
            mixed[at, g * LANES : (g + 1) * LANES] = jnp.concatenate(parts, axis=0).T.astype(BF)

    if callable(key_bias):
        loop(images, attend)
    else:
        wide_attention(width, heads, rows, triple, key_bias, probs, mixed)
    done("probs", "mixed")
    proj_w = need("proj_w")

    def middle(j):
        at = rows_at(j, 256)
        x[:, at] += dot_nn(mixed[...], proj_w[:, at])

    loop(width // 256, middle, width // 256)

    def second(i):
        at = rows_at(i, rows)
        plain, scale = norm(x[at, :])
        plain2[at, :] = plain
        scale2[at, :] = scale
        inner[at, :] = (plain * norms[2:3, :] + norms[3:4, :]).astype(BF)

    loop(images, second, 2)
    done("plain2", "scale2", "inner")
    up_w = need("up_w")
    hidden = up_w.shape[1]

    def up(j):
        at = rows_at(j, 256)
        value, gradient = gelu_pair(dot_nn(inner[...], up_w[:, at]))
        act[:, at] = value.astype(BF)
        slope[:, at] = gradient

    loop(hidden // 256, up, 4)
    done("act", "slope")
    down_w = need("down_w")

    def down(j):
        at = rows_at(j, 256)
        x[:, at] += dot_nn(act[...], down_w[:, at])

    loop(width // 256, down, width // 256)


class Writer:
    def __init__(self, flat, stage, sem):
        self.flat, self.stage, self.sem = flat, stage, sem
        self.pending = {}

    def settle(self, s):
        if s in self.pending:
            self.pending.pop(s).wait()

    def outer(self, number, left, right, chunk=256):
        _, _, cols, tile, _ = ENTRIES[number]
        rows = left.shape[1]
        count = rows // chunk
        tall = chunk // 8
        before = dict(self.pending)

        def copy(i, s):
            return pltpu.make_async_copy(
                self.stage.at[s, pl.ds(0, tall * cols)], self.flat.at[pl.ds(tile + i * tall * cols, tall * cols)], self.sem.at[s]
            )

        def body(i):
            s = lax.rem(i, 2)
            for early in before:
                pl.when(i == early)(before[early].wait)

            @pl.when(i >= 2)
            def _():
                copy(i - 2, s).wait()

            side = left[:, rows_at(i, chunk)].T
            for c in range(0, cols, 2):
                value = dot_nn(side, right[:, c * LANES : (c + 2) * LANES])
                for d in range(2):
                    self.stage[s, pl.ds(c + d, tall, stride=cols)] = value[:, d * LANES : (d + 1) * LANES].reshape(tall, 8, LANES)
            copy(i, s).start()

        loop(count, body)
        self.pending = {(count - 2) % 2: copy(count - 2, (count - 2) % 2), (count - 1) % 2: copy(count - 1, (count - 1) % 2)}

    def small(self, number, norm_sums, count, extra=0):
        _, _, _, tile, groups = ENTRIES[number]
        per = SHAPES[number][1] // LANES
        self.settle(0)
        self.stage[0, 0 : groups + extra] = jnp.zeros((groups + extra, 8, LANES), F32)
        for r in range(count):
            for c in range(per):
                line = r * per + c
                self.stage[0, line // 8, line % 8 : line % 8 + 1, :] = norm_sums[r : r + 1, c * LANES : (c + 1) * LANES]
        copy = pltpu.make_async_copy(self.stage.at[0, pl.ds(0, groups + extra)], self.flat.at[pl.ds(tile, groups + extra)], self.sem.at[0])
        copy.start()
        copy.wait()
        self.settle(1)


def block_backward(grad, rows, images, heads, need, norms, norm_sums, extra, writer, numbers, tick=lambda: None):
    low, grad_hidden, side, low_mixed, grad_triple = extra
    width = grad.shape[1]
    size = width // heads
    per = LANES // size
    groups = width // LANES
    low[...] = grad[...].astype(BF)
    down_w, slope = need("down_w"), need("slope")
    hidden = down_w.shape[0]

    def back_up(j):
        at = rows_at(j, 256)
        grad_hidden[:, at] = (dot_nt(low[...], down_w[at, :]) * slope[:, at]).astype(BF)

    loop(hidden // 256, back_up, 4)
    tick()
    writer.outer(numbers[3], need("act"), low)
    tick()
    writer.outer(numbers[2], need("inner"), grad_hidden)
    tick()
    up_w = need("up_w")

    def back_inner(j):
        at = rows_at(j, 256)
        side[:, at] = dot_nt(grad_hidden[...], up_w[at, :])

    loop(width // 256, back_inner, width // 256)
    tick()
    plain2, scale2 = need("plain2"), need("scale2")

    def second(i):
        at = rows_at(i, rows)
        back, gain, shift = norm_grad(side[at, :], plain2[at, :], scale2[at, :], norms[2:3, :])
        norm_sums[2:3, :] += gain
        norm_sums[3:4, :] += shift
        total = grad[at, :] + back
        grad[at, :] = total
        low[at, :] = total.astype(BF)

    loop(images, second, 2)
    writer.outer(numbers[1], need("mixed"), low)
    proj_w = need("proj_w")

    def back_mixed(j):
        at = rows_at(j, 256)
        low_mixed[:, at] = dot_nt(low[...], proj_w[at, :]).astype(BF)

    loop(width // 256, back_mixed, width // 256)
    tick()
    triple, probs = need("triple"), need("probs")
    masks = head_masks(size)

    def attend(i):
        at = rows_at(i, rows)
        for g in range(groups):
            lanes = [slice(t * width + g * LANES, t * width + (g + 1) * LANES) for t in range(3)]
            q, k, v = (triple[at, lane] for lane in lanes)
            dm = low_mixed[at, g * LANES : (g + 1) * LANES]
            k_side = k.T
            parts, dk, dv = [], 0.0, 0.0
            for h in range(per):
                p = probs[i * groups + g, h * rows : (h + 1) * rows, :]
                dp = dot_nt(v * masks[h], dm)
                ds = (p * (dp - jnp.sum(p * dp, axis=0, keepdims=True))).astype(BF)
                dv = dv + dot_nn(p.astype(BF), dm * masks[h])
                dk = dk + dot_nn(ds, q * masks[h])
                parts.append(dot_nn(k_side[h * size : (h + 1) * size, :], ds))
            dq = jnp.concatenate(parts, axis=0).T
            grad_triple[at, lanes[0]] = (dq * size ** (-0.5)).astype(BF)
            grad_triple[at, lanes[1]] = (dk * size ** (-0.5)).astype(BF)
            grad_triple[at, lanes[2]] = dv.astype(BF)

    if probs.shape[1] == probs.shape[2] and probs.shape[0] == heads:
        wide_attention_back(width, heads, triple, probs, low_mixed, grad_triple)
    else:
        loop(images, attend)
    tick()
    writer.outer(numbers[0], need("entry"), grad_triple)
    tick()
    triple_w = need("triple_w")

    def back_entry(j):
        at = rows_at(j, 256)
        side[:, at] = dot_nt(grad_triple[...], triple_w[at, :])

    loop(width // 256, back_entry, width // 256)
    tick()
    plain1, scale1 = need("plain1"), need("scale1")

    def first(i):
        at = rows_at(i, rows)
        back, gain, shift = norm_grad(side[at, :], plain1[at, :], scale1[at, :], norms[0:1, :])
        norm_sums[0:1, :] += gain
        norm_sums[1:2, :] += shift
        grad[at, :] += back

    loop(images, first, 2)


TICKS = 11
SAVED = ("seen", "entry", "plain1", "scale1", "triple", "probs", "mixed", "plain2", "scale2", "inner", "act", "slope", "plain3", "scale3", "encoded")
ENC_NAMES = ("embed_w", "triple_w", "proj_w", "up_w", "down_w", "dec_embed_w")
DEC_NAMES = ("triple_w", "proj_w", "up_w", "down_w", "head_w")


def saved_shapes(rows):
    s = jax.ShapeDtypeStruct
    return [
        s((rows, D), BF), s((rows, D), BF), s((rows, D), F32), s((rows, 1), F32), s((rows, 3 * D), BF),
        s((HEADS, rows, rows), F32), s((rows, D), BF), s((rows, D), F32), s((rows, 1), F32), s((rows, D), BF),
        s((rows, F), BF), s((rows, F), F32), s((rows, D), F32), s((rows, 1), F32), s((rows, D), BF),
    ]


def like(shape):
    return pltpu.VMEM(shape.shape, shape.dtype)


def pad_patches(patches, padded, images):
    padded[...] = jnp.zeros_like(padded)
    for i in range(images):
        padded[i * P_ROWS : i * P_ROWS + PATCHES, :] = patches[i]


def encoder_kernel(images, counts_ref, cols_ref, norms_ref, *refs):
    pos_hbm, patches_hbm, *weights_hbm = refs[:8]
    outs = refs[8:23]
    entering = refs[23]
    pos, patches, *weights = refs[24:32]
    saved = dict(zip(SAVED, refs[32:47]))
    x, place_, pos_split, padded, bias, in_sem, out_sem = refs[47:]
    need = Moves(("pos", "patches") + ENC_NAMES, [pos_hbm, patches_hbm] + weights_hbm, [pos, patches] + weights, in_sem)
    need.start()
    put = Moves(SAVED, [saved[name] for name in SAVED], outs, out_sem)
    rows = images * KEEP
    key = lax.broadcasted_iota(jnp.int32, (KEEP, rows), 0)
    query = lax.broadcasted_iota(jnp.int32, (KEEP, rows), 1)
    for i in range(images):
        inside = jnp.logical_and(jnp.logical_and(query >= i * KEEP, query < (i + 1) * KEEP), key < counts_ref[i])
        bias[i * KEEP : (i + 1) * KEEP, :] = jnp.where(inside, 0.0, NEG_FILL)
    need("pos")
    for t, part in enumerate(three(pos[...])):
        pos_split[t] = part
    pad_patches(need("patches"), padded, images)
    spots = lax.broadcasted_iota(jnp.int32, (KEEP, P_ROWS), 1)
    seen = saved["seen"]

    def select(i):
        at = rows_at(i, KEEP)
        pick = jnp.where(spots == cols_ref[i], 1.0, 0.0).astype(BF)
        seen[at, :] = dot_nn(pick, padded[rows_at(i, P_ROWS), :]).astype(BF)
        place_[at, :] = dot_nn(pick, pos_split[0]) + dot_nn(pick, pos_split[1]) + dot_nn(pick, pos_split[2])

    loop(images, select, 2)
    put.start("seen")
    embed_w = need("embed_w")

    def embed(j):
        at = rows_at(j, 256)
        x[:, at] = dot_nn(seen[...], embed_w[:, at]) + place_[:, at]

    loop(D // 256, embed, D // 256)
    block_forward(x, KEEP, images, HEADS, need, norms_ref, bias, [saved[name] for name in SAVED[1:12]], put.start)
    plain3, scale3, encoded = (saved[name] for name in SAVED[12:])

    def last(i):
        at = rows_at(i, KEEP)
        plain, scale = norm(x[at, :])
        plain3[at, :] = plain
        scale3[at, :] = scale
        encoded[at, :] = (plain * norms_ref[4:5, :] + norms_ref[5:6, :]).astype(BF)

    loop(images, last, 2)
    put.start("plain3", "scale3", "encoded")
    entering[...] = dot_nn(encoded[...], need("dec_embed_w")[...])
    put.close()


def encoder(counts, patches, cols, pos, weights, norms):
    images = counts.shape[0]
    rows = images * KEEP
    vmem = pl.BlockSpec(memory_space=pltpu.VMEM)
    anyspec = pl.BlockSpec(memory_space=pl.ANY)
    shapes = saved_shapes(rows)
    return pl.pallas_call(
        functools.partial(encoder_kernel, images),
        name="encoder",
        out_shape=shapes + [jax.ShapeDtypeStruct((rows, DD), F32)],
        in_specs=[pl.BlockSpec(memory_space=pltpu.SMEM), vmem, vmem] + [anyspec] * 8,
        out_specs=[anyspec] * 15 + [vmem],
        scratch_shapes=[like(one) for one in [pos, patches] + weights + shapes]
        + [
            pltpu.VMEM((rows, D), F32), pltpu.VMEM((rows, D), F32), pltpu.VMEM((3, P_ROWS, D), BF), pltpu.VMEM((images * P_ROWS, PIX), BF),
            pltpu.VMEM((rows, rows), F32), pltpu.SemaphoreType.DMA((8,)), pltpu.SemaphoreType.DMA((15,)),
        ],
        compiler_params=pltpu.CompilerParams(vmem_limit_bytes=60 * MB),
    )(counts, cols, norms, pos, patches, *weights)


def decoder_kernel(images, counts_ref, masked_ref, cols_ref, rows_ref, entering_ref, norms_ref, *refs):
    pos_hbm, patches_hbm, *weights_hbm = refs[:7]
    flat, grad_entering, loss_ref = refs[7:10]
    pos, patches, *weights = refs[10:17]
    (x, hide, entry, plain1, scale1, triple, probs, mixed, plain2, scale2, inner, act, slope, plain3, scale3, final, grad_pred,
     low, grad_hidden, side, low_mixed, grad_triple, norm_sums, padded, stage, sem, in_sem) = refs[17:]
    need = Moves(("pos", "patches") + DEC_NAMES, [pos_hbm, patches_hbm] + weights_hbm, [pos, patches] + weights, in_sem)
    need.start()
    saved = (entry, plain1, scale1, triple, probs, mixed, plain2, scale2, inner, act, slope)
    need.targets.update(zip(SAVED[1:12], saved))
    lane = lax.broadcasted_iota(jnp.int32, (P_ROWS, KEEP), 1)
    spot = lax.broadcasted_iota(jnp.int32, (P_ROWS, KEEP), 0)
    line = lax.broadcasted_iota(jnp.int32, (P_ROWS, 1), 0)
    need("pos")

    def start(i):
        at = rows_at(i, P_ROWS)
        hit = jnp.where(jnp.logical_and(spot == rows_ref[pl.ds(i, 1), 0:KEEP], lane < counts_ref[i]), 1.0, 0.0)
        shown = jnp.max(hit, axis=1, keepdims=True)
        pick = hit.astype(BF)
        top, mid, end = three(entering_ref[rows_at(i, KEEP), :])
        picked = dot_nn(pick, top) + dot_nn(pick, mid) + dot_nn(pick, end)
        x[at, :] = jnp.where(shown > 0.0, picked, norms_ref[6:7, :]) + pos[...]
        hide[at, :] = jnp.where(jnp.logical_and(line < PATCHES, shown == 0.0), 1.0, 0.0)

    loop(images, start, 2)
    bias = jnp.where(line < PATCHES, 0.0, NEG_FILL)
    block_forward(x, P_ROWS, images, DHEADS, need, norms_ref, lambda i: bias, saved)

    def last(i):
        at = rows_at(i, P_ROWS)
        plain, scale = norm(x[at, :])
        plain3[at, :] = plain
        scale3[at, :] = scale
        final[at, :] = (plain * norms_ref[4:5, :] + norms_ref[5:6, :]).astype(BF)

    loop(images, last, 2)
    loss_ref[...] = jnp.zeros_like(loss_ref)
    masked = masked_ref[0:1, 0:1]
    head_w = need("head_w")
    pad_patches(need("patches"), padded, images)

    def score(i):
        at = rows_at(i, P_ROWS)
        target, _ = norm(padded[at, :].astype(F32))
        diff = dot_nn(final[at, :], head_w[...]) - target
        hidden = hide[at, :]
        loss_ref[...] += jnp.sum(jnp.mean(diff * diff, axis=-1, keepdims=True) * hidden, axis=0, keepdims=True)
        grad_pred[at, :] = (diff * (hidden * (2.0 / PIX)) / masked).astype(BF)

    loop(images, score, 2)
    writer = Writer(flat, stage, sem)
    writer.outer(11, final, grad_pred)
    norm_sums[...] = jnp.zeros_like(norm_sums)

    def back_final(i):
        at = rows_at(i, P_ROWS)
        back, gain, shift = norm_grad(dot_nt(grad_pred[at, :], head_w[...]), plain3[at, :], scale3[at, :], norms_ref[4:5, :])
        norm_sums[4:5, :] += gain
        norm_sums[5:6, :] += shift
        x[at, :] = back

    loop(images, back_final, 2)
    block_backward(x, P_ROWS, images, DHEADS, need, norms_ref, norm_sums, (low, grad_hidden, side, low_mixed, grad_triple), writer, (7, 8, 9, 10))
    spots = lax.broadcasted_iota(jnp.int32, (KEEP, P_ROWS), 1)
    slot = lax.broadcasted_iota(jnp.int32, (KEEP, P_ROWS), 0)

    def finish(i):
        at = rows_at(i, P_ROWS)
        grad = x[at, :]
        norm_sums[6:7, :] += jnp.sum(grad * hide[at, :], axis=0, keepdims=True)
        pick = jnp.where(jnp.logical_and(spots == cols_ref[i], slot < counts_ref[i]), 1.0, 0.0).astype(BF)
        grad_entering[rows_at(i, KEEP), :] = dot_nn(pick, grad.astype(BF)).astype(BF)

    loop(images, finish, 2)
    writer.small(12, norm_sums, 7, flat.shape[0] - TILES)


def decoder(total, counts, masked, patches, cols, order, pos, entering, weights, norms):
    images = counts.shape[0]
    rows = images * P_ROWS
    vmem = pl.BlockSpec(memory_space=pltpu.VMEM)
    anyspec = pl.BlockSpec(memory_space=pl.ANY)

    def v(shape, kind=F32):
        return pltpu.VMEM(shape, kind)

    return pl.pallas_call(
        functools.partial(decoder_kernel, images),
        name="decoder",
        out_shape=[
            jax.ShapeDtypeStruct((total, 8, LANES), F32),
            jax.ShapeDtypeStruct((images * KEEP, DD), BF),
            jax.ShapeDtypeStruct((1, 1), F32),
        ],
        in_specs=[pl.BlockSpec(memory_space=pltpu.SMEM)] + [vmem] * 5 + [anyspec] * 7,
        out_specs=[anyspec, vmem, vmem],
        scratch_shapes=[like(one) for one in [pos, patches] + weights]
        + [
            v((rows, DD)), v((rows, 1)), v((rows, DD), BF), v((rows, DD)), v((rows, 1)), v((rows, 3 * DD), BF),
            v((images * DD // LANES, 4 * P_ROWS, P_ROWS)), v((rows, DD), BF), v((rows, DD)), v((rows, 1)), v((rows, DD), BF),
            v((rows, FD), BF), v((rows, FD)), v((rows, DD)), v((rows, 1)), v((rows, DD), BF), v((rows, PIX), BF),
            v((rows, DD), BF), v((rows, FD), BF), v((rows, DD)), v((rows, DD), BF), v((rows, 3 * DD), BF),
            v((8, DD)), v((rows, PIX), BF), v((2, 32 * 16, 8, LANES)), pltpu.SemaphoreType.DMA((2,)), pltpu.SemaphoreType.DMA((7,)),
        ],
        compiler_params=pltpu.CompilerParams(vmem_limit_bytes=63 * MB),
    )(counts, masked, cols, order, entering, norms, pos, patches, *weights)


def encoder_back_kernel(images, share, n, chunks, flat_in, grad_entering, norms_ref, *refs):
    names = SAVED + ENC_NAMES[1:]
    sources = refs[:20]
    flat, late_ref, sib_ref = refs[20:23]
    targets = refs[23:43]
    x, low, grad_hidden, side, low_mixed, grad_triple, norm_sums, stage, sem, in_sem = refs[43:53]
    cut = late_cut(share)
    steps = late_ref.shape[0] * chunks
    plane = Plane(share, n, chunks, steps, lambda group: cut + group, flat, sib_ref, late_ref, 0, refs[53:])
    barrier = pltpu.get_barrier_semaphore()
    for name in ("x", "y", "c"):
        pl.semaphore_signal(barrier, inc=1, device_id=plane.to[name], device_id_type=MESH)
    need = Moves(names, sources, targets, in_sem)
    need.start(
        "encoded", "dec_embed_w", "plain3", "scale3", "down_w", "slope", "act", "inner", "up_w", "plain2", "scale2",
        "mixed", "proj_w", "triple", "probs", "entry", "triple_w", "plain1", "scale1", "seen",
    )
    pl.semaphore_wait(barrier, 3)
    plane.begin()
    one, two, three_, load = plane.stage_one, plane.stage_two, plane.stage_three, plane.load
    if steps == 4:
        plan = [
            [(load, 0)], [(one, 0), (load, 1)], [(one, 1)], [(two, 0), (load, 2)], [(one, 2), (two, 1), (load, 3)], [(one, 3)],
            [(two, 2), (three_, 0), (three_, 1)], [(two, 3), (three_, 2)], [], [], [(three_, 3)],
        ]
    else:
        flow = [(load, 0)]
        for t in range(steps + 2):
            flow += [(stage_, s) for stage_, s in ((one, t), (two, t - 1), (load, t + 1), (three_, t - 2)) if 0 <= s < steps]
        size = -(-len(flow) // TICKS)
        plan = [flow[i * size : (i + 1) * size] for i in range(TICKS)]

    def tick():
        for stage_, s in plan.pop(0):
            stage_(s)

    writer = Writer(flat, stage, sem)
    writer.outer(6, need("encoded"), grad_entering)
    norm_sums[...] = jnp.zeros_like(norm_sums)
    side[...] = dot_nt(grad_entering[...], need("dec_embed_w")[...])
    plain3, scale3 = need("plain3"), need("scale3")

    def last(i):
        at = rows_at(i, KEEP)
        back, gain, shift = norm_grad(side[at, :], plain3[at, :], scale3[at, :], norms_ref[4:5, :])
        norm_sums[4:5, :] += gain
        norm_sums[5:6, :] += shift
        x[at, :] = back

    loop(images, last, 2)
    tick()
    block_backward(x, KEEP, images, HEADS, need, norms_ref, norm_sums, (low, grad_hidden, side, low_mixed, grad_triple), writer, (1, 2, 3, 4), tick)
    low[...] = x[...].astype(BF)
    tick()
    writer.outer(0, need("seen"), low)
    tick()
    writer.small(5, norm_sums, 6)
    plane.finish()


def encoder_back(flat, grad_entering, saved, weights, norms, share, n_dp, n_pair):
    chunks = reduce_chunks(share, n_dp * n_pair)
    slab = slab_tiles(share, n_dp * n_pair) * 8
    groups = n_dp // 2 - late_cut(share)
    part = slab // chunks
    rows = grad_entering.shape[0]
    images = rows // KEEP
    vmem = pl.BlockSpec(memory_space=pltpu.VMEM)
    anyspec = pl.BlockSpec(memory_space=pl.ANY)

    def v(shape, kind=F32):
        return pltpu.VMEM(shape, kind)

    return pl.pallas_call(
        functools.partial(encoder_back_kernel, images, share, n_dp * n_pair, chunks),
        name="encoder_back",
        out_shape=[
            jax.ShapeDtypeStruct(flat.shape, flat.dtype),
            jax.ShapeDtypeStruct((groups, slab, LANES), F32),
            jax.ShapeDtypeStruct((groups * chunks, 4, part // 8, 8, LANES), F32),
        ],
        in_specs=[anyspec, vmem, vmem] + [anyspec] * 20,
        out_specs=[anyspec, vmem, anyspec],
        scratch_shapes=[like(one) for one in saved + weights]
        + [
            v((rows, D)), v((rows, D), BF), v((rows, F), BF), v((rows, D)), v((rows, D), BF), v((rows, 3 * D), BF),
            v((8, D)), v((2, 32 * 24, 8, LANES)), pltpu.SemaphoreType.DMA((2,)), pltpu.SemaphoreType.DMA((20,)),
        ]
        + plane_scratch(groups * chunks, part),
        input_output_aliases={0: 0},
        compiler_params=pltpu.CompilerParams(collective_id=2, has_side_effects=True, vmem_limit_bytes=63 * MB),
    )(flat, grad_entering, norms, *saved, *weights)[:2]


def positions(width):
    index = np.arange(PATCHES)
    quarter = width // 4
    freq = 10000.0 ** (-np.arange(quarter).astype(np.float32) / np.float32(quarter))
    row = (index // GRID).astype(np.float32)[:, None] * freq[None, :].astype(np.float32)
    column = (index % GRID).astype(np.float32)[:, None] * freq[None, :].astype(np.float32)
    table = np.concatenate([np.sin(row), np.cos(row), np.sin(column), np.cos(column)], axis=1).astype(np.float32)
    return jnp.asarray(np.pad(table, ((0, P_ROWS - PATCHES), (0, 0))))


def own_lines(flat, share, index):
    if share % LANES == 0:
        return flat.reshape(-1, LANES)
    rows = (share + LANES - 1) // LANES + 1
    return lax.dynamic_update_slice(jnp.zeros((rows * LANES,), flat.dtype), flat, (share * index % LANES,)).reshape(rows, LANES)


def own_flat(lines, share, index):
    if share % LANES == 0:
        return lines.reshape(-1)
    return lax.dynamic_slice(lines.reshape(-1), (share * index % LANES,), (share,))


def body(n_dp, n_pair, patches, patch_order, counts, master, moment1, moment2, block_rates, clip_limit, step_count):
    n = n_dp * n_pair
    share = master.shape[0]
    images = counts.shape[0]
    index = lax.axis_index("dp") * n_pair + lax.axis_index("pair")
    extra = jnp.zeros((8, LANES), F32).at[0, :images].set((PATCHES - counts).astype(F32))
    lines = own_lines(master, share, index)
    *held, enc_norms, dec_norms, masked = gather(lines, extra, share, n_dp, n_pair)
    parts = {i: matrix(one, i) for i, one in zip(BIG, held)}
    slots_at = patch_order[:, :KEEP]
    cols = slots_at[:, :, None]
    enc_weights = [parts[i] for i in (1, 2, 3, 4, 6)]
    *saved, entering = encoder(counts, patches, cols, positions(D), [parts[0]] + enc_weights, enc_norms)
    total = max(a for a, _ in ranges(share, n)) + slab_tiles(share, n)
    dec_weights = [parts[i] for i in (7, 8, 9, 10, 11)]
    flat, grad_entering, loss_local = decoder(total, counts, masked, patches, cols, slots_at, positions(DD), entering, dec_weights, dec_norms)
    flat, late = encoder_back(flat, grad_entering, saved, enc_weights, enc_norms, share, n_dp, n_pair)
    grad_lines, totals = reduce(flat, late, loss_local, lines.shape, share, n_dp, n_pair)
    grad_norm = totals[0, 0:1]
    loss = totals[1, 0:1] / masked[0]
    clipped = own_flat(grad_lines, share, index) * (clip_limit[0] / (grad_norm[0] + NORM_EPS))
    first = BETA_ONE * moment1 + (1.0 - BETA_ONE) * clipped
    second = BETA_TWO * moment2 + (1.0 - BETA_TWO) * clipped * clipped
    steps_done = step_count[0].astype(F32)
    position = index * share + jnp.arange(share)
    rate = jnp.where(position < ENC_PARAMS, block_rates[0], block_rates[1])
    update = first / (1.0 - BETA_ONE**steps_done) / (jnp.sqrt(second / (1.0 - BETA_TWO**steps_done)) + ADAM_EPS)
    master_new = master - rate * (update + DECAY * master)
    return (loss, grad_norm, first, second, master_new)


def solution(mesh):
    whole = P(("dp", "pair"))
    in_specs = (P(("dp", "pair"), None, None), P(("dp", "pair"), None), whole, whole, whole, whole, P(), P(), P())
    out_specs = (P(), P(), whole, whole, whole)
    step = functools.partial(body, mesh.shape["dp"], mesh.shape["pair"])
    return jax.shard_map(step, mesh=mesh, in_specs=in_specs, out_specs=out_specs, check_vma=False)
```

```python
import functools

import jax
import jax.numpy as jnp
import numpy as np
from jax import lax
from jax.experimental import pallas as pl
from jax.experimental.pallas import tpu as pltpu
from jax.sharding import PartitionSpec as P

MESH = pl.DeviceIdType.MESH
LANES = 128
TILE = 16 * LANES


def place():
    dp, pair = lax.axis_index("dp"), lax.axis_index("pair")
    return dp // 2, dp % 2, pair // 2, pair % 2


def slot_of(z, x, y, c):
    return (z * 2 + x) * 4 + y * 2 + c


def partners(z, x, y, c):
    return {
        "x": {"dp": z * 2 + (1 - x)},
        "y": {"pair": (1 - y) * 2 + c},
        "c": {"pair": y * 2 + (1 - c)},
        "up": {"dp": (z + 1) * 2 + x},
        "down": {"dp": (z - 1) * 2 + x},
    }


def greet(n_z, z, to):
    barrier = pltpu.get_barrier_semaphore()
    for name in ("x", "y", "c"):
        pl.semaphore_signal(barrier, inc=1, device_id=to[name], device_id_type=MESH)

    @pl.when(z < n_z - 1)
    def _():
        pl.semaphore_signal(barrier, inc=1, device_id=to["up"], device_id_type=MESH)

    @pl.when(z > 0)
    def _():
        pl.semaphore_signal(barrier, inc=1, device_id=to["down"], device_id_type=MESH)

    pl.semaphore_wait(barrier, 3 + jnp.where(z < n_z - 1, 1, 0) + jnp.where(z > 0, 1, 0))


def both(*conditions):
    total = conditions[0]
    for one in conditions[1:]:
        total = jnp.logical_and(total, one)
    return total


PIX, HEADS, F, DHEADS, FD, GRID, KEEP, D, DD, PATCHES = 768, 12, 3072, 16, 2048, 14, 64, 768, 512, 196
SHAPES = [(PIX, D), (D, 3 * D), (D, D), (D, F), (F, D), (6, D), (D, DD), (DD, 3 * DD), (DD, DD), (DD, FD), (FD, DD), (DD, PIX), (7, DD)]
SMALL = (5, 12)
ENC_PARAMS = 7672320
NORM_EPS = 1e-06
ADAM_EPS = 1e-08
BETA_ONE = 0.9
BETA_TWO = 0.95
DECAY = 0.05
MB = 1 << 20
CELL = 8 * LANES
BLOCK = 96


def make_entries():
    entries, row, tile = [], 0, 0
    for number, (rows, width) in enumerate(SHAPES):
        lines = rows * width // LANES
        cols = 1 if number in SMALL else width // LANES
        groups = -(-lines // (8 * cols))
        entries.append((row, lines, cols, tile, groups))
        row += lines
        tile += groups * cols
    return entries, row, tile


ENTRIES, ROWS, TILES = make_entries()
BIG = tuple(i for i in range(len(SHAPES)) if i not in SMALL)
MARGIN = 8 * max(cols for _, _, cols, _, _ in ENTRIES)


def first_tile(share, k):
    lo = share * k
    total = 0
    for row, lines, cols, tile, _ in ENTRIES:
        inside = jnp.logical_and(lo >= row * LANES, lo < (row + lines) * LANES)
        total = total + jnp.where(inside, tile + (lo - row * LANES) // (CELL * cols) * cols, 0)
    return total


def ranges(share, n):
    found = []
    for k in range(n):
        lo, hi = share * k, share * (k + 1)
        spans = []
        for row, lines, cols, tile, _ in ENTRIES:
            low, high = max(lo, row * LANES), min(hi, (row + lines) * LANES)
            if low < high:
                size = CELL * cols
                spans.append((tile + (low - row * LANES) // size * cols, tile + -(-(high - row * LANES) // size) * cols))
        found.append((spans[0][0], spans[-1][1]))
    return found


def slab_tiles(share, n):
    longest = max(b - a for a, b in ranges(share, n))
    return -(-longest // 24) * 24


def line_span(share, k):
    return share * k // LANES, (share * (k + 1) + LANES - 1) // LANES


def tiled(share, k, body):
    lo, hi = line_span(share, k)
    begin = first_tile(share, k)
    for number in SMALL + tuple(i for i in range(len(ENTRIES)) if i not in SMALL):
        row, lines, cols, tile, _ = ENTRIES[number]
        low = jnp.maximum(lo, row) - row
        high = jnp.minimum(hi, row + lines) - row
        size = 8 * cols

        def group(g, _, row=row, cols=cols, tile=tile, size=size):
            body(row + g * size - lo + MARGIN, tile + g * cols - begin, cols)
            return 0

        lax.fori_loop(jnp.where(low < high, low // size, 0), jnp.where(low < high, (high + size - 1) // size, 0), group, 0)


def wide_rows(rows):
    return -(-(rows + 2 * MARGIN) // 8) * 8


def pieces(share, n):
    spans = ranges(share, n)
    shared = [spans[k][1] > spans[k + 1][0] for k in range(n - 1)]
    plain, seams = [], []
    for number, (_, _, cols, tile, groups) in enumerate(ENTRIES):
        end = tile + groups * cols
        for k, (a, b) in enumerate(spans):
            low, high = max(a, tile), min(b, end)
            if low >= high:
                continue
            inner_low, inner_high = low, high
            if k > 0 and spans[k - 1][1] > low:
                inner_low = spans[k - 1][1]
            if k < n - 1 and spans[k + 1][0] < high:
                inner_high = spans[k + 1][0]
                seams.append((number, k, inner_high, high))
            if inner_low < inner_high:
                plain.append((number, k, inner_low, inner_high))
    return spans, plain, seams


def matrix(tiles_, number):
    rows, width = SHAPES[number]
    cols = width // LANES
    return tiles_.reshape(rows // 8, cols, 8, LANES).transpose(0, 2, 1, 3).reshape(rows, width)


def matrix_tiles(value):
    rows, width = value.shape
    cols = width // LANES
    return value.reshape(rows // 8, 8, cols, LANES).transpose(0, 2, 1, 3).reshape(rows * cols, LANES)


def gather_kernel(n_z, n_pair, share, lines_ref, extra_ref, *refs):
    outs = dict(zip(BIG, refs[: len(BIG)]))
    enc_norms, dec_norms, masked_ref = refs[len(BIG) : len(BIG) + 3]
    wide, out_ref, z_sem, plane_sem, second_sem, third_sem, flat_sem, line_sem, core_sem, recv_sem, put_sem = refs[len(BIG) + 3 :]
    n = n_z * 2 * n_pair
    total_tiles = out_ref.shape[1]
    small = total_tiles // 2 * 2 // 9
    large = total_tiles // 2 - small
    spans_of = ((0, large), (large, large), (2 * large, small), (2 * large + small, small), (2 * large, 2 * small))
    z, x, y, c = place()
    to = partners(z, x, y, c)
    me = slot_of(z, x, y, c)
    rows = lines_ref.shape[0]
    wide[0:MARGIN, :] = jnp.zeros((MARGIN, LANES), jnp.float32)
    wide[MARGIN + rows :, :] = jnp.zeros((wide.shape[0] - MARGIN - rows, LANES), jnp.float32)
    wide[MARGIN : MARGIN + rows, :] = lines_ref[...]

    def fill(line, tile, cols):
        for col in range(cols):
            out_ref[me, tile + col] = wide[pl.ds(line + col, 8, stride=cols), :].astype(out_ref.dtype)

    tiled(share, me, fill)
    out_ref[me, total_tiles - 2] = extra_ref[...].astype(out_ref.dtype)
    greet(n_z, z, to)

    def copy(slot, part, name, sem):
        at = pl.ds(*spans_of[part])
        return pltpu.make_async_remote_copy(
            out_ref.at[slot, at], out_ref.at[slot, at], sem, recv_sem.at[slot, 2 if part == 4 else part], device_id=to[name], device_id_type=MESH
        )

    def arrived(slot, part):
        copy(slot, part, "c", plane_sem.at[0, 0, 0]).wait_recv()

    def start(one):
        one.start()

    def stop(one):
        one.wait_send()

    def lines(t):
        for d in (0, 1):
            zz = z - t if d == 0 else z + t
            inside = zz >= 0 if d == 0 else zz < n_z
            more = z < n_z - 1 if d == 0 else z > 0
            fresh = both(t > 0, inside)
            held = jnp.logical_or(fresh, t == 0) if d == 0 else fresh
            yield d, zz, fresh, held, more

    def own_z(act):
        for d, more in ((0, z < n_z - 1), (1, z > 0)):
            for part in (0, 1):
                pl.when(more)(lambda d=d, part=part: act(copy(me, part, ("up", "down")[d], z_sem.at[0, d, part])))

    def onward_z(t, d, zz, fresh, more, act):
        for part in (0, 1):
            pl.when(both(fresh, more))(lambda part=part: act(copy(slot_of(zz, x, y, c), part, ("up", "down")[d], z_sem.at[t, d, part])))

    def plane_sends(t, d, zz, held, act):
        @pl.when(held)
        def _():
            for i, (part, name) in enumerate(((0, "x"), (1, "y"), (0, "y"), (1, "x"), (0, "c"), (1, "c"))):
                act(copy(slot_of(zz, x, y, c), part, name, plane_sem.at[t, d, i]))

    def first(t):
        for d, zz, fresh, held, more in lines(t):

            @pl.when(fresh)
            def _():
                for part in (0, 1):
                    arrived(slot_of(zz, x, y, c), part)

            onward_z(t, d, zz, fresh, more, start)
            plane_sends(t, d, zz, held, start)

    def second_items(zz):
        return ((0, slot_of(zz, 1 - x, y, c), "y"), (1, slot_of(zz, x, 1 - y, c), "x"))

    def second(t):
        for d, zz, _, held, _ in lines(t):

            @pl.when(held)
            def _():
                for part, slot, name in second_items(zz):
                    arrived(slot, part)
                    copy(slot, part, name, second_sem.at[t, d, part, 0]).start()
                    copy(slot, part, "c", second_sem.at[t, d, part, 1]).start()

    def third_items(zz):
        return ((0, slot_of(zz, x, 1 - y, c)), (1, slot_of(zz, 1 - x, y, c)), (0, slot_of(zz, 1 - x, 1 - y, c)), (1, slot_of(zz, 1 - x, 1 - y, c)))

    def third(t):
        for d, zz, _, held, _ in lines(t):

            @pl.when(held)
            def _():
                for i, (part, slot) in enumerate(third_items(zz)):
                    arrived(slot, part)
                    copy(slot, part, "c", third_sem.at[t, d, i]).start()

    near = ((2, me, "x"), (3, me, "y"), (2, me, "y"), (3, me, "x"), (2, me, "c"), (3, me, "c"))
    beside = ((2, slot_of(z, 1 - x, y, c), "y"), (3, slot_of(z, x, 1 - y, c), "x"))
    across = ((2, slot_of(z, x, 1 - y, c)), (3, slot_of(z, 1 - x, y, c)), (2, slot_of(z, 1 - x, 1 - y, c)), (3, slot_of(z, 1 - x, 1 - y, c)))

    def flat_sends(act, which):
        for i, (part, slot, name) in enumerate(near):
            if which == 0:
                act(copy(slot, part, name, flat_sem.at[i]))
        for i, (part, slot, name) in enumerate(beside):
            if which == 1:
                act(copy(slot, part, name, flat_sem.at[6 + i]))
                act(copy(slot, part, "c", flat_sem.at[8 + i]))
        for i, (part, slot) in enumerate(across):
            if which == 2:
                act(copy(slot, part, "c", flat_sem.at[10 + i]))

    def corner(zz, i):
        return slot_of(zz, i // 2, i % 2, c)

    def line_sends(t, act):
        for d, zz, fresh, _, more in lines(t):
            for i in range(4):
                go = jnp.logical_or(fresh, t == 0)
                pl.when(both(go, more))(lambda d=d, zz=zz, i=i: act(copy(corner(zz, i), 4, ("up", "down")[d], line_sem.at[t, d, i])))
                pl.when(fresh)(lambda d=d, zz=zz, i=i: act(copy(corner(zz, i), 4, "c", core_sem.at[t, d, i])))

    def along(t):
        for d, zz, fresh, _, _ in lines(t):

            @pl.when(fresh)
            def _():
                for i in range(4):
                    arrived(corner(zz, i), 4)

        @pl.when(t == 0)
        def _():
            for part, slot in across:
                arrived(slot, part)
            flat_sends(start, 2)

        line_sends(t, start)

    own_z(start)
    flat_sends(start, 0)
    for part, slot, _ in beside:
        arrived(slot, part)
    flat_sends(start, 1)

    def turn(t, _):
        pl.when(t < n_z)(lambda: first(t))
        pl.when(both(t >= 1, t < n_z + 1))(lambda: second(t - 1))
        pl.when(both(t >= 1, t < n_z + 1))(lambda: along(t - 1))
        pl.when(t >= 2)(lambda: third(t - 2))
        return 0

    lax.fori_loop(0, n_z + 2, turn, 0)
    own_z(stop)
    for which in range(3):
        flat_sends(stop, which)

    def finish(t, _):
        line_sends(t, stop)
        for d, zz, fresh, held, more in lines(t):
            onward_z(t, d, zz, fresh, more, stop)
            plane_sends(t, d, zz, held, stop)

            @pl.when(held)
            def _():
                for part, slot, name in second_items(zz):
                    copy(slot, part, name, second_sem.at[t, d, part, 0]).wait_send()
                    copy(slot, part, "c", second_sem.at[t, d, part, 1]).wait_send()
                for i, (part, slot) in enumerate(third_items(zz)):
                    copy(slot, part, "c", third_sem.at[t, d, i]).wait_send()
                for i in range(4):
                    for part in (0, 1):
                        arrived(slot_of(zz, i // 2, i % 2, 1 - c), part)

            @pl.when(fresh)
            def _():
                for i in range(4):
                    arrived(slot_of(zz, i // 2, i % 2, 1 - c), 4)

        return 0

    lax.fori_loop(0, n_z, finish, 0)
    for i in range(4):
        for part in (2, 3):
            arrived(slot_of(z, i // 2, i % 2, 1 - c), part)
    spans, plain, seams = pieces(share, n)
    puts = []

    def put(number, k, low, high):
        copy = pltpu.make_async_copy(
            out_ref.at[k, pl.ds(low - spans[k][0], high - low)], outs[number].at[pl.ds(low - ENTRIES[number][3], high - low)], put_sem.at[len(puts)]
        )
        copy.start()
        puts.append(copy)

    home = {}
    for number, k, low, high in plain + seams:
        if number in SMALL:
            home.update({tile: (k, tile - spans[k][0]) for tile in range(low, high)})
        elif (number, k, low, high) in plain:
            put(number, k, low, high)
    for number, k, low, high in seams:
        left = pl.ds(low - spans[k][0], high - low)
        right = pl.ds(low - spans[k + 1][0], high - low)
        total = out_ref[k, left].astype(jnp.float32) + out_ref[k + 1, right].astype(jnp.float32)
        out_ref[k, left] = total.astype(out_ref.dtype)
        if number not in SMALL:
            put(number, k, low, high)
    for number, target in zip(SMALL, (enc_norms, dec_norms)):
        row, lines_, _, tile, groups = ENTRIES[number]
        per = SHAPES[number][1] // LANES
        for group in range(groups):
            k, at = home[tile + group]
            value = out_ref[k, at].astype(jnp.float32)
            for line in range(group * 8, min(group * 8 + 8, lines_)):
                target[line // per : line // per + 1, line % per * LANES : (line % per + 1) * LANES] = value[line % 8 : line % 8 + 1, :]
    masked_ref[...] = jnp.zeros_like(masked_ref)

    def count(k, _):
        masked_ref[...] += jnp.sum(out_ref[k, out_ref.shape[1] - 2].astype(jnp.float32)[0:1, :], axis=1, keepdims=True)
        return 0

    lax.fori_loop(0, n, count, 0)
    for copy in puts:
        copy.wait()


def gather(lines, extra, share, n_dp, n_pair):
    n_z = n_dp // 2
    n = n_dp * n_pair
    tiles_ = slab_tiles(share, n) + 2
    _, plain, seams = pieces(share, n)
    dma = pltpu.SemaphoreType.DMA
    anyspec = pl.BlockSpec(memory_space=pl.ANY)
    vmem = pl.BlockSpec(memory_space=pltpu.VMEM)

    def s(shape, kind=jnp.float32):
        return jax.ShapeDtypeStruct(shape, kind)

    return pl.pallas_call(
        functools.partial(gather_kernel, n_z, n_pair, share),
        name="gather",
        out_shape=[s((ENTRIES[i][4] * ENTRIES[i][2], 8, LANES), jnp.bfloat16) for i in BIG] + [s(SHAPES[5]), s(SHAPES[12]), s((1, 1))],
        in_specs=[vmem, vmem],
        out_specs=[anyspec] * len(BIG) + [vmem] * 3,
        scratch_shapes=[
            pltpu.VMEM((wide_rows(lines.shape[0]), LANES), jnp.float32),
            pltpu.VMEM((n, tiles_, 8, LANES), jnp.bfloat16),
            dma((n_z, 2, 2)), dma((n_z, 2, 6)), dma((n_z, 2, 2, 2)), dma((n_z, 2, 4)), dma((14,)), dma((n_z, 2, 4)), dma((n_z, 2, 4)), dma((n, 4)),
            dma((len(plain) + len(seams),)),
        ],
        compiler_params=pltpu.CompilerParams(collective_id=0, has_side_effects=True, vmem_limit_bytes=60 * MB),
    )(lines, extra)


def reduce_chunks(share, n):
    rows = slab_tiles(share, n) * 8
    return max(d for d in (1, 2, 4) if rows % (2 * BLOCK * d) == 0)


def late_cut(share):
    return -(-ENTRIES[7][0] * LANES // (share * 8))


def pack(value, q_ref, t_ref, b):
    top = jnp.max(jnp.abs(value), axis=0, keepdims=True)
    inverse = jnp.where(top > 1e-30, 32767.0 / jnp.maximum(top, 1e-30), 0.0)
    q_ref[pl.ds(pl.multiple_of(b * BLOCK, BLOCK), BLOCK), :] = jnp.round(value * inverse).astype(jnp.int32).astype(jnp.int16)
    t_ref[pl.ds(b, 1), :] = top * (1.0 / 32767.0)


def unpack(q_ref, t_ref, b):
    return q_ref[pl.ds(pl.multiple_of(b * BLOCK, BLOCK), BLOCK), :].astype(jnp.int32).astype(jnp.float32) * t_ref[pl.ds(b, 1), :]


def message(qs, ts, qr, tr, sem, to):
    return (
        pltpu.make_async_remote_copy(qs, qr, sem.at[0, 0], sem.at[0, 1], device_id=to, device_id_type=MESH),
        pltpu.make_async_remote_copy(ts, tr, sem.at[1, 0], sem.at[1, 1], device_id=to, device_id_type=MESH),
    )


def slab_start(share, n, k):
    if n > 64:
        return first_tile(share, k)
    starts = [a for a, _ in ranges(share, n)]
    found = starts[0]
    for i in range(1, n):
        found = jnp.where(k >= i, starts[i], found)
    return found


class Plane:
    def __init__(self, share, n, chunks, steps, plane_of, grad, sib, keep, base, scratch):
        self.share, self.n, self.chunks, self.steps, self.plane_of = share, n, chunks, steps, plane_of
        self.grad, self.sib, self.keep, self.base = grad, sib, keep, base
        (self.gbuf, self.rbuf, self.q1s, self.q1r, self.q2s, self.q2r, self.t1s, self.t1r, self.t2s, self.t2r,
         self.sib_sem, self.load_sem, self.s1_sem, self.s2_sem) = scratch
        self.z, self.x, self.y, self.c = place()
        self.to = partners(self.z, self.x, self.y, self.c)
        self.rows = keep.shape[1] // chunks
        self.half = self.rows // 2

    def tiles_of(self, s, xx, yy, core):
        k = slot_of(self.plane_of(s // self.chunks), xx, yy, core)
        return pl.ds(slab_start(self.share, self.n, k) + s % self.chunks * (self.rows // 8), self.rows // 8)

    def kept(self, s, part, b):
        return self.base + s // self.chunks, pl.ds(pl.multiple_of(s % self.chunks * self.rows + part * self.half + b * BLOCK, BLOCK), BLOCK)

    def sibling(self, s, q, at=None):
        return pltpu.make_async_remote_copy(
            self.grad.at[at if at is not None else pl.ds(0, self.rows // 8)],
            self.sib.at[s, q],
            self.sib_sem.at[0, s, q],
            self.sib_sem.at[1, s, q],
            device_id=self.to["c"],
            device_id_type=MESH,
        )

    def begin(self):
        def one(s, _):
            for q in range(4):
                self.sibling(s, q, self.tiles_of(s, q // 2, q % 2, 1 - self.c)).start()
            return 0

        lax.fori_loop(0, self.steps, one, 0)

    def loads(self, s, q, at=None):
        slot = s % 2
        return pltpu.make_async_copy(self.grad.at[at if at is not None else pl.ds(0, self.rows // 8)], self.gbuf.at[slot, q], self.load_sem.at[slot, q])

    def other(self, s):
        return pltpu.make_async_copy(self.sib.at[s], self.rbuf.at[s % 2], self.load_sem.at[s % 2, 4])

    def load(self, s):
        for q in range(4):
            self.loads(s, q, self.tiles_of(s, q // 2, q % 2, self.c)).start()
        for q in range(4):
            self.sibling(s, q).wait_recv()
        self.other(s).start()

    def each(self, body):
        def one(b, _):
            body(b)
            return 0

        lax.fori_loop(0, self.half // BLOCK, one, 0, unroll=self.half // BLOCK)

    def own(self, slot, q, part, b):
        at = pl.ds(part * (self.half // 8) + b * (BLOCK // 8), BLOCK // 8)
        return (self.gbuf[slot, q, at] + self.rbuf[slot, q, at]).reshape(BLOCK, LANES)

    def first_message(self, s, part):
        i = pl.ds(part * 2, 2)
        return message(self.q1s.at[s, i], self.t1s.at[s, i], self.q1r.at[s, i], self.t1r.at[s, i], self.s1_sem.at[s, part], self.to[("x", "y")[part]])

    def second_message(self, s, part):
        return message(
            self.q2s.at[s, part], self.t2s.at[s, part], self.q2r.at[s, part], self.t2r.at[s, part], self.s2_sem.at[s, part], self.to[("y", "x")[part]]
        )

    def quarter(self, part, other, mine):
        if part == 0:
            return (self.x if mine else 1 - self.x) * 2 + other
        return other * 2 + (self.y if mine else 1 - self.y)

    def stage_one(self, s):
        slot = s % 2
        for q in range(4):
            self.loads(s, q).wait()
        self.other(s).wait()
        for part in (0, 1):
            for other in (0, 1):
                q = self.quarter(part, other, False)
                i = part * 2 + other
                self.each(lambda b: pack(self.own(slot, q, part, b), self.q1s.at[s, i], self.t1s.at[s, i], b))
            for one in self.first_message(s, part):
                one.start()

    def stage_two(self, s):
        slot = s % 2
        for part in (0, 1):
            for one in self.first_message(s, part):
                one.wait_recv()
            here = (self.y, self.x)[part]
            away = self.quarter(part, 1 - here, True)
            i = part * 2 + 1 - here
            self.each(
                lambda b: pack(
                    self.own(slot, away, part, b) + unpack(self.q1r.at[s, i], self.t1r.at[s, i], b), self.q2s.at[s, part], self.t2s.at[s, part], b
                )
            )
            for one in self.second_message(s, part):
                one.start()
        for part in (0, 1):
            here = (self.y, self.x)[part]
            k = part * 2 + here

            def store(b, part=part, k=k):
                group, at = self.kept(s, part, b)
                self.keep[group, at, :] = self.own(slot, self.x * 2 + self.y, part, b) + unpack(self.q1r.at[s, k], self.t1r.at[s, k], b)

            self.each(store)

    def stage_three(self, s):
        for part in (0, 1):
            for one in self.second_message(s, part):
                one.wait_recv()

            def body(b, part=part):
                group, at = self.kept(s, part, b)
                self.keep[group, at, :] += unpack(self.q2r.at[s, part], self.t2r.at[s, part], b)

            self.each(body)

    def finish(self):
        def one(s, _):
            for q in range(4):
                self.sibling(s, q).wait_send()
            for part in (0, 1):
                for two in self.first_message(s, part):
                    two.wait_send()
                for two in self.second_message(s, part):
                    two.wait_send()
            return 0

        lax.fori_loop(0, self.steps, one, 0)


def message_scratch(part, *leads):
    half = part // 2
    marks = (half // BLOCK + 7) // 8 * 8
    return [pltpu.VMEM(lead + (half, LANES), jnp.int16) for lead in leads] + [pltpu.VMEM(lead + (marks, LANES), jnp.float32) for lead in leads]


def plane_scratch(steps, part):
    dma = pltpu.SemaphoreType.DMA
    return [
        pltpu.VMEM((2, 4, part // 8, 8, LANES), jnp.float32),
        pltpu.VMEM((2, 4, part // 8, 8, LANES), jnp.float32),
        *message_scratch(part, (steps, 4), (steps, 4), (steps, 2), (steps, 2)),
        dma((2, steps, 4)), dma((2, 5)), dma((steps, 2, 2, 2)), dma((steps, 2, 2, 2)),
    ]


def reduce_kernel(n_z, n_pair, chunks, share, grad_ref, late_ref, loss_in, lines_ref, total_ref, sib_ref,
                  wide, mine, shared, send_sem, recv_sem, keep, late_sem, zs, zr, tzs, tzr, z_sem, *scratch):
    z, x, y, c = place()
    to = partners(z, x, y, c)
    n = n_z * 2 * n_pair
    me = slot_of(z, x, y, c)
    cut = late_cut(share)
    steps, late = cut * chunks, (n_z - cut) * chunks
    home = jnp.where(z < cut, cut - 1, z)

    def order(j):
        low = z < cut // 2
        far = jnp.where(low, cut - 1 - j, j)
        moved = jnp.where(low, jnp.where(far > z, far, far - 1), jnp.where(far < z, far, far + 1))
        return jnp.where(z >= cut, j, jnp.where(j == cut - 1, z, moved))

    plane = Plane(share, n, chunks, steps, order, grad_ref, sib_ref, keep, 0, scratch)

    def z_message(spot, name):
        d = 0 if name == "up" else 1
        return message(zs.at[spot], tzs.at[spot], zr.at[d, spot], tzr.at[d, spot], z_sem.at[d, spot], to[name])

    def stage_four(group, chunk, zz):
        spot = zz * chunks + chunk

        def lines(part, b):
            return pl.ds(pl.multiple_of(chunk * plane.rows + part * plane.half + b * BLOCK, BLOCK), BLOCK)

        for d, name, has, onward in ((0, "up", z > 0, zz > z), (1, "down", z < n_z - 1, zz < z)):
            back = zz >= z if d == 0 else zz <= z

            @pl.when(both(has, back))
            def _():
                for one in z_message(spot, name):
                    one.wait_recv()
                for part in (0, 1):

                    def add(b, part=part):
                        keep[group, lines(part, b), :] += unpack(zr.at[d, spot, part], tzr.at[d, spot, part], b)

                    plane.each(add)

            @pl.when(onward)
            def _():
                for part in (0, 1):
                    plane.each(lambda b, part=part: pack(keep[group, lines(part, b), :], zs.at[spot, part], tzs.at[spot, part], b))
                for one in z_message(spot, name):
                    one.start()

    def spread_lines(line, tile, cols):
        for col in range(cols):
            wide[pl.ds(line + col, 8, stride=cols), :] = keep[home, pl.ds(pl.multiple_of((tile + col) * 8, 8), 8), :]

    count_lines = lines_ref.shape[0]
    tall = 128

    def by_lines(body):
        def one(i, _):
            body(pl.multiple_of(i * tall, tall), tall)
            return 0

        lax.fori_loop(0, count_lines // tall, one, 0)
        if count_lines % tall:
            body(count_lines // tall * tall, count_lines % tall)

    barrier = pltpu.get_barrier_semaphore()

    def peer(d):
        k = lax.rem(me + d, n)
        return {"dp": k // n_pair, "pair": lax.rem(k, n_pair)}

    def hello(d, _):
        pl.semaphore_signal(barrier, inc=1, device_id=peer(d), device_id_type=MESH)
        return 0

    lax.fori_loop(1, n, hello, 0)
    kept = pltpu.make_async_copy(late_ref, keep.at[pl.ds(cut, n_z - cut)], late_sem)
    kept.start()
    pl.semaphore_wait(barrier, n - 1)
    plane.begin()
    plane.load(0)
    kept.wait()
    lag = 0

    def turn(t, _):
        pl.when(t < steps)(lambda: plane.stage_one(t))
        pl.when(both(t >= 1, t <= steps))(lambda: plane.stage_two(t - 1))
        pl.when(t + 1 < steps)(lambda: plane.load(t + 1))
        pl.when(both(t >= 2, t <= steps + 1))(lambda: plane.stage_three(t - 2))
        early, main = t - z, t - 3 - lag
        pl.when(both(early >= 0, early < late))(lambda: stage_four(cut + early // chunks, lax.rem(early, chunks), cut + early // chunks))
        pl.when(both(main >= 0, main < steps))(lambda: stage_four(main // chunks, lax.rem(main, chunks), order(main // chunks)))
        return 0

    lax.fori_loop(0, max(steps + 3, late + n_z), turn, 0)
    tiled(share, me, spread_lines)
    lo, _ = line_span(share, me)
    mine[...] = jnp.zeros_like(mine)

    def squares(start, size):
        value = wide[pl.ds(MARGIN + start, size), :]
        if share % LANES:
            line = lax.broadcasted_iota(jnp.int32, (size, LANES), 0) + lo + start
            spot = line * LANES + lax.broadcasted_iota(jnp.int32, (size, LANES), 1)
            inside = jnp.logical_and(spot >= share * me, spot < share * (me + 1))
            value = jnp.where(inside, value, 0.0)
        lines_ref[pl.ds(start, size), :] = value
        mine[0:1, :] += jnp.sum(value * value, axis=0, keepdims=True)

    by_lines(squares)
    lane = lax.broadcasted_iota(jnp.int32, (1, LANES), 1)
    mine[1:2, :] = jnp.where(lane == 0, loss_in[0:1, 0:1], 0.0)
    shared[me] = mine[...]

    def send(d):
        return pltpu.make_async_remote_copy(mine, shared.at[me], send_sem.at[d], recv_sem.at[d], device_id=peer(d), device_id_type=MESH)

    def go(d, _):
        send(d).start()
        return 0

    def stop(d, _):
        send(d).wait()
        return 0

    lax.fori_loop(1, n, go, 0)
    plane.finish()

    def finish(spot, _):
        zz = spot // chunks
        for name, sent in (("up", zz > z), ("down", zz < z)):

            @pl.when(sent)
            def _():
                for one in z_message(spot, name):
                    one.wait_send()

        return 0

    lax.fori_loop(0, n_z * chunks, finish, 0)
    lax.fori_loop(1, n, stop, 0)

    def add(k, total):
        return total + shared[k]

    total = lax.fori_loop(0, n, add, jnp.zeros((8, LANES), jnp.float32))
    norm_ = jnp.sqrt(jnp.sum(total[0:1, :], axis=1, keepdims=True))
    loss_sum = jnp.sum(total[1:2, :], axis=1, keepdims=True)
    total_ref[...] = jnp.where(lax.broadcasted_iota(jnp.int32, (8, LANES), 0) == 0, norm_, loss_sum)


def reduce(flat, late, loss, shape, share, n_dp, n_pair):
    n_z, n = n_dp // 2, n_dp * n_pair
    chunks = reduce_chunks(share, n)
    rows = slab_tiles(share, n) * 8
    part = rows // chunks
    steps = late_cut(share) * chunks
    spots = n_z * chunks
    anyspec = pl.BlockSpec(memory_space=pl.ANY)
    vmem = pl.BlockSpec(memory_space=pltpu.VMEM)
    line = jax.ShapeDtypeStruct(shape, jnp.float32)
    dma = pltpu.SemaphoreType.DMA
    return pl.pallas_call(
        functools.partial(reduce_kernel, n_z, n_pair, chunks, share),
        name="reduce_scatter",
        out_shape=[line, jax.ShapeDtypeStruct((8, LANES), jnp.float32), jax.ShapeDtypeStruct((steps, 4, part // 8, 8, LANES), jnp.float32)],
        in_specs=[anyspec, anyspec, vmem],
        out_specs=[vmem, vmem, anyspec],
        scratch_shapes=[
            pltpu.VMEM((wide_rows(shape[0]), LANES), jnp.float32),
            pltpu.VMEM((8, LANES), jnp.float32),
            pltpu.VMEM((n, 8, LANES), jnp.float32),
            dma((n,)),
            dma((n,)),
            pltpu.VMEM((n_z, rows, LANES), jnp.float32),
            dma,
            *message_scratch(part, (spots, 2), (2, spots, 2)),
            dma((2, spots, 2, 2)),
            *plane_scratch(steps, part),
        ],
        compiler_params=pltpu.CompilerParams(collective_id=1, has_side_effects=True, vmem_limit_bytes=60 * MB),
    )(flat, late, loss)[:2]


NEG_FILL = -1000000000.0
P_ROWS = 208
BF = jnp.bfloat16
F32 = jnp.float32


def dot_nn(left, right):
    return lax.dot_general(left, right, (((1,), (0,)), ((), ())), preferred_element_type=F32)


def dot_nt(left, right):
    return lax.dot_general(left, right, (((1,), (1,)), ((), ())), preferred_element_type=F32)


def loop(count, body, unroll=1):
    def step(i, _):
        body(i)
        return 0

    lax.fori_loop(0, count, step, 0, unroll=unroll)


def rows_at(i, size):
    return pl.ds(pl.multiple_of(i * size, size), size)


def norm(x):
    centered = x - jnp.mean(x, axis=-1, keepdims=True)
    scale = lax.rsqrt(jnp.mean(centered * centered, axis=-1, keepdims=True) + NORM_EPS)
    return centered * scale, scale


def norm_grad(grad, plain, scale, gain):
    inner = grad * gain
    back = scale * (inner - jnp.mean(inner, axis=-1, keepdims=True) - plain * jnp.mean(inner * plain, axis=-1, keepdims=True))
    return back, jnp.sum(grad * plain, axis=0, keepdims=True), jnp.sum(grad, axis=0, keepdims=True)


def gelu_pair(h):
    cumulative = 0.5 * (1.0 + lax.erf(h * 0.7071067811865476))
    density = jnp.exp(-0.5 * h * h) * 0.3989422804014327
    return h * cumulative, cumulative + h * density


def head_masks(size):
    lane = lax.broadcasted_iota(jnp.int32, (1, LANES), 1)
    shift = size.bit_length() - 1
    return [jnp.where((lane >> shift) == h, 1.0, 0.0).astype(BF) for h in range(LANES // size)]


def three(value):
    top = value.astype(BF)
    rest = value - top.astype(F32)
    mid = rest.astype(BF)
    return top, mid, (rest - mid.astype(F32)).astype(BF)


class Moves:
    def __init__(self, names, sources, targets, sems):
        self.targets = dict(zip(names, targets))
        self.copies = {name: pltpu.make_async_copy(a, b, sems.at[i]) for i, (name, a, b) in enumerate(zip(names, sources, targets))}
        self.open = []

    def start(self, *names):
        for name in names or self.copies:
            self.copies[name].start()
            self.open.append(name)

    def __call__(self, name):
        if name in self.open:
            self.copies[name].wait()
            self.open.remove(name)
        return self.targets[name]

    def close(self):
        for name in list(self.open):
            self(name)


def wide_attention(width, heads, rows, triple, bias, probs, mixed):
    size = width // heads
    per = LANES // size
    masks = head_masks(size)
    for g in range(width // LANES):
        q, k, v = (triple[:, t * width + g * LANES : t * width + (g + 1) * LANES] for t in range(3))
        v_side = v.T
        parts = []
        for h in range(per):
            s = dot_nt(k * masks[h], q) * size ** (-0.5) + bias[...]
            e = jnp.exp(s - jnp.max(s, axis=0, keepdims=True))
            p = e * (1.0 / jnp.sum(e, axis=0, keepdims=True))
            probs[g * per + h] = p
            parts.append(dot_nn(v_side[h * size : (h + 1) * size, :], p.astype(BF)))
        mixed[:, g * LANES : (g + 1) * LANES] = jnp.concatenate(parts, axis=0).T.astype(BF)


def wide_attention_back(width, heads, triple, probs, low_mixed, grad_triple):
    size = width // heads
    per = LANES // size
    masks = head_masks(size)
    for g in range(width // LANES):
        lanes = [slice(t * width + g * LANES, t * width + (g + 1) * LANES) for t in range(3)]
        q, k, v = (triple[:, lane] for lane in lanes)
        dm = low_mixed[:, g * LANES : (g + 1) * LANES]
        k_side = k.T
        parts, dk, dv = [], 0.0, 0.0
        for h in range(per):
            p = probs[g * per + h]
            dp = dot_nt(v * masks[h], dm)
            ds = (p * (dp - jnp.sum(p * dp, axis=0, keepdims=True))).astype(BF)
            dv = dv + dot_nn(p.astype(BF), dm * masks[h])
            dk = dk + dot_nn(ds, q * masks[h])
            parts.append(dot_nn(k_side[h * size : (h + 1) * size, :], ds))
        grad_triple[:, lanes[0]] = (jnp.concatenate(parts, axis=0).T * size ** (-0.5)).astype(BF)
        grad_triple[:, lanes[1]] = (dk * size ** (-0.5)).astype(BF)
        grad_triple[:, lanes[2]] = dv.astype(BF)


def block_forward(x, rows, images, heads, need, norms, key_bias, saved, done=lambda *names: None):
    entry, plain1, scale1, triple, probs, mixed, plain2, scale2, inner, act, slope = saved
    width = x.shape[1]
    size = width // heads
    per = LANES // size
    groups = width // LANES

    def first(i):
        at = rows_at(i, rows)
        plain, scale = norm(x[at, :])
        plain1[at, :] = plain
        scale1[at, :] = scale
        entry[at, :] = (plain * norms[0:1, :] + norms[1:2, :]).astype(BF)

    loop(images, first, 2)

    done("entry", "plain1", "scale1")
    triple_w = need("triple_w")

    def project(j):
        at = rows_at(j, 256)
        triple[:, at] = dot_nn(entry[...], triple_w[:, at]).astype(BF)

    loop(3 * width // 256, project, 3)
    done("triple")
    masks = head_masks(size)

    def attend(i):
        at = rows_at(i, rows)
        bias = key_bias(i)
        for g in range(groups):
            q = triple[at, g * LANES : (g + 1) * LANES]
            k = triple[at, width + g * LANES : width + (g + 1) * LANES]
            v = triple[at, 2 * width + g * LANES : 2 * width + (g + 1) * LANES]
            v_side = v.T
            parts = []
            for h in range(per):
                s = dot_nt(k * masks[h], q) * size ** (-0.5) + bias
                e = jnp.exp(s - jnp.max(s, axis=0, keepdims=True))
                p = e * (1.0 / jnp.sum(e, axis=0, keepdims=True))
                probs[i * groups + g, h * rows : (h + 1) * rows, :] = p
                parts.append(dot_nn(v_side[h * size : (h + 1) * size, :], p.astype(BF)))
            mixed[at, g * LANES : (g + 1) * LANES] = jnp.concatenate(parts, axis=0).T.astype(BF)

    if callable(key_bias):
        loop(images, attend)
    else:
        wide_attention(width, heads, rows, triple, key_bias, probs, mixed)
    done("probs", "mixed")
    proj_w = need("proj_w")

    def middle(j):
        at = rows_at(j, 256)
        x[:, at] += dot_nn(mixed[...], proj_w[:, at])

    loop(width // 256, middle, width // 256)

    def second(i):
        at = rows_at(i, rows)
        plain, scale = norm(x[at, :])
        plain2[at, :] = plain
        scale2[at, :] = scale
        inner[at, :] = (plain * norms[2:3, :] + norms[3:4, :]).astype(BF)

    loop(images, second, 2)
    done("plain2", "scale2", "inner")
    up_w = need("up_w")
    hidden = up_w.shape[1]

    def up(j):
        at = rows_at(j, 256)
        value, gradient = gelu_pair(dot_nn(inner[...], up_w[:, at]))
        act[:, at] = value.astype(BF)
        slope[:, at] = gradient

    loop(hidden // 256, up, 4)
    done("act", "slope")
    down_w = need("down_w")

    def down(j):
        at = rows_at(j, 256)
        x[:, at] += dot_nn(act[...], down_w[:, at])

    loop(width // 256, down, width // 256)


class Writer:
    def __init__(self, flat, stage, sem):
        self.flat, self.stage, self.sem = flat, stage, sem
        self.pending = {}

    def settle(self, s):
        if s in self.pending:
            self.pending.pop(s).wait()

    def outer(self, number, left, right, chunk=256):
        _, _, cols, tile, _ = ENTRIES[number]
        rows = left.shape[1]
        count = rows // chunk
        tall = chunk // 8
        before = dict(self.pending)

        def copy(i, s):
            return pltpu.make_async_copy(
                self.stage.at[s, pl.ds(0, tall * cols)], self.flat.at[pl.ds(tile + i * tall * cols, tall * cols)], self.sem.at[s]
            )

        def body(i):
            s = lax.rem(i, 2)
            for early in before:
                pl.when(i == early)(before[early].wait)

            @pl.when(i >= 2)
            def _():
                copy(i - 2, s).wait()

            side = left[:, rows_at(i, chunk)].T
            for c in range(0, cols, 2):
                value = dot_nn(side, right[:, c * LANES : (c + 2) * LANES])
                for d in range(2):
                    self.stage[s, pl.ds(c + d, tall, stride=cols)] = value[:, d * LANES : (d + 1) * LANES].reshape(tall, 8, LANES)
            copy(i, s).start()

        loop(count, body)
        self.pending = {(count - 2) % 2: copy(count - 2, (count - 2) % 2), (count - 1) % 2: copy(count - 1, (count - 1) % 2)}

    def small(self, number, norm_sums, count, extra=0):
        _, _, _, tile, groups = ENTRIES[number]
        per = SHAPES[number][1] // LANES
        self.settle(0)
        self.stage[0, 0 : groups + extra] = jnp.zeros((groups + extra, 8, LANES), F32)
        for r in range(count):
            for c in range(per):
                line = r * per + c
                self.stage[0, line // 8, line % 8 : line % 8 + 1, :] = norm_sums[r : r + 1, c * LANES : (c + 1) * LANES]
        copy = pltpu.make_async_copy(self.stage.at[0, pl.ds(0, groups + extra)], self.flat.at[pl.ds(tile, groups + extra)], self.sem.at[0])
        copy.start()
        copy.wait()
        self.settle(1)


def block_backward(grad, rows, images, heads, need, norms, norm_sums, extra, writer, numbers, tick=lambda: None):
    low, grad_hidden, side, low_mixed, grad_triple = extra
    width = grad.shape[1]
    size = width // heads
    per = LANES // size
    groups = width // LANES
    low[...] = grad[...].astype(BF)
    down_w, slope = need("down_w"), need("slope")
    hidden = down_w.shape[0]

    def back_up(j):
        at = rows_at(j, 256)
        grad_hidden[:, at] = (dot_nt(low[...], down_w[at, :]) * slope[:, at]).astype(BF)

    loop(hidden // 256, back_up, 4)
    tick()
    writer.outer(numbers[3], need("act"), low)
    tick()
    writer.outer(numbers[2], need("inner"), grad_hidden)
    tick()
    up_w = need("up_w")

    def back_inner(j):
        at = rows_at(j, 256)
        side[:, at] = dot_nt(grad_hidden[...], up_w[at, :])

    loop(width // 256, back_inner, width // 256)
    tick()
    plain2, scale2 = need("plain2"), need("scale2")

    def second(i):
        at = rows_at(i, rows)
        back, gain, shift = norm_grad(side[at, :], plain2[at, :], scale2[at, :], norms[2:3, :])
        norm_sums[2:3, :] += gain
        norm_sums[3:4, :] += shift
        total = grad[at, :] + back
        grad[at, :] = total
        low[at, :] = total.astype(BF)

    loop(images, second, 2)
    writer.outer(numbers[1], need("mixed"), low)
    proj_w = need("proj_w")

    def back_mixed(j):
        at = rows_at(j, 256)
        low_mixed[:, at] = dot_nt(low[...], proj_w[at, :]).astype(BF)

    loop(width // 256, back_mixed, width // 256)
    tick()
    triple, probs = need("triple"), need("probs")
    masks = head_masks(size)

    def attend(i):
        at = rows_at(i, rows)
        for g in range(groups):
            lanes = [slice(t * width + g * LANES, t * width + (g + 1) * LANES) for t in range(3)]
            q, k, v = (triple[at, lane] for lane in lanes)
            dm = low_mixed[at, g * LANES : (g + 1) * LANES]
            k_side = k.T
            parts, dk, dv = [], 0.0, 0.0
            for h in range(per):
                p = probs[i * groups + g, h * rows : (h + 1) * rows, :]
                dp = dot_nt(v * masks[h], dm)
                ds = (p * (dp - jnp.sum(p * dp, axis=0, keepdims=True))).astype(BF)
                dv = dv + dot_nn(p.astype(BF), dm * masks[h])
                dk = dk + dot_nn(ds, q * masks[h])
                parts.append(dot_nn(k_side[h * size : (h + 1) * size, :], ds))
            dq = jnp.concatenate(parts, axis=0).T
            grad_triple[at, lanes[0]] = (dq * size ** (-0.5)).astype(BF)
            grad_triple[at, lanes[1]] = (dk * size ** (-0.5)).astype(BF)
            grad_triple[at, lanes[2]] = dv.astype(BF)

    if probs.shape[1] == probs.shape[2] and probs.shape[0] == heads:
        wide_attention_back(width, heads, triple, probs, low_mixed, grad_triple)
    else:
        loop(images, attend)
    tick()
    writer.outer(numbers[0], need("entry"), grad_triple)
    tick()
    triple_w = need("triple_w")

    def back_entry(j):
        at = rows_at(j, 256)
        side[:, at] = dot_nt(grad_triple[...], triple_w[at, :])

    loop(width // 256, back_entry, width // 256)
    tick()
    plain1, scale1 = need("plain1"), need("scale1")

    def first(i):
        at = rows_at(i, rows)
        back, gain, shift = norm_grad(side[at, :], plain1[at, :], scale1[at, :], norms[0:1, :])
        norm_sums[0:1, :] += gain
        norm_sums[1:2, :] += shift
        grad[at, :] += back

    loop(images, first, 2)


TICKS = 11
SAVED = ("seen", "entry", "plain1", "scale1", "triple", "probs", "mixed", "plain2", "scale2", "inner", "act", "slope", "plain3", "scale3", "encoded")
ENC_NAMES = ("embed_w", "triple_w", "proj_w", "up_w", "down_w", "dec_embed_w")
DEC_NAMES = ("triple_w", "proj_w", "up_w", "down_w", "head_w")


def saved_shapes(rows):
    s = jax.ShapeDtypeStruct
    return [
        s((rows, D), BF), s((rows, D), BF), s((rows, D), F32), s((rows, 1), F32), s((rows, 3 * D), BF),
        s((HEADS, rows, rows), F32), s((rows, D), BF), s((rows, D), F32), s((rows, 1), F32), s((rows, D), BF),
        s((rows, F), BF), s((rows, F), F32), s((rows, D), F32), s((rows, 1), F32), s((rows, D), BF),
    ]


def like(shape):
    return pltpu.VMEM(shape.shape, shape.dtype)


def pad_patches(patches, padded, images):
    padded[...] = jnp.zeros_like(padded)
    for i in range(images):
        padded[i * P_ROWS : i * P_ROWS + PATCHES, :] = patches[i]


def encoder_kernel(images, counts_ref, rows_ref, norms_ref, *refs):
    pos_hbm, patches_hbm, *weights_hbm = refs[:8]
    outs = refs[8:23]
    entering = refs[23]
    pos, patches, *weights = refs[24:32]
    saved = dict(zip(SAVED, refs[32:47]))
    x, place_, pos_split, padded, bias, in_sem, out_sem = refs[47:]
    need = Moves(("pos", "patches") + ENC_NAMES, [pos_hbm, patches_hbm] + weights_hbm, [pos, patches] + weights, in_sem)
    need.start()
    put = Moves(SAVED, [saved[name] for name in SAVED], outs, out_sem)
    rows = images * KEEP
    key = lax.broadcasted_iota(jnp.int32, (KEEP, rows), 0)
    query = lax.broadcasted_iota(jnp.int32, (KEEP, rows), 1)
    for i in range(images):
        inside = jnp.logical_and(jnp.logical_and(query >= i * KEEP, query < (i + 1) * KEEP), key < counts_ref[i])
        bias[i * KEEP : (i + 1) * KEEP, :] = jnp.where(inside, 0.0, NEG_FILL)
    need("pos")
    for t, part in enumerate(three(pos[...])):
        pos_split[t] = part
    pad_patches(need("patches"), padded, images)
    spot = lax.broadcasted_iota(jnp.int32, (P_ROWS, KEEP), 0)
    seen = saved["seen"]

    def select(i):
        at = rows_at(i, KEEP)
        pick = jnp.where(spot == rows_ref[pl.ds(i, 1), 0:KEEP], 1.0, 0.0).T.astype(BF)
        seen[at, :] = dot_nn(pick, padded[rows_at(i, P_ROWS), :]).astype(BF)
        place_[at, :] = dot_nn(pick, pos_split[0]) + dot_nn(pick, pos_split[1]) + dot_nn(pick, pos_split[2])

    loop(images, select, 2)
    put.start("seen")
    embed_w = need("embed_w")

    def embed(j):
        at = rows_at(j, 256)
        x[:, at] = dot_nn(seen[...], embed_w[:, at]) + place_[:, at]

    loop(D // 256, embed, D // 256)
    block_forward(x, KEEP, images, HEADS, need, norms_ref, bias, [saved[name] for name in SAVED[1:12]], put.start)
    plain3, scale3, encoded = (saved[name] for name in SAVED[12:])

    def last(i):
        at = rows_at(i, KEEP)
        plain, scale = norm(x[at, :])
        plain3[at, :] = plain
        scale3[at, :] = scale
        encoded[at, :] = (plain * norms_ref[4:5, :] + norms_ref[5:6, :]).astype(BF)

    loop(images, last, 2)
    put.start("plain3", "scale3", "encoded")
    entering[...] = dot_nn(encoded[...], need("dec_embed_w")[...])
    put.close()


def encoder(counts, patches, order, pos, weights, norms):
    images = counts.shape[0]
    rows = images * KEEP
    vmem = pl.BlockSpec(memory_space=pltpu.VMEM)
    anyspec = pl.BlockSpec(memory_space=pl.ANY)
    shapes = saved_shapes(rows)
    return pl.pallas_call(
        functools.partial(encoder_kernel, images),
        name="encoder",
        out_shape=shapes + [jax.ShapeDtypeStruct((rows, DD), F32)],
        in_specs=[pl.BlockSpec(memory_space=pltpu.SMEM), vmem, vmem] + [anyspec] * 8,
        out_specs=[anyspec] * 15 + [vmem],
        scratch_shapes=[like(one) for one in [pos, patches] + weights + shapes]
        + [
            pltpu.VMEM((rows, D), F32), pltpu.VMEM((rows, D), F32), pltpu.VMEM((3, P_ROWS, D), BF), pltpu.VMEM((images * P_ROWS, PIX), BF),
            pltpu.VMEM((rows, rows), F32), pltpu.SemaphoreType.DMA((8,)), pltpu.SemaphoreType.DMA((15,)),
        ],
        compiler_params=pltpu.CompilerParams(vmem_limit_bytes=60 * MB),
    )(counts, order, norms, pos, patches, *weights)


def decoder_kernel(images, counts_ref, masked_ref, rows_ref, entering_ref, norms_ref, *refs):
    pos_hbm, patches_hbm, *weights_hbm = refs[:7]
    flat, grad_entering, loss_ref = refs[7:10]
    pos, patches, *weights = refs[10:17]
    (x, hide, entry, plain1, scale1, triple, probs, mixed, plain2, scale2, inner, act, slope, plain3, scale3, final, grad_pred,
     low, grad_hidden, side, low_mixed, grad_triple, norm_sums, padded, stage, sem, in_sem) = refs[17:]
    need = Moves(("pos", "patches") + DEC_NAMES, [pos_hbm, patches_hbm] + weights_hbm, [pos, patches] + weights, in_sem)
    need.start()
    saved = (entry, plain1, scale1, triple, probs, mixed, plain2, scale2, inner, act, slope)
    need.targets.update(zip(SAVED[1:12], saved))
    lane = lax.broadcasted_iota(jnp.int32, (P_ROWS, KEEP), 1)
    spot = lax.broadcasted_iota(jnp.int32, (P_ROWS, KEEP), 0)
    line = lax.broadcasted_iota(jnp.int32, (P_ROWS, 1), 0)
    need("pos")

    def start(i):
        at = rows_at(i, P_ROWS)
        hit = jnp.where(jnp.logical_and(spot == rows_ref[pl.ds(i, 1), 0:KEEP], lane < counts_ref[i]), 1.0, 0.0)
        shown = jnp.max(hit, axis=1, keepdims=True)
        pick = hit.astype(BF)
        top, mid, end = three(entering_ref[rows_at(i, KEEP), :])
        picked = dot_nn(pick, top) + dot_nn(pick, mid) + dot_nn(pick, end)
        x[at, :] = jnp.where(shown > 0.0, picked, norms_ref[6:7, :]) + pos[...]
        hide[at, :] = jnp.where(jnp.logical_and(line < PATCHES, shown == 0.0), 1.0, 0.0)

    loop(images, start, 2)
    bias = jnp.where(line < PATCHES, 0.0, NEG_FILL)
    block_forward(x, P_ROWS, images, DHEADS, need, norms_ref, lambda i: bias, saved)

    def last(i):
        at = rows_at(i, P_ROWS)
        plain, scale = norm(x[at, :])
        plain3[at, :] = plain
        scale3[at, :] = scale
        final[at, :] = (plain * norms_ref[4:5, :] + norms_ref[5:6, :]).astype(BF)

    loop(images, last, 2)
    loss_ref[...] = jnp.zeros_like(loss_ref)
    masked = masked_ref[0:1, 0:1]
    head_w = need("head_w")
    pad_patches(need("patches"), padded, images)

    def score(i):
        at = rows_at(i, P_ROWS)
        target, _ = norm(padded[at, :].astype(F32))
        diff = dot_nn(final[at, :], head_w[...]) - target
        hidden = hide[at, :]
        loss_ref[...] += jnp.sum(jnp.mean(diff * diff, axis=-1, keepdims=True) * hidden, axis=0, keepdims=True)
        grad_pred[at, :] = (diff * (hidden * (2.0 / PIX)) / masked).astype(BF)

    loop(images, score, 2)
    writer = Writer(flat, stage, sem)
    writer.outer(11, final, grad_pred)
    norm_sums[...] = jnp.zeros_like(norm_sums)

    def back_final(i):
        at = rows_at(i, P_ROWS)
        back, gain, shift = norm_grad(dot_nt(grad_pred[at, :], head_w[...]), plain3[at, :], scale3[at, :], norms_ref[4:5, :])
        norm_sums[4:5, :] += gain
        norm_sums[5:6, :] += shift
        x[at, :] = back

    loop(images, back_final, 2)
    block_backward(x, P_ROWS, images, DHEADS, need, norms_ref, norm_sums, (low, grad_hidden, side, low_mixed, grad_triple), writer, (7, 8, 9, 10))

    def finish(i):
        at = rows_at(i, P_ROWS)
        grad = x[at, :]
        norm_sums[6:7, :] += jnp.sum(grad * hide[at, :], axis=0, keepdims=True)
        pick = jnp.where(jnp.logical_and(spot == rows_ref[pl.ds(i, 1), 0:KEEP], lane < counts_ref[i]), 1.0, 0.0).T.astype(BF)
        grad_entering[rows_at(i, KEEP), :] = dot_nn(pick, grad.astype(BF)).astype(BF)

    loop(images, finish, 2)
    writer.small(12, norm_sums, 7, flat.shape[0] - TILES)


def decoder(total, counts, masked, patches, order, pos, entering, weights, norms):
    images = counts.shape[0]
    rows = images * P_ROWS
    vmem = pl.BlockSpec(memory_space=pltpu.VMEM)
    anyspec = pl.BlockSpec(memory_space=pl.ANY)

    def v(shape, kind=F32):
        return pltpu.VMEM(shape, kind)

    return pl.pallas_call(
        functools.partial(decoder_kernel, images),
        name="decoder",
        out_shape=[
            jax.ShapeDtypeStruct((total, 8, LANES), F32),
            jax.ShapeDtypeStruct((images * KEEP, DD), BF),
            jax.ShapeDtypeStruct((1, 1), F32),
        ],
        in_specs=[pl.BlockSpec(memory_space=pltpu.SMEM)] + [vmem] * 4 + [anyspec] * 7,
        out_specs=[anyspec, vmem, vmem],
        scratch_shapes=[like(one) for one in [pos, patches] + weights]
        + [
            v((rows, DD)), v((rows, 1)), v((rows, DD), BF), v((rows, DD)), v((rows, 1)), v((rows, 3 * DD), BF),
            v((images * DD // LANES, 4 * P_ROWS, P_ROWS)), v((rows, DD), BF), v((rows, DD)), v((rows, 1)), v((rows, DD), BF),
            v((rows, FD), BF), v((rows, FD)), v((rows, DD)), v((rows, 1)), v((rows, DD), BF), v((rows, PIX), BF),
            v((rows, DD), BF), v((rows, FD), BF), v((rows, DD)), v((rows, DD), BF), v((rows, 3 * DD), BF),
            v((8, DD)), v((rows, PIX), BF), v((2, 32 * 16, 8, LANES)), pltpu.SemaphoreType.DMA((2,)), pltpu.SemaphoreType.DMA((7,)),
        ],
        compiler_params=pltpu.CompilerParams(vmem_limit_bytes=63 * MB),
    )(counts, masked, order, entering, norms, pos, patches, *weights)


def encoder_back_kernel(images, share, n, chunks, flat_in, grad_entering, norms_ref, *refs):
    names = SAVED + ENC_NAMES[1:]
    sources = refs[:20]
    flat, late_ref, sib_ref = refs[20:23]
    targets = refs[23:43]
    x, low, grad_hidden, side, low_mixed, grad_triple, norm_sums, stage, sem, in_sem = refs[43:53]
    cut = late_cut(share)
    steps = late_ref.shape[0] * chunks
    plane = Plane(share, n, chunks, steps, lambda group: cut + group, flat, sib_ref, late_ref, 0, refs[53:])
    barrier = pltpu.get_barrier_semaphore()
    for name in ("x", "y", "c"):
        pl.semaphore_signal(barrier, inc=1, device_id=plane.to[name], device_id_type=MESH)
    need = Moves(names, sources, targets, in_sem)
    need.start(
        "encoded", "dec_embed_w", "plain3", "scale3", "down_w", "slope", "act", "inner", "up_w", "plain2", "scale2",
        "mixed", "proj_w", "triple", "probs", "entry", "triple_w", "plain1", "scale1", "seen",
    )
    pl.semaphore_wait(barrier, 3)
    plane.begin()
    one, two, three_, load = plane.stage_one, plane.stage_two, plane.stage_three, plane.load
    if steps == 4:
        plan = [
            [(load, 0)], [(one, 0), (load, 1)], [(one, 1)], [(two, 0), (load, 2)], [(one, 2), (two, 1), (load, 3)], [(one, 3)],
            [(two, 2), (three_, 0), (three_, 1)], [(two, 3), (three_, 2)], [], [], [(three_, 3)],
        ]
    else:
        flow = [(load, 0)]
        for t in range(steps + 2):
            flow += [(stage_, s) for stage_, s in ((one, t), (two, t - 1), (load, t + 1), (three_, t - 2)) if 0 <= s < steps]
        size = -(-len(flow) // TICKS)
        plan = [flow[i * size : (i + 1) * size] for i in range(TICKS)]

    def tick():
        for stage_, s in plan.pop(0):
            stage_(s)

    writer = Writer(flat, stage, sem)
    writer.outer(6, need("encoded"), grad_entering)
    norm_sums[...] = jnp.zeros_like(norm_sums)
    side[...] = dot_nt(grad_entering[...], need("dec_embed_w")[...])
    plain3, scale3 = need("plain3"), need("scale3")

    def last(i):
        at = rows_at(i, KEEP)
        back, gain, shift = norm_grad(side[at, :], plain3[at, :], scale3[at, :], norms_ref[4:5, :])
        norm_sums[4:5, :] += gain
        norm_sums[5:6, :] += shift
        x[at, :] = back

    loop(images, last, 2)
    tick()
    block_backward(x, KEEP, images, HEADS, need, norms_ref, norm_sums, (low, grad_hidden, side, low_mixed, grad_triple), writer, (1, 2, 3, 4), tick)
    low[...] = x[...].astype(BF)
    tick()
    writer.outer(0, need("seen"), low)
    tick()
    writer.small(5, norm_sums, 6)
    plane.finish()


def encoder_back(flat, grad_entering, saved, weights, norms, share, n_dp, n_pair):
    chunks = reduce_chunks(share, n_dp * n_pair)
    slab = slab_tiles(share, n_dp * n_pair) * 8
    groups = n_dp // 2 - late_cut(share)
    part = slab // chunks
    rows = grad_entering.shape[0]
    images = rows // KEEP
    vmem = pl.BlockSpec(memory_space=pltpu.VMEM)
    anyspec = pl.BlockSpec(memory_space=pl.ANY)

    def v(shape, kind=F32):
        return pltpu.VMEM(shape, kind)

    return pl.pallas_call(
        functools.partial(encoder_back_kernel, images, share, n_dp * n_pair, chunks),
        name="encoder_back",
        out_shape=[
            jax.ShapeDtypeStruct(flat.shape, flat.dtype),
            jax.ShapeDtypeStruct((groups, slab, LANES), F32),
            jax.ShapeDtypeStruct((groups * chunks, 4, part // 8, 8, LANES), F32),
        ],
        in_specs=[anyspec, vmem, vmem] + [anyspec] * 20,
        out_specs=[anyspec, vmem, anyspec],
        scratch_shapes=[like(one) for one in saved + weights]
        + [
            v((rows, D)), v((rows, D), BF), v((rows, F), BF), v((rows, D)), v((rows, D), BF), v((rows, 3 * D), BF),
            v((8, D)), v((2, 32 * 24, 8, LANES)), pltpu.SemaphoreType.DMA((2,)), pltpu.SemaphoreType.DMA((20,)),
        ]
        + plane_scratch(groups * chunks, part),
        input_output_aliases={0: 0},
        compiler_params=pltpu.CompilerParams(collective_id=2, has_side_effects=True, vmem_limit_bytes=63 * MB),
    )(flat, grad_entering, norms, *saved, *weights)[:2]


def positions(width):
    index = np.arange(PATCHES)
    quarter = width // 4
    freq = 10000.0 ** (-np.arange(quarter).astype(np.float32) / np.float32(quarter))
    row = (index // GRID).astype(np.float32)[:, None] * freq[None, :].astype(np.float32)
    column = (index % GRID).astype(np.float32)[:, None] * freq[None, :].astype(np.float32)
    table = np.concatenate([np.sin(row), np.cos(row), np.sin(column), np.cos(column)], axis=1).astype(np.float32)
    return jnp.asarray(np.pad(table, ((0, P_ROWS - PATCHES), (0, 0))))


def own_lines(flat, share, index):
    if share % LANES == 0:
        return flat.reshape(-1, LANES)
    rows = (share + LANES - 1) // LANES + 1
    return lax.dynamic_update_slice(jnp.zeros((rows * LANES,), flat.dtype), flat, (share * index % LANES,)).reshape(rows, LANES)


def own_flat(lines, share, index):
    if share % LANES == 0:
        return lines.reshape(-1)
    return lax.dynamic_slice(lines.reshape(-1), (share * index % LANES,), (share,))


def body(n_dp, n_pair, patches, patch_order, counts, master, moment1, moment2, block_rates, clip_limit, step_count):
    n = n_dp * n_pair
    share = master.shape[0]
    images = counts.shape[0]
    index = lax.axis_index("dp") * n_pair + lax.axis_index("pair")
    extra = jnp.zeros((8, LANES), F32).at[0, :images].set((PATCHES - counts).astype(F32))
    lines = own_lines(master, share, index)
    *held, enc_norms, dec_norms, masked = gather(lines, extra, share, n_dp, n_pair)
    parts = {i: matrix(one, i) for i, one in zip(BIG, held)}
    enc_weights = [parts[i] for i in (1, 2, 3, 4, 6)]
    *saved, entering = encoder(counts, patches, patch_order[:, :KEEP], positions(D), [parts[0]] + enc_weights, enc_norms)
    total = max(a for a, _ in ranges(share, n)) + slab_tiles(share, n)
    dec_weights = [parts[i] for i in (7, 8, 9, 10, 11)]
    flat, grad_entering, loss_local = decoder(total, counts, masked, patches, patch_order[:, :KEEP], positions(DD), entering, dec_weights, dec_norms)
    flat, late = encoder_back(flat, grad_entering, saved, enc_weights, enc_norms, share, n_dp, n_pair)
    grad_lines, totals = reduce(flat, late, loss_local, lines.shape, share, n_dp, n_pair)
    grad_norm = totals[0, 0:1]
    loss = totals[1, 0:1] / masked[0]
    clipped = own_flat(grad_lines, share, index) * (clip_limit[0] / (grad_norm[0] + NORM_EPS))
    first = BETA_ONE * moment1 + (1.0 - BETA_ONE) * clipped
    second = BETA_TWO * moment2 + (1.0 - BETA_TWO) * clipped * clipped
    steps_done = step_count[0].astype(F32)
    position = index * share + jnp.arange(share)
    rate = jnp.where(position < ENC_PARAMS, block_rates[0], block_rates[1])
    update = first / (1.0 - BETA_ONE**steps_done) / (jnp.sqrt(second / (1.0 - BETA_TWO**steps_done)) + ADAM_EPS)
    master_new = master - rate * (update + DECAY * master)
    return (loss, grad_norm, first, second, master_new)


def solution(mesh):
    whole = P(("dp", "pair"))
    in_specs = (P(("dp", "pair"), None, None), P(("dp", "pair"), None), whole, whole, whole, whole, P(), P(), P())
    out_specs = (P(), P(), whole, whole, whole)
    step = functools.partial(body, mesh.shape["dp"], mesh.shape["pair"])
    return jax.shard_map(step, mesh=mesh, in_specs=in_specs, out_specs=out_specs, check_vma=False)
```

```python
import functools

import jax
import jax.numpy as jnp
import numpy as np
from jax import lax
from jax.experimental import pallas as pl
from jax.experimental.pallas import tpu as pltpu
from jax.sharding import PartitionSpec as P

MESH = pl.DeviceIdType.MESH
LANES = 128
TILE = 16 * LANES


def place():
    dp, pair = lax.axis_index("dp"), lax.axis_index("pair")
    return dp // 2, dp % 2, pair // 2, pair % 2


def slot_of(z, x, y, c):
    return (z * 2 + x) * 4 + y * 2 + c


def partners(z, x, y, c):
    return {
        "x": {"dp": z * 2 + (1 - x)},
        "y": {"pair": (1 - y) * 2 + c},
        "c": {"pair": y * 2 + (1 - c)},
        "up": {"dp": (z + 1) * 2 + x},
        "down": {"dp": (z - 1) * 2 + x},
    }


def greet(n_z, z, to):
    barrier = pltpu.get_barrier_semaphore()
    for name in ("x", "y", "c"):
        pl.semaphore_signal(barrier, inc=1, device_id=to[name], device_id_type=MESH)

    @pl.when(z < n_z - 1)
    def _():
        pl.semaphore_signal(barrier, inc=1, device_id=to["up"], device_id_type=MESH)

    @pl.when(z > 0)
    def _():
        pl.semaphore_signal(barrier, inc=1, device_id=to["down"], device_id_type=MESH)

    pl.semaphore_wait(barrier, 3 + jnp.where(z < n_z - 1, 1, 0) + jnp.where(z > 0, 1, 0))


def both(*conditions):
    total = conditions[0]
    for one in conditions[1:]:
        total = jnp.logical_and(total, one)
    return total


PIX, HEADS, F, DHEADS, FD, GRID, KEEP, D, DD, PATCHES = 768, 12, 3072, 16, 2048, 14, 64, 768, 512, 196
SHAPES = [(PIX, D), (D, 3 * D), (D, D), (D, F), (F, D), (6, D), (D, DD), (DD, 3 * DD), (DD, DD), (DD, FD), (FD, DD), (DD, PIX), (7, DD)]
SMALL = (5, 12)
ENC_PARAMS = 7672320
NORM_EPS = 1e-06
ADAM_EPS = 1e-08
BETA_ONE = 0.9
BETA_TWO = 0.95
DECAY = 0.05
MB = 1 << 20
CELL = 8 * LANES
BLOCK = 96


def make_entries():
    entries, row, tile = [], 0, 0
    for number, (rows, width) in enumerate(SHAPES):
        lines = rows * width // LANES
        cols = 1 if number in SMALL else width // LANES
        groups = -(-lines // (8 * cols))
        entries.append((row, lines, cols, tile, groups))
        row += lines
        tile += groups * cols
    return entries, row, tile


ENTRIES, ROWS, TILES = make_entries()
BIG = tuple(i for i in range(len(SHAPES)) if i not in SMALL)
MARGIN = 8 * max(cols for _, _, cols, _, _ in ENTRIES)


def first_tile(share, k):
    lo = share * k
    total = 0
    for row, lines, cols, tile, _ in ENTRIES:
        inside = jnp.logical_and(lo >= row * LANES, lo < (row + lines) * LANES)
        total = total + jnp.where(inside, tile + (lo - row * LANES) // (CELL * cols) * cols, 0)
    return total


def ranges(share, n):
    found = []
    for k in range(n):
        lo, hi = share * k, share * (k + 1)
        spans = []
        for row, lines, cols, tile, _ in ENTRIES:
            low, high = max(lo, row * LANES), min(hi, (row + lines) * LANES)
            if low < high:
                size = CELL * cols
                spans.append((tile + (low - row * LANES) // size * cols, tile + -(-(high - row * LANES) // size) * cols))
        found.append((spans[0][0], spans[-1][1]))
    return found


def slab_tiles(share, n):
    longest = max(b - a for a, b in ranges(share, n))
    return -(-longest // 24) * 24


def line_span(share, k):
    return share * k // LANES, (share * (k + 1) + LANES - 1) // LANES


def tiled(share, k, body):
    lo, hi = line_span(share, k)
    begin = first_tile(share, k)
    for number in SMALL + tuple(i for i in range(len(ENTRIES)) if i not in SMALL):
        row, lines, cols, tile, _ = ENTRIES[number]
        low = jnp.maximum(lo, row) - row
        high = jnp.minimum(hi, row + lines) - row
        size = 8 * cols

        def group(g, _, row=row, cols=cols, tile=tile, size=size):
            body(row + g * size - lo + MARGIN, tile + g * cols - begin, cols)
            return 0

        lax.fori_loop(jnp.where(low < high, low // size, 0), jnp.where(low < high, (high + size - 1) // size, 0), group, 0)


def wide_rows(rows):
    return -(-(rows + 2 * MARGIN) // 8) * 8


def pieces(share, n):
    spans = ranges(share, n)
    shared = [spans[k][1] > spans[k + 1][0] for k in range(n - 1)]
    plain, seams = [], []
    for number, (_, _, cols, tile, groups) in enumerate(ENTRIES):
        end = tile + groups * cols
        for k, (a, b) in enumerate(spans):
            low, high = max(a, tile), min(b, end)
            if low >= high:
                continue
            inner_low, inner_high = low, high
            if k > 0 and spans[k - 1][1] > low:
                inner_low = spans[k - 1][1]
            if k < n - 1 and spans[k + 1][0] < high:
                inner_high = spans[k + 1][0]
                seams.append((number, k, inner_high, high))
            if inner_low < inner_high:
                plain.append((number, k, inner_low, inner_high))
    return spans, plain, seams


def matrix(tiles_, number):
    rows, width = SHAPES[number]
    cols = width // LANES
    return tiles_.reshape(rows // 8, cols, 8, LANES).transpose(0, 2, 1, 3).reshape(rows, width)


def matrix_tiles(value):
    rows, width = value.shape
    cols = width // LANES
    return value.reshape(rows // 8, 8, cols, LANES).transpose(0, 2, 1, 3).reshape(rows * cols, LANES)


def gather_kernel(n_z, n_pair, share, lines_ref, extra_ref, *refs):
    outs = dict(zip(BIG, refs[: len(BIG)]))
    enc_norms, dec_norms, masked_ref = refs[len(BIG) : len(BIG) + 3]
    wide, out_ref, z_sem, plane_sem, second_sem, third_sem, flat_sem, line_sem, core_sem, recv_sem, put_sem = refs[len(BIG) + 3 :]
    n = n_z * 2 * n_pair
    total_tiles = out_ref.shape[1]
    small = total_tiles // 2 * 2 // 9
    large = total_tiles // 2 - small
    spans_of = ((0, large), (large, large), (2 * large, small), (2 * large + small, small), (2 * large, 2 * small))
    z, x, y, c = place()
    to = partners(z, x, y, c)
    me = slot_of(z, x, y, c)
    rows = lines_ref.shape[0]
    wide[0:MARGIN, :] = jnp.zeros((MARGIN, LANES), jnp.float32)
    wide[MARGIN + rows :, :] = jnp.zeros((wide.shape[0] - MARGIN - rows, LANES), jnp.float32)
    wide[MARGIN : MARGIN + rows, :] = lines_ref[...]

    def fill(line, tile, cols):
        for col in range(cols):
            out_ref[me, tile + col] = wide[pl.ds(line + col, 8, stride=cols), :].astype(out_ref.dtype)

    tiled(share, me, fill)
    out_ref[me, total_tiles - 2] = extra_ref[...].astype(out_ref.dtype)
    greet(n_z, z, to)

    def copy(slot, part, name, sem):
        at = pl.ds(*spans_of[part])
        return pltpu.make_async_remote_copy(
            out_ref.at[slot, at], out_ref.at[slot, at], sem, recv_sem.at[slot, 2 if part == 4 else part], device_id=to[name], device_id_type=MESH
        )

    def arrived(slot, part):
        copy(slot, part, "c", plane_sem.at[0, 0, 0]).wait_recv()

    def start(one):
        one.start()

    def stop(one):
        one.wait_send()

    def lines(t):
        for d in (0, 1):
            zz = z - t if d == 0 else z + t
            inside = zz >= 0 if d == 0 else zz < n_z
            more = z < n_z - 1 if d == 0 else z > 0
            fresh = both(t > 0, inside)
            held = jnp.logical_or(fresh, t == 0) if d == 0 else fresh
            yield d, zz, fresh, held, more

    def own_z(act):
        for d, more in ((0, z < n_z - 1), (1, z > 0)):
            for part in (0, 1):
                pl.when(more)(lambda d=d, part=part: act(copy(me, part, ("up", "down")[d], z_sem.at[0, d, part])))

    def onward_z(t, d, zz, fresh, more, act):
        for part in (0, 1):
            pl.when(both(fresh, more))(lambda part=part: act(copy(slot_of(zz, x, y, c), part, ("up", "down")[d], z_sem.at[t, d, part])))

    def plane_sends(t, d, zz, held, act):
        @pl.when(held)
        def _():
            for i, (part, name) in enumerate(((0, "x"), (1, "y"), (0, "y"), (1, "x"), (0, "c"), (1, "c"))):
                act(copy(slot_of(zz, x, y, c), part, name, plane_sem.at[t, d, i]))

    def first(t):
        for d, zz, fresh, held, more in lines(t):

            @pl.when(fresh)
            def _():
                for part in (0, 1):
                    arrived(slot_of(zz, x, y, c), part)

            onward_z(t, d, zz, fresh, more, start)
            plane_sends(t, d, zz, held, start)

    def second_items(zz):
        return ((0, slot_of(zz, 1 - x, y, c), "y"), (1, slot_of(zz, x, 1 - y, c), "x"))

    def second(t):
        for d, zz, _, held, _ in lines(t):

            @pl.when(held)
            def _():
                for part, slot, name in second_items(zz):
                    arrived(slot, part)
                    copy(slot, part, name, second_sem.at[t, d, part, 0]).start()
                    copy(slot, part, "c", second_sem.at[t, d, part, 1]).start()

    def third_items(zz):
        return ((0, slot_of(zz, x, 1 - y, c)), (1, slot_of(zz, 1 - x, y, c)), (0, slot_of(zz, 1 - x, 1 - y, c)), (1, slot_of(zz, 1 - x, 1 - y, c)))

    def third(t):
        for d, zz, _, held, _ in lines(t):

            @pl.when(held)
            def _():
                for i, (part, slot) in enumerate(third_items(zz)):
                    arrived(slot, part)
                    copy(slot, part, "c", third_sem.at[t, d, i]).start()

    near = ((2, me, "x"), (3, me, "y"), (2, me, "y"), (3, me, "x"), (2, me, "c"), (3, me, "c"))
    beside = ((2, slot_of(z, 1 - x, y, c), "y"), (3, slot_of(z, x, 1 - y, c), "x"))
    across = ((2, slot_of(z, x, 1 - y, c)), (3, slot_of(z, 1 - x, y, c)), (2, slot_of(z, 1 - x, 1 - y, c)), (3, slot_of(z, 1 - x, 1 - y, c)))

    def flat_sends(act, which):
        for i, (part, slot, name) in enumerate(near):
            if which == 0:
                act(copy(slot, part, name, flat_sem.at[i]))
        for i, (part, slot, name) in enumerate(beside):
            if which == 1:
                act(copy(slot, part, name, flat_sem.at[6 + i]))
                act(copy(slot, part, "c", flat_sem.at[8 + i]))
        for i, (part, slot) in enumerate(across):
            if which == 2:
                act(copy(slot, part, "c", flat_sem.at[10 + i]))

    def corner(zz, i):
        return slot_of(zz, i // 2, i % 2, c)

    def line_sends(t, act):
        for d, zz, fresh, _, more in lines(t):
            for i in range(4):
                go = jnp.logical_or(fresh, t == 0)
                pl.when(both(go, more))(lambda d=d, zz=zz, i=i: act(copy(corner(zz, i), 4, ("up", "down")[d], line_sem.at[t, d, i])))
                pl.when(fresh)(lambda d=d, zz=zz, i=i: act(copy(corner(zz, i), 4, "c", core_sem.at[t, d, i])))

    def along(t):
        for d, zz, fresh, _, _ in lines(t):

            @pl.when(fresh)
            def _():
                for i in range(4):
                    arrived(corner(zz, i), 4)

        @pl.when(t == 0)
        def _():
            for part, slot in across:
                arrived(slot, part)
            flat_sends(start, 2)

        line_sends(t, start)

    own_z(start)
    flat_sends(start, 0)
    for part, slot, _ in beside:
        arrived(slot, part)
    flat_sends(start, 1)

    def turn(t, _):
        pl.when(t < n_z)(lambda: first(t))
        pl.when(both(t >= 1, t < n_z + 1))(lambda: second(t - 1))
        pl.when(both(t >= 1, t < n_z + 1))(lambda: along(t - 1))
        pl.when(t >= 2)(lambda: third(t - 2))
        return 0

    lax.fori_loop(0, n_z + 2, turn, 0)
    own_z(stop)
    for which in range(3):
        flat_sends(stop, which)

    def finish(t, _):
        line_sends(t, stop)
        for d, zz, fresh, held, more in lines(t):
            onward_z(t, d, zz, fresh, more, stop)
            plane_sends(t, d, zz, held, stop)

            @pl.when(held)
            def _():
                for part, slot, name in second_items(zz):
                    copy(slot, part, name, second_sem.at[t, d, part, 0]).wait_send()
                    copy(slot, part, "c", second_sem.at[t, d, part, 1]).wait_send()
                for i, (part, slot) in enumerate(third_items(zz)):
                    copy(slot, part, "c", third_sem.at[t, d, i]).wait_send()
                for i in range(4):
                    for part in (0, 1):
                        arrived(slot_of(zz, i // 2, i % 2, 1 - c), part)

            @pl.when(fresh)
            def _():
                for i in range(4):
                    arrived(slot_of(zz, i // 2, i % 2, 1 - c), 4)

        return 0

    lax.fori_loop(0, n_z, finish, 0)
    for i in range(4):
        for part in (2, 3):
            arrived(slot_of(z, i // 2, i % 2, 1 - c), part)
    spans, plain, seams = pieces(share, n)
    puts = []

    def put(number, k, low, high):
        copy = pltpu.make_async_copy(
            out_ref.at[k, pl.ds(low - spans[k][0], high - low)], outs[number].at[pl.ds(low - ENTRIES[number][3], high - low)], put_sem.at[len(puts)]
        )
        copy.start()
        puts.append(copy)

    home = {}
    for number, k, low, high in plain + seams:
        if number in SMALL:
            home.update({tile: (k, tile - spans[k][0]) for tile in range(low, high)})
        elif (number, k, low, high) in plain:
            put(number, k, low, high)
    for number, k, low, high in seams:
        left = pl.ds(low - spans[k][0], high - low)
        right = pl.ds(low - spans[k + 1][0], high - low)
        total = out_ref[k, left].astype(jnp.float32) + out_ref[k + 1, right].astype(jnp.float32)
        out_ref[k, left] = total.astype(out_ref.dtype)
        if number not in SMALL:
            put(number, k, low, high)
    for number, target in zip(SMALL, (enc_norms, dec_norms)):
        row, lines_, _, tile, groups = ENTRIES[number]
        per = SHAPES[number][1] // LANES
        for group in range(groups):
            k, at = home[tile + group]
            value = out_ref[k, at].astype(jnp.float32)
            for line in range(group * 8, min(group * 8 + 8, lines_)):
                target[line // per : line // per + 1, line % per * LANES : (line % per + 1) * LANES] = value[line % 8 : line % 8 + 1, :]
    masked_ref[...] = jnp.zeros_like(masked_ref)

    def count(k, _):
        masked_ref[...] += jnp.sum(out_ref[k, out_ref.shape[1] - 2].astype(jnp.float32)[0:1, :], axis=1, keepdims=True)
        return 0

    lax.fori_loop(0, n, count, 0)
    for copy in puts:
        copy.wait()


def gather(lines, extra, share, n_dp, n_pair):
    n_z = n_dp // 2
    n = n_dp * n_pair
    tiles_ = slab_tiles(share, n) + 2
    _, plain, seams = pieces(share, n)
    dma = pltpu.SemaphoreType.DMA
    anyspec = pl.BlockSpec(memory_space=pl.ANY)
    vmem = pl.BlockSpec(memory_space=pltpu.VMEM)

    def s(shape, kind=jnp.float32):
        return jax.ShapeDtypeStruct(shape, kind)

    return pl.pallas_call(
        functools.partial(gather_kernel, n_z, n_pair, share),
        name="gather",
        out_shape=[s((ENTRIES[i][4] * ENTRIES[i][2], 8, LANES), jnp.bfloat16) for i in BIG] + [s(SHAPES[5]), s(SHAPES[12]), s((1, 1))],
        in_specs=[vmem, vmem],
        out_specs=[anyspec] * len(BIG) + [vmem] * 3,
        scratch_shapes=[
            pltpu.VMEM((wide_rows(lines.shape[0]), LANES), jnp.float32),
            pltpu.VMEM((n, tiles_, 8, LANES), jnp.bfloat16),
            dma((n_z, 2, 2)), dma((n_z, 2, 6)), dma((n_z, 2, 2, 2)), dma((n_z, 2, 4)), dma((14,)), dma((n_z, 2, 4)), dma((n_z, 2, 4)), dma((n, 4)),
            dma((len(plain) + len(seams),)),
        ],
        compiler_params=pltpu.CompilerParams(collective_id=0, has_side_effects=True, vmem_limit_bytes=60 * MB),
    )(lines, extra)


def reduce_chunks(share, n):
    rows = slab_tiles(share, n) * 8
    return max(d for d in (1, 2, 4) if rows % (2 * BLOCK * d) == 0)


def late_cut(share):
    return -(-ENTRIES[7][0] * LANES // (share * 8))


def pack(value, q_ref, t_ref, b):
    top = jnp.max(jnp.abs(value), axis=0, keepdims=True)
    inverse = jnp.where(top > 1e-30, 32767.0 / jnp.maximum(top, 1e-30), 0.0)
    q_ref[pl.ds(pl.multiple_of(b * BLOCK, BLOCK), BLOCK), :] = jnp.round(value * inverse).astype(jnp.int32).astype(jnp.int16)
    t_ref[pl.ds(b, 1), :] = top * (1.0 / 32767.0)


def unpack(q_ref, t_ref, b):
    return q_ref[pl.ds(pl.multiple_of(b * BLOCK, BLOCK), BLOCK), :].astype(jnp.int32).astype(jnp.float32) * t_ref[pl.ds(b, 1), :]


def message(qs, ts, qr, tr, sem, to):
    return (
        pltpu.make_async_remote_copy(qs, qr, sem.at[0, 0], sem.at[0, 1], device_id=to, device_id_type=MESH),
        pltpu.make_async_remote_copy(ts, tr, sem.at[1, 0], sem.at[1, 1], device_id=to, device_id_type=MESH),
    )


def slab_start(share, n, k):
    if n > 64:
        return first_tile(share, k)
    starts = [a for a, _ in ranges(share, n)]
    found = starts[0]
    for i in range(1, n):
        found = jnp.where(k >= i, starts[i], found)
    return found


class Plane:
    def __init__(self, share, n, chunks, steps, plane_of, grad, sib, keep, base, scratch):
        self.share, self.n, self.chunks, self.steps, self.plane_of = share, n, chunks, steps, plane_of
        self.grad, self.sib, self.keep, self.base = grad, sib, keep, base
        (self.gbuf, self.rbuf, self.q1s, self.q1r, self.q2s, self.q2r, self.t1s, self.t1r, self.t2s, self.t2r,
         self.sib_sem, self.load_sem, self.s1_sem, self.s2_sem) = scratch
        self.z, self.x, self.y, self.c = place()
        self.to = partners(self.z, self.x, self.y, self.c)
        self.rows = keep.shape[1] // chunks
        self.half = self.rows // 2

    def tiles_of(self, s, xx, yy, core):
        k = slot_of(self.plane_of(s // self.chunks), xx, yy, core)
        return pl.ds(slab_start(self.share, self.n, k) + s % self.chunks * (self.rows // 8), self.rows // 8)

    def kept(self, s, part, b):
        return self.base + s // self.chunks, pl.ds(pl.multiple_of(s % self.chunks * self.rows + part * self.half + b * BLOCK, BLOCK), BLOCK)

    def sibling(self, s, q, at=None):
        return pltpu.make_async_remote_copy(
            self.grad.at[at if at is not None else pl.ds(0, self.rows // 8)],
            self.sib.at[s, q],
            self.sib_sem.at[0, s, q],
            self.sib_sem.at[1, s, q],
            device_id=self.to["c"],
            device_id_type=MESH,
        )

    def begin(self):
        def one(s, _):
            for q in range(4):
                self.sibling(s, q, self.tiles_of(s, q // 2, q % 2, 1 - self.c)).start()
            return 0

        lax.fori_loop(0, self.steps, one, 0)

    def loads(self, s, q, at=None):
        slot = s % 2
        return pltpu.make_async_copy(self.grad.at[at if at is not None else pl.ds(0, self.rows // 8)], self.gbuf.at[slot, q], self.load_sem.at[slot, q])

    def other(self, s):
        return pltpu.make_async_copy(self.sib.at[s], self.rbuf.at[s % 2], self.load_sem.at[s % 2, 4])

    def load(self, s):
        for q in range(4):
            self.loads(s, q, self.tiles_of(s, q // 2, q % 2, self.c)).start()
        for q in range(4):
            self.sibling(s, q).wait_recv()
        self.other(s).start()

    def each(self, body):
        def one(b, _):
            body(b)
            return 0

        lax.fori_loop(0, self.half // BLOCK, one, 0, unroll=self.half // BLOCK)

    def own(self, slot, q, part, b):
        at = pl.ds(part * (self.half // 8) + b * (BLOCK // 8), BLOCK // 8)
        return (self.gbuf[slot, q, at] + self.rbuf[slot, q, at]).reshape(BLOCK, LANES)

    def first_message(self, s, part):
        i = pl.ds(part * 2, 2)
        return message(self.q1s.at[s, i], self.t1s.at[s, i], self.q1r.at[s, i], self.t1r.at[s, i], self.s1_sem.at[s, part], self.to[("x", "y")[part]])

    def second_message(self, s, part):
        return message(
            self.q2s.at[s, part], self.t2s.at[s, part], self.q2r.at[s, part], self.t2r.at[s, part], self.s2_sem.at[s, part], self.to[("y", "x")[part]]
        )

    def quarter(self, part, other, mine):
        if part == 0:
            return (self.x if mine else 1 - self.x) * 2 + other
        return other * 2 + (self.y if mine else 1 - self.y)

    def stage_one(self, s):
        slot = s % 2
        for q in range(4):
            self.loads(s, q).wait()
        self.other(s).wait()
        for part in (0, 1):
            for other in (0, 1):
                q = self.quarter(part, other, False)
                i = part * 2 + other
                self.each(lambda b: pack(self.own(slot, q, part, b), self.q1s.at[s, i], self.t1s.at[s, i], b))
            for one in self.first_message(s, part):
                one.start()

    def stage_two(self, s):
        slot = s % 2
        for part in (0, 1):
            for one in self.first_message(s, part):
                one.wait_recv()
            here = (self.y, self.x)[part]
            away = self.quarter(part, 1 - here, True)
            i = part * 2 + 1 - here
            self.each(
                lambda b: pack(
                    self.own(slot, away, part, b) + unpack(self.q1r.at[s, i], self.t1r.at[s, i], b), self.q2s.at[s, part], self.t2s.at[s, part], b
                )
            )
            for one in self.second_message(s, part):
                one.start()
        for part in (0, 1):
            here = (self.y, self.x)[part]
            k = part * 2 + here

            def store(b, part=part, k=k):
                group, at = self.kept(s, part, b)
                self.keep[group, at, :] = self.own(slot, self.x * 2 + self.y, part, b) + unpack(self.q1r.at[s, k], self.t1r.at[s, k], b)

            self.each(store)

    def stage_three(self, s):
        for part in (0, 1):
            for one in self.second_message(s, part):
                one.wait_recv()

            def body(b, part=part):
                group, at = self.kept(s, part, b)
                self.keep[group, at, :] += unpack(self.q2r.at[s, part], self.t2r.at[s, part], b)

            self.each(body)

    def finish(self):
        def one(s, _):
            for q in range(4):
                self.sibling(s, q).wait_send()
            for part in (0, 1):
                for two in self.first_message(s, part):
                    two.wait_send()
                for two in self.second_message(s, part):
                    two.wait_send()
            return 0

        lax.fori_loop(0, self.steps, one, 0)


def message_scratch(part, *leads):
    half = part // 2
    marks = (half // BLOCK + 7) // 8 * 8
    return [pltpu.VMEM(lead + (half, LANES), jnp.int16) for lead in leads] + [pltpu.VMEM(lead + (marks, LANES), jnp.float32) for lead in leads]


def plane_scratch(steps, part):
    dma = pltpu.SemaphoreType.DMA
    return [
        pltpu.VMEM((2, 4, part // 8, 8, LANES), jnp.float32),
        pltpu.VMEM((2, 4, part // 8, 8, LANES), jnp.float32),
        *message_scratch(part, (steps, 4), (steps, 4), (steps, 2), (steps, 2)),
        dma((2, steps, 4)), dma((2, 5)), dma((steps, 2, 2, 2)), dma((steps, 2, 2, 2)),
    ]


def reduce_kernel(n_z, n_pair, chunks, share, grad_ref, late_ref, loss_in, lines_ref, total_ref, sib_ref,
                  wide, mine, shared, send_sem, recv_sem, keep, late_sem, zs, zr, tzs, tzr, z_sem, *scratch):
    z, x, y, c = place()
    to = partners(z, x, y, c)
    n = n_z * 2 * n_pair
    me = slot_of(z, x, y, c)
    cut = late_cut(share)
    steps, late = cut * chunks, (n_z - cut) * chunks
    home = jnp.where(z < cut, cut - 1, z)

    def order(j):
        low = z < cut // 2
        far = jnp.where(low, cut - 1 - j, j)
        moved = jnp.where(low, jnp.where(far > z, far, far - 1), jnp.where(far < z, far, far + 1))
        return jnp.where(z >= cut, j, jnp.where(j == cut - 1, z, moved))

    plane = Plane(share, n, chunks, steps, order, grad_ref, sib_ref, keep, 0, scratch)

    def z_message(spot, name):
        d = 0 if name == "up" else 1
        return message(zs.at[spot], tzs.at[spot], zr.at[d, spot], tzr.at[d, spot], z_sem.at[d, spot], to[name])

    def stage_four(group, chunk, zz):
        spot = zz * chunks + chunk

        def lines(part, b):
            return pl.ds(pl.multiple_of(chunk * plane.rows + part * plane.half + b * BLOCK, BLOCK), BLOCK)

        for d, name, has, onward in ((0, "up", z > 0, zz > z), (1, "down", z < n_z - 1, zz < z)):
            back = zz >= z if d == 0 else zz <= z

            @pl.when(both(has, back))
            def _():
                for one in z_message(spot, name):
                    one.wait_recv()
                for part in (0, 1):

                    def add(b, part=part):
                        keep[group, lines(part, b), :] += unpack(zr.at[d, spot, part], tzr.at[d, spot, part], b)

                    plane.each(add)

            @pl.when(onward)
            def _():
                for part in (0, 1):
                    plane.each(lambda b, part=part: pack(keep[group, lines(part, b), :], zs.at[spot, part], tzs.at[spot, part], b))
                for one in z_message(spot, name):
                    one.start()

    def spread_lines(line, tile, cols):
        for col in range(cols):
            wide[pl.ds(line + col, 8, stride=cols), :] = keep[home, pl.ds(pl.multiple_of((tile + col) * 8, 8), 8), :]

    count_lines = lines_ref.shape[0]
    tall = 128

    def by_lines(body):
        def one(i, _):
            body(pl.multiple_of(i * tall, tall), tall)
            return 0

        lax.fori_loop(0, count_lines // tall, one, 0)
        if count_lines % tall:
            body(count_lines // tall * tall, count_lines % tall)

    barrier = pltpu.get_barrier_semaphore()

    def peer(d):
        k = lax.rem(me + d, n)
        return {"dp": k // n_pair, "pair": lax.rem(k, n_pair)}

    def hello(d, _):
        pl.semaphore_signal(barrier, inc=1, device_id=peer(d), device_id_type=MESH)
        return 0

    lax.fori_loop(1, n, hello, 0)
    kept = pltpu.make_async_copy(late_ref, keep.at[pl.ds(cut, n_z - cut)], late_sem)
    kept.start()
    pl.semaphore_wait(barrier, n - 1)
    plane.begin()
    plane.load(0)
    kept.wait()
    lag = 0

    def turn(t, _):
        pl.when(t < steps)(lambda: plane.stage_one(t))
        pl.when(both(t >= 1, t <= steps))(lambda: plane.stage_two(t - 1))
        pl.when(t + 1 < steps)(lambda: plane.load(t + 1))
        pl.when(both(t >= 2, t <= steps + 1))(lambda: plane.stage_three(t - 2))
        early, main = t - z, t - 3 - lag
        pl.when(both(early >= 0, early < late))(lambda: stage_four(cut + early // chunks, lax.rem(early, chunks), cut + early // chunks))
        pl.when(both(main >= 0, main < steps))(lambda: stage_four(main // chunks, lax.rem(main, chunks), order(main // chunks)))
        return 0

    lax.fori_loop(0, max(steps + 3, late + n_z), turn, 0)
    tiled(share, me, spread_lines)
    lo, _ = line_span(share, me)
    mine[...] = jnp.zeros_like(mine)

    def squares(start, size):
        value = wide[pl.ds(MARGIN + start, size), :]
        if share % LANES:
            line = lax.broadcasted_iota(jnp.int32, (size, LANES), 0) + lo + start
            spot = line * LANES + lax.broadcasted_iota(jnp.int32, (size, LANES), 1)
            inside = jnp.logical_and(spot >= share * me, spot < share * (me + 1))
            value = jnp.where(inside, value, 0.0)
        lines_ref[pl.ds(start, size), :] = value
        mine[0:1, :] += jnp.sum(value * value, axis=0, keepdims=True)

    by_lines(squares)
    lane = lax.broadcasted_iota(jnp.int32, (1, LANES), 1)
    mine[1:2, :] = jnp.where(lane == 0, loss_in[0:1, 0:1], 0.0)
    shared[me] = mine[...]

    def send(d):
        return pltpu.make_async_remote_copy(mine, shared.at[me], send_sem.at[d], recv_sem.at[d], device_id=peer(d), device_id_type=MESH)

    def go(d, _):
        send(d).start()
        return 0

    def stop(d, _):
        send(d).wait()
        return 0

    lax.fori_loop(1, n, go, 0)
    plane.finish()

    def finish(spot, _):
        zz = spot // chunks
        for name, sent in (("up", zz > z), ("down", zz < z)):

            @pl.when(sent)
            def _():
                for one in z_message(spot, name):
                    one.wait_send()

        return 0

    lax.fori_loop(0, n_z * chunks, finish, 0)
    lax.fori_loop(1, n, stop, 0)

    def add(k, total):
        return total + shared[k]

    total = lax.fori_loop(0, n, add, jnp.zeros((8, LANES), jnp.float32))
    norm_ = jnp.sqrt(jnp.sum(total[0:1, :], axis=1, keepdims=True))
    loss_sum = jnp.sum(total[1:2, :], axis=1, keepdims=True)
    total_ref[...] = jnp.where(lax.broadcasted_iota(jnp.int32, (8, LANES), 0) == 0, norm_, loss_sum)


def reduce(flat, late, loss, shape, share, n_dp, n_pair):
    n_z, n = n_dp // 2, n_dp * n_pair
    chunks = reduce_chunks(share, n)
    rows = slab_tiles(share, n) * 8
    part = rows // chunks
    steps = late_cut(share) * chunks
    spots = n_z * chunks
    anyspec = pl.BlockSpec(memory_space=pl.ANY)
    vmem = pl.BlockSpec(memory_space=pltpu.VMEM)
    line = jax.ShapeDtypeStruct(shape, jnp.float32)
    dma = pltpu.SemaphoreType.DMA
    return pl.pallas_call(
        functools.partial(reduce_kernel, n_z, n_pair, chunks, share),
        name="reduce_scatter",
        out_shape=[line, jax.ShapeDtypeStruct((8, LANES), jnp.float32), jax.ShapeDtypeStruct((steps, 4, part // 8, 8, LANES), jnp.float32)],
        in_specs=[anyspec, anyspec, vmem],
        out_specs=[vmem, vmem, anyspec],
        scratch_shapes=[
            pltpu.VMEM((wide_rows(shape[0]), LANES), jnp.float32),
            pltpu.VMEM((8, LANES), jnp.float32),
            pltpu.VMEM((n, 8, LANES), jnp.float32),
            dma((n,)),
            dma((n,)),
            pltpu.VMEM((n_z, rows, LANES), jnp.float32),
            dma,
            *message_scratch(part, (spots, 2), (2, spots, 2)),
            dma((2, spots, 2, 2)),
            *plane_scratch(steps, part),
        ],
        compiler_params=pltpu.CompilerParams(collective_id=1, has_side_effects=True, vmem_limit_bytes=60 * MB),
    )(flat, late, loss)[:2]


NEG_FILL = -1000000000.0
P_ROWS = 208
BF = jnp.bfloat16
F32 = jnp.float32


def dot_nn(left, right):
    return lax.dot_general(left, right, (((1,), (0,)), ((), ())), preferred_element_type=F32)


def dot_nt(left, right):
    return lax.dot_general(left, right, (((1,), (1,)), ((), ())), preferred_element_type=F32)


def loop(count, body, unroll=1):
    def step(i, _):
        body(i)
        return 0

    lax.fori_loop(0, count, step, 0, unroll=unroll)


def rows_at(i, size):
    return pl.ds(pl.multiple_of(i * size, size), size)


def norm(x):
    centered = x - jnp.mean(x, axis=-1, keepdims=True)
    scale = lax.rsqrt(jnp.mean(centered * centered, axis=-1, keepdims=True) + NORM_EPS)
    return centered * scale, scale


def norm_grad(grad, plain, scale, gain):
    inner = grad * gain
    back = scale * (inner - jnp.mean(inner, axis=-1, keepdims=True) - plain * jnp.mean(inner * plain, axis=-1, keepdims=True))
    return back, jnp.sum(grad * plain, axis=0, keepdims=True), jnp.sum(grad, axis=0, keepdims=True)


def gelu_pair(h):
    cumulative = 0.5 * (1.0 + lax.erf(h * 0.7071067811865476))
    density = jnp.exp(-0.5 * h * h) * 0.3989422804014327
    return h * cumulative, cumulative + h * density


def head_masks(size):
    lane = lax.broadcasted_iota(jnp.int32, (1, LANES), 1)
    shift = size.bit_length() - 1
    return [jnp.where((lane >> shift) == h, 1.0, 0.0).astype(BF) for h in range(LANES // size)]


def three(value):
    top = value.astype(BF)
    rest = value - top.astype(F32)
    mid = rest.astype(BF)
    return top, mid, (rest - mid.astype(F32)).astype(BF)


class Moves:
    def __init__(self, names, sources, targets, sems):
        self.targets = dict(zip(names, targets))
        self.copies = {name: pltpu.make_async_copy(a, b, sems.at[i]) for i, (name, a, b) in enumerate(zip(names, sources, targets))}
        self.open = []

    def start(self, *names):
        for name in names or self.copies:
            self.copies[name].start()
            self.open.append(name)

    def __call__(self, name):
        if name in self.open:
            self.copies[name].wait()
            self.open.remove(name)
        return self.targets[name]

    def close(self):
        for name in list(self.open):
            self(name)


def wide_attention(width, heads, rows, triple, bias, probs, mixed):
    size = width // heads
    per = LANES // size
    masks = head_masks(size)
    for g in range(width // LANES):
        q, k, v = (triple[:, t * width + g * LANES : t * width + (g + 1) * LANES] for t in range(3))
        v_side = v.T
        parts = []
        for h in range(per):
            s = dot_nt(k * masks[h], q) * size ** (-0.5) + bias[...]
            e = jnp.exp(s - jnp.max(s, axis=0, keepdims=True))
            p = e * (1.0 / jnp.sum(e, axis=0, keepdims=True))
            probs[g * per + h] = p
            parts.append(dot_nn(v_side[h * size : (h + 1) * size, :], p.astype(BF)))
        mixed[:, g * LANES : (g + 1) * LANES] = jnp.concatenate(parts, axis=0).T.astype(BF)


def wide_attention_back(width, heads, triple, probs, low_mixed, grad_triple):
    size = width // heads
    per = LANES // size
    masks = head_masks(size)
    for g in range(width // LANES):
        lanes = [slice(t * width + g * LANES, t * width + (g + 1) * LANES) for t in range(3)]
        q, k, v = (triple[:, lane] for lane in lanes)
        dm = low_mixed[:, g * LANES : (g + 1) * LANES]
        k_side = k.T
        parts, dk, dv = [], 0.0, 0.0
        for h in range(per):
            p = probs[g * per + h]
            dp = dot_nt(v * masks[h], dm)
            ds = (p * (dp - jnp.sum(p * dp, axis=0, keepdims=True))).astype(BF)
            dv = dv + dot_nn(p.astype(BF), dm * masks[h])
            dk = dk + dot_nn(ds, q * masks[h])
            parts.append(dot_nn(k_side[h * size : (h + 1) * size, :], ds))
        grad_triple[:, lanes[0]] = (jnp.concatenate(parts, axis=0).T * size ** (-0.5)).astype(BF)
        grad_triple[:, lanes[1]] = (dk * size ** (-0.5)).astype(BF)
        grad_triple[:, lanes[2]] = dv.astype(BF)


def block_forward(x, rows, images, heads, need, norms, key_bias, saved, done=lambda *names: None):
    entry, plain1, scale1, triple, probs, mixed, plain2, scale2, inner, act, slope = saved
    width = x.shape[1]
    size = width // heads
    per = LANES // size
    groups = width // LANES

    def first(i):
        at = rows_at(i, rows)
        plain, scale = norm(x[at, :])
        plain1[at, :] = plain
        scale1[at, :] = scale
        entry[at, :] = (plain * norms[0:1, :] + norms[1:2, :]).astype(BF)

    loop(images, first, 2)

    done("entry", "plain1", "scale1")
    triple_w = need("triple_w")

    def project(j):
        at = rows_at(j, 256)
        triple[:, at] = dot_nn(entry[...], triple_w[:, at]).astype(BF)

    loop(3 * width // 256, project, 3)
    done("triple")
    masks = head_masks(size)

    def attend(i):
        at = rows_at(i, rows)
        bias = key_bias(i)
        for g in range(groups):
            q = triple[at, g * LANES : (g + 1) * LANES]
            k = triple[at, width + g * LANES : width + (g + 1) * LANES]
            v = triple[at, 2 * width + g * LANES : 2 * width + (g + 1) * LANES]
            v_side = v.T
            parts = []
            for h in range(per):
                s = dot_nt(k * masks[h], q) * size ** (-0.5) + bias
                e = jnp.exp(s - jnp.max(s, axis=0, keepdims=True))
                p = e * (1.0 / jnp.sum(e, axis=0, keepdims=True))
                probs[i * groups + g, h * rows : (h + 1) * rows, :] = p
                parts.append(dot_nn(v_side[h * size : (h + 1) * size, :], p.astype(BF)))
            mixed[at, g * LANES : (g + 1) * LANES] = jnp.concatenate(parts, axis=0).T.astype(BF)

    if callable(key_bias):
        loop(images, attend)
    else:
        wide_attention(width, heads, rows, triple, key_bias, probs, mixed)
    done("probs", "mixed")
    proj_w = need("proj_w")

    def middle(j):
        at = rows_at(j, 256)
        x[:, at] += dot_nn(mixed[...], proj_w[:, at])

    loop(width // 256, middle, width // 256)

    def second(i):
        at = rows_at(i, rows)
        plain, scale = norm(x[at, :])
        plain2[at, :] = plain
        scale2[at, :] = scale
        inner[at, :] = (plain * norms[2:3, :] + norms[3:4, :]).astype(BF)

    loop(images, second, 2)
    done("plain2", "scale2", "inner")
    up_w = need("up_w")
    hidden = up_w.shape[1]

    def up(j):
        at = rows_at(j, 256)
        value, gradient = gelu_pair(dot_nn(inner[...], up_w[:, at]))
        act[:, at] = value.astype(BF)
        slope[:, at] = gradient

    loop(hidden // 256, up, 4)
    done("act", "slope")
    down_w = need("down_w")

    def down(j):
        at = rows_at(j, 256)
        x[:, at] += dot_nn(act[...], down_w[:, at])

    loop(width // 256, down, width // 256)


class Writer:
    def __init__(self, flat, stage, sem):
        self.flat, self.stage, self.sem = flat, stage, sem
        self.pending = {}

    def settle(self, s):
        if s in self.pending:
            self.pending.pop(s).wait()

    def outer(self, number, left, right, chunk=256):
        _, _, cols, tile, _ = ENTRIES[number]
        rows = left.shape[1]
        count = rows // chunk
        tall = chunk // 8
        before = dict(self.pending)

        def copy(i, s):
            return pltpu.make_async_copy(
                self.stage.at[s, pl.ds(0, tall * cols)], self.flat.at[pl.ds(tile + i * tall * cols, tall * cols)], self.sem.at[s]
            )

        def body(i):
            s = lax.rem(i, 2)
            for early in before:
                pl.when(i == early)(before[early].wait)

            @pl.when(i >= 2)
            def _():
                copy(i - 2, s).wait()

            side = left[:, rows_at(i, chunk)].T
            for c in range(0, cols, 2):
                value = dot_nn(side, right[:, c * LANES : (c + 2) * LANES])
                for d in range(2):
                    self.stage[s, pl.ds(c + d, tall, stride=cols)] = value[:, d * LANES : (d + 1) * LANES].reshape(tall, 8, LANES)
            copy(i, s).start()

        loop(count, body)
        self.pending = {(count - 2) % 2: copy(count - 2, (count - 2) % 2), (count - 1) % 2: copy(count - 1, (count - 1) % 2)}

    def small(self, number, norm_sums, count, extra=0):
        _, _, _, tile, groups = ENTRIES[number]
        per = SHAPES[number][1] // LANES
        self.settle(0)
        self.stage[0, 0 : groups + extra] = jnp.zeros((groups + extra, 8, LANES), F32)
        for r in range(count):
            for c in range(per):
                line = r * per + c
                self.stage[0, line // 8, line % 8 : line % 8 + 1, :] = norm_sums[r : r + 1, c * LANES : (c + 1) * LANES]
        copy = pltpu.make_async_copy(self.stage.at[0, pl.ds(0, groups + extra)], self.flat.at[pl.ds(tile, groups + extra)], self.sem.at[0])
        copy.start()
        copy.wait()
        self.settle(1)


def block_backward(grad, rows, images, heads, need, norms, norm_sums, extra, writer, numbers, tick=lambda: None):
    low, grad_hidden, side, low_mixed, grad_triple = extra
    width = grad.shape[1]
    size = width // heads
    per = LANES // size
    groups = width // LANES
    low[...] = grad[...].astype(BF)
    down_w, slope = need("down_w"), need("slope")
    hidden = down_w.shape[0]

    def back_up(j):
        at = rows_at(j, 256)
        grad_hidden[:, at] = (dot_nt(low[...], down_w[at, :]) * slope[:, at]).astype(BF)

    loop(hidden // 256, back_up, 4)
    tick()
    writer.outer(numbers[3], need("act"), low)
    tick()
    writer.outer(numbers[2], need("inner"), grad_hidden)
    tick()
    up_w = need("up_w")

    def back_inner(j):
        at = rows_at(j, 256)
        side[:, at] = dot_nt(grad_hidden[...], up_w[at, :])

    loop(width // 256, back_inner, width // 256)
    tick()
    plain2, scale2 = need("plain2"), need("scale2")

    def second(i):
        at = rows_at(i, rows)
        back, gain, shift = norm_grad(side[at, :], plain2[at, :], scale2[at, :], norms[2:3, :])
        norm_sums[2:3, :] += gain
        norm_sums[3:4, :] += shift
        total = grad[at, :] + back
        grad[at, :] = total
        low[at, :] = total.astype(BF)

    loop(images, second, 2)
    writer.outer(numbers[1], need("mixed"), low)
    proj_w = need("proj_w")

    def back_mixed(j):
        at = rows_at(j, 256)
        low_mixed[:, at] = dot_nt(low[...], proj_w[at, :]).astype(BF)

    loop(width // 256, back_mixed, width // 256)
    tick()
    triple, probs = need("triple"), need("probs")
    masks = head_masks(size)

    def attend(i):
        at = rows_at(i, rows)
        for g in range(groups):
            lanes = [slice(t * width + g * LANES, t * width + (g + 1) * LANES) for t in range(3)]
            q, k, v = (triple[at, lane] for lane in lanes)
            dm = low_mixed[at, g * LANES : (g + 1) * LANES]
            k_side = k.T
            parts, dk, dv = [], 0.0, 0.0
            for h in range(per):
                p = probs[i * groups + g, h * rows : (h + 1) * rows, :]
                dp = dot_nt(v * masks[h], dm)
                ds = (p * (dp - jnp.sum(p * dp, axis=0, keepdims=True))).astype(BF)
                dv = dv + dot_nn(p.astype(BF), dm * masks[h])
                dk = dk + dot_nn(ds, q * masks[h])
                parts.append(dot_nn(k_side[h * size : (h + 1) * size, :], ds))
            dq = jnp.concatenate(parts, axis=0).T
            grad_triple[at, lanes[0]] = (dq * size ** (-0.5)).astype(BF)
            grad_triple[at, lanes[1]] = (dk * size ** (-0.5)).astype(BF)
            grad_triple[at, lanes[2]] = dv.astype(BF)

    if probs.shape[1] == probs.shape[2] and probs.shape[0] == heads:
        wide_attention_back(width, heads, triple, probs, low_mixed, grad_triple)
    else:
        loop(images, attend)
    tick()
    writer.outer(numbers[0], need("entry"), grad_triple)
    tick()
    triple_w = need("triple_w")

    def back_entry(j):
        at = rows_at(j, 256)
        side[:, at] = dot_nt(grad_triple[...], triple_w[at, :])

    loop(width // 256, back_entry, width // 256)
    tick()
    plain1, scale1 = need("plain1"), need("scale1")

    def first(i):
        at = rows_at(i, rows)
        back, gain, shift = norm_grad(side[at, :], plain1[at, :], scale1[at, :], norms[0:1, :])
        norm_sums[0:1, :] += gain
        norm_sums[1:2, :] += shift
        grad[at, :] += back

    loop(images, first, 2)


TICKS = 11
SAVED = ("seen", "entry", "plain1", "scale1", "triple", "probs", "mixed", "plain2", "scale2", "inner", "act", "slope", "plain3", "scale3", "encoded")
ENC_NAMES = ("embed_w", "triple_w", "proj_w", "up_w", "down_w", "dec_embed_w")
DEC_NAMES = ("triple_w", "proj_w", "up_w", "down_w", "head_w")


def saved_shapes(rows):
    s = jax.ShapeDtypeStruct
    return [
        s((rows, D), BF), s((rows, D), BF), s((rows, D), F32), s((rows, 1), F32), s((rows, 3 * D), BF),
        s((HEADS, rows, rows), F32), s((rows, D), BF), s((rows, D), F32), s((rows, 1), F32), s((rows, D), BF),
        s((rows, F), BF), s((rows, F), F32), s((rows, D), F32), s((rows, 1), F32), s((rows, D), BF),
    ]


def like(shape):
    return pltpu.VMEM(shape.shape, shape.dtype)


def pad_patches(patches, padded, images):
    padded[...] = jnp.zeros_like(padded)
    for i in range(images):
        padded[i * P_ROWS : i * P_ROWS + PATCHES, :] = patches[i]


def encoder_kernel(images, counts_ref, rows_ref, norms_ref, *refs):
    pos_hbm, patches_hbm, *weights_hbm = refs[:8]
    outs = refs[8:23]
    entering = refs[23]
    pos, patches, *weights = refs[24:32]
    saved = dict(zip(SAVED, refs[32:47]))
    x, place_, pos_split, padded, bias, in_sem, out_sem = refs[47:]
    need = Moves(("pos", "patches") + ENC_NAMES, [pos_hbm, patches_hbm] + weights_hbm, [pos, patches] + weights, in_sem)
    need.start()
    put = Moves(SAVED, [saved[name] for name in SAVED], outs, out_sem)
    rows = images * KEEP
    key = lax.broadcasted_iota(jnp.int32, (KEEP, rows), 0)
    query = lax.broadcasted_iota(jnp.int32, (KEEP, rows), 1)
    for i in range(images):
        inside = jnp.logical_and(jnp.logical_and(query >= i * KEEP, query < (i + 1) * KEEP), key < counts_ref[i])
        bias[i * KEEP : (i + 1) * KEEP, :] = jnp.where(inside, 0.0, NEG_FILL)
    need("pos")
    for t, part in enumerate(three(pos[...])):
        pos_split[t] = part
    pad_patches(need("patches"), padded, images)
    spot = lax.broadcasted_iota(jnp.int32, (P_ROWS, KEEP), 0)
    seen = saved["seen"]

    def select(i):
        at = rows_at(i, KEEP)
        pick = jnp.where(spot == rows_ref[pl.ds(i, 1), 0:KEEP], 1.0, 0.0).T.astype(BF)
        seen[at, :] = dot_nn(pick, padded[rows_at(i, P_ROWS), :]).astype(BF)
        place_[at, :] = dot_nn(pick, pos_split[0]) + dot_nn(pick, pos_split[1]) + dot_nn(pick, pos_split[2])

    loop(images, select, 2)
    put.start("seen")
    embed_w = need("embed_w")

    def embed(j):
        at = rows_at(j, 256)
        x[:, at] = dot_nn(seen[...], embed_w[:, at]) + place_[:, at]

    loop(D // 256, embed, D // 256)
    block_forward(x, KEEP, images, HEADS, need, norms_ref, bias, [saved[name] for name in SAVED[1:12]], put.start)
    plain3, scale3, encoded = (saved[name] for name in SAVED[12:])

    def last(i):
        at = rows_at(i, KEEP)
        plain, scale = norm(x[at, :])
        plain3[at, :] = plain
        scale3[at, :] = scale
        encoded[at, :] = (plain * norms_ref[4:5, :] + norms_ref[5:6, :]).astype(BF)

    loop(images, last, 2)
    put.start("plain3", "scale3", "encoded")
    entering[...] = dot_nn(encoded[...], need("dec_embed_w")[...])
    put.close()


def encoder(counts, patches, order, pos, weights, norms):
    images = counts.shape[0]
    rows = images * KEEP
    vmem = pl.BlockSpec(memory_space=pltpu.VMEM)
    anyspec = pl.BlockSpec(memory_space=pl.ANY)
    shapes = saved_shapes(rows)
    return pl.pallas_call(
        functools.partial(encoder_kernel, images),
        name="encoder",
        out_shape=shapes + [jax.ShapeDtypeStruct((rows, DD), F32)],
        in_specs=[pl.BlockSpec(memory_space=pltpu.SMEM), vmem, vmem] + [anyspec] * 8,
        out_specs=[anyspec] * 15 + [vmem],
        scratch_shapes=[like(one) for one in [pos, patches] + weights + shapes]
        + [
            pltpu.VMEM((rows, D), F32), pltpu.VMEM((rows, D), F32), pltpu.VMEM((3, P_ROWS, D), BF), pltpu.VMEM((images * P_ROWS, PIX), BF),
            pltpu.VMEM((rows, rows), F32), pltpu.SemaphoreType.DMA((8,)), pltpu.SemaphoreType.DMA((15,)),
        ],
        compiler_params=pltpu.CompilerParams(vmem_limit_bytes=60 * MB),
    )(counts, order, norms, pos, patches, *weights)


def decoder_kernel(images, counts_ref, masked_ref, rows_ref, entering_ref, norms_ref, *refs):
    pos_hbm, patches_hbm, *weights_hbm = refs[:7]
    flat, grad_entering, loss_ref = refs[7:10]
    pos, patches, *weights = refs[10:17]
    (x, hide, entry, plain1, scale1, triple, probs, mixed, plain2, scale2, inner, act, slope, plain3, scale3, final, grad_pred,
     low, grad_hidden, side, low_mixed, grad_triple, norm_sums, padded, stage, sem, in_sem) = refs[17:]
    need = Moves(("pos", "patches") + DEC_NAMES, [pos_hbm, patches_hbm] + weights_hbm, [pos, patches] + weights, in_sem)
    need.start()
    saved = (entry, plain1, scale1, triple, probs, mixed, plain2, scale2, inner, act, slope)
    need.targets.update(zip(SAVED[1:12], saved))
    lane = lax.broadcasted_iota(jnp.int32, (P_ROWS, KEEP), 1)
    spot = lax.broadcasted_iota(jnp.int32, (P_ROWS, KEEP), 0)
    line = lax.broadcasted_iota(jnp.int32, (P_ROWS, 1), 0)
    need("pos")

    def start(i):
        at = rows_at(i, P_ROWS)
        hit = jnp.where(jnp.logical_and(spot == rows_ref[pl.ds(i, 1), 0:KEEP], lane < counts_ref[i]), 1.0, 0.0)
        shown = jnp.max(hit, axis=1, keepdims=True)
        pick = hit.astype(BF)
        top, mid, end = three(entering_ref[rows_at(i, KEEP), :])
        picked = dot_nn(pick, top) + dot_nn(pick, mid) + dot_nn(pick, end)
        x[at, :] = jnp.where(shown > 0.0, picked, norms_ref[6:7, :]) + pos[...]
        hide[at, :] = jnp.where(jnp.logical_and(line < PATCHES, shown == 0.0), 1.0, 0.0)

    loop(images, start, 2)
    bias = jnp.where(line < PATCHES, 0.0, NEG_FILL)
    block_forward(x, P_ROWS, images, DHEADS, need, norms_ref, lambda i: bias, saved)

    def last(i):
        at = rows_at(i, P_ROWS)
        plain, scale = norm(x[at, :])
        plain3[at, :] = plain
        scale3[at, :] = scale
        final[at, :] = (plain * norms_ref[4:5, :] + norms_ref[5:6, :]).astype(BF)

    loop(images, last, 2)
    loss_ref[...] = jnp.zeros_like(loss_ref)
    masked = masked_ref[0:1, 0:1]
    head_w = need("head_w")
    pad_patches(need("patches"), padded, images)

    def score(i):
        at = rows_at(i, P_ROWS)
        target, _ = norm(padded[at, :].astype(F32))
        diff = dot_nn(final[at, :], head_w[...]) - target
        hidden = hide[at, :]
        loss_ref[...] += jnp.sum(jnp.mean(diff * diff, axis=-1, keepdims=True) * hidden, axis=0, keepdims=True)
        grad_pred[at, :] = (diff * (hidden * (2.0 / PIX)) / masked).astype(BF)

    loop(images, score, 2)
    writer = Writer(flat, stage, sem)
    writer.outer(11, final, grad_pred)
    norm_sums[...] = jnp.zeros_like(norm_sums)

    def back_final(i):
        at = rows_at(i, P_ROWS)
        back, gain, shift = norm_grad(dot_nt(grad_pred[at, :], head_w[...]), plain3[at, :], scale3[at, :], norms_ref[4:5, :])
        norm_sums[4:5, :] += gain
        norm_sums[5:6, :] += shift
        x[at, :] = back

    loop(images, back_final, 2)
    block_backward(x, P_ROWS, images, DHEADS, need, norms_ref, norm_sums, (low, grad_hidden, side, low_mixed, grad_triple), writer, (7, 8, 9, 10))

    def finish(i):
        at = rows_at(i, P_ROWS)
        grad = x[at, :]
        norm_sums[6:7, :] += jnp.sum(grad * hide[at, :], axis=0, keepdims=True)
        pick = jnp.where(jnp.logical_and(spot == rows_ref[pl.ds(i, 1), 0:KEEP], lane < counts_ref[i]), 1.0, 0.0).T.astype(BF)
        grad_entering[rows_at(i, KEEP), :] = dot_nn(pick, grad.astype(BF)).astype(BF)

    loop(images, finish, 2)
    writer.small(12, norm_sums, 7, flat.shape[0] - TILES)


def decoder(total, counts, masked, patches, order, pos, entering, weights, norms):
    images = counts.shape[0]
    rows = images * P_ROWS
    vmem = pl.BlockSpec(memory_space=pltpu.VMEM)
    anyspec = pl.BlockSpec(memory_space=pl.ANY)

    def v(shape, kind=F32):
        return pltpu.VMEM(shape, kind)

    return pl.pallas_call(
        functools.partial(decoder_kernel, images),
        name="decoder",
        out_shape=[
            jax.ShapeDtypeStruct((total, 8, LANES), F32),
            jax.ShapeDtypeStruct((images * KEEP, DD), BF),
            jax.ShapeDtypeStruct((1, 1), F32),
        ],
        in_specs=[pl.BlockSpec(memory_space=pltpu.SMEM)] + [vmem] * 4 + [anyspec] * 7,
        out_specs=[anyspec, vmem, vmem],
        scratch_shapes=[like(one) for one in [pos, patches] + weights]
        + [
            v((rows, DD)), v((rows, 1)), v((rows, DD), BF), v((rows, DD)), v((rows, 1)), v((rows, 3 * DD), BF),
            v((images * DD // LANES, 4 * P_ROWS, P_ROWS)), v((rows, DD), BF), v((rows, DD)), v((rows, 1)), v((rows, DD), BF),
            v((rows, FD), BF), v((rows, FD)), v((rows, DD)), v((rows, 1)), v((rows, DD), BF), v((rows, PIX), BF),
            v((rows, DD), BF), v((rows, FD), BF), v((rows, DD)), v((rows, DD), BF), v((rows, 3 * DD), BF),
            v((8, DD)), v((rows, PIX), BF), v((2, 32 * 16, 8, LANES)), pltpu.SemaphoreType.DMA((2,)), pltpu.SemaphoreType.DMA((7,)),
        ],
        compiler_params=pltpu.CompilerParams(vmem_limit_bytes=63 * MB),
    )(counts, masked, order, entering, norms, pos, patches, *weights)


def encoder_back_kernel(images, share, n, chunks, flat_in, grad_entering, norms_ref, *refs):
    names = SAVED + ENC_NAMES[1:]
    sources = refs[:20]
    flat, late_ref, sib_ref = refs[20:23]
    targets = refs[23:43]
    x, low, grad_hidden, side, low_mixed, grad_triple, norm_sums, stage, sem, in_sem = refs[43:53]
    cut = late_cut(share)
    steps = late_ref.shape[0] * chunks
    plane = Plane(share, n, chunks, steps, lambda group: cut + group, flat, sib_ref, late_ref, 0, refs[53:])
    barrier = pltpu.get_barrier_semaphore()
    for name in ("x", "y", "c"):
        pl.semaphore_signal(barrier, inc=1, device_id=plane.to[name], device_id_type=MESH)
    need = Moves(names, sources, targets, in_sem)
    need.start(
        "encoded", "dec_embed_w", "plain3", "scale3", "down_w", "slope", "act", "inner", "up_w", "plain2", "scale2",
        "mixed", "proj_w", "triple", "probs", "entry", "triple_w", "plain1", "scale1", "seen",
    )
    pl.semaphore_wait(barrier, 3)
    plane.begin()
    one, two, three_, load = plane.stage_one, plane.stage_two, plane.stage_three, plane.load
    if steps == 4:
        plan = [
            [], [(load, 0)], [(one, 0), (load, 1)], [(one, 1)], [(two, 0), (load, 2)], [(one, 2), (two, 1), (load, 3)],
            [(one, 3)], [(two, 2), (three_, 0), (three_, 1)], [(two, 3)], [(three_, 2)], [(three_, 3)],
        ]
    else:
        flow = [(load, 0)]
        for t in range(steps + 2):
            flow += [(stage_, s) for stage_, s in ((one, t), (two, t - 1), (load, t + 1), (three_, t - 2)) if 0 <= s < steps]
        size = -(-len(flow) // TICKS)
        plan = [flow[i * size : (i + 1) * size] for i in range(TICKS)]

    def tick():
        for stage_, s in plan.pop(0):
            stage_(s)

    writer = Writer(flat, stage, sem)
    writer.outer(6, need("encoded"), grad_entering)
    norm_sums[...] = jnp.zeros_like(norm_sums)
    side[...] = dot_nt(grad_entering[...], need("dec_embed_w")[...])
    plain3, scale3 = need("plain3"), need("scale3")

    def last(i):
        at = rows_at(i, KEEP)
        back, gain, shift = norm_grad(side[at, :], plain3[at, :], scale3[at, :], norms_ref[4:5, :])
        norm_sums[4:5, :] += gain
        norm_sums[5:6, :] += shift
        x[at, :] = back

    loop(images, last, 2)
    tick()
    block_backward(x, KEEP, images, HEADS, need, norms_ref, norm_sums, (low, grad_hidden, side, low_mixed, grad_triple), writer, (1, 2, 3, 4), tick)
    low[...] = x[...].astype(BF)
    tick()
    writer.outer(0, need("seen"), low)
    tick()
    writer.small(5, norm_sums, 6)
    plane.finish()


def encoder_back(flat, grad_entering, saved, weights, norms, share, n_dp, n_pair):
    chunks = reduce_chunks(share, n_dp * n_pair)
    slab = slab_tiles(share, n_dp * n_pair) * 8
    groups = n_dp // 2 - late_cut(share)
    part = slab // chunks
    rows = grad_entering.shape[0]
    images = rows // KEEP
    vmem = pl.BlockSpec(memory_space=pltpu.VMEM)
    anyspec = pl.BlockSpec(memory_space=pl.ANY)

    def v(shape, kind=F32):
        return pltpu.VMEM(shape, kind)

    return pl.pallas_call(
        functools.partial(encoder_back_kernel, images, share, n_dp * n_pair, chunks),
        name="encoder_back",
        out_shape=[
            jax.ShapeDtypeStruct(flat.shape, flat.dtype),
            jax.ShapeDtypeStruct((groups, slab, LANES), F32),
            jax.ShapeDtypeStruct((groups * chunks, 4, part // 8, 8, LANES), F32),
        ],
        in_specs=[anyspec, vmem, vmem] + [anyspec] * 20,
        out_specs=[anyspec, vmem, anyspec],
        scratch_shapes=[like(one) for one in saved + weights]
        + [
            v((rows, D)), v((rows, D), BF), v((rows, F), BF), v((rows, D)), v((rows, D), BF), v((rows, 3 * D), BF),
            v((8, D)), v((2, 32 * 24, 8, LANES)), pltpu.SemaphoreType.DMA((2,)), pltpu.SemaphoreType.DMA((20,)),
        ]
        + plane_scratch(groups * chunks, part),
        input_output_aliases={0: 0},
        compiler_params=pltpu.CompilerParams(collective_id=2, has_side_effects=True, vmem_limit_bytes=63 * MB),
    )(flat, grad_entering, norms, *saved, *weights)[:2]


def positions(width):
    index = np.arange(PATCHES)
    quarter = width // 4
    freq = 10000.0 ** (-np.arange(quarter).astype(np.float32) / np.float32(quarter))
    row = (index // GRID).astype(np.float32)[:, None] * freq[None, :].astype(np.float32)
    column = (index % GRID).astype(np.float32)[:, None] * freq[None, :].astype(np.float32)
    table = np.concatenate([np.sin(row), np.cos(row), np.sin(column), np.cos(column)], axis=1).astype(np.float32)
    return jnp.asarray(np.pad(table, ((0, P_ROWS - PATCHES), (0, 0))))


def own_lines(flat, share, index):
    if share % LANES == 0:
        return flat.reshape(-1, LANES)
    rows = (share + LANES - 1) // LANES + 1
    return lax.dynamic_update_slice(jnp.zeros((rows * LANES,), flat.dtype), flat, (share * index % LANES,)).reshape(rows, LANES)


def own_flat(lines, share, index):
    if share % LANES == 0:
        return lines.reshape(-1)
    return lax.dynamic_slice(lines.reshape(-1), (share * index % LANES,), (share,))


def body(n_dp, n_pair, patches, patch_order, counts, master, moment1, moment2, block_rates, clip_limit, step_count):
    n = n_dp * n_pair
    share = master.shape[0]
    images = counts.shape[0]
    index = lax.axis_index("dp") * n_pair + lax.axis_index("pair")
    extra = jnp.zeros((8, LANES), F32).at[0, :images].set((PATCHES - counts).astype(F32))
    lines = own_lines(master, share, index)
    *held, enc_norms, dec_norms, masked = gather(lines, extra, share, n_dp, n_pair)
    parts = {i: matrix(one, i) for i, one in zip(BIG, held)}
    enc_weights = [parts[i] for i in (1, 2, 3, 4, 6)]
    *saved, entering = encoder(counts, patches, patch_order[:, :KEEP], positions(D), [parts[0]] + enc_weights, enc_norms)
    total = max(a for a, _ in ranges(share, n)) + slab_tiles(share, n)
    dec_weights = [parts[i] for i in (7, 8, 9, 10, 11)]
    flat, grad_entering, loss_local = decoder(total, counts, masked, patches, patch_order[:, :KEEP], positions(DD), entering, dec_weights, dec_norms)
    flat, late = encoder_back(flat, grad_entering, saved, enc_weights, enc_norms, share, n_dp, n_pair)
    grad_lines, totals = reduce(flat, late, loss_local, lines.shape, share, n_dp, n_pair)
    grad_norm = totals[0, 0:1]
    loss = totals[1, 0:1] / masked[0]
    clipped = own_flat(grad_lines, share, index) * (clip_limit[0] / (grad_norm[0] + NORM_EPS))
    first = BETA_ONE * moment1 + (1.0 - BETA_ONE) * clipped
    second = BETA_TWO * moment2 + (1.0 - BETA_TWO) * clipped * clipped
    steps_done = step_count[0].astype(F32)
    position = index * share + jnp.arange(share)
    rate = jnp.where(position < ENC_PARAMS, block_rates[0], block_rates[1])
    update = first / (1.0 - BETA_ONE**steps_done) / (jnp.sqrt(second / (1.0 - BETA_TWO**steps_done)) + ADAM_EPS)
    master_new = master - rate * (update + DECAY * master)
    return (loss, grad_norm, first, second, master_new)


def solution(mesh):
    whole = P(("dp", "pair"))
    in_specs = (P(("dp", "pair"), None, None), P(("dp", "pair"), None), whole, whole, whole, whole, P(), P(), P())
    out_specs = (P(), P(), whole, whole, whole)
    step = functools.partial(body, mesh.shape["dp"], mesh.shape["pair"])
    return jax.shard_map(step, mesh=mesh, in_specs=in_specs, out_specs=out_specs, check_vma=False)
```
